32 devices in a mesh: segment: 4 (over z), seq: 4 (over y, core), dp: 2 (over x).
Axes of the slice: x: 2, y: 2, z: 4, core: 2. Of those that a mesh axis runs over, the one named last changes fastest.
Arguments:
- clean: bfloat16 [2, 512, 64], P('dp', 'seq'), may hold values from -16 to 16
- noise: bfloat16 [2, 512, 128], P('dp', 'seq'), may hold values from -24 to 24
- timesteps: int32 [2, 2], replicated, may hold values from 20 to 979
- text_vec: float32 [2, 256], P('dp'), may hold values from -6 to 6
- w_embed: bfloat16 [4, 64, 3072], P('segment'), may hold values from -0.75 to 0.75
- w_time: bfloat16 [4, 256, 3072], P('segment'), may hold values from -0.375 to 0.375
- w_mod: bfloat16 [4, 3072, 15360], P('segment', None, 'seq'), may hold values from -0.109375 to 0.109375
- w_qkv: bfloat16 [4, 3072, 4, 3, 128], P('segment', None, 'seq'), may hold values from -0.109375 to 0.109375
- w_out: bfloat16 [4, 4, 128, 3072], P('segment', 'seq'), may hold values from -0.25 to 0.25
- qk_gain: float32 [4, 2, 128], P('segment'), may hold values from 1.5 to 2.5
- w_final: bfloat16 [4, 3072, 64], P('segment'), may hold values from -0.109375 to 0.109375
Outputs:
- sample_grad: float32 [2, 512, 64], P('dp', 'seq')
- final_grads: float32 [4, 3072, 64], P('segment')
The draws below stay inside these ranges and needn't reach their ends.
All inputs are finite; a program needn't handle non-finite values. Where the reference program divides by a largest or mean magnitude, that divisor is 1e-20 or more.
Results may differ from the reference program's by a relative error of at most 0.025.
Values may be sent and summed in bfloat16 or wider, within the bound.
No kernel may reach another device: no remote copies, remote signals or barrier semaphores. Data moves between devices by JAX's collectives and lax.ppermute only.
A program may use at most 192 MiB of HBM per device.

```python
import math
import jax
import jax.numpy as jnp
from jax import lax

D = 3072
HEAD_DIM = 128
LATENT = 64
FREQS = 256
HEADS = 4
LENGTH = 512
BATCH = 2
N_SEGMENT = 4


def draw_clean(key, part):
    positions = jnp.arange(LENGTH, dtype=jnp.float32) / LENGTH
    growth = jnp.exp(jnp.log(3.0) * positions)[None, :, None]
    draws = jax.random.normal(key, (BATCH, LENGTH, LATENT), jnp.float32)
    values = jnp.clip(draws, -5.0, 5.0) * growth
    return values.astype(jnp.bfloat16)


def draw_noise(key, part):
    noise_key = jax.random.fold_in(key, 23)
    positions = jnp.arange(LENGTH, dtype=jnp.float32) / LENGTH
    growth = jnp.exp(jnp.log(6.0) * positions)[None, :, None]
    draws = jax.random.normal(noise_key, (BATCH, LENGTH, 2 * LATENT), jnp.float32)
    values = jnp.clip(draws, -4.0, 4.0) * growth
    return values.astype(jnp.bfloat16)


def with_ends(values, key, least, largest):
    longest = values.shape.index(max(values.shape))
    spots = []
    for shift in (0, 1):
        where = [jax.random.randint(jax.random.fold_in(key, axis), (), 0, length) for axis, length in enumerate(values.shape)]
        where[longest] = (where[longest] + shift) % values.shape[longest]
        spots.append(tuple(where))
    return values.at[spots[0]].set(least).at[spots[1]].set(largest)


def block_levels(own_key, dims, split, low, largest):
    loudness, own = 1.0, jax.random.fold_in(own_key, 6)
    for axis_at, parts in split:
        heights = jnp.exp(jax.random.uniform(jax.random.fold_in(own, axis_at), (parts,), jnp.float32, low / len(split), largest / len(split)))
        loudness = loudness * jnp.repeat(heights, dims[axis_at] // parts).reshape([-1 if axis == axis_at else 1 for axis in range(len(dims))])
    return loudness


def bell_draw(own_key, dims, width, limit, shards=(), kind=jnp.bfloat16):
    entries = width * jax.random.normal(own_key, dims, jnp.float32)
    if shards:
        entries = entries * block_levels(own_key, dims, shards, -0.22, 0.18)
    return jnp.clip(entries, -limit, limit).astype(kind)


def setup_inputs(seed: int = 0) -> dict:
    keys = jax.random.split(jax.random.key(seed), 12)
    return {
        "clean": draw_clean(jax.random.fold_in(keys[11], 71), 0),
        "noise": draw_noise(jax.random.fold_in(keys[11], 71), 0),
        "timesteps": with_ends(jax.random.randint(keys[2], (BATCH, 2), 20, 980), jax.random.fold_in(keys[2], 1), 20, 979).astype(jnp.int32),
        "text_vec": bell_draw(keys[3], (BATCH, FREQS), 1.0, 6.0, ((0, 2),), jnp.float32),
        "w_embed": bell_draw(keys[4], (N_SEGMENT, LATENT, D), LATENT ** -0.5, 0.75, ((0, 4),)),
        "w_time": bell_draw(keys[5], (N_SEGMENT, FREQS, D), FREQS ** -0.5, 0.375, ((0, 4),)),
        "w_mod": bell_draw(keys[6], (N_SEGMENT, D, 5 * D), D ** -0.5, 0.109375, ((0, 4), (2, 4))),
        "w_qkv": bell_draw(keys[7], (N_SEGMENT, D, HEADS, 3, HEAD_DIM), D ** -0.5, 0.109375, ((0, 4), (2, 4))),
        "w_out": bell_draw(keys[8], (N_SEGMENT, HEADS, HEAD_DIM, D), (HEADS * HEAD_DIM) ** -0.5, 0.25, ((0, 4), (1, 4))),
        "qk_gain": jnp.clip(1.5 + 1.0 * jax.random.uniform(keys[9], (N_SEGMENT, 2, HEAD_DIM), jnp.float32) ** block_levels(keys[9], (N_SEGMENT, 2, HEAD_DIM), ((0, 4),), -0.2, 0.2), 1.5, 2.5),
        "w_final": bell_draw(keys[10], (N_SEGMENT, D, LATENT), D ** -0.5, 0.109375, ((0, 4),)),
    }


SHIFT = 7.0
EPS = 1e-06
ADV_WEIGHT = 3.0

def noise_level(step):
    fraction = step.astype(jnp.float32) / 1000.0
    return SHIFT * fraction / (1.0 + (SHIFT - 1.0) * fraction)

def time_features(step, feature_count):
    half_width = feature_count // 2
    frequency = jnp.exp(-math.log(10000.0) * jnp.arange(half_width, dtype=jnp.float32) / half_width)
    angles = step.astype(jnp.float32) * frequency
    return jnp.concatenate([jnp.cos(angles), jnp.sin(angles)])

def condition(step, text_row, time_w, mod_w):
    features = (time_features(step, text_row.shape[0]) + text_row).astype(jnp.bfloat16)
    hidden = jax.nn.silu(jnp.dot(features, time_w, preferred_element_type=jnp.float32)).astype(jnp.bfloat16)
    return jnp.dot(hidden, mod_w, preferred_element_type=jnp.float32)

def normalize(values):
    row_mean = lax.optimization_barrier(jnp.mean(values, axis=-1, keepdims=True))
    centered = values - row_mean
    inverse = lax.rsqrt(lax.optimization_barrier(jnp.mean(centered * centered, axis=-1, keepdims=True)) + EPS)
    return (centered * inverse, inverse)

def normalize_back(gradient, normed, inverse):
    return inverse * (gradient - lax.optimization_barrier(jnp.mean(gradient, axis=-1, keepdims=True)) - normed * lax.optimization_barrier(jnp.mean(gradient * normed, axis=-1, keepdims=True)))

def rms_scale(values, gain_vec):
    inverse = lax.rsqrt(lax.optimization_barrier(jnp.mean(values * values, axis=-1, keepdims=True)) + EPS)
    unit_vec = values * inverse
    return (unit_vec * gain_vec, unit_vec, inverse)

def rms_back(gradient, unit_vec, inverse, gain_vec):
    scaled = gradient * gain_vec
    return inverse * (scaled - unit_vec * lax.optimization_barrier(jnp.mean(scaled * unit_vec, axis=-1, keepdims=True)))

def head_front(normed_in, head_w, gains):
    head_width = head_w.shape[-1]
    flat_w = head_w.reshape(head_w.shape[0], 3 * head_width)
    projected = jnp.dot(normed_in, flat_w, preferred_element_type=jnp.float32)
    queries, q_unit, q_inverse = rms_scale(projected[:, :head_width], gains[0])
    key_vecs, k_unit, k_inverse = rms_scale(projected[:, head_width:2 * head_width], gains[1])
    query_b = queries.astype(jnp.bfloat16)
    key_b = key_vecs.astype(jnp.bfloat16)
    value_b = projected[:, 2 * head_width:].astype(jnp.bfloat16)
    scores = jnp.dot(query_b, key_b.T, preferred_element_type=jnp.float32) / math.sqrt(head_width)
    weights = jnp.exp(scores)
    soft_max = weights / lax.optimization_barrier(jnp.sum(weights, axis=-1, keepdims=True))
    head_out = jnp.dot(soft_max.astype(jnp.bfloat16), value_b, preferred_element_type=jnp.float32).astype(jnp.bfloat16)
    return (head_out, (q_unit, q_inverse, k_unit, k_inverse, query_b, key_b, value_b, soft_max))

def head_back(grad_out, stored, gains):
    q_unit, q_inverse, k_unit, k_inverse, query_b, key_b, value_b, soft_max = stored
    head_width = query_b.shape[-1]
    grad_soft = jnp.dot(grad_out, value_b.T, preferred_element_type=jnp.float32)
    grad_value = jnp.dot(soft_max.astype(jnp.bfloat16).T, grad_out, preferred_element_type=jnp.float32)
    grad_scores = soft_max * (grad_soft - lax.optimization_barrier(jnp.sum(soft_max * grad_soft, axis=-1, keepdims=True)))
    grad_scores_b = (grad_scores / math.sqrt(head_width)).astype(jnp.bfloat16)
    grad_query = jnp.dot(grad_scores_b, key_b, preferred_element_type=jnp.float32)
    grad_key = jnp.dot(grad_scores_b.T, query_b, preferred_element_type=jnp.float32)
    grad_q = rms_back(grad_query, q_unit, q_inverse, gains[0])
    grad_k = rms_back(grad_key, k_unit, k_inverse, gains[1])
    return jnp.concatenate([grad_q, grad_k, grad_value], axis=1).astype(jnp.bfloat16)

def mod_pieces(modulation, model_width):
    return [modulation[slot * model_width:(slot + 1) * model_width] for slot in range(5)]

def block_forward(latent, modulation, embed_w, qkv_w, out_w, gains, final_w):
    model_width = embed_w.shape[1]
    shift_in, scale_in, gate_vec, shift_out, scale_out = mod_pieces(modulation, model_width)
    embedded = jnp.dot(latent, embed_w, preferred_element_type=jnp.float32)
    normed, inverse = normalize(embedded)
    normed_in = (normed * (1.0 + scale_in) + shift_in).astype(jnp.bfloat16)
    heads_first = jnp.moveaxis(qkv_w, 1, 0)

    def add_head(running, weights):
        head_w, rows_w = weights
        head_out, _ = head_front(normed_in, head_w, gains)
        product = jnp.dot(head_out, rows_w, preferred_element_type=jnp.float32).astype(jnp.bfloat16)
        return (running + lax.optimization_barrier(product).astype(jnp.float32), None)
    attended, _ = lax.scan(add_head, jnp.zeros(embedded.shape, jnp.float32), (heads_first, out_w))
    residual = embedded + gate_vec * attended
    normed_out, inverse_out = normalize(residual)
    final_in = (normed_out * (1.0 + scale_out) + shift_out).astype(jnp.bfloat16)
    result = jnp.dot(final_in, final_w, preferred_element_type=jnp.float32)
    return (result, final_in, (normed, inverse, normed_in, normed_out, inverse_out))

def block_backward(grad_logit, cache, modulation, embed_w, qkv_w, out_w, gains, final_w):
    model_width = embed_w.shape[1]
    shift_in, scale_in, gate_vec, shift_out, scale_out = mod_pieces(modulation, model_width)
    normed, inverse, normed_in, normed_out, inverse_out = cache
    grad_final = jnp.dot(grad_logit.astype(jnp.bfloat16), final_w.T, preferred_element_type=jnp.float32)
    grad_residual = normalize_back(grad_final * (1.0 + scale_out), normed_out, inverse_out)
    grad_attended = (gate_vec * grad_residual).astype(jnp.bfloat16)
    heads_first = jnp.moveaxis(qkv_w, 1, 0)

    def add_head(running, weights):
        head_w, rows_w = weights
        _, stored = head_front(normed_in, head_w, gains)
        grad_out = jnp.dot(grad_attended, rows_w.T, preferred_element_type=jnp.float32).astype(jnp.bfloat16)
        grad_proj = head_back(grad_out, stored, gains)
        flat_w = head_w.reshape(head_w.shape[0], -1)
        return (running + jnp.dot(grad_proj, flat_w.T, preferred_element_type=jnp.float32), None)
    grad_normed, _ = lax.scan(add_head, jnp.zeros(normed.shape, jnp.float32), (heads_first, out_w))
    grad_embedded = grad_residual + normalize_back(grad_normed * (1.0 + scale_in), normed, inverse)
    return jnp.dot(grad_embedded, embed_w.astype(jnp.float32).T, precision=lax.Precision.HIGHEST)

def reference(clean, noise, timesteps, text_vec, w_embed, w_time, w_mod, w_qkv, w_out, qk_gain, w_final):
    latent_width = clean.shape[2]
    sections = w_embed.shape[0]
    sample_rows = []
    weight_terms = jnp.zeros((sections, w_embed.shape[2], latent_width), jnp.float32)
    for batch_idx in range(clean.shape[0]):
        step_student = timesteps[batch_idx, 0]
        step_critic = timesteps[batch_idx, 1]
        sigma_student = noise_level(step_student)
        sigma_critic = noise_level(step_critic)

        def run(section_id, latent):
            chosen = step_student if section_id == 0 else step_critic
            modulation = condition(chosen, text_vec[batch_idx], w_time[section_id], w_mod[section_id])
            outcome = block_forward(latent, modulation, w_embed[section_id], w_qkv[section_id], w_out[section_id], qk_gain[section_id], w_final[section_id])
            return (outcome, modulation)
        first_noise = noise[batch_idx, :, :latent_width].astype(jnp.float32)
        second_noise = noise[batch_idx, :, latent_width:].astype(jnp.float32)
        noisy_student = ((1.0 - sigma_student) * clean[batch_idx].astype(jnp.float32) + sigma_student * first_noise).astype(jnp.bfloat16)
        (velocity, student_in, _), _ = run(0, noisy_student)
        sample = noisy_student.astype(jnp.float32) - sigma_student * velocity
        noisy_critic = ((1.0 - sigma_critic) * sample + sigma_critic * second_noise).astype(jnp.bfloat16)
        (teacher_v, _, _), _ = run(1, noisy_critic)
        (critic_v, critic_in, _), _ = run(2, noisy_critic)
        (logits, judge_in, cache), judge_mod = run(3, noisy_critic)
        grad_logit = -jax.nn.sigmoid(-logits)
        adverse = (1.0 - sigma_critic) * block_backward(grad_logit, cache, judge_mod, w_embed[3], w_qkv[3], w_out[3], qk_gain[3], w_final[3])
        real_term = sigma_critic * teacher_v
        fake_term = sigma_critic * critic_v
        spread = jnp.mean(jnp.abs(sample - noisy_critic.astype(jnp.float32) + real_term)) + EPS
        sample_grad = (real_term - fake_term) / spread + ADV_WEIGHT * adverse
        sample_rows.append(sample_grad)
        target_student = (-sigma_student * sample_grad).astype(jnp.bfloat16)
        target_critic = (2.0 * (critic_v - (second_noise - sample))).astype(jnp.bfloat16)
        target_judge = jax.nn.sigmoid(logits).astype(jnp.bfloat16)
        weight_terms = weight_terms.at[0].add(jnp.dot(student_in.T, target_student, preferred_element_type=jnp.float32))
        weight_terms = weight_terms.at[2].add(jnp.dot(critic_in.T, target_critic, preferred_element_type=jnp.float32))
        weight_terms = weight_terms.at[3].add(jnp.dot(judge_in.T, target_judge, preferred_element_type=jnp.float32))
    final_grads = weight_terms / clean.shape[1]
    return (jnp.stack(sample_rows), final_grads)
```

```python
import math

import jax
import jax.numpy as jnp
from jax import lax
from jax.sharding import PartitionSpec as P

SHIFT = 7.0
EPS = 1e-06
ADV_WEIGHT = 3.0


def halves(values):
    top = lax.reduce_precision(values, 8, 7)
    return (top.astype(jnp.bfloat16), (values - top).astype(jnp.bfloat16))


def swaps(count, offset):
    return [(place, place ^ offset) for place in range(count)]


def gather_near(value, axis, count):
    return [value] + [
        lax.ppermute(value, axis, swaps(count, offset)) for offset in range(1, count)
    ]


def scatter_near(blocks, axis, count):
    return [blocks[0]] + [
        lax.ppermute(blocks[offset], axis, swaps(count, offset)) for offset in range(1, count)
    ]


def gather_doubling(value, axis, count):
    held = {0: value}
    bit = count // 2
    while bit:
        offsets = sorted(held)
        joined = jnp.concatenate([held[offset] for offset in offsets], axis=0)
        moved = lax.ppermute(joined, axis, swaps(count, bit))
        rows = value.shape[0]
        for place, offset in enumerate(offsets):
            held[offset | bit] = moved[place * rows : (place + 1) * rows]
        bit //= 2
    return [held[offset] for offset in range(count)]


def in_order(pieces, own_place):
    ordered = list(pieces)
    bit = 1
    while bit < len(ordered):
        flipped = (own_place & bit) != 0
        ordered = [
            jnp.where(flipped, ordered[place ^ bit], ordered[place])
            for place in range(len(ordered))
        ]
        bit *= 2
    return ordered


def dot32(left, right):
    return jnp.dot(left, right, preferred_element_type=jnp.float32)


def dot32_t(left, right):
    return lax.dot_general(
        left, right, (((1,), (1,)), ((), ())), preferred_element_type=jnp.float32
    )


def noise_level(step):
    fraction = step.astype(jnp.float32) / 1000.0
    return SHIFT * fraction / (1.0 + (SHIFT - 1.0) * fraction)


def time_features(step, feature_count):
    half_width = feature_count // 2
    frequency = jnp.exp(-math.log(10000.0) * jnp.arange(half_width, dtype=jnp.float32) / half_width)
    angles = step.astype(jnp.float32) * frequency
    return jnp.concatenate([jnp.cos(angles), jnp.sin(angles)])


def condition(step, text_row, time_w, mod_w):
    features = (time_features(step, text_row.shape[0]) + text_row).astype(jnp.bfloat16)
    hidden = jax.nn.silu(jnp.dot(features, time_w, preferred_element_type=jnp.float32)).astype(
        jnp.bfloat16
    )
    return jnp.dot(hidden, mod_w, preferred_element_type=jnp.float32)


def normalize(values):
    row_mean = jnp.mean(values, axis=-1, keepdims=True)
    centered = values - row_mean
    inverse = lax.rsqrt(jnp.mean(centered * centered, axis=-1, keepdims=True) + EPS)
    return (centered * inverse, inverse)


def normalize_back(gradient, normed, inverse):
    return inverse * (
        gradient
        - jnp.mean(gradient, axis=-1, keepdims=True)
        - normed * jnp.mean(gradient * normed, axis=-1, keepdims=True)
    )


def rms_scale(values, gain_vec):
    inverse = lax.rsqrt(jnp.mean(values * values, axis=-1, keepdims=True) + EPS)
    unit_vec = values * inverse
    return (unit_vec * gain_vec, unit_vec, inverse)


def rms_back(gradient, unit_vec, inverse, gain_vec):
    scaled = gradient * gain_vec
    return inverse * (scaled - unit_vec * jnp.mean(scaled * unit_vec, axis=-1, keepdims=True))


def attend(projected, gains):
    head_width = projected.shape[1] // 3
    queries, q_unit, q_inverse = rms_scale(projected[:, :head_width], gains[0])
    key_vecs, k_unit, k_inverse = rms_scale(projected[:, head_width : 2 * head_width], gains[1])
    query_b = queries.astype(jnp.bfloat16)
    key_b = key_vecs.astype(jnp.bfloat16)
    value_b = projected[:, 2 * head_width :].astype(jnp.bfloat16)
    scores = dot32_t(query_b, key_b) / math.sqrt(head_width)
    weights = jnp.exp(scores)
    soft_max = weights / jnp.sum(weights, axis=-1, keepdims=True)
    head_out = dot32(soft_max.astype(jnp.bfloat16), value_b).astype(jnp.bfloat16)
    return (head_out, (q_unit, q_inverse, k_unit, k_inverse, query_b, key_b, value_b, soft_max))


def attend_back(grad_out, stored, gains):
    q_unit, q_inverse, k_unit, k_inverse, query_b, key_b, value_b, soft_max = stored
    head_width = query_b.shape[-1]
    grad_soft = dot32_t(grad_out, value_b)
    grad_value = dot32(soft_max.astype(jnp.bfloat16).T, grad_out)
    grad_scores = soft_max * (grad_soft - jnp.sum(soft_max * grad_soft, axis=-1, keepdims=True))
    grad_scores_b = (grad_scores / math.sqrt(head_width)).astype(jnp.bfloat16)
    grad_query = dot32(grad_scores_b, key_b)
    grad_key = dot32(grad_scores_b.T, query_b)
    grad_q = rms_back(grad_query, q_unit, q_inverse, gains[0])
    grad_k = rms_back(grad_key, k_unit, k_inverse, gains[1])
    return jnp.concatenate([grad_q, grad_k, grad_value], axis=1).astype(jnp.bfloat16)


def shards(
    clean, noise, timesteps, text_vec, w_embed, w_time, w_mod, w_qkv, w_out, qk_gain, w_final
):
    section = lax.axis_index("segment")
    sections = lax.axis_size("segment")
    batch_idx = lax.axis_index("dp")
    seq_place = lax.axis_index("seq")
    tok_rows = clean.shape[1]
    latent_width = clean.shape[2]
    model_width = w_embed.shape[2]
    seq_devices = lax.axis_size("seq")
    full_rows = tok_rows * seq_devices
    head_width = w_qkv.shape[4]
    embed_w = w_embed[0]
    embed_f32 = embed_w.astype(jnp.float32)
    flat_head_w = w_qkv[0, :, 0].reshape(model_width, 3 * head_width)
    gains = qk_gain[0]
    final_w = w_final[0]
    step_pair = lax.dynamic_index_in_dim(timesteps, batch_idx, 0, keepdims=False)
    sigma_student = noise_level(step_pair[0])
    sigma_critic = noise_level(step_pair[1])
    own_step = jnp.where(section == 0, step_pair[0], step_pair[1])
    noisy_student = (
        (1.0 - sigma_student) * clean[0].astype(jnp.float32)
        + sigma_student * noise[0, :, :latent_width].astype(jnp.float32)
    ).astype(jnp.bfloat16)
    second_noise = noise[0, :, latent_width:].astype(jnp.float32)
    all_heads_w = jnp.concatenate(
        gather_doubling(w_out[0, 0], "seq", seq_devices), axis=0
    )
    student_rows = jnp.concatenate(gather_near(noisy_student, "seq", seq_devices), axis=0)

    mod_piece = condition(own_step, text_vec[0], w_time[0], w_mod[0])
    mod_parts = gather_near(mod_piece.reshape(1, -1), "seq", seq_devices)
    modulation = jnp.concatenate(in_order(mod_parts, seq_place), axis=1)
    shift_in, scale_in, gate_vec, shift_out, scale_out = [
        modulation[:, slot * model_width : (slot + 1) * model_width] for slot in range(5)
    ]

    centred_w = embed_f32 - jnp.mean(embed_f32, axis=1, keepdims=True)
    centred_top, _ = halves(centred_w)
    in_rows = jnp.concatenate([centred_w * (1.0 + scale_in), shift_in], axis=0)
    in_top, in_low = halves(in_rows)
    short = dot32(in_top, flat_head_w) + dot32(in_low, flat_head_w)
    short_w, short_shift = short[:latent_width], short[latent_width:]
    short_top, short_low = halves(short_w)
    gram = jnp.dot(centred_w, centred_w.T, precision=lax.Precision.HIGHEST)

    def forward(latent_rows, latent_local):
        centred = dot32(latent_rows, centred_top)
        inverse = lax.rsqrt(jnp.mean(centred * centred, axis=-1, keepdims=True) + EPS)
        projected = (
            inverse * (dot32(latent_rows, short_top) + dot32(latent_rows, short_low)) + short_shift
        )
        head_out, stored = attend(projected, gains)
        blocks = [
            head_out[place * tok_rows : (place + 1) * tok_rows] for place in range(seq_devices)
        ]
        mixed = jnp.concatenate(scatter_near(blocks, "seq", seq_devices), axis=1)
        residual = dot32(latent_local, embed_w) + gate_vec * dot32(mixed, all_heads_w)
        normed_out, inverse_out = normalize(residual)
        final_in = (normed_out * (1.0 + scale_out) + shift_out).astype(jnp.bfloat16)
        result = dot32(final_in, final_w)
        return (result, final_in, (inverse, stored, normed_out, inverse_out))

    velocity, student_in, _ = forward(student_rows, noisy_student)
    own_sample = noisy_student.astype(jnp.float32) - sigma_student * velocity
    own_critic = (1.0 - sigma_critic) * own_sample + sigma_critic * second_noise
    pair = jnp.concatenate([own_critic, own_sample], axis=1).astype(jnp.bfloat16)
    arrived = [
        lax.ppermute(pair, "segment", [(0, place)]) for place in range(sections - 1, 0, -1)
    ]
    pair = jnp.where(section == 0, pair, sum(arrived[1:], arrived[0]))
    noisy_critic = pair[:, :latent_width]
    sample = pair[:, latent_width:].astype(jnp.float32)
    critic_rows = jnp.concatenate(gather_near(noisy_critic, "seq", seq_devices), axis=0)
    critic_out, critic_in, cache = forward(critic_rows, noisy_critic)
    inverse, stored, normed_out, inverse_out = cache

    is_judge = section == 3
    grad_logit = -jax.nn.sigmoid(-critic_out)
    grad_final = dot32_t(grad_logit.astype(jnp.bfloat16), final_w)
    grad_residual = normalize_back(grad_final * (1.0 + scale_out), normed_out, inverse_out)
    grad_attended = (gate_vec * grad_residual).astype(jnp.bfloat16)
    grad_heads = dot32_t(grad_attended, all_heads_w).astype(jnp.bfloat16)
    grad_blocks = [
        grad_heads[:, place * head_width : (place + 1) * head_width]
        for place in range(seq_devices)
    ]
    grad_head = jnp.concatenate(scatter_near(grad_blocks, "seq", seq_devices), axis=0)
    grad_proj = attend_back(grad_head, stored, gains)
    through = dot32_t(grad_proj, short_top) + dot32_t(grad_proj, short_low)
    critic_f32 = critic_rows.astype(jnp.float32)
    along = jnp.sum(through * critic_f32, axis=-1, keepdims=True) / model_width
    spanned = jnp.dot(critic_f32, gram, precision=lax.Precision.HIGHEST)
    grad_rows = inverse * (through - spanned * (inverse * inverse * along))

    noisy_critic_f32 = noisy_critic.astype(jnp.float32)
    scaled_out = sigma_critic * critic_out
    error_local = jnp.sum(jnp.abs(sample - noisy_critic_f32 + scaled_out))
    error_top, error_low = halves(error_local / (tok_rows * latent_width))
    error_row = jnp.concatenate(
        [jnp.full((8, latent_width), error_top), jnp.full((8, latent_width), error_low)], axis=0
    )
    grad_parts = scatter_near(
        [
            jnp.concatenate(
                [
                    grad_rows[place * tok_rows : (place + 1) * tok_rows].astype(jnp.bfloat16),
                    error_row,
                ],
                axis=0,
            )
            for place in range(seq_devices)
        ],
        "seq",
        seq_devices,
    )
    grad_total = sum([part.astype(jnp.float32) for part in grad_parts[1:]], grad_parts[0].astype(jnp.float32))
    error_mean = (grad_total[tok_rows : tok_rows + 1] + grad_total[tok_rows + 8 : tok_rows + 9])[
        :, :1
    ] / seq_devices
    direct = jnp.dot(grad_residual, embed_f32.T, precision=lax.Precision.HIGHEST)
    adverse = (1.0 - sigma_critic) * (grad_total[:tok_rows] + direct)
    term_rows = jnp.where(is_judge, adverse, scaled_out)
    spread_top, spread_low = halves(error_mean + EPS)
    payload = jnp.concatenate(
        [
            term_rows.astype(jnp.bfloat16),
            jnp.broadcast_to(spread_top, (8, latent_width)),
            jnp.broadcast_to(spread_low, (8, latent_width)),
        ],
        axis=0,
    )
    received = [payload] + [
        lax.ppermute(
            payload, "segment", [(place, (place + offset) % sections) for place in range(sections)]
        )
        for offset in range(1, sections)
    ]

    def payload_of(source):
        chosen = received[0]
        for offset in range(1, sections):
            chosen = jnp.where((section - offset) % sections == source, received[offset], chosen)
        return chosen.astype(jnp.float32)

    real_rows, fake_rows, adverse_rows = [payload_of(source) for source in (1, 2, 3)]
    spread = (real_rows[tok_rows : tok_rows + 1] + real_rows[tok_rows + 8 : tok_rows + 9])[:, :1]
    sample_grad = (real_rows[:tok_rows] - fake_rows[:tok_rows]) / spread + ADV_WEIGHT * adverse_rows[
        :tok_rows
    ]
    target = jnp.where(
        section == 0,
        -sigma_student * sample_grad,
        jnp.where(
            section == 2,
            2.0 * (critic_out - (second_noise - sample)),
            jnp.where(is_judge, jax.nn.sigmoid(critic_out), 0.0),
        ),
    )
    final_rows = jnp.where(section == 0, student_in, critic_in)
    term = lax.dot_general(
        final_rows,
        target.astype(jnp.bfloat16),
        (((0,), (0,)), ((), ())),
        preferred_element_type=jnp.float32,
    ).astype(jnp.bfloat16)
    share_count = seq_devices * lax.axis_size("dp")
    share = model_width // share_count
    exchanged = lax.all_to_all(
        term.reshape(share_count, share, latent_width),
        ("seq", "dp"),
        split_axis=0,
        concat_axis=0,
        tiled=True,
    )
    own_total = jnp.sum(exchanged.astype(jnp.float32), axis=0).astype(jnp.bfloat16)
    total = lax.all_to_all(
        jnp.broadcast_to(own_total[None], (share_count, share, latent_width)),
        ("seq", "dp"),
        split_axis=0,
        concat_axis=0,
        tiled=True,
    )
    final_grads = total.astype(jnp.float32).reshape(model_width, latent_width) / full_rows
    return (sample_grad[None], final_grads[None])


def solution(mesh):
    placed = (
        P("dp", "seq", None),
        P("dp", "seq", None),
        P(),
        P("dp", None),
        P("segment", None, None),
        P("segment", None, None),
        P("segment", None, "seq"),
        P("segment", None, "seq", None, None),
        P("segment", "seq", None, None),
        P("segment", None, None),
        P("segment", None, None),
    )
    return jax.shard_map(
        shards,
        mesh=mesh,
        in_specs=placed,
        out_specs=(P("dp", "seq", None), P("segment", None, None)),
        check_vma=False,
    )
```

```python
import functools
import math

import jax
import jax.numpy as jnp
from jax import lax
from jax.experimental import pallas as pl
from jax.experimental.pallas import tpu as pltpu
from jax.sharding import PartitionSpec as P

SHIFT = 7.0
EPS = 1e-06
ADV_WEIGHT = 3.0
TILE = 512
STREAMS = 6
VMEM = pl.BlockSpec(memory_space=pltpu.VMEM)
SMEM = pl.BlockSpec(memory_space=pltpu.SMEM)
ANY = pl.BlockSpec(memory_space=pl.ANY)


def halves(values):
    top = values.astype(jnp.bfloat16)
    return (top, (values - top.astype(jnp.float32)).astype(jnp.bfloat16))


def split_halves(values):
    top = lax.reduce_precision(values, 8, 7)
    return (top.astype(jnp.bfloat16), (values - top).astype(jnp.bfloat16))


def swaps(count, offset):
    return [(place, place ^ offset) for place in range(count)]


def gather_near(value, axis, count):
    return [value] + [
        lax.ppermute(value, axis, swaps(count, offset)) for offset in range(1, count)
    ]


def scatter_near(blocks, axis, count):
    return [blocks[0]] + [
        lax.ppermute(blocks[offset], axis, swaps(count, offset)) for offset in range(1, count)
    ]


def gather_doubling(value, axis, count):
    held = {0: value}
    bit = count // 2
    while bit:
        offsets = sorted(held)
        joined = jnp.concatenate([held[offset] for offset in offsets], axis=0)
        moved = lax.ppermute(joined, axis, swaps(count, bit))
        rows = value.shape[0]
        for place, offset in enumerate(offsets):
            held[offset | bit] = moved[place * rows : (place + 1) * rows]
        bit //= 2
    return [held[offset] for offset in range(count)]


def in_order(pieces, own_place):
    ordered = list(pieces)
    bit = 1
    while bit < len(ordered):
        flipped = (own_place & bit) != 0
        ordered = [
            jnp.where(flipped, ordered[place ^ bit], ordered[place])
            for place in range(len(ordered))
        ]
        bit *= 2
    return ordered


def dot32(left, right):
    return jnp.dot(left, right, preferred_element_type=jnp.float32)


def dot32_t(left, right):
    return lax.dot_general(
        left, right, (((1,), (1,)), ((), ())), preferred_element_type=jnp.float32
    )


def dot32_first(left, right):
    return lax.dot_general(
        left, right, (((0,), (0,)), ((), ())), preferred_element_type=jnp.float32
    )


def steps_of(times_ref):
    place = lax.axis_index("dp")
    return (times_ref[place, 0], times_ref[place, 1])


def noise_level(step):
    fraction = jnp.full((1, 1), step, jnp.int32).astype(jnp.float32) / 1000.0
    return SHIFT * fraction / (1.0 + (SHIFT - 1.0) * fraction)


def slot_of(mod_ref, slot, width, first, size):
    return mod_ref[:, slot * width + first : slot * width + first + size]


def lane_sum(values):
    total = values[:, :128]
    for first in range(128, values.shape[1], 128):
        total = total + values[:, first : first + 128]
    return total


def run(kernel, outputs, operands, specs, flops, scratch=(), **params):
    in_bytes = sum(operand.size * operand.dtype.itemsize for operand in operands)
    out_bytes = sum(output.size * output.dtype.itemsize for output in outputs)
    return pl.pallas_call(
        kernel,
        out_shape=outputs,
        in_specs=specs,
        out_specs=[VMEM] * len(outputs),
        scratch_shapes=list(scratch),
        compiler_params=pltpu.CompilerParams(**params),
        cost_estimate=pl.CostEstimate(
            flops=flops, bytes_accessed=in_bytes + out_bytes, transcendentals=0
        ),
    )(*operands)


def array(shape, dtype):
    return jax.ShapeDtypeStruct(shape, dtype)


def condition_kernel(times, text, time_w, mod_w, mod_out, held, arrivals):
    model_width = mod_w.shape[1]
    rows = model_width // STREAMS
    copies = [
        pltpu.make_async_copy(
            mod_w.at[0, pl.ds(part * rows, rows)], held.at[pl.ds(part * rows, rows)], arrivals.at[part]
        )
        for part in range(STREAMS)
    ]
    for copy in copies:
        copy.start()
    student_step, critic_step = steps_of(times)
    step = jnp.where(lax.axis_index("segment") == 0, student_step, critic_step)
    half = text.shape[1] // 2
    places = lax.broadcasted_iota(jnp.int32, (1, half), 1).astype(jnp.float32)
    frequency = jnp.exp(-math.log(10000.0) * places / half)
    angles = jnp.full((1, half), step, jnp.int32).astype(jnp.float32) * frequency
    features = jnp.concatenate([jnp.cos(angles), jnp.sin(angles)], axis=1) + text[...]
    features = jnp.broadcast_to(features, (8, 2 * half)).astype(jnp.bfloat16)
    hidden = dot32(features, time_w[0])
    hidden = (hidden / (1.0 + jnp.exp(-hidden))).astype(jnp.bfloat16)
    total = None
    for part in range(STREAMS):
        copies[part].wait()
        piece = dot32(
            hidden[:, part * rows : (part + 1) * rows], held[part * rows : (part + 1) * rows]
        )
        total = piece if total is None else total + piece
    mod_out[...] = total[:1]


def rms_scale(values, gain_vec):
    inverse = lax.rsqrt(jnp.mean(values * values, axis=-1, keepdims=True) + EPS)
    unit_vec = values * inverse
    return (unit_vec * gain_vec, unit_vec, inverse)


def rms_back(gradient, unit_vec, inverse, gain_vec):
    scaled = gradient * gain_vec
    return inverse * (scaled - unit_vec * jnp.mean(scaled * unit_vec, axis=-1, keepdims=True))


def centred(embed_ref):
    values = embed_ref[0].astype(jnp.float32)
    return values - jnp.mean(values, axis=1, keepdims=True)


def front(rows, central, short, gains, head_outs, proj_ref, inverse_ref, key_ref, value_ref):
    latent_width = central.shape[0]
    model_width = central.shape[1]
    count = len(rows)
    head_width = gains.shape[2]
    short_top, short_low = halves(short[:latent_width])
    short_shift = short[latent_width : latent_width + 1]
    scale = 1.0 / math.sqrt(head_width)
    size = rows[0].shape[0]
    for place in range(count):
        block = rows[place][...]
        squares = None
        for first in range(0, model_width, TILE):
            piece = dot32(block, central[:, first : first + TILE])
            piece = lane_sum(piece * piece)
            squares = piece if squares is None else squares + piece
        inverse = lax.rsqrt(jnp.sum(squares, axis=1, keepdims=True) / model_width + EPS)
        projected = inverse * (dot32(block, short_top) + dot32(block, short_low)) + short_shift
        low = place * size
        proj_ref[low : low + size] = projected
        inverse_ref[low : low + size] = jnp.broadcast_to(inverse, (size, 128))
        keys, _, _ = rms_scale(projected[:, head_width : 2 * head_width], gains[0, 1:2])
        key_ref[low : low + size] = keys.astype(jnp.bfloat16)
        value_ref[low : low + size] = projected[:, 2 * head_width :].astype(jnp.bfloat16)
    for place in range(count):
        low = place * size
        queries, _, _ = rms_scale(proj_ref[low : low + size, :head_width], gains[0, :1])
        scores = dot32_t(queries.astype(jnp.bfloat16), key_ref[...]) * scale
        weights = jnp.exp(scores)
        soft_max = weights * (1.0 / jnp.sum(weights, axis=-1, keepdims=True))
        head_outs[place][...] = dot32(soft_max.astype(jnp.bfloat16), value_ref[...]).astype(
            jnp.bfloat16
        )


def student_front_kernel(count, mod, embed_w, head_w, gains, *refs):
    rows = refs[:count]
    head_outs = refs[count : 2 * count]
    short_ref, proj_ref, inverse_ref, key_ref, value_ref = refs[2 * count :]
    model_width = embed_w.shape[2]
    central = centred(embed_w)
    scale_in = slot_of(mod, 1, model_width, 0, model_width)
    shift_in = slot_of(mod, 0, model_width, 0, model_width)
    in_rows = jnp.concatenate(
        [central * (1.0 + scale_in), jnp.broadcast_to(shift_in, (16, model_width))], axis=0
    )
    in_top, in_low = halves(in_rows)
    both = dot32(jnp.concatenate([in_top, in_low], axis=0), head_w[...])
    short = both[: in_rows.shape[0]] + both[in_rows.shape[0] :]
    short_ref[...] = short

    @pl.when(lax.axis_index("segment") == 0)
    def _():
        front(
            rows,
            central.astype(jnp.bfloat16),
            short,
            gains,
            head_outs,
            proj_ref,
            inverse_ref,
            key_ref,
            value_ref,
        )


def critic_front_kernel(count, short_in, embed_w, gains, *refs):
    rows = refs[:count]
    head_outs = refs[count : 2 * count]
    proj_ref, inverse_ref, key_ref, value_ref = refs[2 * count :]

    @pl.when(lax.axis_index("segment") != 0)
    def _():
        front(
            rows,
            centred(embed_w).astype(jnp.bfloat16),
            short_in[...],
            gains,
            head_outs,
            proj_ref,
            inverse_ref,
            key_ref,
            value_ref,
        )


def tail(mod, latent, embed_w, final_w, mixed, heads_w, final_in_ref, work):
    model_width = embed_w.shape[2]
    block = latent[...]
    sums = None
    for first in range(0, model_width, TILE):
        span = slice(first, first + TILE)
        attended = None
        for piece, rows_w in zip(mixed, heads_w):
            product = dot32(piece[...], rows_w[:, span])
            attended = product if attended is None else attended + product
        residual = (
            dot32(block, embed_w[0, :, span]) + slot_of(mod, 2, model_width, first, TILE) * attended
        )
        work[:, span] = residual
        part = lane_sum(residual)
        sums = part if sums is None else sums + part
    row_mean = jnp.sum(sums, axis=1, keepdims=True) / model_width
    sums = None
    for first in range(0, model_width, TILE):
        span = slice(first, first + TILE)
        middle = work[:, span] - row_mean
        work[:, span] = middle
        part = lane_sum(middle * middle)
        sums = part if sums is None else sums + part
    inverse = lax.rsqrt(jnp.sum(sums, axis=1, keepdims=True) / model_width + EPS)
    result = None
    for first in range(0, model_width, TILE):
        span = slice(first, first + TILE)
        normed = work[:, span] * inverse
        work[:, span] = normed
        final_in = (
            normed * (1.0 + slot_of(mod, 4, model_width, first, TILE))
            + slot_of(mod, 3, model_width, first, TILE)
        ).astype(jnp.bfloat16)
        final_in_ref[:, span] = final_in
        product = dot32(final_in, final_w[0, span])
        result = product if result is None else result + product
    return (result, inverse)


def student_tail_kernel(count, times, mod, latent, noise, embed_w, final_w, *refs):
    mixed = refs[:count]
    heads_w = refs[count : 2 * count]
    pair_ref, final_in_ref, work = refs[2 * count :]
    latent_width = latent.shape[1]

    @pl.when(lax.axis_index("segment") == 0)
    def _():
        student_step, critic_step = steps_of(times)
        sigma_student, sigma_critic = noise_level(student_step), noise_level(critic_step)
        velocity, _ = tail(mod, latent, embed_w, final_w, mixed, heads_w, final_in_ref, work)
        sample = latent[...].astype(jnp.float32) - sigma_student * velocity
        second = noise[0, :, latent_width:].astype(jnp.float32)
        critic = (1.0 - sigma_critic) * sample + sigma_critic * second
        pair_ref[...] = jnp.concatenate([critic, sample], axis=1).astype(jnp.bfloat16)


def critic_tail_kernel(count, times, mod, pair, noise, embed_w, final_w, *refs):
    mixed = refs[:count]
    heads_w = refs[count : 2 * count]
    grads = refs[2 * count : 3 * count]
    final_in_ref, term_ref, target_ref, error_ref, direct_ref, latent, work, other = refs[
        3 * count :
    ]
    model_width = embed_w.shape[2]
    latent_width = latent.shape[1]
    section = lax.axis_index("segment")

    @pl.when(section != 0)
    def _():
        _, critic_step = steps_of(times)
        sigma_critic = noise_level(critic_step)
        both = pair[...].astype(jnp.float32)
        sample = both[:, latent_width:]
        latent[...] = pair[:, :latent_width]
        result, inverse = tail(mod, latent, embed_w, final_w, mixed, heads_w, final_in_ref, work)
        scaled = sigma_critic * result
        term_ref[...] = scaled
        second = noise[0, :, latent_width:].astype(jnp.float32)
        target_ref[...] = jnp.where(
            section == 2,
            2.0 * (result - (second - sample)),
            jnp.where(section == 3, 1.0 / (1.0 + jnp.exp(-result)), 0.0),
        )
        gaps = jnp.abs(sample - both[:, :latent_width] + scaled)
        error = jnp.sum(jnp.sum(gaps, axis=1, keepdims=True), axis=0, keepdims=True)
        error = error / (gaps.shape[0] * latent_width)
        error_top, error_low = halves(jnp.broadcast_to(error, (16, latent_width)))
        error_ref[:16] = error_top
        error_ref[16:] = error_low

        @pl.when(section == 3)
        def _():
            grad_logit = (-1.0 / (1.0 + jnp.exp(result))).astype(jnp.bfloat16)
            plain, along = None, None
            for first in range(0, model_width, TILE):
                span = slice(first, first + TILE)
                gradient = dot32_t(grad_logit, final_w[0, span]) * (
                    1.0 + slot_of(mod, 4, model_width, first, TILE)
                )
                other[:, span] = gradient
                part = lane_sum(gradient)
                plain = part if plain is None else plain + part
                part = lane_sum(gradient * work[:, span])
                along = part if along is None else along + part
            plain = jnp.sum(plain, axis=1, keepdims=True) / model_width
            along = jnp.sum(along, axis=1, keepdims=True) / model_width
            direct = None
            totals = [None] * count
            for first in range(0, model_width, TILE):
                span = slice(first, first + TILE)
                grad_residual = inverse * (other[:, span] - plain - work[:, span] * along)
                top, low = halves(grad_residual)
                product = dot32_t(top, embed_w[0, :, span]) + dot32_t(low, embed_w[0, :, span])
                direct = product if direct is None else direct + product
                grad_attended = (slot_of(mod, 2, model_width, first, TILE) * grad_residual).astype(
                    jnp.bfloat16
                )
                for place in range(count):
                    product = dot32_t(grad_attended, heads_w[place][:, span])
                    held = totals[place]
                    totals[place] = product if held is None else held + product
            direct_ref[...] = direct
            for place in range(count):
                grads[place][...] = totals[place].astype(jnp.bfloat16)


def judge_back_kernel(count, short_in, embed_w, gains, proj_ref, inverse_ref, key_ref, value_ref, error, *refs):
    rows = refs[:count]
    grads = refs[count : 2 * count]
    outs = refs[2 * count : 3 * count]
    grad_key_ref, grad_value_ref, grad_query_ref = refs[3 * count :]
    section = lax.axis_index("segment")
    latent_width = rows[0].shape[1]
    model_width = embed_w.shape[2]
    head_width = gains.shape[2]
    scale = 1.0 / math.sqrt(head_width)
    size = rows[0].shape[0]
    for place in range(count):
        outs[place][size:] = error[...]

    @pl.when(section == 3)
    def _():
        for place in range(count):
            low = place * size
            span = slice(low, low + size)
            queries, _, _ = rms_scale(proj_ref[span, :head_width], gains[0, :1])
            query_b = queries.astype(jnp.bfloat16)
            weights = jnp.exp(dot32_t(query_b, key_ref[...]) * scale)
            soft_max = weights * (1.0 / jnp.sum(weights, axis=-1, keepdims=True))
            grad_out = grads[place][...]
            grad_soft = dot32_t(grad_out, value_ref[...])
            grad_value = dot32_first(soft_max.astype(jnp.bfloat16), grad_out)
            grad_scores = soft_max * (
                grad_soft - jnp.sum(soft_max * grad_soft, axis=-1, keepdims=True)
            )
            grad_scores_b = (grad_scores * scale).astype(jnp.bfloat16)
            grad_query_ref[span] = dot32(grad_scores_b, key_ref[...])
            grad_key = dot32_first(grad_scores_b, query_b)
            if place == 0:
                grad_value_ref[...] = grad_value
                grad_key_ref[...] = grad_key
            else:
                grad_value_ref[...] += grad_value
                grad_key_ref[...] += grad_key
        central = centred(embed_w)
        central_top, central_low = halves(central)
        gram = (
            dot32_t(central_top, central_top)
            + dot32_t(central_top, central_low)
            + dot32_t(central_low, central_top)
        )
        gram_top, gram_low = halves(gram)
        short_top, short_low = halves(short_in[:latent_width])
        for place in range(count):
            low = place * size
            span = slice(low, low + size)
            projected = proj_ref[span]
            _, q_unit, q_inverse = rms_scale(projected[:, :head_width], gains[0, :1])
            _, k_unit, k_inverse = rms_scale(
                projected[:, head_width : 2 * head_width], gains[0, 1:2]
            )
            grad_q = rms_back(grad_query_ref[span], q_unit, q_inverse, gains[0, :1])
            grad_k = rms_back(grad_key_ref[span], k_unit, k_inverse, gains[0, 1:2])
            grad_proj = jnp.concatenate([grad_q, grad_k, grad_value_ref[span]], axis=1).astype(
                jnp.bfloat16
            )
            through = dot32_t(grad_proj, short_top) + dot32_t(grad_proj, short_low)
            block = rows[place][...]
            along = jnp.sum(through * block.astype(jnp.float32), axis=1, keepdims=True) / model_width
            spanned = dot32(block, gram_top) + dot32(block, gram_low)
            inverse = inverse_ref[span, :1]
            outs[place][:size] = (
                inverse * (through - spanned * (inverse * inverse * along))
            ).astype(jnp.bfloat16)


def merge_kernel(count, times, direct, term, *refs):
    parts = refs[:count]
    payload_ref = refs[count]
    section = lax.axis_index("segment")
    rows = direct.shape[0]
    total = parts[0][...].astype(jnp.float32)
    for part in parts[1:]:
        total = total + part[...].astype(jnp.float32)
    _, critic_step = steps_of(times)
    sigma_critic = noise_level(critic_step)
    adverse = (1.0 - sigma_critic) * (total[:rows] + direct[...])
    spread = (total[rows : rows + 16] + total[rows + 16 :]) / count + EPS
    spread_top, spread_low = halves(spread)
    payload_ref[:rows] = jnp.where(section == 3, adverse, term[...]).astype(jnp.bfloat16)
    payload_ref[rows : rows + 16] = spread_top
    payload_ref[rows + 16 :] = spread_low


def finish_kernel(sections, times, target_in, student_in, critic_in, *refs):
    received = refs[:sections]
    grad_ref, term_ref = refs[sections:]
    section = lax.axis_index("segment")
    rows = target_in.shape[0]

    def payload_of(source):
        chosen = received[0][...].astype(jnp.float32)
        for offset in range(1, sections):
            chosen = jnp.where(
                lax.rem(section - offset + sections, sections) == source,
                received[offset][...].astype(jnp.float32),
                chosen,
            )
        return chosen

    real, fake, adverse = [payload_of(source) for source in (1, 2, 3)]
    spread = (real[rows : rows + 16] + real[rows + 16 :])[:1, :1]
    sample_grad = (real[:rows] - fake[:rows]) / spread + ADV_WEIGHT * adverse[:rows]
    grad_ref[0] = sample_grad

    @pl.when(section == 0)
    def _():
        student_step, _ = steps_of(times)
        target = (-noise_level(student_step) * sample_grad).astype(jnp.bfloat16)
        term_ref[...] = dot32_first(student_in[...], target).astype(jnp.bfloat16)

    @pl.when(section == 1)
    def _():
        term_ref[...] = jnp.zeros_like(term_ref)

    @pl.when(section >= 2)
    def _():
        term_ref[...] = dot32_first(critic_in[...], target_in[...].astype(jnp.bfloat16)).astype(
            jnp.bfloat16
        )


def reduce_everywhere(term, seq_devices, seq_place):
    rows = term.shape[0]
    held = term
    trail = []
    bit = 1
    while bit < seq_devices:
        half = held.shape[0] // 2
        upper = (seq_place & bit) != 0
        away = jnp.where(upper, held[:half], held[half:])
        kept = jnp.where(upper, held[half:], held[:half])
        moved = lax.ppermute(away, "seq", swaps(seq_devices, bit))
        held = (kept.astype(jnp.float32) + moved.astype(jnp.float32)).astype(jnp.bfloat16)
        trail.append((bit, upper))
        bit *= 2
    batch_devices = lax.axis_size("dp")
    bit = 1
    while bit < batch_devices:
        moved = lax.ppermute(held, "dp", swaps(batch_devices, bit))
        held = (held.astype(jnp.float32) + moved.astype(jnp.float32)).astype(jnp.bfloat16)
        bit *= 2
    for bit, upper in reversed(trail):
        moved = lax.ppermute(held, "seq", swaps(seq_devices, bit))
        held = jnp.concatenate(
            [jnp.where(upper, moved, held), jnp.where(upper, held, moved)], axis=0
        )
    return held


def shards(
    clean, noise, timesteps, text_vec, w_embed, w_time, w_mod, w_qkv, w_out, qk_gain, w_final
):
    section = lax.axis_index("segment")
    sections = lax.axis_size("segment")
    batch_idx = lax.axis_index("dp")
    seq_place = lax.axis_index("seq")
    tok_rows = clean.shape[1]
    latent_width = clean.shape[2]
    model_width = w_embed.shape[2]
    mod_width = w_mod.shape[2]
    count = lax.axis_size("seq")
    full_rows = tok_rows * count
    head_width = w_qkv.shape[4]
    flat_head_w = w_qkv[0, :, 0].reshape(model_width, 3 * head_width)
    step_pair = lax.dynamic_index_in_dim(timesteps, batch_idx, 0, keepdims=False)
    fraction = step_pair[0].astype(jnp.float32) / 1000.0
    sigma_student = SHIFT * fraction / (1.0 + (SHIFT - 1.0) * fraction)
    noisy_student = (
        (1.0 - sigma_student) * clean[0].astype(jnp.float32)
        + sigma_student * noise[0, :, :latent_width].astype(jnp.float32)
    ).astype(jnp.bfloat16)
    with jax.named_scope("heads"):
        heads_w = gather_doubling(w_out[0, 0], "seq", count)
    with jax.named_scope("student_rows"):
        student_rows = gather_near(noisy_student, "seq", count)
    bf16, f32 = jnp.bfloat16, jnp.float32

    (mod_piece,) = run(
        condition_kernel,
        [array((1, mod_width), f32)],
        (timesteps, text_vec, w_time, w_mod),
        [SMEM, VMEM, VMEM, ANY],
        2 * model_width * mod_width,
        scratch=(
            pltpu.VMEM((model_width, mod_width), bf16),
            pltpu.SemaphoreType.DMA((STREAMS,)),
        ),
    )
    with jax.named_scope("modulation"):
        mod_parts = gather_near(mod_piece, "seq", count)
    mod = jnp.concatenate(in_order(mod_parts, seq_place), axis=1)

    head_blocks = [array((tok_rows, head_width), bf16)] * count
    stored = [
        array((full_rows, 3 * head_width), f32),
        array((full_rows, 128), f32),
        array((full_rows, head_width), bf16),
        array((full_rows, head_width), bf16),
    ]
    *head_outs, short, _, _, _, _ = run(
        functools.partial(student_front_kernel, count),
        head_blocks + [array((latent_width + 16, 3 * head_width), f32)] + stored,
        (mod, w_embed, flat_head_w, qk_gain, *student_rows),
        [VMEM] * (4 + count),
        4 * latent_width * model_width * 3 * head_width,
    )
    mixed = scatter_near(head_outs, "seq", count)
    work = pltpu.VMEM((tok_rows, model_width), f32)
    pair, student_in = run(
        functools.partial(student_tail_kernel, count),
        [array((tok_rows, 2 * latent_width), bf16), array((tok_rows, model_width), bf16)],
        (timesteps, mod, noisy_student, noise, w_embed, w_final, *mixed, *heads_w),
        [SMEM] + [VMEM] * (5 + 2 * count),
        2 * tok_rows * model_width * head_width * count,
        scratch=(work,),
    )
    arrived = [
        lax.ppermute(pair, "segment", [(0, place)]) for place in range(sections - 1, 0, -1)
    ]
    pair = jnp.where(section == 0, pair, sum(arrived[1:], arrived[0]))
    critic_rows = gather_near(pair[:, :latent_width], "seq", count)
    *head_outs, proj, inverse, keys, values = run(
        functools.partial(critic_front_kernel, count),
        head_blocks + stored,
        (short, w_embed, qk_gain, *critic_rows),
        [VMEM] * (3 + count),
        4 * latent_width * model_width * full_rows,
    )
    mixed = scatter_near(head_outs, "seq", count)
    small = array((tok_rows, latent_width), f32)
    *grad_heads, critic_in, term_rows, target, error, direct = run(
        functools.partial(critic_tail_kernel, count),
        head_blocks
        + [array((tok_rows, model_width), bf16), small, small, array((32, latent_width), bf16), small],
        (timesteps, mod, pair, noise, w_embed, w_final, *mixed, *heads_w),
        [SMEM] + [VMEM] * (5 + 2 * count),
        4 * tok_rows * model_width * head_width * count,
        scratch=(pltpu.VMEM((tok_rows, latent_width), bf16), work, work),
    )
    grad_blocks = scatter_near(grad_heads, "seq", count)
    parts = run(
        functools.partial(judge_back_kernel, count),
        [array((tok_rows + 32, latent_width), bf16)] * count,
        (short, w_embed, qk_gain, proj, inverse, keys, values, error, *critic_rows, *grad_blocks),
        [VMEM] * (8 + 2 * count),
        10 * full_rows * full_rows * head_width,
        scratch=(pltpu.VMEM((full_rows, head_width), f32),) * 3,
    )
    parts = scatter_near(parts, "seq", count)
    (payload,) = run(
        functools.partial(merge_kernel, count),
        [array((tok_rows + 32, latent_width), bf16)],
        (timesteps, direct, term_rows, *parts),
        [SMEM] + [VMEM] * (2 + count),
        1000,
    )
    received = [payload] + [
        lax.ppermute(
            payload, "segment", [(place, (place + offset) % sections) for place in range(sections)]
        )
        for offset in range(1, sections)
    ]
    sample_grad, term = run(
        functools.partial(finish_kernel, sections),
        [array((1, tok_rows, latent_width), f32), array((model_width, latent_width), bf16)],
        (timesteps, target, student_in, critic_in, *received),
        [SMEM] + [VMEM] * (3 + sections),
        2 * tok_rows * model_width * latent_width,
    )
    total = reduce_everywhere(term, count, seq_place)
    final_grads = total.astype(f32) / full_rows
    return (sample_grad, final_grads[None])


def solution(mesh):
    placed = (
        P("dp", "seq", None),
        P("dp", "seq", None),
        P(),
        P("dp", None),
        P("segment", None, None),
        P("segment", None, None),
        P("segment", None, "seq"),
        P("segment", None, "seq", None, None),
        P("segment", "seq", None, None),
        P("segment", None, None),
        P("segment", None, None),
    )
    return jax.shard_map(
        shards,
        mesh=mesh,
        in_specs=placed,
        out_specs=(P("dp", "seq", None), P("segment", None, None)),
        check_vma=False,
    )
```

```python
import functools
import math

import jax
import jax.numpy as jnp
from jax import lax
from jax.experimental import pallas as pl
from jax.experimental.pallas import tpu as pltpu
from jax.sharding import PartitionSpec as P

SHIFT = 7.0
EPS = 1e-06
ADV_WEIGHT = 3.0
TILE = 512
STREAMS = 6
SPARE = 8 << 20
VMEM = pl.BlockSpec(memory_space=pltpu.VMEM)
SMEM = pl.BlockSpec(memory_space=pltpu.SMEM)
ANY = pl.BlockSpec(memory_space=pl.ANY)


def halves(values):
    top = values.astype(jnp.bfloat16)
    return (top, (values - top.astype(jnp.float32)).astype(jnp.bfloat16))


def split_halves(values):
    top = lax.reduce_precision(values, 8, 7)
    return (top.astype(jnp.bfloat16), (values - top).astype(jnp.bfloat16))


def swaps(count, offset):
    return [(place, place ^ offset) for place in range(count)]


def gather_near(value, axis, count):
    return [value] + [
        lax.ppermute(value, axis, swaps(count, offset)) for offset in range(1, count)
    ]


def scatter_near(blocks, axis, count):
    return [blocks[0]] + [
        lax.ppermute(blocks[offset], axis, swaps(count, offset)) for offset in range(1, count)
    ]


def gather_doubling(value, axis, count):
    held = {0: value}
    bit = count // 2
    while bit:
        offsets = sorted(held)
        joined = jnp.concatenate([held[offset] for offset in offsets], axis=0)
        moved = lax.ppermute(joined, axis, swaps(count, bit))
        rows = value.shape[0]
        for place, offset in enumerate(offsets):
            held[offset | bit] = moved[place * rows : (place + 1) * rows]
        bit //= 2
    return [held[offset] for offset in range(count)]


def in_order(pieces, own_place):
    ordered = list(pieces)
    bit = 1
    while bit < len(ordered):
        flipped = (own_place & bit) != 0
        ordered = [
            jnp.where(flipped, ordered[place ^ bit], ordered[place])
            for place in range(len(ordered))
        ]
        bit *= 2
    return ordered


def dot32(left, right):
    return jnp.dot(left, right, preferred_element_type=jnp.float32)


def dot32_t(left, right):
    return lax.dot_general(
        left, right, (((1,), (1,)), ((), ())), preferred_element_type=jnp.float32
    )


def dot32_first(left, right):
    return lax.dot_general(
        left, right, (((0,), (0,)), ((), ())), preferred_element_type=jnp.float32
    )


def steps_of(times_ref):
    place = lax.axis_index("dp")
    return (times_ref[place, 0], times_ref[place, 1])


def noise_level(step):
    fraction = jnp.full((1, 1), step, jnp.int32).astype(jnp.float32) / 1000.0
    return SHIFT * fraction / (1.0 + (SHIFT - 1.0) * fraction)


def slot_of(mod_ref, slot, width, first, size):
    return mod_ref[:, slot * width + first : slot * width + first + size]


def lane_sum(values):
    total = values[:, :128]
    for first in range(128, values.shape[1], 128):
        total = total + values[:, first : first + 128]
    return total


def run(kernel, outputs, operands, specs, flops, scratch=()):
    in_bytes = sum(operand.size * operand.dtype.itemsize for operand in operands)
    out_bytes = sum(output.size * output.dtype.itemsize for output in outputs)
    held = sum(
        math.prod(ref.shape) * jnp.dtype(ref.dtype).itemsize
        for ref in scratch
        if ref.memory_space == pltpu.VMEM
    )
    small = sum(
        operand.size * operand.dtype.itemsize
        for operand, spec in zip(operands, specs)
        if spec is VMEM
    )
    limit = min(60 << 20, SPARE + held + small + 2 * out_bytes)
    return pl.pallas_call(
        kernel,
        out_shape=outputs,
        in_specs=specs,
        out_specs=[VMEM] * len(outputs),
        scratch_shapes=list(scratch),
        compiler_params=pltpu.CompilerParams(vmem_limit_bytes=limit),
        cost_estimate=pl.CostEstimate(
            flops=flops, bytes_accessed=in_bytes + out_bytes, transcendentals=0
        ),
    )(*operands)


def array(shape, dtype):
    return jax.ShapeDtypeStruct(shape, dtype)


def condition_kernel(times, text, time_w, clean_t, noise, mod_w, mod_out, noisy_out, held, arrivals):
    model_width = mod_w.shape[1]
    rows = model_width // STREAMS
    copies = [
        pltpu.make_async_copy(
            mod_w.at[0, pl.ds(part * rows, rows)], held.at[pl.ds(part * rows, rows)], arrivals.at[part]
        )
        for part in range(STREAMS)
    ]
    for copy in copies:
        copy.start()
    student_step, critic_step = steps_of(times)
    sigma_student = noise_level(student_step)
    noisy_out[...] = (
        (1.0 - sigma_student) * clean_t[...].astype(jnp.float32).T
        + sigma_student * noise[0, :, : clean_t.shape[0]].astype(jnp.float32)
    ).astype(jnp.bfloat16)
    step = jnp.where(lax.axis_index("segment") == 0, student_step, critic_step)
    half = text.shape[1] // 2
    places = lax.broadcasted_iota(jnp.int32, (1, half), 1).astype(jnp.float32)
    frequency = jnp.exp(-math.log(10000.0) * places / half)
    angles = jnp.full((1, half), step, jnp.int32).astype(jnp.float32) * frequency
    features = jnp.concatenate([jnp.cos(angles), jnp.sin(angles)], axis=1) + text[...]
    features = jnp.broadcast_to(features, (8, 2 * half)).astype(jnp.bfloat16)
    hidden = dot32(features, time_w[0])
    hidden = (hidden / (1.0 + jnp.exp(-hidden))).astype(jnp.bfloat16)
    total = None
    for part in range(STREAMS):
        copies[part].wait()
        piece = dot32(
            hidden[:, part * rows : (part + 1) * rows], held[part * rows : (part + 1) * rows]
        )
        total = piece if total is None else total + piece
    mod_out[...] = total[:1]


def rms_scale(values, gain_vec):
    inverse = lax.rsqrt(jnp.mean(values * values, axis=-1, keepdims=True) + EPS)
    unit_vec = values * inverse
    return (unit_vec * gain_vec, unit_vec, inverse)


def rms_back(gradient, unit_vec, inverse, gain_vec):
    scaled = gradient * gain_vec
    return inverse * (scaled - unit_vec * jnp.mean(scaled * unit_vec, axis=-1, keepdims=True))


def centred(embed_ref):
    values = embed_ref[0].astype(jnp.float32)
    return values - jnp.mean(values, axis=1, keepdims=True)


def front(rows, central, short, gains, head_outs, proj_ref, inverse_ref, key_ref, value_ref):
    latent_width = central.shape[0]
    model_width = central.shape[1]
    count = len(rows)
    head_width = gains.shape[2]
    short_top, short_low = halves(short[:latent_width])
    short_shift = short[latent_width : latent_width + 1]
    scale = 1.0 / math.sqrt(head_width)
    size = rows[0].shape[0]
    for place in range(count):
        block = rows[place][...]
        squares = None
        for first in range(0, model_width, TILE):
            piece = dot32(block, central[:, first : first + TILE])
            piece = lane_sum(piece * piece)
            squares = piece if squares is None else squares + piece
        inverse = lax.rsqrt(jnp.sum(squares, axis=1, keepdims=True) / model_width + EPS)
        projected = inverse * (dot32(block, short_top) + dot32(block, short_low)) + short_shift
        low = place * size
        proj_ref[low : low + size] = projected
        inverse_ref[low : low + size] = jnp.broadcast_to(inverse, (size, 128))
        keys, _, _ = rms_scale(projected[:, head_width : 2 * head_width], gains[0, 1:2])
        key_ref[low : low + size] = keys.astype(jnp.bfloat16)
        value_ref[low : low + size] = projected[:, 2 * head_width :].astype(jnp.bfloat16)
    for place in range(count):
        low = place * size
        queries, _, _ = rms_scale(proj_ref[low : low + size, :head_width], gains[0, :1])
        scores = dot32_t(queries.astype(jnp.bfloat16), key_ref[...]) * scale
        weights = jnp.exp(scores)
        soft_max = weights * (1.0 / jnp.sum(weights, axis=-1, keepdims=True))
        head_outs[place][...] = dot32(soft_max.astype(jnp.bfloat16), value_ref[...]).astype(
            jnp.bfloat16
        )


def student_front_kernel(count, embed_w, head_w, gains, *refs):
    mod_parts = refs[:count]
    rows = refs[count : 2 * count]
    head_outs = refs[2 * count : 3 * count]
    short_ref, late_ref, mod, proj_ref, inverse_ref, key_ref, value_ref = refs[3 * count :]
    model_width = embed_w.shape[2]
    width = mod_parts[0].shape[1]
    for place in range(count):
        first = pl.multiple_of((lax.axis_index("seq") ^ place) * width, 128)
        mod[:, pl.ds(first, width)] = mod_parts[place][...]
    late_ref[...] = mod[:, 2 * model_width :]
    central = centred(embed_w)
    scale_in = slot_of(mod, 1, model_width, 0, model_width)
    shift_in = slot_of(mod, 0, model_width, 0, model_width)
    in_rows = jnp.concatenate(
        [central * (1.0 + scale_in), jnp.broadcast_to(shift_in, (16, model_width))], axis=0
    )
    in_top, in_low = halves(in_rows)
    in_both = jnp.concatenate([in_top, in_low], axis=0)
    both = jnp.concatenate([dot32(in_both, head_w[kind]) for kind in range(3)], axis=1)
    short = both[: in_rows.shape[0]] + both[in_rows.shape[0] :]
    short_ref[...] = short

    @pl.when(lax.axis_index("segment") == 0)
    def _():
        front(
            rows,
            central.astype(jnp.bfloat16),
            short,
            gains,
            head_outs,
            proj_ref,
            inverse_ref,
            key_ref,
            value_ref,
        )


def critic_front_kernel(count, short_in, embed_w, gains, *refs):
    rows = refs[:count]
    head_outs = refs[count : 2 * count]
    proj_ref, inverse_ref, key_ref, value_ref = refs[2 * count :]

    @pl.when(lax.axis_index("segment") != 0)
    def _():
        front(
            rows,
            centred(embed_w).astype(jnp.bfloat16),
            short_in[...],
            gains,
            head_outs,
            proj_ref,
            inverse_ref,
            key_ref,
            value_ref,
        )


def tail(mod, latent, embed_w, final_w, mixed, heads_w, work):
    model_width = embed_w.shape[2]
    block = latent[...]
    sums = None
    for first in range(0, model_width, TILE):
        span = slice(first, first + TILE)
        attended = None
        for piece, rows_w in zip(mixed, heads_w):
            product = dot32(piece[...], rows_w[:, span])
            attended = product if attended is None else attended + product
        residual = (
            dot32(block, embed_w[0, :, span]) + slot_of(mod, 0, model_width, first, TILE) * attended
        )
        work[:, span] = residual
        part = lane_sum(residual)
        sums = part if sums is None else sums + part
    row_mean = jnp.sum(sums, axis=1, keepdims=True) / model_width
    sums = None
    for first in range(0, model_width, TILE):
        span = slice(first, first + TILE)
        middle = work[:, span] - row_mean
        work[:, span] = middle
        part = lane_sum(middle * middle)
        sums = part if sums is None else sums + part
    inverse = lax.rsqrt(jnp.sum(sums, axis=1, keepdims=True) / model_width + EPS)
    result = None
    for first in range(0, model_width, TILE):
        span = slice(first, first + TILE)
        normed = work[:, span] * inverse
        work[:, span] = normed
        final_in = (
            normed * (1.0 + slot_of(mod, 2, model_width, first, TILE))
            + slot_of(mod, 1, model_width, first, TILE)
        ).astype(jnp.bfloat16)
        product = dot32_t(final_in, final_w[:, span])
        result = product if result is None else result + product
    return (result, inverse)


def student_tail_kernel(count, times, mod, latent, noise, embed_w, final_w, *refs):
    mixed = refs[:count]
    heads_w = refs[count : 2 * count]
    pair_ref, inverse_ref, work = refs[2 * count :]
    latent_width = latent.shape[1]

    @pl.when(lax.axis_index("segment") == 0)
    def _():
        student_step, critic_step = steps_of(times)
        sigma_student, sigma_critic = noise_level(student_step), noise_level(critic_step)
        velocity, inverse = tail(mod, latent, embed_w, final_w, mixed, heads_w, work)
        inverse_ref[...] = jnp.broadcast_to(inverse, inverse_ref.shape)
        sample = latent[...].astype(jnp.float32) - sigma_student * velocity
        second = noise[0, :, latent_width:].astype(jnp.float32)
        critic = (1.0 - sigma_critic) * sample + sigma_critic * second
        pair_ref[...] = jnp.concatenate([critic, sample], axis=1).astype(jnp.bfloat16)


def critic_tail_kernel(count, times, mod, pair, noise, embed_w, final_w, *refs):
    mixed = refs[:count]
    heads_w = refs[count : 2 * count]
    grads = refs[2 * count : 3 * count]
    inverse_ref, term_ref, target_ref, direct_ref, latent, work, other = refs[3 * count :]
    model_width = embed_w.shape[2]
    latent_width = latent.shape[1]
    section = lax.axis_index("segment")

    @pl.when(section != 0)
    def _():
        _, critic_step = steps_of(times)
        sigma_critic = noise_level(critic_step)
        both = pair[...].astype(jnp.float32)
        sample = both[:, latent_width:]
        latent[...] = pair[:, :latent_width]
        result, inverse = tail(mod, latent, embed_w, final_w, mixed, heads_w, work)
        inverse_ref[...] = jnp.broadcast_to(inverse, inverse_ref.shape)
        term_ref[...] = (sigma_critic * result).astype(jnp.bfloat16)
        second = noise[0, :, latent_width:].astype(jnp.float32)
        target_ref[...] = jnp.where(
            section == 2,
            2.0 * (result - (second - sample)),
            jnp.where(section == 3, 1.0 / (1.0 + jnp.exp(-result)), 0.0),
        )
        @pl.when(section == 3)
        def _():
            grad_logit = (-1.0 / (1.0 + jnp.exp(result))).astype(jnp.bfloat16)
            plain, along = None, None
            for first in range(0, model_width, TILE):
                span = slice(first, first + TILE)
                gradient = dot32(grad_logit, final_w[:, span]) * (
                    1.0 + slot_of(mod, 2, model_width, first, TILE)
                )
                other[:, span] = gradient
                part = lane_sum(gradient)
                plain = part if plain is None else plain + part
                part = lane_sum(gradient * work[:, span])
                along = part if along is None else along + part
            plain = jnp.sum(plain, axis=1, keepdims=True) / model_width
            along = jnp.sum(along, axis=1, keepdims=True) / model_width
            direct = None
            totals = [None] * count
            for first in range(0, model_width, TILE):
                span = slice(first, first + TILE)
                grad_residual = inverse * (other[:, span] - plain - work[:, span] * along)
                top, low = halves(grad_residual)
                product = dot32_t(top, embed_w[0, :, span]) + dot32_t(low, embed_w[0, :, span])
                direct = product if direct is None else direct + product
                grad_attended = (slot_of(mod, 0, model_width, first, TILE) * grad_residual).astype(
                    jnp.bfloat16
                )
                for place in range(count):
                    product = dot32_t(grad_attended, heads_w[place][:, span])
                    held = totals[place]
                    totals[place] = product if held is None else held + product
            direct_ref[...] = direct
            for place in range(count):
                grads[place][...] = totals[place].astype(jnp.bfloat16)


def judge_back_kernel(count, short_in, embed_w, gains, proj_ref, inverse_ref, key_ref, value_ref, pair, real, *refs):
    rows = refs[:count]
    grads = refs[count : 2 * count]
    outs = refs[2 * count : 3 * count]
    grad_key_ref, grad_value_ref, grad_query_ref = refs[3 * count :]
    section = lax.axis_index("segment")
    latent_width = rows[0].shape[1]
    model_width = embed_w.shape[2]
    head_width = gains.shape[2]
    scale = 1.0 / math.sqrt(head_width)
    size = rows[0].shape[0]

    @pl.when(section == 3)
    def _():
        both = pair[...].astype(jnp.float32)
        gaps = jnp.abs(
            both[:, latent_width:] - both[:, :latent_width] + real[...].astype(jnp.float32)
        )
        error = jnp.sum(jnp.sum(gaps, axis=1, keepdims=True), axis=0, keepdims=True)
        error = error / (size * latent_width)
        error_top, error_low = halves(jnp.broadcast_to(error, (16, latent_width)))
        for place in range(count):
            outs[place][size : size + 16] = error_top
            outs[place][size + 16 :] = error_low
            low = place * size
            span = slice(low, low + size)
            queries, _, _ = rms_scale(proj_ref[span, :head_width], gains[0, :1])
            query_b = queries.astype(jnp.bfloat16)
            weights = jnp.exp(dot32_t(query_b, key_ref[...]) * scale)
            soft_max = weights * (1.0 / jnp.sum(weights, axis=-1, keepdims=True))
            grad_out = grads[place][...]
            grad_soft = dot32_t(grad_out, value_ref[...])
            grad_value = dot32_first(soft_max.astype(jnp.bfloat16), grad_out)
            grad_scores = soft_max * (
                grad_soft - jnp.sum(soft_max * grad_soft, axis=-1, keepdims=True)
            )
            grad_scores_b = (grad_scores * scale).astype(jnp.bfloat16)
            grad_query_ref[span] = dot32(grad_scores_b, key_ref[...])
            grad_key = dot32_first(grad_scores_b, query_b)
            if place == 0:
                grad_value_ref[...] = grad_value
                grad_key_ref[...] = grad_key
            else:
                grad_value_ref[...] += grad_value
                grad_key_ref[...] += grad_key
        central = centred(embed_w)
        central_top, central_low = halves(central)
        gram = (
            dot32_t(central_top, central_top)
            + dot32_t(central_top, central_low)
            + dot32_t(central_low, central_top)
        )
        gram_top, gram_low = halves(gram)
        short_top, short_low = halves(short_in[:latent_width])
        for place in range(count):
            low = place * size
            span = slice(low, low + size)
            projected = proj_ref[span]
            _, q_unit, q_inverse = rms_scale(projected[:, :head_width], gains[0, :1])
            _, k_unit, k_inverse = rms_scale(
                projected[:, head_width : 2 * head_width], gains[0, 1:2]
            )
            grad_q = rms_back(grad_query_ref[span], q_unit, q_inverse, gains[0, :1])
            grad_k = rms_back(grad_key_ref[span], k_unit, k_inverse, gains[0, 1:2])
            grad_proj = jnp.concatenate([grad_q, grad_k, grad_value_ref[span]], axis=1).astype(
                jnp.bfloat16
            )
            through = dot32_t(grad_proj, short_top) + dot32_t(grad_proj, short_low)
            block = rows[place][...]
            along = jnp.sum(through * block.astype(jnp.float32), axis=1, keepdims=True) / model_width
            spanned = dot32(block, gram_top) + dot32(block, gram_low)
            inverse = inverse_ref[span, :1]
            outs[place][:size] = (
                inverse * (through - spanned * (inverse * inverse * along))
            ).astype(jnp.bfloat16)


def merge_kernel(count, times, direct, real, fake, *refs):
    parts = refs[:count]
    payload_ref = refs[count]
    rows = direct.shape[0]

    @pl.when(lax.axis_index("segment") == 3)
    def _():
        total = parts[0][...].astype(jnp.float32)
        for part in parts[1:]:
            total = total + part[...].astype(jnp.float32)
        _, critic_step = steps_of(times)
        adverse = (1.0 - noise_level(critic_step)) * (total[:rows] + direct[...])
        spread = (total[rows : rows + 16] + total[rows + 16 :])[:1, :1] / count + EPS
        gap = real[...].astype(jnp.float32) - fake[...].astype(jnp.float32)
        payload_ref[...] = (gap / spread + ADV_WEIGHT * adverse).astype(jnp.bfloat16)


def outer_kernel(
    count, times, arrived, target_in, student_rows, pair, student_inverse, critic_inverse, *refs
):
    student_mixed = refs[:count]
    critic_mixed = refs[count : 2 * count]
    sums_ref = refs[2 * count]
    section = lax.axis_index("segment")
    place = lax.axis_index("seq")
    latent_width = student_rows.shape[1]

    def collect(target, inverse, latent, mixed):
        target = target.astype(jnp.bfloat16)
        weighted = inverse[:, :latent_width] * target.astype(jnp.float32)
        top, low = halves(weighted)
        for offset in range(count):
            piece = mixed[offset][...]
            sums_ref[place ^ offset] = (dot32_first(top, piece) + dot32_first(low, piece)).astype(
                jnp.bfloat16
            )
        near = dot32_first(top, latent) + dot32_first(low, latent)
        ones = jnp.ones((target.shape[0], sums_ref.shape[2] - latent_width), jnp.bfloat16)
        sums_ref[count] = jnp.concatenate([near, dot32_first(target, ones)], axis=1).astype(
            jnp.bfloat16
        )

    @pl.when(section == 0)
    def _():
        student_step, _ = steps_of(times)
        target = -noise_level(student_step) * arrived[...].astype(jnp.float32)
        collect(target, student_inverse, student_rows[...], student_mixed)

    @pl.when(section == 1)
    def _():
        sums_ref[...] = jnp.zeros_like(sums_ref)

    @pl.when(section >= 2)
    def _():
        collect(target_in[...], critic_inverse, pair[:, :latent_width], critic_mixed)


def expand_kernel(count, groups, full_rows, own, from_first, from_second, from_third, embed_w, *refs):
    heads_w = refs[:count]
    mods = refs[count : count + groups]
    sums = refs[count + groups : count + 3 * groups]
    grad_ref, total_ref, work, joined = refs[count + 3 * groups :]
    section = lax.axis_index("segment")
    place = lax.axis_index("seq")
    latent_width = embed_w.shape[1]
    model_width = embed_w.shape[2]
    picked = own[...].astype(jnp.float32)
    for source, value in ((0, from_first), (2, from_second), (1, from_third)):
        picked = jnp.where(section == source, value[...].astype(jnp.float32), picked)
    grad_ref[...] = picked.T

    @pl.when(section == 1)
    def _():
        total_ref[...] = jnp.zeros_like(total_ref)

    @pl.when(section != 1)
    def _():
        for group in range(groups):
            low = group * latent_width
            joined[:, low : low + latent_width] = sums[2 * group][...].astype(jnp.float32) + sums[
                2 * group + 1
            ][...].astype(jnp.float32)
        near_top, near_low = halves(joined[count])
        heads = [halves(joined[place ^ offset]) for offset in range(count)]
        averages = None
        for first in range(0, model_width, TILE):
            span = slice(first, first + TILE)
            spread = None
            for (top, low), rows_w in zip(heads, heads_w):
                product = dot32(top, rows_w[:, span]) + dot32(low, rows_w[:, span])
                spread = product if spread is None else spread + product
            near = dot32(near_top[:, :latent_width], embed_w[0, :, span]) + dot32(
                near_low[:, :latent_width], embed_w[0, :, span]
            )
            gates = jnp.concatenate(
                [
                    jnp.broadcast_to(
                        slot_of(mod, 0, model_width, first, TILE), (latent_width, TILE)
                    )
                    for mod in mods
                ],
                axis=0,
            )
            value = near + gates * spread
            work[:, span] = value
            part = lane_sum(value)
            averages = part if averages is None else averages + part
        averages = jnp.sum(averages, axis=1, keepdims=True) / model_width
        counts = joined[count][:, latent_width : latent_width + 1]
        for first in range(0, model_width, TILE):
            span = slice(first, first + TILE)
            value = work[:, span] - averages
            total = None
            for group in range(groups):
                mine = slice(group * latent_width, (group + 1) * latent_width)
                product = value[mine] * (
                    1.0 + slot_of(mods[group], 2, model_width, first, TILE)
                ) + counts[mine] * slot_of(mods[group], 1, model_width, first, TILE)
                total = product if total is None else total + product
            total_ref[:, span] = total / full_rows


def shards(
    clean, noise, timesteps, text_vec, w_embed, w_time, w_mod, w_qkv, w_out, qk_gain, w_final
):
    section = lax.axis_index("segment")
    sections = lax.axis_size("segment")
    batch_idx = lax.axis_index("dp")
    seq_place = lax.axis_index("seq")
    tok_rows = clean.shape[1]
    latent_width = clean.shape[2]
    model_width = w_embed.shape[2]
    mod_width = w_mod.shape[2]
    count = lax.axis_size("seq")
    full_rows = tok_rows * count
    head_width = w_qkv.shape[4]
    kind_w = jnp.transpose(w_qkv[0, :, 0], (1, 0, 2))
    final_w = jnp.transpose(w_final[0])
    with jax.named_scope("heads"):
        heads_w = gather_doubling(w_out[0, 0], "seq", count)
    bf16, f32 = jnp.bfloat16, jnp.float32

    with jax.named_scope("conditioning"):
        mod_piece, noisy_student = run(
            condition_kernel,
            [array((1, mod_width), f32), array((tok_rows, latent_width), bf16)],
            (timesteps, text_vec, w_time, jnp.transpose(clean[0]), noise, w_mod),
            [SMEM, VMEM, VMEM, VMEM, VMEM, ANY],
            2 * model_width * mod_width,
            scratch=(
                pltpu.VMEM((model_width, mod_width), bf16),
                pltpu.SemaphoreType.DMA((STREAMS,)),
            ),
        )
    with jax.named_scope("modulation"):
        mod_parts = gather_near(mod_piece, "seq", count)
    with jax.named_scope("student_rows"):
        student_rows = gather_near(noisy_student, "seq", count)

    head_blocks = [array((tok_rows, head_width), bf16)] * count
    stored = [
        ((full_rows, 3 * head_width), f32),
        ((full_rows, 128), f32),
        ((full_rows, head_width), bf16),
        ((full_rows, head_width), bf16),
    ]
    with jax.named_scope("student_front"):
        *head_outs, short, late_mod = run(
            functools.partial(student_front_kernel, count),
            head_blocks
            + [
                array((latent_width + 16, 3 * head_width), f32),
                array((1, 3 * model_width), f32),
            ],
            (w_embed, kind_w, qk_gain, *mod_parts, *student_rows),
            [VMEM] * (3 + 2 * count),
            4 * latent_width * model_width * 3 * head_width,
            scratch=[pltpu.VMEM((1, 5 * model_width), f32)]
            + [pltpu.VMEM(shape, kind) for shape, kind in stored],
        )
    with jax.named_scope("student_heads"):
        student_mixed = scatter_near(head_outs, "seq", count)
    with jax.named_scope("other_mod"):
        groups = lax.axis_size("dp")
        late_mods = gather_near(late_mod, "dp", groups)
    work = pltpu.VMEM((tok_rows, model_width), f32)
    inverse_shape = array((tok_rows, 128), f32)
    with jax.named_scope("student_tail"):
        pair, student_inverse = run(
            functools.partial(student_tail_kernel, count),
            [array((tok_rows, 2 * latent_width), bf16), inverse_shape],
            (timesteps, late_mod, noisy_student, noise, w_embed, final_w, *student_mixed, *heads_w),
            [SMEM] + [VMEM] * (5 + 2 * count),
            2 * tok_rows * model_width * head_width * count,
            scratch=(work,),
        )
    with jax.named_scope("sample"):
        for offset in range(sections - 1, 0, -1):
            moved = lax.ppermute(
                pair,
                "segment",
                [(place, (place + offset) % sections) for place in range(sections)],
            )
            held = moved if offset == sections - 1 else jnp.where(section == offset, moved, held)
        pair = jnp.where(section == 0, pair, held)
    with jax.named_scope("critic_rows"):
        critic_rows = gather_near(pair[:, :latent_width], "seq", count)
    with jax.named_scope("critic_front"):
        *head_outs, proj, inverse, keys, values = run(
            functools.partial(critic_front_kernel, count),
            head_blocks + [array(shape, kind) for shape, kind in stored],
            (short, w_embed, qk_gain, *critic_rows),
            [VMEM] * (3 + count),
            4 * latent_width * model_width * full_rows,
        )
    with jax.named_scope("critic_heads"):
        critic_mixed = scatter_near(head_outs, "seq", count)
    small = array((tok_rows, latent_width), f32)
    thin = array((tok_rows, latent_width), bf16)
    with jax.named_scope("critic_tail"):
        *grad_heads, critic_inverse, term_rows, target, direct = run(
            functools.partial(critic_tail_kernel, count),
            head_blocks + [inverse_shape, thin, small, small],
            (timesteps, late_mod, pair, noise, w_embed, final_w, *critic_mixed, *heads_w),
            [SMEM] + [VMEM] * (5 + 2 * count),
            4 * tok_rows * model_width * head_width * count,
            scratch=(pltpu.VMEM((tok_rows, latent_width), bf16), work, work),
        )
    with jax.named_scope("grad_heads"):
        grad_blocks = scatter_near(grad_heads, "seq", count)
    with jax.named_scope("fake"):
        fake = lax.ppermute(term_rows, "segment", swaps(sections, 1))
    with jax.named_scope("real"):
        real = lax.ppermute(term_rows, "segment", swaps(sections, 2))
    with jax.named_scope("judge_back"):
        parts = run(
            functools.partial(judge_back_kernel, count),
            [array((tok_rows + 32, latent_width), bf16)] * count,
            (
                short,
                w_embed,
                qk_gain,
                proj,
                inverse,
                keys,
                values,
                pair,
                real,
                *critic_rows,
                *grad_blocks,
            ),
            [VMEM] * (9 + 2 * count),
            10 * full_rows * full_rows * head_width,
            scratch=(pltpu.VMEM((full_rows, head_width), f32),) * 3,
        )
    with jax.named_scope("grad_rows"):
        parts = scatter_near(parts, "seq", count)
    with jax.named_scope("merge"):
        (payload,) = run(
            functools.partial(merge_kernel, count),
            [thin],
            (timesteps, direct, real, fake, *parts),
            [SMEM] + [VMEM] * (3 + count),
            1000,
        )
    with jax.named_scope("to_student"):
        to_student = lax.ppermute(
            payload, "segment", [(place, sections - 1 - place) for place in range(sections)]
        )
    with jax.named_scope("outer"):
        (sums,) = run(
            functools.partial(outer_kernel, count),
            [array((count + 1, latent_width, 128), bf16)],
            (
                timesteps,
                to_student,
                target,
                noisy_student,
                pair,
                student_inverse,
                critic_inverse,
                *student_mixed,
                *critic_mixed,
            ),
            [SMEM] + [VMEM] * (6 + 2 * count),
            2 * tok_rows * latent_width * head_width * (count + 1),
        )
    last = count // 2
    bit = 1
    while bit < last:
        with jax.named_scope("sums_near"):
            moved = lax.ppermute(sums, "seq", swaps(count, bit))
        sums = (sums.astype(f32) + moved.astype(f32)).astype(bf16)
        bit *= 2
    sums_all = []
    for group in range(groups):
        for offset in (0, last):
            moves = [
                (place * groups + batch, (place ^ offset) * groups + (batch ^ group))
                for place in range(count)
                for batch in range(groups)
            ]
            with jax.named_scope("sums_far"):
                sums_all.append(
                    sums
                    if offset == group == 0
                    else lax.ppermute(sums, ("seq", "dp"), moves)
                )
    with jax.named_scope("to_second"):
        to_second = lax.ppermute(payload, "segment", swaps(sections, 1))
    with jax.named_scope("to_third"):
        to_third = lax.ppermute(payload, "segment", swaps(sections, 2))
    with jax.named_scope("expand"):
        grad_t, total_t = run(
            functools.partial(expand_kernel, count, groups, full_rows),
            [array((latent_width, tok_rows), f32), array((latent_width, model_width), f32)],
            (
                payload,
                to_student,
                to_second,
                to_third,
                w_embed,
                *heads_w,
                *late_mods,
                *sums_all,
            ),
            [VMEM] * (5 + count + 3 * groups),
            4 * groups * latent_width * model_width * head_width * count,
            scratch=(
                pltpu.VMEM((groups * latent_width, model_width), f32),
                pltpu.VMEM((count + 1, groups * latent_width, 128), f32),
            ),
        )
    return (jnp.transpose(grad_t)[None], jnp.transpose(total_t)[None])


def solution(mesh):
    placed = (
        P("dp", "seq", None),
        P("dp", "seq", None),
        P(),
        P("dp", None),
        P("segment", None, None),
        P("segment", None, None),
        P("segment", None, "seq"),
        P("segment", None, "seq", None, None),
        P("segment", "seq", None, None),
        P("segment", None, None),
        P("segment", None, None),
    )
    return jax.shard_map(
        shards,
        mesh=mesh,
        in_specs=placed,
        out_specs=(P("dp", "seq", None), P("segment", None, None)),
        check_vma=False,
    )
```

```python
import functools
import math

import jax
import jax.numpy as jnp
from jax import lax
from jax.experimental import pallas as pl
from jax.experimental.pallas import tpu as pltpu
from jax.sharding import PartitionSpec as P


SHIFT = 7.0
EPS = 1e-06
ADV_WEIGHT = 3.0
TILE = 512
STREAMS = 6
SPARE = 8 << 20
VMEM = pl.BlockSpec(memory_space=pltpu.VMEM)
SMEM = pl.BlockSpec(memory_space=pltpu.SMEM)
ANY = pl.BlockSpec(memory_space=pl.ANY)


def halves(values):
    top = values.astype(jnp.bfloat16)
    return (top, (values - top.astype(jnp.float32)).astype(jnp.bfloat16))


def swaps(count, offset):
    return [(place, place ^ offset) for place in range(count)]


def gather_near(value, axis, count):
    return [value] + [lax.ppermute(value, axis, swaps(count, offset)) for offset in range(1, count)]


def scatter_near(blocks, axis, count):
    return [blocks[0]] + [
        lax.ppermute(blocks[offset], axis, swaps(count, offset))
        for offset in range(1, count)
    ]


def gather_doubling(value, axis, count):
    held = {0: value}
    bit = count // 2
    while bit:
        for offset in sorted(held):
            held[offset | bit] = lax.ppermute(held[offset], axis, swaps(count, bit))
        bit //= 2
    return [held[offset] for offset in range(count)]


def dot32(left, right):
    return jnp.dot(left, right, preferred_element_type=jnp.float32)


def dot32_t(left, right):
    return lax.dot_general(
        left, right, (((1,), (1,)), ((), ())), preferred_element_type=jnp.float32
    )


def dot32_first(left, right):
    return lax.dot_general(
        left, right, (((0,), (0,)), ((), ())), preferred_element_type=jnp.float32
    )


def steps_of(times_ref):
    place = lax.axis_index("dp")
    return (times_ref[place, 0], times_ref[place, 1])


def noise_level(step):
    fraction = jnp.full((1, 1), step, jnp.int32).astype(jnp.float32) / 1000.0
    return SHIFT * fraction / (1.0 + (SHIFT - 1.0) * fraction)


def slot_of(mod_ref, slot, width, first, size):
    return mod_ref[:, slot * width + first : slot * width + first + size]


def lane_sum(values):
    total = values[:, :128]
    for first in range(128, values.shape[1], 128):
        total = total + values[:, first : first + 128]
    return total


def run(kernel, outputs, operands, specs, flops, scratch=()):
    in_bytes = sum(operand.size * operand.dtype.itemsize for operand in operands)
    out_bytes = sum(output.size * output.dtype.itemsize for output in outputs)
    held = sum(
        math.prod(ref.shape) * jnp.dtype(ref.dtype).itemsize
        for ref in scratch
        if ref.memory_space == pltpu.VMEM
    )
    small = sum(
        operand.size * operand.dtype.itemsize
        for operand, spec in zip(operands, specs)
        if spec is VMEM
    )
    limit = min(60 << 20, SPARE + held + small + 2 * out_bytes)
    return pl.pallas_call(
        kernel,
        out_shape=outputs,
        in_specs=specs,
        out_specs=[VMEM] * len(outputs),
        scratch_shapes=list(scratch),
        compiler_params=pltpu.CompilerParams(vmem_limit_bytes=limit),
        cost_estimate=pl.CostEstimate(
            flops=flops, bytes_accessed=in_bytes + out_bytes, transcendentals=0
        ),
    )(*operands)


def array(shape, dtype):
    return jax.ShapeDtypeStruct(shape, dtype)


def condition_kernel(times, text, time_w, clean_t, noise, mod_w, mod_out, noisy_out, held, arrivals):
    model_width = mod_w.shape[1]
    rows = model_width // STREAMS
    copies = [
        pltpu.make_async_copy(
            mod_w.at[0, pl.ds(part * rows, rows)], held.at[pl.ds(part * rows, rows)], arrivals.at[part]
        )
        for part in range(STREAMS)
    ]
    for copy in copies:
        copy.start()
    student_step, critic_step = steps_of(times)
    sigma_student = noise_level(student_step)
    noisy_out[...] = (
        (1.0 - sigma_student) * clean_t[...].astype(jnp.float32).T
        + sigma_student * noise[0, :, : clean_t.shape[0]].astype(jnp.float32)
    ).astype(jnp.bfloat16)
    step = jnp.where(lax.axis_index("segment") == 0, student_step, critic_step)
    half = text.shape[1] // 2
    places = lax.broadcasted_iota(jnp.int32, (1, half), 1).astype(jnp.float32)
    frequency = jnp.exp(-math.log(10000.0) * places / half)
    angles = jnp.full((1, half), step, jnp.int32).astype(jnp.float32) * frequency
    features = jnp.concatenate([jnp.cos(angles), jnp.sin(angles)], axis=1) + text[...]
    features = jnp.broadcast_to(features, (8, 2 * half)).astype(jnp.bfloat16)
    hidden = dot32(features, time_w[0])
    hidden = (hidden / (1.0 + jnp.exp(-hidden))).astype(jnp.bfloat16)
    total = None
    for part in range(STREAMS):
        copies[part].wait()
        piece = dot32(
            hidden[:, part * rows : (part + 1) * rows], held[part * rows : (part + 1) * rows]
        )
        total = piece if total is None else total + piece
    mod_out[...] = total[:1]


def rms_scale(values, gain_vec):
    inverse = lax.rsqrt(jnp.mean(values * values, axis=-1, keepdims=True) + EPS)
    unit_vec = values * inverse
    return (unit_vec * gain_vec, unit_vec, inverse)


def rms_back(gradient, unit_vec, inverse, gain_vec):
    scaled = gradient * gain_vec
    return inverse * (scaled - unit_vec * jnp.mean(scaled * unit_vec, axis=-1, keepdims=True))


def centred(embed_ref):
    values = embed_ref[0].astype(jnp.float32)
    return values - jnp.mean(values, axis=1, keepdims=True)


def front(rows, central, short, gains, head_outs, proj_ref, inverse_ref, key_ref, value_ref):
    latent_width = central.shape[0]
    model_width = central.shape[1]
    count = len(rows)
    head_width = gains.shape[2]
    short_top, short_low = halves(short[:latent_width])
    short_shift = short[latent_width : latent_width + 1]
    scale = 1.0 / math.sqrt(head_width)
    size = rows[0].shape[0]
    for place in range(count):
        block = rows[place][...]
        squares = None
        for first in range(0, model_width, TILE):
            piece = dot32(block, central[:, first : first + TILE])
            piece = lane_sum(piece * piece)
            squares = piece if squares is None else squares + piece
        inverse = lax.rsqrt(jnp.sum(squares, axis=1, keepdims=True) / model_width + EPS)
        projected = inverse * (dot32(block, short_top) + dot32(block, short_low)) + short_shift
        low = place * size
        proj_ref[low : low + size] = projected
        inverse_ref[low : low + size] = jnp.broadcast_to(inverse, (size, 128))
        keys, _, _ = rms_scale(projected[:, head_width : 2 * head_width], gains[0, 1:2])
        key_ref[low : low + size] = keys.astype(jnp.bfloat16)
        value_ref[low : low + size] = projected[:, 2 * head_width :].astype(jnp.bfloat16)
    for place in range(count):
        low = place * size
        queries, _, _ = rms_scale(proj_ref[low : low + size, :head_width], gains[0, :1])
        scores = dot32_t(queries.astype(jnp.bfloat16), key_ref[...]) * scale
        weights = jnp.exp(scores)
        soft_max = weights * (1.0 / jnp.sum(weights, axis=-1, keepdims=True))
        head_outs[place][...] = dot32(soft_max.astype(jnp.bfloat16), value_ref[...]).astype(
            jnp.bfloat16
        )


def student_front_kernel(count, embed_w, head_w, gains, *refs):
    mod_parts = refs[:count]
    rows = refs[count : 2 * count]
    head_outs = refs[2 * count : 3 * count]
    short_ref, late_ref, mod, proj_ref, inverse_ref, key_ref, value_ref = refs[3 * count :]
    model_width = embed_w.shape[2]
    width = mod_parts[0].shape[1]
    for place in range(count):
        first = pl.multiple_of((lax.axis_index("seq") ^ place) * width, 128)
        mod[:, pl.ds(first, width)] = mod_parts[place][...]
    late_ref[...] = mod[:, 2 * model_width :]
    central = centred(embed_w)
    scale_in = slot_of(mod, 1, model_width, 0, model_width)
    shift_in = slot_of(mod, 0, model_width, 0, model_width)
    in_rows = jnp.concatenate(
        [central * (1.0 + scale_in), jnp.broadcast_to(shift_in, (16, model_width))], axis=0
    )
    in_top, in_low = halves(in_rows)
    in_both = jnp.concatenate([in_top, in_low], axis=0)
    both = jnp.concatenate([dot32(in_both, head_w[kind]) for kind in range(3)], axis=1)
    short = both[: in_rows.shape[0]] + both[in_rows.shape[0] :]
    short_ref[...] = short

    @pl.when(lax.axis_index("segment") == 0)
    def _():
        front(
            rows,
            central.astype(jnp.bfloat16),
            short,
            gains,
            head_outs,
            proj_ref,
            inverse_ref,
            key_ref,
            value_ref,
        )


def critic_front_kernel(count, short_in, embed_w, gains, *refs):
    rows = refs[:count]
    head_outs = refs[count : 2 * count]
    proj_ref, inverse_ref, key_ref, value_ref = refs[2 * count :]

    @pl.when(lax.axis_index("segment") != 0)
    def _():
        front(
            rows,
            centred(embed_w).astype(jnp.bfloat16),
            short_in[...],
            gains,
            head_outs,
            proj_ref,
            inverse_ref,
            key_ref,
            value_ref,
        )


def tail(mod, latent, embed_w, final_w, mixed, heads_w, work):
    model_width = embed_w.shape[2]
    block = latent[...]
    sums = None
    for first in range(0, model_width, TILE):
        span = slice(first, first + TILE)
        attended = None
        for piece, rows_w in zip(mixed, heads_w):
            product = dot32(piece[...], rows_w[:, span])
            attended = product if attended is None else attended + product
        residual = (
            dot32(block, embed_w[0, :, span]) + slot_of(mod, 0, model_width, first, TILE) * attended
        )
        work[:, span] = residual
        part = lane_sum(residual)
        sums = part if sums is None else sums + part
    row_mean = jnp.sum(sums, axis=1, keepdims=True) / model_width
    sums = None
    for first in range(0, model_width, TILE):
        span = slice(first, first + TILE)
        middle = work[:, span] - row_mean
        work[:, span] = middle
        part = lane_sum(middle * middle)
        sums = part if sums is None else sums + part
    inverse = lax.rsqrt(jnp.sum(sums, axis=1, keepdims=True) / model_width + EPS)
    result = None
    for first in range(0, model_width, TILE):
        span = slice(first, first + TILE)
        normed = work[:, span] * inverse
        work[:, span] = normed
        final_in = (
            normed * (1.0 + slot_of(mod, 2, model_width, first, TILE))
            + slot_of(mod, 1, model_width, first, TILE)
        ).astype(jnp.bfloat16)
        product = dot32_t(final_in, final_w[:, span])
        result = product if result is None else result + product
    return (result, inverse)


def student_tail_kernel(count, times, mod, latent, noise, embed_w, final_w, *refs):
    mixed = refs[:count]
    heads_w = refs[count : 2 * count]
    pair_ref, inverse_ref, work = refs[2 * count :]
    latent_width = latent.shape[1]

    @pl.when(lax.axis_index("segment") == 0)
    def _():
        student_step, critic_step = steps_of(times)
        sigma_student, sigma_critic = noise_level(student_step), noise_level(critic_step)
        velocity, inverse = tail(mod, latent, embed_w, final_w, mixed, heads_w, work)
        inverse_ref[...] = jnp.broadcast_to(inverse, inverse_ref.shape)
        sample = latent[...].astype(jnp.float32) - sigma_student * velocity
        second = noise[0, :, latent_width:].astype(jnp.float32)
        critic = (1.0 - sigma_critic) * sample + sigma_critic * second
        pair_ref[...] = jnp.concatenate([critic, sample], axis=1).astype(jnp.bfloat16)


def critic_tail_kernel(count, times, mod, pair, noise, embed_w, final_w, *refs):
    mixed = refs[:count]
    heads_w = refs[count : 2 * count]
    grads = refs[2 * count : 3 * count]
    inverse_ref, term_ref, target_ref, direct_ref, latent, work, other = refs[3 * count :]
    model_width = embed_w.shape[2]
    latent_width = latent.shape[1]
    section = lax.axis_index("segment")

    @pl.when(section != 0)
    def _():
        _, critic_step = steps_of(times)
        sigma_critic = noise_level(critic_step)
        both = pair[...].astype(jnp.float32)
        sample = both[:, latent_width:]
        latent[...] = pair[:, :latent_width]
        result, inverse = tail(mod, latent, embed_w, final_w, mixed, heads_w, work)
        inverse_ref[...] = jnp.broadcast_to(inverse, inverse_ref.shape)
        term_ref[...] = (sigma_critic * result).astype(jnp.bfloat16)
        second = noise[0, :, latent_width:].astype(jnp.float32)
        target_ref[...] = jnp.where(
            section == 2,
            2.0 * (result - (second - sample)),
            jnp.where(section == 3, 1.0 / (1.0 + jnp.exp(-result)), 0.0),
        )

        @pl.when(section == 3)
        def _():
            grad_logit = (-1.0 / (1.0 + jnp.exp(result))).astype(jnp.bfloat16)
            plain, along = None, None
            for first in range(0, model_width, TILE):
                span = slice(first, first + TILE)
                gradient = dot32(grad_logit, final_w[:, span]) * (
                    1.0 + slot_of(mod, 2, model_width, first, TILE)
                )
                other[:, span] = gradient
                part = lane_sum(gradient)
                plain = part if plain is None else plain + part
                part = lane_sum(gradient * work[:, span])
                along = part if along is None else along + part
            plain = jnp.sum(plain, axis=1, keepdims=True) / model_width
            along = jnp.sum(along, axis=1, keepdims=True) / model_width
            direct = None
            totals = [None] * count
            for first in range(0, model_width, TILE):
                span = slice(first, first + TILE)
                grad_residual = inverse * (other[:, span] - plain - work[:, span] * along)
                top, low = halves(grad_residual)
                product = dot32_t(top, embed_w[0, :, span]) + dot32_t(low, embed_w[0, :, span])
                direct = product if direct is None else direct + product
                grad_attended = (slot_of(mod, 0, model_width, first, TILE) * grad_residual).astype(
                    jnp.bfloat16
                )
                for place in range(count):
                    product = dot32_t(grad_attended, heads_w[place][:, span])
                    held = totals[place]
                    totals[place] = product if held is None else held + product
            direct_ref[...] = direct
            for place in range(count):
                grads[place][...] = totals[place].astype(jnp.bfloat16)


def gram_kernel(embed_w, gram_ref):
    central_top, central_low = halves(centred(embed_w))
    gram = (
        dot32_t(central_top, central_top)
        + dot32_t(central_top, central_low)
        + dot32_t(central_low, central_top)
    )
    gram_ref[0], gram_ref[1] = halves(gram)


def judge_back_kernel(count, model_width, short_in, gram, gains, proj_ref, inverse_ref, key_ref, value_ref, pair, real, *refs):
    rows = refs[:count]
    grads = refs[count : 2 * count]
    outs = refs[2 * count : 3 * count]
    grad_key_ref, grad_value_ref, grad_query_ref = refs[3 * count :]
    section = lax.axis_index("segment")
    latent_width = rows[0].shape[1]
    head_width = gains.shape[2]
    scale = 1.0 / math.sqrt(head_width)
    size = rows[0].shape[0]

    @pl.when(section == 3)
    def _():
        both = pair[...].astype(jnp.float32)
        gaps = jnp.abs(
            both[:, latent_width:] - both[:, :latent_width] + real[...].astype(jnp.float32)
        )
        error = jnp.sum(jnp.sum(gaps, axis=1, keepdims=True), axis=0, keepdims=True)
        error = error / (size * latent_width)
        error_top, error_low = halves(jnp.broadcast_to(error, (16, latent_width)))
        for place in range(count):
            outs[place][size : size + 16] = error_top
            outs[place][size + 16 :] = error_low
            low = place * size
            span = slice(low, low + size)
            queries, _, _ = rms_scale(proj_ref[span, :head_width], gains[0, :1])
            query_b = queries.astype(jnp.bfloat16)
            weights = jnp.exp(dot32_t(query_b, key_ref[...]) * scale)
            soft_max = weights * (1.0 / jnp.sum(weights, axis=-1, keepdims=True))
            grad_out = grads[place][...]
            grad_soft = dot32_t(grad_out, value_ref[...])
            grad_value = dot32_first(soft_max.astype(jnp.bfloat16), grad_out)
            grad_scores = soft_max * (
                grad_soft - jnp.sum(soft_max * grad_soft, axis=-1, keepdims=True)
            )
            grad_scores_b = (grad_scores * scale).astype(jnp.bfloat16)
            grad_query_ref[span] = dot32(grad_scores_b, key_ref[...])
            grad_key = dot32_first(grad_scores_b, query_b)
            if place == 0:
                grad_value_ref[...] = grad_value
                grad_key_ref[...] = grad_key
            else:
                grad_value_ref[...] += grad_value
                grad_key_ref[...] += grad_key
        gram_top, gram_low = gram[0], gram[1]
        short_top, short_low = halves(short_in[:latent_width])
        for place in range(count):
            low = place * size
            span = slice(low, low + size)
            projected = proj_ref[span]
            _, q_unit, q_inverse = rms_scale(projected[:, :head_width], gains[0, :1])
            _, k_unit, k_inverse = rms_scale(
                projected[:, head_width : 2 * head_width], gains[0, 1:2]
            )
            grad_q = rms_back(grad_query_ref[span], q_unit, q_inverse, gains[0, :1])
            grad_k = rms_back(grad_key_ref[span], k_unit, k_inverse, gains[0, 1:2])
            grad_proj = jnp.concatenate([grad_q, grad_k, grad_value_ref[span]], axis=1).astype(
                jnp.bfloat16
            )
            through = dot32_t(grad_proj, short_top) + dot32_t(grad_proj, short_low)
            block = rows[place][...]
            along = jnp.sum(through * block.astype(jnp.float32), axis=1, keepdims=True) / model_width
            spanned = dot32(block, gram_top) + dot32(block, gram_low)
            inverse = inverse_ref[span, :1]
            outs[place][:size] = (
                inverse * (through - spanned * (inverse * inverse * along))
            ).astype(jnp.bfloat16)


def merge_kernel(count, times, direct, real, fake, *refs):
    parts = refs[:count]
    payload_ref = refs[count]
    rows = direct.shape[0]

    @pl.when(lax.axis_index("segment") == 3)
    def _():
        total = parts[0][...].astype(jnp.float32)
        for part in parts[1:]:
            total = total + part[...].astype(jnp.float32)
        _, critic_step = steps_of(times)
        adverse = (1.0 - noise_level(critic_step)) * (total[:rows] + direct[...])
        spread = (total[rows : rows + 16] + total[rows + 16 :])[:1, :1] / count + EPS
        gap = real[...].astype(jnp.float32) - fake[...].astype(jnp.float32)
        payload_ref[...] = (gap / spread + ADV_WEIGHT * adverse).astype(jnp.bfloat16)


def outer_kernel(
    count, times, arrived, target_in, student_rows, pair, student_inverse, critic_inverse, *refs
):
    student_mixed = refs[:count]
    critic_mixed = refs[count : 2 * count]
    sums_ref = refs[2 * count]
    section = lax.axis_index("segment")
    place = lax.axis_index("seq")
    latent_width = student_rows.shape[1]

    def collect(target, inverse, latent, mixed):
        target = target.astype(jnp.bfloat16)
        weighted = inverse[:, :latent_width] * target.astype(jnp.float32)
        top, low = halves(weighted)
        for offset in range(count):
            piece = mixed[offset][...]
            sums_ref[place ^ offset] = (dot32_first(top, piece) + dot32_first(low, piece)).astype(
                jnp.bfloat16
            )
        near = dot32_first(top, latent) + dot32_first(low, latent)
        ones = jnp.ones((target.shape[0], sums_ref.shape[2] - latent_width), jnp.bfloat16)
        sums_ref[count] = jnp.concatenate([near, dot32_first(target, ones)], axis=1).astype(
            jnp.bfloat16
        )

    @pl.when(section == 0)
    def _():
        student_step, _ = steps_of(times)
        target = -noise_level(student_step) * arrived[...].astype(jnp.float32)
        collect(target, student_inverse, student_rows[...], student_mixed)

    @pl.when(section == 1)
    def _():
        sums_ref[...] = jnp.zeros_like(sums_ref)

    @pl.when(section >= 2)
    def _():
        collect(target_in[...], critic_inverse, pair[:, :latent_width], critic_mixed)


def expand_kernel(count, groups, full_rows, own, from_first, from_second, from_third, embed_w, *refs):
    heads_w = refs[:count]
    mods = refs[count : count + groups]
    sums = refs[count + groups : count + 3 * groups]
    grad_ref, total_ref, work, joined = refs[count + 3 * groups :]
    section = lax.axis_index("segment")
    place = lax.axis_index("seq")
    latent_width = embed_w.shape[1]
    model_width = embed_w.shape[2]
    picked = own[...].astype(jnp.float32)
    for source, value in ((0, from_first), (2, from_second), (1, from_third)):
        picked = jnp.where(section == source, value[...].astype(jnp.float32), picked)
    grad_ref[...] = picked.T

    @pl.when(section == 1)
    def _():
        total_ref[...] = jnp.zeros_like(total_ref)

    @pl.when(section != 1)
    def _():
        for group in range(groups):
            low = group * latent_width
            joined[:, low : low + latent_width] = sums[2 * group][...].astype(jnp.float32) + sums[
                2 * group + 1
            ][...].astype(jnp.float32)
        near_top, near_low = halves(joined[count])
        heads = [halves(joined[place ^ offset]) for offset in range(count)]
        averages = None
        for first in range(0, model_width, TILE):
            span = slice(first, first + TILE)
            spread = None
            for (top, low), rows_w in zip(heads, heads_w):
                product = dot32(top, rows_w[:, span]) + dot32(low, rows_w[:, span])
                spread = product if spread is None else spread + product
            near = dot32(near_top[:, :latent_width], embed_w[0, :, span]) + dot32(
                near_low[:, :latent_width], embed_w[0, :, span]
            )
            gates = jnp.concatenate(
                [
                    jnp.broadcast_to(
                        slot_of(mod, 0, model_width, first, TILE), (latent_width, TILE)
                    )
                    for mod in mods
                ],
                axis=0,
            )
            value = near + gates * spread
            work[:, span] = value
            part = lane_sum(value)
            averages = part if averages is None else averages + part
        averages = jnp.sum(averages, axis=1, keepdims=True) / model_width
        counts = joined[count][:, latent_width : latent_width + 1]
        for first in range(0, model_width, TILE):
            span = slice(first, first + TILE)
            value = work[:, span] - averages
            total = None
            for group in range(groups):
                mine = slice(group * latent_width, (group + 1) * latent_width)
                product = value[mine] * (
                    1.0 + slot_of(mods[group], 2, model_width, first, TILE)
                ) + counts[mine] * slot_of(mods[group], 1, model_width, first, TILE)
                total = product if total is None else total + product
            total_ref[:, span] = total / full_rows


def step(
    clean, noise, timesteps, text_vec, w_embed, w_time, w_mod, w_qkv, w_out, qk_gain, w_final
):
    section = lax.axis_index("segment")
    sections = lax.axis_size("segment")
    tok_rows = clean.shape[1]
    latent_width = clean.shape[2]
    model_width = w_embed.shape[2]
    mod_width = w_mod.shape[2]
    count = lax.axis_size("seq")
    full_rows = tok_rows * count
    head_width = w_qkv.shape[4]
    kind_w = jnp.transpose(w_qkv[0, :, 0], (1, 0, 2))
    final_w = jnp.transpose(w_final[0])
    heads_w = gather_doubling(w_out[0, 0], "seq", count)
    bf16, f32 = jnp.bfloat16, jnp.float32

    mod_piece, noisy_student = run(
        condition_kernel,
        [array((1, mod_width), f32), array((tok_rows, latent_width), bf16)],
        (timesteps, text_vec, w_time, jnp.transpose(clean[0]), noise, w_mod),
        [SMEM, VMEM, VMEM, VMEM, VMEM, ANY],
        2 * model_width * mod_width,
        scratch=(pltpu.VMEM((model_width, mod_width), bf16), pltpu.SemaphoreType.DMA((STREAMS,))),
    )
    mod_parts = gather_near(mod_piece, "seq", count)
    student_rows = gather_near(noisy_student, "seq", count)

    head_blocks = [array((tok_rows, head_width), bf16)] * count
    stored = [
        ((full_rows, 3 * head_width), f32),
        ((full_rows, 128), f32),
        ((full_rows, head_width), bf16),
        ((full_rows, head_width), bf16),
    ]
    *head_outs, short, late_mod = run(
        functools.partial(student_front_kernel, count),
        head_blocks
        + [
            array((latent_width + 16, 3 * head_width), f32),
            array((1, 3 * model_width), f32),
        ],
        (w_embed, kind_w, qk_gain, *mod_parts, *student_rows),
        [VMEM] * (3 + 2 * count),
        4 * latent_width * model_width * 3 * head_width,
        scratch=[pltpu.VMEM((1, 5 * model_width), f32)]
        + [pltpu.VMEM(shape, kind) for shape, kind in stored],
    )
    student_mixed = scatter_near(head_outs, "seq", count)
    groups = lax.axis_size("dp")
    late_mods = gather_near(late_mod, "dp", groups)
    work = pltpu.VMEM((tok_rows, model_width), f32)
    inverse_shape = array((tok_rows, 128), f32)
    pair, student_inverse = run(
        functools.partial(student_tail_kernel, count),
        [array((tok_rows, 2 * latent_width), bf16), inverse_shape],
        (timesteps, late_mod, noisy_student, noise, w_embed, final_w, *student_mixed, *heads_w),
        [SMEM] + [VMEM] * (5 + 2 * count),
        2 * tok_rows * model_width * head_width * count,
        scratch=(work,),
    )
    moved = [
        lax.ppermute(pair, "segment", [(0, place), (place, 0)])
        for place in range(1, sections)
    ]
    held = moved[0]
    for place in range(2, sections):
        held = jnp.where(section == place, moved[place - 1], held)
    pair = jnp.where(section == 0, pair, held)
    critic_rows = gather_near(pair[:, :latent_width], "seq", count)
    *head_outs, proj, inverse, keys, values = run(
        functools.partial(critic_front_kernel, count),
        head_blocks + [array(shape, kind) for shape, kind in stored],
        (short, w_embed, qk_gain, *critic_rows),
        [VMEM] * (3 + count),
        4 * latent_width * model_width * full_rows,
    )
    critic_mixed = scatter_near(head_outs, "seq", count)
    small = array((tok_rows, latent_width), f32)
    thin = array((tok_rows, latent_width), bf16)
    *grad_heads, critic_inverse, term_rows, target, direct = run(
        functools.partial(critic_tail_kernel, count),
        head_blocks + [inverse_shape, thin, small, small],
        (timesteps, late_mod, pair, noise, w_embed, final_w, *critic_mixed, *heads_w),
        [SMEM] + [VMEM] * (5 + 2 * count),
        4 * tok_rows * model_width * head_width * count,
        scratch=(pltpu.VMEM((tok_rows, latent_width), bf16), work, work),
    )
    grad_blocks = scatter_near(grad_heads, "seq", count)
    fake = lax.ppermute(term_rows, "segment", swaps(sections, 1))
    real = lax.ppermute(term_rows, "segment", swaps(sections, 2))
    (gram,) = run(
        gram_kernel,
        [array((2, latent_width, latent_width), bf16)],
        (w_embed,),
        [VMEM],
        6 * latent_width * latent_width * model_width,
    )
    parts = run(
        functools.partial(judge_back_kernel, count, model_width),
        [array((tok_rows + 32, latent_width), bf16)] * count,
        (short, gram, qk_gain, proj, inverse, keys, values, pair, real, *critic_rows, *grad_blocks),
        [VMEM] * (9 + 2 * count),
        10 * full_rows * full_rows * head_width,
        scratch=(pltpu.VMEM((full_rows, head_width), f32),) * 3,
    )
    parts = scatter_near(parts, "seq", count)
    (payload,) = run(
        functools.partial(merge_kernel, count),
        [thin],
        (timesteps, direct, real, fake, *parts),
        [SMEM] + [VMEM] * (3 + count),
        1000,
    )
    ends = [(place, sections - 1 - place) for place in range(sections)]
    to_student = lax.ppermute(payload, "segment", ends)
    to_second = lax.ppermute(payload, "segment", swaps(sections, 1))
    to_third = lax.ppermute(payload, "segment", swaps(sections, 2))
    (sums,) = run(
        functools.partial(outer_kernel, count),
        [array((count + 1, latent_width, 128), bf16)],
        (
            timesteps,
            to_student,
            target,
            noisy_student,
            pair,
            student_inverse,
            critic_inverse,
            *student_mixed,
            *critic_mixed,
        ),
        [SMEM] + [VMEM] * (6 + 2 * count),
        2 * tok_rows * latent_width * head_width * (count + 1),
    )
    last = count // 2
    bit = 1
    while bit < last:
        moved = lax.ppermute(sums, "seq", swaps(count, bit))
        sums = (sums.astype(f32) + moved.astype(f32)).astype(bf16)
        bit *= 2
    sums_all = []
    for group in range(groups):
        for offset in (0, last):
            moves = [
                (place * groups + batch, (place ^ offset) * groups + (batch ^ group))
                for place in range(count)
                for batch in range(groups)
            ]
            sums_all.append(
                sums if offset == group == 0 else lax.ppermute(sums, ("seq", "dp"), moves)
            )
    grad_t, total_t = run(
        functools.partial(expand_kernel, count, groups, full_rows),
        [array((latent_width, tok_rows), f32), array((latent_width, model_width), f32)],
        (
            payload,
            to_student,
            to_second,
            to_third,
            w_embed,
            *heads_w,
            *late_mods,
            *sums_all,
        ),
        [VMEM] * (5 + count + 3 * groups),
        4 * groups * latent_width * model_width * head_width * count,
        scratch=(
            pltpu.VMEM((groups * latent_width, model_width), f32),
            pltpu.VMEM((count + 1, groups * latent_width, 128), f32),
        ),
    )
    return (jnp.transpose(grad_t)[None], jnp.transpose(total_t)[None])


def solution(mesh):
    placed = (
        P("dp", "seq", None),
        P("dp", "seq", None),
        P(),
        P("dp", None),
        P("segment", None, None),
        P("segment", None, None),
        P("segment", None, "seq"),
        P("segment", None, "seq", None, None),
        P("segment", "seq", None, None),
        P("segment", None, None),
        P("segment", None, None),
    )
    return jax.shard_map(
        step,
        mesh=mesh,
        in_specs=placed,
        out_specs=(P("dp", "seq", None), P("segment", None, None)),
        check_vma=False,
    )
```

```python
import functools
import math

import jax
import jax.numpy as jnp
from jax import lax
from jax.experimental import pallas as pl
from jax.experimental.pallas import tpu as pltpu
from jax.sharding import PartitionSpec as P


SHIFT = 7.0
EPS = 1e-06
ADV_WEIGHT = 3.0
TILE = 512
STREAMS = 6
SPARE = 8 << 20
VMEM = pl.BlockSpec(memory_space=pltpu.VMEM)
HBM = pl.BlockSpec(memory_space=pltpu.HBM)


def halves(values):
    top = values.astype(jnp.bfloat16)
    return (top, (values - top.astype(jnp.float32)).astype(jnp.bfloat16))


def swaps(count, offset):
    return [(place, place ^ offset) for place in range(count)]


def gather_near(value, axis, count):
    return [value] + [lax.ppermute(value, axis, swaps(count, offset)) for offset in range(1, count)]


def scatter_near(blocks, axis, count):
    return [blocks[0]] + [
        lax.ppermute(blocks[offset], axis, swaps(count, offset))
        for offset in range(1, count)
    ]


def gather_doubling(value, axis, count):
    held = {0: value}
    bit = count // 2
    while bit:
        for offset in sorted(held):
            held[offset | bit] = lax.ppermute(held[offset], axis, swaps(count, bit))
        bit //= 2
    return [held[offset] for offset in range(count)]


def in_order(pieces, own_place):
    ordered = list(pieces)
    bit = 1
    while bit < len(ordered):
        flipped = (own_place & bit) != 0
        ordered = [
            jnp.where(flipped, ordered[place ^ bit], ordered[place])
            for place in range(len(ordered))
        ]
        bit *= 2
    return ordered


def dot32(left, right):
    return jnp.dot(left, right, preferred_element_type=jnp.float32)


def dot32_t(left, right):
    return lax.dot_general(
        left, right, (((1,), (1,)), ((), ())), preferred_element_type=jnp.float32
    )


def dot32_first(left, right):
    return lax.dot_general(
        left, right, (((0,), (0,)), ((), ())), preferred_element_type=jnp.float32
    )


def steps_of(times):
    times_ref = times.ready()
    place = lax.axis_index("dp")
    return (times_ref[place, 0], times_ref[place, 1])


def noise_level(step):
    fraction = jnp.full((1, 1), step, jnp.int32).astype(jnp.float32) / 1000.0
    return SHIFT * fraction / (1.0 + (SHIFT - 1.0) * fraction)


def slot_of(mod_ref, slot, width, first, size):
    return mod_ref[:, slot * width + first : slot * width + first + size]


def lane_sum(values):
    total = values[:, :128]
    for first in range(128, values.shape[1], 128):
        total = total + values[:, first : first + 128]
    return total


class Fetch:
    def __init__(self, source, target, arrival):
        self.copy = pltpu.make_async_copy(source, target, arrival)
        self.target = target
        self.waiting = True

    def start(self):
        self.copy.start()

    def ready(self):
        if self.waiting:
            self.copy.wait()
            self.waiting = False
        return self.target


def bytes_of(items):
    return sum(math.prod(item.shape) * jnp.dtype(item.dtype).itemsize for item in items)


def run(kernel, outputs, operands, flops, scratch=(), fetched=(), streamed=(), sent=()):
    inputs = len(operands)
    total = inputs + len(fetched) + len(streamed)
    results = len(outputs) + len(sent)

    def body(*refs):
        sources = refs[inputs:total]
        outs = refs[total : total + results]
        own = refs[total + results : total + results + len(scratch)]
        rest = refs[total + results + len(scratch) :]
        fetches = [
            Fetch(source, target, rest[-1].at[place])
            for place, (source, target) in enumerate(zip(sources, rest[:-1]))
        ]
        fetches += sources[len(fetched) :]
        kernel(fetches, *refs[:inputs], *outs, *own)

    places = [
        (pltpu.SMEM if item.dtype == jnp.int32 else pltpu.VMEM)(item.shape, item.dtype)
        for item in fetched
    ]
    held = bytes_of(
        [ref for ref in list(scratch) + places if ref.memory_space == pltpu.VMEM]
    )
    limit = min(60 << 20, SPARE + held + bytes_of(operands) + 2 * bytes_of(outputs))
    return pl.pallas_call(
        body,
        out_shape=list(outputs) + list(sent),
        in_specs=[VMEM] * inputs + [HBM] * (total - inputs),
        out_specs=[VMEM] * len(outputs) + [HBM] * len(sent),
        scratch_shapes=list(scratch)
        + places
        + [pltpu.SemaphoreType.DMA((max(1, len(fetched)),))],
        compiler_params=pltpu.CompilerParams(vmem_limit_bytes=limit),
        cost_estimate=pl.CostEstimate(
            flops=flops,
            bytes_accessed=bytes_of(list(operands) + list(fetched) + list(outputs)),
            transcendentals=0,
        ),
    )(*operands, *fetched, *streamed)


def array(shape, dtype):
    return jax.ShapeDtypeStruct(shape, dtype)


def packed_rows(width):
    return -(-width // 2048) * 16


def condition_kernel(fetches, packed_out, noisy_out, held, mod_rows, arrivals):
    times, text, time_w, clean_t, noise, mod_w = fetches
    model_width = held.shape[0]
    rows = model_width // STREAMS
    for fetch in fetches[:-1]:
        fetch.start()
    copies = [
        pltpu.make_async_copy(
            mod_w.at[pl.ds(part * rows, rows)], held.at[pl.ds(part * rows, rows)], arrivals.at[part]
        )
        for part in range(STREAMS)
    ]
    for copy in copies:
        copy.start()
    student_step, critic_step = steps_of(times)
    step = jnp.where(lax.axis_index("segment") == 0, student_step, critic_step)
    text_ref = text.ready()
    half = text_ref.shape[1] // 2
    places = lax.broadcasted_iota(jnp.int32, (1, half), 1).astype(jnp.float32)
    frequency = jnp.exp(-math.log(10000.0) * places / half)
    angles = jnp.full((1, half), step, jnp.int32).astype(jnp.float32) * frequency
    features = jnp.concatenate([jnp.cos(angles), jnp.sin(angles)], axis=1) + text_ref[...]
    features = jnp.broadcast_to(features, (8, 2 * half)).astype(jnp.bfloat16)
    hidden = dot32(features, time_w.ready()[...])
    hidden = (hidden / (1.0 + jnp.exp(-hidden))).astype(jnp.bfloat16)
    sigma_student = noise_level(student_step)
    clean_ref, noise_ref = clean_t.ready(), noise.ready()
    noisy = (1.0 - sigma_student) * clean_ref[...].astype(jnp.float32).T + sigma_student * noise_ref[
        :, : clean_ref.shape[0]
    ].astype(jnp.float32)
    noisy = noisy.astype(jnp.bfloat16)
    noisy_out[...] = noisy
    top = noisy.shape[0] // 2
    packed_out[:top] = jnp.concatenate([noisy[:top], noisy[top:]], axis=1)
    mod_rows[...] = jnp.zeros_like(mod_rows)
    total = None
    for part in range(STREAMS):
        copies[part].wait()
        piece = dot32(
            hidden[:, part * rows : (part + 1) * rows], held[part * rows : (part + 1) * rows]
        )
        total = piece if total is None else total + piece
    width = total.shape[1]
    for row, first in enumerate(range(0, width, 128)):
        size = min(128, width - first)
        mod_rows[row : row + 1, :size] = total[:1, first : first + size]
    depth = mod_rows.shape[0]
    packed_out[top : top + depth], packed_out[top + depth :] = halves(mod_rows[...])


def rms_scale(values, gain_vec):
    inverse = lax.rsqrt(jnp.mean(values * values, axis=-1, keepdims=True) + EPS)
    unit_vec = values * inverse
    return (unit_vec * gain_vec, unit_vec, inverse)


def rms_back(gradient, unit_vec, inverse, gain_vec):
    scaled = gradient * gain_vec
    return inverse * (scaled - unit_vec * jnp.mean(scaled * unit_vec, axis=-1, keepdims=True))


def centred(embed_ref):
    values = embed_ref[0].astype(jnp.float32)
    return values - jnp.mean(values, axis=1, keepdims=True)


def front(rows, central, short, gains, head_outs, proj_ref, inverse_ref, key_ref, value_ref):
    latent_width = central.shape[0]
    model_width = central.shape[1]
    count = len(rows)
    head_width = gains.shape[2]
    scale = 1.0 / math.sqrt(head_width)
    size = rows[0].shape[0]
    short_top = None
    for place in range(count):
        block = rows[place][...]
        squares = None
        for first in range(0, model_width, TILE):
            piece = dot32(block, central[:, first : first + TILE])
            piece = lane_sum(piece * piece)
            squares = piece if squares is None else squares + piece
        inverse = lax.rsqrt(jnp.sum(squares, axis=1, keepdims=True) / model_width + EPS)
        if short_top is None:
            values = short()
            short_top, short_low = halves(values[:latent_width])
            short_shift = values[latent_width : latent_width + 1]
        projected = inverse * (dot32(block, short_top) + dot32(block, short_low)) + short_shift
        low = place * size
        proj_ref[low : low + size] = projected
        inverse_ref[low : low + size] = jnp.broadcast_to(inverse, (size, 128))
        keys, _, _ = rms_scale(projected[:, head_width : 2 * head_width], gains[0, 1:2])
        key_ref[low : low + size] = keys.astype(jnp.bfloat16)
        value_ref[low : low + size] = projected[:, 2 * head_width :].astype(jnp.bfloat16)
    for place in range(count):
        low = place * size
        queries, _, _ = rms_scale(proj_ref[low : low + size, :head_width], gains[0, :1])
        scores = dot32_t(queries.astype(jnp.bfloat16), key_ref[...]) * scale
        weights = jnp.exp(scores)
        soft_max = weights * (1.0 / jnp.sum(weights, axis=-1, keepdims=True))
        head_outs[place][...] = dot32(soft_max.astype(jnp.bfloat16), value_ref[...]).astype(
            jnp.bfloat16
        )


def student_front_kernel(count, width, fetches, embed_w, head_w, gains, *refs):
    packed = refs[:count]
    head_outs = refs[count : 2 * count]
    short_out, late_out, mod, short_ref, rows_ref, sends, *kept = refs[2 * count :]
    model_width = embed_w.shape[2]
    latent_width = embed_w.shape[1]
    size = rows_ref.shape[1]
    half = size // 2
    depth = packed_rows(width)
    parts = [
        piece[half : half + depth].astype(jnp.float32) + piece[half + depth :].astype(jnp.float32)
        for piece in packed
    ]
    for place, part in enumerate(in_order(parts, lax.axis_index("seq"))):
        for row, first in enumerate(range(0, width, 128)):
            lanes = min(128, width - first)
            low = place * width + first
            mod[:, low : low + lanes] = part[row : row + 1, :lanes]
    late = pltpu.make_async_copy(
        mod.at[:, pl.ds(2 * model_width, 3 * model_width)], late_out, sends.at[0]
    )
    late.start()
    for place in range(count):
        rows_ref[place, :half] = packed[place][:half, :latent_width]
        rows_ref[place, half:] = packed[place][:half, latent_width:]
    central = centred(embed_w)
    scale_in = slot_of(mod, 1, model_width, 0, model_width)
    shift_in = slot_of(mod, 0, model_width, 0, model_width)
    in_rows = jnp.concatenate(
        [central * (1.0 + scale_in), jnp.broadcast_to(shift_in, (16, model_width))], axis=0
    )
    in_top, in_low = halves(in_rows)
    in_both = jnp.concatenate([in_top, in_low], axis=0)
    both = jnp.concatenate([dot32(in_both, head_w[kind]) for kind in range(3)], axis=1)
    short = both[: in_rows.shape[0]] + both[in_rows.shape[0] :]
    short_ref[...] = short
    send = pltpu.make_async_copy(short_ref, short_out, sends.at[1])
    send.start()

    @pl.when(lax.axis_index("segment") == 0)
    def _():
        front(
            [rows_ref.at[place] for place in range(count)],
            central.astype(jnp.bfloat16),
            lambda: short,
            gains,
            head_outs,
            *kept,
        )

    late.wait()
    send.wait()


def critic_front_kernel(count, fetches, embed_w, gains, *refs):
    rows = refs[:count]
    head_outs = refs[count : 2 * count]
    kept = refs[2 * count :]
    (short,) = fetches

    @pl.when(lax.axis_index("segment") != 0)
    def _():
        short.start()
        front(
            rows,
            centred(embed_w).astype(jnp.bfloat16),
            lambda: short.ready()[...],
            gains,
            head_outs,
            *kept,
        )


def tail(late, latent, embed_w, final_t, mixed, heads_w, work):
    model_width = embed_w.shape[2]
    block = latent[...]
    sums = None
    for first in range(0, model_width, TILE):
        span = slice(first, first + TILE)
        attended = None
        for piece, rows_w in zip(mixed, heads_w):
            product = dot32(piece[...], rows_w[:, span])
            attended = product if attended is None else attended + product
        mod = late.ready()
        residual = (
            dot32(block, embed_w[0, :, span]) + slot_of(mod, 0, model_width, first, TILE) * attended
        )
        work[:, span] = residual
        part = lane_sum(residual)
        sums = part if sums is None else sums + part
    row_mean = jnp.sum(sums, axis=1, keepdims=True) / model_width
    sums = None
    for first in range(0, model_width, TILE):
        span = slice(first, first + TILE)
        middle = work[:, span] - row_mean
        work[:, span] = middle
        part = lane_sum(middle * middle)
        sums = part if sums is None else sums + part
    inverse = lax.rsqrt(jnp.sum(sums, axis=1, keepdims=True) / model_width + EPS)
    result = None
    final_w = final_t.ready()
    for first in range(0, model_width, TILE):
        span = slice(first, first + TILE)
        normed = work[:, span] * inverse
        work[:, span] = normed
        final_in = (
            normed * (1.0 + slot_of(mod, 2, model_width, first, TILE))
            + slot_of(mod, 1, model_width, first, TILE)
        ).astype(jnp.bfloat16)
        product = dot32_t(final_in, final_w[:, span])
        result = product if result is None else result + product
    return (result, inverse)


def student_tail_kernel(count, fetches, latent, embed_w, *refs):
    mixed = refs[:count]
    heads_w = refs[count : 2 * count]
    pair_ref, saved_out, inverse_out, work, inverse_ref, sends = refs[2 * count :]
    late, final_t, noise, times = fetches
    latent_width = latent.shape[1]

    @pl.when(lax.axis_index("segment") == 0)
    def _():
        for fetch in fetches:
            fetch.start()
        copies = [
            pltpu.make_async_copy(mixed[place], saved_out.at[place], sends.at[place])
            for place in range(count)
        ]
        for copy in copies:
            copy.start()
        velocity, inverse = tail(late, latent, embed_w, final_t, mixed, heads_w, work)
        inverse_ref[...] = jnp.broadcast_to(inverse, inverse_ref.shape)
        copies.append(pltpu.make_async_copy(inverse_ref, inverse_out, sends.at[count]))
        copies[-1].start()
        student_step, critic_step = steps_of(times)
        sigma_student, sigma_critic = noise_level(student_step), noise_level(critic_step)
        sample = latent[...].astype(jnp.float32) - sigma_student * velocity
        second = noise.ready()[:, latent_width:].astype(jnp.float32)
        critic = (1.0 - sigma_critic) * sample + sigma_critic * second
        pair_ref[...] = jnp.concatenate([critic, sample], axis=1).astype(jnp.bfloat16)
        for copy in copies:
            copy.wait()


def critic_tail_kernel(count, fetches, pair, embed_w, *refs):
    mixed = refs[:count]
    heads_w = refs[count : 2 * count]
    grads = refs[2 * count : 3 * count]
    inverse_ref, term_ref, target_ref, direct_ref, latent, work, other = refs[3 * count :]
    late, final_t, noise, times = fetches
    model_width = embed_w.shape[2]
    latent_width = latent.shape[1]
    section = lax.axis_index("segment")

    @pl.when(section != 0)
    def _():
        for fetch in fetches:
            fetch.start()
        both = pair[...].astype(jnp.float32)
        sample = both[:, latent_width:]
        latent[...] = pair[:, :latent_width]
        result, inverse = tail(late, latent, embed_w, final_t, mixed, heads_w, work)
        mod, final_w = late.ready(), final_t.ready()
        _, critic_step = steps_of(times)
        sigma_critic = noise_level(critic_step)
        inverse_ref[...] = jnp.broadcast_to(inverse, inverse_ref.shape)
        term_ref[...] = (sigma_critic * result).astype(jnp.bfloat16)
        second = noise.ready()[:, latent_width:].astype(jnp.float32)
        target_ref[...] = jnp.where(
            section == 2,
            2.0 * (result - (second - sample)),
            jnp.where(section == 3, 1.0 / (1.0 + jnp.exp(-result)), 0.0),
        )

        @pl.when(section == 3)
        def _():
            grad_logit = (-1.0 / (1.0 + jnp.exp(result))).astype(jnp.bfloat16)
            plain, along = None, None
            for first in range(0, model_width, TILE):
                span = slice(first, first + TILE)
                gradient = dot32(grad_logit, final_w[:, span]) * (
                    1.0 + slot_of(mod, 2, model_width, first, TILE)
                )
                other[:, span] = gradient
                part = lane_sum(gradient)
                plain = part if plain is None else plain + part
                part = lane_sum(gradient * work[:, span])
                along = part if along is None else along + part
            plain = jnp.sum(plain, axis=1, keepdims=True) / model_width
            along = jnp.sum(along, axis=1, keepdims=True) / model_width
            direct = None
            totals = [None] * count
            for first in range(0, model_width, TILE):
                span = slice(first, first + TILE)
                grad_residual = inverse * (other[:, span] - plain - work[:, span] * along)
                top, low = halves(grad_residual)
                product = dot32_t(top, embed_w[0, :, span]) + dot32_t(low, embed_w[0, :, span])
                direct = product if direct is None else direct + product
                grad_attended = (slot_of(mod, 0, model_width, first, TILE) * grad_residual).astype(
                    jnp.bfloat16
                )
                for place in range(count):
                    product = dot32_t(grad_attended, heads_w[place][:, span])
                    held = totals[place]
                    totals[place] = product if held is None else held + product
            direct_ref[...] = direct
            for place in range(count):
                grads[place][...] = totals[place].astype(jnp.bfloat16)


def gram_kernel(fetches, embed_w, gram_ref):
    central_top, central_low = halves(centred(embed_w))
    gram = (
        dot32_t(central_top, central_top)
        + dot32_t(central_top, central_low)
        + dot32_t(central_low, central_top)
    )
    gram_ref[0], gram_ref[1] = halves(gram)


def judge_back_kernel(count, model_width, fetches, short_in, gram, gains, proj_ref, inverse_ref, key_ref, value_ref, pair, real, *refs):
    rows = refs[:count]
    grads = refs[count : 2 * count]
    outs = refs[2 * count : 3 * count]
    grad_key_ref, grad_value_ref, grad_query_ref = refs[3 * count :]
    section = lax.axis_index("segment")
    latent_width = rows[0].shape[1]
    head_width = gains.shape[2]
    scale = 1.0 / math.sqrt(head_width)
    size = rows[0].shape[0]

    @pl.when(section == 3)
    def _():
        both = pair[...].astype(jnp.float32)
        gaps = jnp.abs(
            both[:, latent_width:] - both[:, :latent_width] + real[...].astype(jnp.float32)
        )
        error = jnp.sum(jnp.sum(gaps, axis=1, keepdims=True), axis=0, keepdims=True)
        error = error / (size * latent_width)
        error_top, error_low = halves(jnp.broadcast_to(error, (16, latent_width)))
        for place in range(count):
            outs[place][size : size + 16] = error_top
            outs[place][size + 16 :] = error_low
            low = place * size
            span = slice(low, low + size)
            queries, _, _ = rms_scale(proj_ref[span, :head_width], gains[0, :1])
            query_b = queries.astype(jnp.bfloat16)
            weights = jnp.exp(dot32_t(query_b, key_ref[...]) * scale)
            soft_max = weights * (1.0 / jnp.sum(weights, axis=-1, keepdims=True))
            grad_out = grads[place][...]
            grad_soft = dot32_t(grad_out, value_ref[...])
            grad_value = dot32_first(soft_max.astype(jnp.bfloat16), grad_out)
            grad_scores = soft_max * (
                grad_soft - jnp.sum(soft_max * grad_soft, axis=-1, keepdims=True)
            )
            grad_scores_b = (grad_scores * scale).astype(jnp.bfloat16)
            grad_query_ref[span] = dot32(grad_scores_b, key_ref[...])
            grad_key = dot32_first(grad_scores_b, query_b)
            if place == 0:
                grad_value_ref[...] = grad_value
                grad_key_ref[...] = grad_key
            else:
                grad_value_ref[...] += grad_value
                grad_key_ref[...] += grad_key
        gram_top, gram_low = gram[0], gram[1]
        short_top, short_low = halves(short_in[:latent_width])
        for place in range(count):
            low = place * size
            span = slice(low, low + size)
            projected = proj_ref[span]
            _, q_unit, q_inverse = rms_scale(projected[:, :head_width], gains[0, :1])
            _, k_unit, k_inverse = rms_scale(
                projected[:, head_width : 2 * head_width], gains[0, 1:2]
            )
            grad_q = rms_back(grad_query_ref[span], q_unit, q_inverse, gains[0, :1])
            grad_k = rms_back(grad_key_ref[span], k_unit, k_inverse, gains[0, 1:2])
            grad_proj = jnp.concatenate([grad_q, grad_k, grad_value_ref[span]], axis=1).astype(
                jnp.bfloat16
            )
            through = dot32_t(grad_proj, short_top) + dot32_t(grad_proj, short_low)
            block = rows[place][...]
            along = jnp.sum(through * block.astype(jnp.float32), axis=1, keepdims=True) / model_width
            spanned = dot32(block, gram_top) + dot32(block, gram_low)
            inverse = inverse_ref[span, :1]
            outs[place][:size] = (
                inverse * (through - spanned * (inverse * inverse * along))
            ).astype(jnp.bfloat16)


def merge_kernel(count, fetches, direct, real, fake, *refs):
    parts = refs[:count]
    payload_ref = refs[count]
    rows = direct.shape[0]

    @pl.when(lax.axis_index("segment") == 3)
    def _():
        (times,) = fetches
        times.start()
        total = parts[0][...].astype(jnp.float32)
        for part in parts[1:]:
            total = total + part[...].astype(jnp.float32)
        _, critic_step = steps_of(times)
        adverse = (1.0 - noise_level(critic_step)) * (total[:rows] + direct[...])
        spread = (total[rows : rows + 16] + total[rows + 16 :])[:1, :1] / count + EPS
        gap = real[...].astype(jnp.float32) - fake[...].astype(jnp.float32)
        payload_ref[...] = (gap / spread + ADV_WEIGHT * adverse).astype(jnp.bfloat16)


def outer_kernel(
    count,
    fetches,
    arrived,
    target_in,
    student_rows,
    pair,
    student_mixed,
    student_inverse,
    critic_inverse,
    *refs,
):
    critic_mixed = refs[:count]
    sums_ref = refs[count]
    section = lax.axis_index("segment")
    place = lax.axis_index("seq")
    latent_width = student_rows.shape[1]

    def collect(target, inverse, latent, mixed):
        target = target.astype(jnp.bfloat16)
        weighted = inverse[:, :latent_width] * target.astype(jnp.float32)
        top, low = halves(weighted)
        for offset in range(count):
            piece = mixed[offset][...]
            sums_ref[place ^ offset] = (dot32_first(top, piece) + dot32_first(low, piece)).astype(
                jnp.bfloat16
            )
        near = dot32_first(top, latent) + dot32_first(low, latent)
        ones = jnp.ones((target.shape[0], sums_ref.shape[2] - latent_width), jnp.bfloat16)
        sums_ref[count] = jnp.concatenate([near, dot32_first(target, ones)], axis=1).astype(
            jnp.bfloat16
        )

    @pl.when(section == 0)
    def _():
        (times,) = fetches
        times.start()
        student_step, _ = steps_of(times)
        target = -noise_level(student_step) * arrived[...].astype(jnp.float32)
        mixed = [student_mixed.at[offset] for offset in range(count)]
        collect(target, student_inverse, student_rows[...], mixed)

    @pl.when(section == 1)
    def _():
        sums_ref[...] = jnp.zeros_like(sums_ref)

    @pl.when(section >= 2)
    def _():
        collect(target_in[...], critic_inverse, pair[:, :latent_width], critic_mixed)


def expand_kernel(
    count, groups, full_rows, fetches, own, from_first, from_second, from_third, embed_w, *refs
):
    heads_w = refs[:count]
    other_mods = refs[count : count + groups - 1]
    sums = refs[count + groups - 1 : count + 3 * groups - 1]
    grad_ref, total_ref, work, joined = refs[count + 3 * groups - 1 :]
    section = lax.axis_index("segment")
    place = lax.axis_index("seq")
    latent_width = embed_w.shape[1]
    model_width = embed_w.shape[2]
    picked = own[...].astype(jnp.float32)
    for source, value in ((0, from_first), (2, from_second), (1, from_third)):
        picked = jnp.where(section == source, value[...].astype(jnp.float32), picked)
    grad_ref[...] = picked.T

    @pl.when(section == 1)
    def _():
        total_ref[...] = jnp.zeros_like(total_ref)

    @pl.when(section != 1)
    def _():
        (late,) = fetches
        late.start()
        for group in range(groups):
            low = group * latent_width
            joined[:, low : low + latent_width] = sums[2 * group][...].astype(jnp.float32) + sums[
                2 * group + 1
            ][...].astype(jnp.float32)
        near_top = joined[count].astype(jnp.bfloat16)
        heads = [joined[place ^ offset].astype(jnp.bfloat16) for offset in range(count)]
        averages = None
        for first in range(0, model_width, TILE):
            span = slice(first, first + TILE)
            spread = None
            for head, rows_w in zip(heads, heads_w):
                product = dot32(head, rows_w[:, span])
                spread = product if spread is None else spread + product
            near = dot32(near_top[:, :latent_width], embed_w[0, :, span])
            mods = [late.ready(), *other_mods]
            gates = jnp.concatenate(
                [
                    jnp.broadcast_to(
                        slot_of(mod, 0, model_width, first, TILE), (latent_width, TILE)
                    )
                    for mod in mods
                ],
                axis=0,
            )
            value = near + gates * spread
            work[:, span] = value
            part = lane_sum(value)
            averages = part if averages is None else averages + part
        averages = jnp.sum(averages, axis=1, keepdims=True) / model_width
        counts = joined[count][:, latent_width : latent_width + 1]
        for first in range(0, model_width, TILE):
            span = slice(first, first + TILE)
            value = work[:, span] - averages
            total = None
            for group in range(groups):
                mine = slice(group * latent_width, (group + 1) * latent_width)
                product = value[mine] * (
                    1.0 + slot_of(mods[group], 2, model_width, first, TILE)
                ) + counts[mine] * slot_of(mods[group], 1, model_width, first, TILE)
                total = product if total is None else total + product
            total_ref[:, span] = total / full_rows


def step(
    clean, noise, timesteps, text_vec, w_embed, w_time, w_mod, w_qkv, w_out, qk_gain, w_final
):
    section = lax.axis_index("segment")
    sections = lax.axis_size("segment")
    tok_rows = clean.shape[1]
    latent_width = clean.shape[2]
    model_width = w_embed.shape[2]
    mod_width = w_mod.shape[2]
    count = lax.axis_size("seq")
    full_rows = tok_rows * count
    head_width = w_qkv.shape[4]
    kind_w = jnp.transpose(w_qkv[0, :, 0], (1, 0, 2))
    final_w = jnp.transpose(w_final[0])
    heads_w = gather_doubling(w_out[0, 0], "seq", count)
    bf16, f32 = jnp.bfloat16, jnp.float32

    depth = packed_rows(mod_width)
    packed, noisy_student = run(
        condition_kernel,
        [
            array((tok_rows // 2 + 2 * depth, 2 * latent_width), bf16),
            array((tok_rows, latent_width), bf16),
        ],
        (),
        2 * model_width * mod_width,
        scratch=(
            pltpu.VMEM((model_width, mod_width), bf16),
            pltpu.VMEM((depth, 128), f32),
            pltpu.SemaphoreType.DMA((STREAMS,)),
        ),
        fetched=(timesteps, text_vec, w_time[0], jnp.transpose(clean[0]), noise[0]),
        streamed=(w_mod[0],),
    )
    packed_all = gather_near(packed, "seq", count)

    head_blocks = [array((tok_rows, head_width), bf16)] * count
    stored = [
        ((full_rows, 3 * head_width), f32),
        ((full_rows, 128), f32),
        ((full_rows, head_width), bf16),
        ((full_rows, head_width), bf16),
    ]
    short_shape = ((latent_width + 16, 3 * head_width), f32)
    *head_outs, short, late_mod = run(
        functools.partial(student_front_kernel, count, mod_width),
        head_blocks,
        (w_embed, kind_w, qk_gain, *packed_all),
        4 * latent_width * model_width * 3 * head_width,
        scratch=[
            pltpu.VMEM((1, 5 * model_width), f32),
            pltpu.VMEM(*short_shape),
            pltpu.VMEM((count, tok_rows, latent_width), bf16),
            pltpu.SemaphoreType.DMA((2,)),
        ]
        + [pltpu.VMEM(shape, kind) for shape, kind in stored],
        sent=[array(*short_shape), array((1, 3 * model_width), f32)],
    )
    student_mixed = scatter_near(head_outs, "seq", count)
    groups = lax.axis_size("dp")
    late_mods = gather_near(late_mod, "dp", groups)
    work = pltpu.VMEM((tok_rows, model_width), f32)
    inverse_shape = array((tok_rows, 128), f32)
    pair, saved, student_inverse = run(
        functools.partial(student_tail_kernel, count),
        [array((tok_rows, 2 * latent_width), bf16)],
        (noisy_student, w_embed, *student_mixed, *heads_w),
        2 * tok_rows * model_width * head_width * count,
        scratch=(
            work,
            pltpu.VMEM((tok_rows, 128), f32),
            pltpu.SemaphoreType.DMA((count + 1,)),
        ),
        fetched=(late_mod, final_w, noise[0], timesteps),
        sent=[array((count, tok_rows, head_width), bf16), inverse_shape],
    )
    moved = [lax.ppermute(pair, "segment", [(0, place)]) for place in range(1, sections)]
    held = moved[0]
    for place in range(2, sections):
        held = jnp.where(section == place, moved[place - 1], held)
    pair = jnp.where(section == 0, pair, held)
    critic_rows = gather_near(pair[:, :latent_width], "seq", count)
    *head_outs, proj, inverse, keys, values = run(
        functools.partial(critic_front_kernel, count),
        head_blocks + [array(shape, kind) for shape, kind in stored],
        (w_embed, qk_gain, *critic_rows),
        4 * latent_width * model_width * full_rows,
        fetched=(short,),
    )
    critic_mixed = scatter_near(head_outs, "seq", count)
    small = array((tok_rows, latent_width), f32)
    thin = array((tok_rows, latent_width), bf16)
    *grad_heads, critic_inverse, term_rows, target, direct = run(
        functools.partial(critic_tail_kernel, count),
        head_blocks + [inverse_shape, thin, small, small],
        (pair, w_embed, *critic_mixed, *heads_w),
        4 * tok_rows * model_width * head_width * count,
        scratch=(pltpu.VMEM((tok_rows, latent_width), bf16), work, work),
        fetched=(late_mod, final_w, noise[0], timesteps),
    )
    grad_blocks = scatter_near(grad_heads, "seq", count)
    fake = lax.ppermute(term_rows, "segment", swaps(sections, 1))
    real = lax.ppermute(term_rows, "segment", swaps(sections, 2))
    (gram,) = run(
        gram_kernel,
        [array((2, latent_width, latent_width), bf16)],
        (w_embed,),
        6 * latent_width * latent_width * model_width,
    )
    parts = run(
        functools.partial(judge_back_kernel, count, model_width),
        [array((tok_rows + 32, latent_width), bf16)] * count,
        (short, gram, qk_gain, proj, inverse, keys, values, pair, real, *critic_rows, *grad_blocks),
        10 * full_rows * full_rows * head_width,
        scratch=(pltpu.VMEM((full_rows, head_width), f32),) * 3,
    )
    parts = scatter_near(parts, "seq", count)
    (payload,) = run(
        functools.partial(merge_kernel, count),
        [thin],
        (direct, real, fake, *parts),
        1000,
        fetched=(timesteps,),
    )
    ends = [(place, sections - 1 - place) for place in range(sections)]
    to_student = lax.ppermute(payload, "segment", ends)
    to_second = lax.ppermute(payload, "segment", swaps(sections, 1))
    to_third = lax.ppermute(payload, "segment", swaps(sections, 2))
    (sums,) = run(
        functools.partial(outer_kernel, count),
        [array((count + 1, latent_width, 128), bf16)],
        (
            to_student,
            target,
            noisy_student,
            pair,
            saved,
            student_inverse,
            critic_inverse,
            *critic_mixed,
        ),
        2 * tok_rows * latent_width * head_width * (count + 1),
        fetched=(timesteps,),
    )
    last = count // 2
    bit = 1
    while bit < last:
        moved = lax.ppermute(sums, "seq", swaps(count, bit))
        sums = (sums.astype(f32) + moved.astype(f32)).astype(bf16)
        bit *= 2
    sums_all = []
    for group in range(groups):
        for offset in (0, last):
            moves = [
                (place * groups + batch, (place ^ offset) * groups + (batch ^ group))
                for place in range(count)
                for batch in range(groups)
            ]
            sums_all.append(
                sums if offset == group == 0 else lax.ppermute(sums, ("seq", "dp"), moves)
            )
    grad_t, total_t = run(
        functools.partial(expand_kernel, count, groups, full_rows),
        [array((latent_width, tok_rows), f32), array((latent_width, model_width), f32)],
        (payload, to_student, to_second, to_third, w_embed, *heads_w, *late_mods[1:], *sums_all),
        4 * groups * latent_width * model_width * head_width * count,
        scratch=(
            pltpu.VMEM((groups * latent_width, model_width), f32),
            pltpu.VMEM((count + 1, groups * latent_width, 128), f32),
        ),
        fetched=(late_mod,),
    )
    return (jnp.transpose(grad_t)[None], jnp.transpose(total_t)[None])


def solution(mesh):
    placed = (
        P("dp", "seq", None),
        P("dp", "seq", None),
        P(),
        P("dp", None),
        P("segment", None, None),
        P("segment", None, None),
        P("segment", None, "seq"),
        P("segment", None, "seq", None, None),
        P("segment", "seq", None, None),
        P("segment", None, None),
        P("segment", None, None),
    )
    return jax.shard_map(
        step,
        mesh=mesh,
        in_specs=placed,
        out_specs=(P("dp", "seq", None), P("segment", None, None)),
        check_vma=False,
    )
```

```python
import functools
import math

import jax
import jax.numpy as jnp
from jax import lax
from jax.experimental import pallas as pl
from jax.experimental.pallas import tpu as pltpu
from jax.sharding import PartitionSpec as P


SHIFT = 7.0
EPS = 1e-06
ADV_WEIGHT = 3.0
TILE = 512
STREAMS = 6
SPARE = 8 << 20
VMEM = pl.BlockSpec(memory_space=pltpu.VMEM)
HBM = pl.BlockSpec(memory_space=pltpu.HBM)


def halves(values):
    top = values.astype(jnp.bfloat16)
    return (top, (values - top.astype(jnp.float32)).astype(jnp.bfloat16))


def swaps(count, offset):
    return [(place, place ^ offset) for place in range(count)]


def gather_near(value, axis, count):
    return [value] + [lax.ppermute(value, axis, swaps(count, offset)) for offset in range(1, count)]


def scatter_near(blocks, axis, count):
    return [blocks[0]] + [
        lax.ppermute(blocks[offset], axis, swaps(count, offset))
        for offset in range(1, count)
    ]


def gather_doubling(value, axis, count):
    held = {0: value}
    bit = count // 2
    while bit:
        for offset in sorted(held):
            held[offset | bit] = lax.ppermute(held[offset], axis, swaps(count, bit))
        bit //= 2
    return [held[offset] for offset in range(count)]


def in_order(pieces, own_place):
    ordered = list(pieces)
    bit = 1
    while bit < len(ordered):
        flipped = (own_place & bit) != 0
        ordered = [
            jnp.where(flipped, ordered[place ^ bit], ordered[place])
            for place in range(len(ordered))
        ]
        bit *= 2
    return ordered


def dot32(left, right):
    return jnp.dot(left, right, preferred_element_type=jnp.float32)


def dot32_t(left, right):
    return lax.dot_general(
        left, right, (((1,), (1,)), ((), ())), preferred_element_type=jnp.float32
    )


def dot32_first(left, right):
    return lax.dot_general(
        left, right, (((0,), (0,)), ((), ())), preferred_element_type=jnp.float32
    )


def steps_of(times):
    times_ref = times.ready()
    place = lax.axis_index("dp")
    return (times_ref[place, 0], times_ref[place, 1])


def noise_level(step):
    fraction = jnp.full((1, 1), step, jnp.int32).astype(jnp.float32) / 1000.0
    return SHIFT * fraction / (1.0 + (SHIFT - 1.0) * fraction)


def slot_of(mod_ref, slot, width, first, size):
    return mod_ref[:, slot * width + first : slot * width + first + size]


def lane_sum(values):
    total = values[:, :128]
    for first in range(128, values.shape[1], 128):
        total = total + values[:, first : first + 128]
    return total


class Fetch:
    def __init__(self, source, target, arrival):
        self.copy = pltpu.make_async_copy(source, target, arrival)
        self.target = target
        self.waiting = True

    def start(self):
        self.copy.start()

    def ready(self):
        if self.waiting:
            self.copy.wait()
            self.waiting = False
        return self.target


def bytes_of(items):
    return sum(math.prod(item.shape) * jnp.dtype(item.dtype).itemsize for item in items)


def in_hbm(item):
    return pltpu.with_memory_space_constraint(item, pltpu.HBM)


def run(kernel, outputs, operands, flops, scratch=(), fetched=(), streamed=(), sent=()):
    inputs = len(operands)
    total = inputs + len(fetched) + len(streamed)
    results = len(outputs) + len(sent)

    def body(*refs):
        sources = refs[inputs:total]
        outs = refs[total : total + results]
        own = refs[total + results : total + results + len(scratch)]
        rest = refs[total + results + len(scratch) :]
        fetches = [
            Fetch(source, target, rest[-1].at[place])
            for place, (source, target) in enumerate(zip(sources, rest[:-1]))
        ]
        fetches += sources[len(fetched) :]
        kernel(fetches, *refs[:inputs], *outs, *own)

    places = [
        (pltpu.SMEM if item.dtype == jnp.int32 else pltpu.VMEM)(item.shape, item.dtype)
        for item in fetched
    ]
    held = bytes_of(
        [ref for ref in list(scratch) + places if ref.memory_space == pltpu.VMEM]
    )
    limit = min(60 << 20, SPARE + held + bytes_of(operands) + 2 * bytes_of(outputs))
    return pl.pallas_call(
        body,
        out_shape=list(outputs) + [pltpu.HBM(item.shape, item.dtype) for item in sent],
        in_specs=[VMEM] * inputs + [HBM] * (total - inputs),
        out_specs=[VMEM] * len(outputs) + [HBM] * len(sent),
        scratch_shapes=list(scratch)
        + places
        + [pltpu.SemaphoreType.DMA((max(1, len(fetched)),))],
        compiler_params=pltpu.CompilerParams(vmem_limit_bytes=limit),
        cost_estimate=pl.CostEstimate(
            flops=flops,
            bytes_accessed=bytes_of(list(operands) + list(fetched) + list(outputs)),
            transcendentals=0,
        ),
    )(*operands, *[in_hbm(item) for item in (*fetched, *streamed)])


def array(shape, dtype):
    return jax.ShapeDtypeStruct(shape, dtype)


def packed_rows(width):
    return -(-width // 2048) * 16


def condition_kernel(fetches, packed_out, noisy_out, held, mod_rows, arrivals):
    times, text, time_w, clean_t, noise, mod_w = fetches
    model_width = held.shape[0]
    rows = model_width // STREAMS
    for fetch in fetches[:-1]:
        fetch.start()
    copies = [
        pltpu.make_async_copy(
            mod_w.at[pl.ds(part * rows, rows)], held.at[pl.ds(part * rows, rows)], arrivals.at[part]
        )
        for part in range(STREAMS)
    ]
    for copy in copies:
        copy.start()
    student_step, critic_step = steps_of(times)
    step = jnp.where(lax.axis_index("segment") == 0, student_step, critic_step)
    text_ref = text.ready()
    half = text_ref.shape[1] // 2
    places = lax.broadcasted_iota(jnp.int32, (1, half), 1).astype(jnp.float32)
    frequency = jnp.exp(-math.log(10000.0) * places / half)
    angles = jnp.full((1, half), step, jnp.int32).astype(jnp.float32) * frequency
    features = jnp.concatenate([jnp.cos(angles), jnp.sin(angles)], axis=1) + text_ref[...]
    features = jnp.broadcast_to(features, (8, 2 * half)).astype(jnp.bfloat16)
    hidden = dot32(features, time_w.ready()[...])
    hidden = (hidden / (1.0 + jnp.exp(-hidden))).astype(jnp.bfloat16)
    sigma_student = noise_level(student_step)
    clean_ref, noise_ref = clean_t.ready(), noise.ready()
    noisy = (1.0 - sigma_student) * clean_ref[...].astype(jnp.float32).T + sigma_student * noise_ref[
        :, : clean_ref.shape[0]
    ].astype(jnp.float32)
    noisy = noisy.astype(jnp.bfloat16)
    noisy_out[...] = noisy
    top = noisy.shape[0] // 2
    packed_out[:top] = jnp.concatenate([noisy[:top], noisy[top:]], axis=1)
    mod_rows[...] = jnp.zeros_like(mod_rows)
    total = None
    for part in range(STREAMS):
        copies[part].wait()
        piece = dot32(
            hidden[:, part * rows : (part + 1) * rows], held[part * rows : (part + 1) * rows]
        )
        total = piece if total is None else total + piece
    width = total.shape[1]
    for row, first in enumerate(range(0, width, 128)):
        size = min(128, width - first)
        mod_rows[row : row + 1, :size] = total[:1, first : first + size]
    depth = mod_rows.shape[0]
    packed_out[top : top + depth], packed_out[top + depth :] = halves(mod_rows[...])


def rms_scale(values, gain_vec):
    inverse = lax.rsqrt(jnp.mean(values * values, axis=-1, keepdims=True) + EPS)
    unit_vec = values * inverse
    return (unit_vec * gain_vec, unit_vec, inverse)


def rms_back(gradient, unit_vec, inverse, gain_vec):
    scaled = gradient * gain_vec
    return inverse * (scaled - unit_vec * jnp.mean(scaled * unit_vec, axis=-1, keepdims=True))


def centred(embed_ref):
    values = embed_ref[0].astype(jnp.float32)
    return values - jnp.mean(values, axis=1, keepdims=True)


def front(rows, central, short, gains, head_outs, proj_ref, inverse_ref, key_ref, value_ref):
    latent_width = central.shape[0]
    model_width = central.shape[1]
    count = len(rows)
    head_width = gains.shape[2]
    scale = 1.0 / math.sqrt(head_width)
    size = rows[0].shape[0]
    short_top = None
    for place in range(count):
        block = rows[place][...]
        squares = None
        for first in range(0, model_width, TILE):
            piece = dot32(block, central[:, first : first + TILE])
            piece = lane_sum(piece * piece)
            squares = piece if squares is None else squares + piece
        inverse = lax.rsqrt(jnp.sum(squares, axis=1, keepdims=True) / model_width + EPS)
        if short_top is None:
            values = short()
            short_top, short_low = halves(values[:latent_width])
            short_shift = values[latent_width : latent_width + 1]
        projected = inverse * (dot32(block, short_top) + dot32(block, short_low)) + short_shift
        low = place * size
        proj_ref[low : low + size] = projected
        inverse_ref[low : low + size] = jnp.broadcast_to(inverse, (size, 128))
        keys, _, _ = rms_scale(projected[:, head_width : 2 * head_width], gains[0, 1:2])
        key_ref[low : low + size] = keys.astype(jnp.bfloat16)
        value_ref[low : low + size] = projected[:, 2 * head_width :].astype(jnp.bfloat16)
    for place in range(count):
        low = place * size
        queries, _, _ = rms_scale(proj_ref[low : low + size, :head_width], gains[0, :1])
        scores = dot32_t(queries.astype(jnp.bfloat16), key_ref[...]) * scale
        weights = jnp.exp(scores)
        soft_max = weights * (1.0 / jnp.sum(weights, axis=-1, keepdims=True))
        head_outs[place][...] = dot32(soft_max.astype(jnp.bfloat16), value_ref[...]).astype(
            jnp.bfloat16
        )


def student_front_kernel(count, width, fetches, embed_w, head_w, gains, *refs):
    packed = refs[:count]
    head_outs = refs[count : 2 * count]
    short_out, late_out, mod, short_ref, rows_ref, sends, *kept = refs[2 * count :]
    model_width = embed_w.shape[2]
    latent_width = embed_w.shape[1]
    size = rows_ref.shape[1]
    half = size // 2
    depth = packed_rows(width)
    parts = [
        piece[half : half + depth].astype(jnp.float32) + piece[half + depth :].astype(jnp.float32)
        for piece in packed
    ]
    for place, part in enumerate(in_order(parts, lax.axis_index("seq"))):
        for row, first in enumerate(range(0, width, 128)):
            lanes = min(128, width - first)
            low = place * width + first
            mod[:, low : low + lanes] = part[row : row + 1, :lanes]
    late = pltpu.make_async_copy(
        mod.at[:, pl.ds(2 * model_width, 3 * model_width)], late_out, sends.at[0]
    )
    late.start()
    for place in range(count):
        rows_ref[place, :half] = packed[place][:half, :latent_width]
        rows_ref[place, half:] = packed[place][:half, latent_width:]
    central = centred(embed_w)
    scale_in = slot_of(mod, 1, model_width, 0, model_width)
    shift_in = slot_of(mod, 0, model_width, 0, model_width)
    in_rows = jnp.concatenate(
        [central * (1.0 + scale_in), jnp.broadcast_to(shift_in, (16, model_width))], axis=0
    )
    in_top, in_low = halves(in_rows)
    in_both = jnp.concatenate([in_top, in_low], axis=0)
    both = jnp.concatenate([dot32(in_both, head_w[kind]) for kind in range(3)], axis=1)
    short = both[: in_rows.shape[0]] + both[in_rows.shape[0] :]
    short_ref[...] = short
    send = pltpu.make_async_copy(short_ref, short_out, sends.at[1])
    send.start()

    @pl.when(lax.axis_index("segment") == 0)
    def _():
        front(
            [rows_ref.at[place] for place in range(count)],
            central.astype(jnp.bfloat16),
            lambda: short,
            gains,
            head_outs,
            *kept,
        )

    late.wait()
    send.wait()


def critic_front_kernel(count, fetches, embed_w, gains, *refs):
    rows = refs[:count]
    head_outs = refs[count : 2 * count]
    kept = refs[2 * count :]
    (short,) = fetches

    @pl.when(lax.axis_index("segment") != 0)
    def _():
        short.start()
        front(
            rows,
            centred(embed_w).astype(jnp.bfloat16),
            lambda: short.ready()[...],
            gains,
            head_outs,
            *kept,
        )


def tail(late, latent, embed_w, final_t, mixed, heads_w, work):
    model_width = embed_w.shape[2]
    block = latent[...]
    sums = None
    for first in range(0, model_width, TILE):
        span = slice(first, first + TILE)
        attended = None
        for piece, rows_w in zip(mixed, heads_w):
            product = dot32(piece[...], rows_w[:, span])
            attended = product if attended is None else attended + product
        mod = late.ready()
        residual = (
            dot32(block, embed_w[0, :, span]) + slot_of(mod, 0, model_width, first, TILE) * attended
        )
        work[:, span] = residual
        part = lane_sum(residual)
        sums = part if sums is None else sums + part
    row_mean = jnp.sum(sums, axis=1, keepdims=True) / model_width
    sums = None
    for first in range(0, model_width, TILE):
        span = slice(first, first + TILE)
        middle = work[:, span] - row_mean
        work[:, span] = middle
        part = lane_sum(middle * middle)
        sums = part if sums is None else sums + part
    inverse = lax.rsqrt(jnp.sum(sums, axis=1, keepdims=True) / model_width + EPS)
    result = None
    final_w = final_t.ready()
    for first in range(0, model_width, TILE):
        span = slice(first, first + TILE)
        normed = work[:, span] * inverse
        work[:, span] = normed
        final_in = (
            normed * (1.0 + slot_of(mod, 2, model_width, first, TILE))
            + slot_of(mod, 1, model_width, first, TILE)
        ).astype(jnp.bfloat16)
        product = dot32_t(final_in, final_w[:, span])
        result = product if result is None else result + product
    return (result, inverse)


def student_tail_kernel(count, fetches, latent, embed_w, *refs):
    mixed = refs[:count]
    heads_w = refs[count : 2 * count]
    pair_ref, saved_out, inverse_out, work, inverse_ref, sends = refs[2 * count :]
    late, final_t, noise, times = fetches
    latent_width = latent.shape[1]

    @pl.when(lax.axis_index("segment") == 0)
    def _():
        for fetch in fetches:
            fetch.start()
        copies = [
            pltpu.make_async_copy(mixed[place], saved_out.at[place], sends.at[place])
            for place in range(count)
        ]
        for copy in copies:
            copy.start()
        velocity, inverse = tail(late, latent, embed_w, final_t, mixed, heads_w, work)
        inverse_ref[...] = jnp.broadcast_to(inverse, inverse_ref.shape)
        copies.append(pltpu.make_async_copy(inverse_ref, inverse_out, sends.at[count]))
        copies[-1].start()
        student_step, critic_step = steps_of(times)
        sigma_student, sigma_critic = noise_level(student_step), noise_level(critic_step)
        sample = latent[...].astype(jnp.float32) - sigma_student * velocity
        second = noise.ready()[:, latent_width:].astype(jnp.float32)
        critic = (1.0 - sigma_critic) * sample + sigma_critic * second
        pair_ref[...] = jnp.concatenate([critic, sample], axis=1).astype(jnp.bfloat16)
        for copy in copies:
            copy.wait()


def pick_kernel(sections, fetches, own, *refs):
    moved = refs[: sections - 1]
    pair_ref, rows_ref = refs[sections - 1 :]
    section = lax.axis_index("segment")
    for place in range(sections):

        @pl.when(section == place)
        def _():
            chosen = own if place == 0 else moved[place - 1]
            pair_ref[...] = chosen[...]
            rows_ref[...] = chosen[:, : rows_ref.shape[1]]


def critic_tail_kernel(count, fetches, pair, embed_w, *refs):
    mixed = refs[:count]
    heads_w = refs[count : 2 * count]
    grads = refs[2 * count : 3 * count]
    inverse_ref, term_ref, target_ref, direct_ref, latent, work, other = refs[3 * count :]
    late, final_t, noise, times = fetches
    model_width = embed_w.shape[2]
    latent_width = latent.shape[1]
    section = lax.axis_index("segment")

    @pl.when(section != 0)
    def _():
        for fetch in fetches:
            fetch.start()
        both = pair[...].astype(jnp.float32)
        sample = both[:, latent_width:]
        latent[...] = pair[:, :latent_width]
        result, inverse = tail(late, latent, embed_w, final_t, mixed, heads_w, work)
        mod, final_w = late.ready(), final_t.ready()
        _, critic_step = steps_of(times)
        sigma_critic = noise_level(critic_step)
        inverse_ref[...] = jnp.broadcast_to(inverse, inverse_ref.shape)
        term_ref[...] = (sigma_critic * result).astype(jnp.bfloat16)
        second = noise.ready()[:, latent_width:].astype(jnp.float32)
        target_ref[...] = jnp.where(
            section == 2,
            2.0 * (result - (second - sample)),
            jnp.where(section == 3, 1.0 / (1.0 + jnp.exp(-result)), 0.0),
        )

        @pl.when(section == 3)
        def _():
            grad_logit = (-1.0 / (1.0 + jnp.exp(result))).astype(jnp.bfloat16)
            plain, along = None, None
            for first in range(0, model_width, TILE):
                span = slice(first, first + TILE)
                gradient = dot32(grad_logit, final_w[:, span]) * (
                    1.0 + slot_of(mod, 2, model_width, first, TILE)
                )
                other[:, span] = gradient
                part = lane_sum(gradient)
                plain = part if plain is None else plain + part
                part = lane_sum(gradient * work[:, span])
                along = part if along is None else along + part
            plain = jnp.sum(plain, axis=1, keepdims=True) / model_width
            along = jnp.sum(along, axis=1, keepdims=True) / model_width
            direct = None
            totals = [None] * count
            for first in range(0, model_width, TILE):
                span = slice(first, first + TILE)
                grad_residual = inverse * (other[:, span] - plain - work[:, span] * along)
                top, low = halves(grad_residual)
                product = dot32_t(top, embed_w[0, :, span]) + dot32_t(low, embed_w[0, :, span])
                direct = product if direct is None else direct + product
                grad_attended = (slot_of(mod, 0, model_width, first, TILE) * grad_residual).astype(
                    jnp.bfloat16
                )
                for place in range(count):
                    product = dot32_t(grad_attended, heads_w[place][:, span])
                    held = totals[place]
                    totals[place] = product if held is None else held + product
            direct_ref[...] = direct
            for place in range(count):
                grads[place][...] = totals[place].astype(jnp.bfloat16)


def gram_kernel(fetches, embed_w, gram_ref):
    central_top, central_low = halves(centred(embed_w))
    gram = (
        dot32_t(central_top, central_top)
        + dot32_t(central_top, central_low)
        + dot32_t(central_low, central_top)
    )
    gram_ref[0], gram_ref[1] = halves(gram)


def judge_back_kernel(count, model_width, fetches, short_in, gram, gains, proj_ref, inverse_ref, key_ref, value_ref, pair, real, *refs):
    rows = refs[:count]
    grads = refs[count : 2 * count]
    outs = refs[2 * count : 3 * count]
    grad_key_ref, grad_value_ref, grad_query_ref = refs[3 * count :]
    section = lax.axis_index("segment")
    latent_width = rows[0].shape[1]
    head_width = gains.shape[2]
    scale = 1.0 / math.sqrt(head_width)
    size = rows[0].shape[0]

    @pl.when(section == 3)
    def _():
        both = pair[...].astype(jnp.float32)
        gaps = jnp.abs(
            both[:, latent_width:] - both[:, :latent_width] + real[...].astype(jnp.float32)
        )
        error = jnp.sum(jnp.sum(gaps, axis=1, keepdims=True), axis=0, keepdims=True)
        error = error / (size * latent_width)
        error_top, error_low = halves(jnp.broadcast_to(error, (16, latent_width)))
        for place in range(count):
            outs[place][size : size + 16] = error_top
            outs[place][size + 16 :] = error_low
            low = place * size
            span = slice(low, low + size)
            queries, _, _ = rms_scale(proj_ref[span, :head_width], gains[0, :1])
            query_b = queries.astype(jnp.bfloat16)
            weights = jnp.exp(dot32_t(query_b, key_ref[...]) * scale)
            soft_max = weights * (1.0 / jnp.sum(weights, axis=-1, keepdims=True))
            grad_out = grads[place][...]
            grad_soft = dot32_t(grad_out, value_ref[...])
            grad_value = dot32_first(soft_max.astype(jnp.bfloat16), grad_out)
            grad_scores = soft_max * (
                grad_soft - jnp.sum(soft_max * grad_soft, axis=-1, keepdims=True)
            )
            grad_scores_b = (grad_scores * scale).astype(jnp.bfloat16)
            grad_query_ref[span] = dot32(grad_scores_b, key_ref[...])
            grad_key = dot32_first(grad_scores_b, query_b)
            if place == 0:
                grad_value_ref[...] = grad_value
                grad_key_ref[...] = grad_key
            else:
                grad_value_ref[...] += grad_value
                grad_key_ref[...] += grad_key
        gram_top, gram_low = gram[0], gram[1]
        short_top, short_low = halves(short_in[:latent_width])
        for place in range(count):
            low = place * size
            span = slice(low, low + size)
            projected = proj_ref[span]
            _, q_unit, q_inverse = rms_scale(projected[:, :head_width], gains[0, :1])
            _, k_unit, k_inverse = rms_scale(
                projected[:, head_width : 2 * head_width], gains[0, 1:2]
            )
            grad_q = rms_back(grad_query_ref[span], q_unit, q_inverse, gains[0, :1])
            grad_k = rms_back(grad_key_ref[span], k_unit, k_inverse, gains[0, 1:2])
            grad_proj = jnp.concatenate([grad_q, grad_k, grad_value_ref[span]], axis=1).astype(
                jnp.bfloat16
            )
            through = dot32_t(grad_proj, short_top) + dot32_t(grad_proj, short_low)
            block = rows[place][...]
            along = jnp.sum(through * block.astype(jnp.float32), axis=1, keepdims=True) / model_width
            spanned = dot32(block, gram_top) + dot32(block, gram_low)
            inverse = inverse_ref[span, :1]
            outs[place][:size] = (
                inverse * (through - spanned * (inverse * inverse * along))
            ).astype(jnp.bfloat16)


def merge_kernel(count, fetches, direct, real, fake, *refs):
    parts = refs[:count]
    payload_ref = refs[count]
    rows = direct.shape[0]

    @pl.when(lax.axis_index("segment") == 3)
    def _():
        (times,) = fetches
        times.start()
        total = parts[0][...].astype(jnp.float32)
        for part in parts[1:]:
            total = total + part[...].astype(jnp.float32)
        _, critic_step = steps_of(times)
        adverse = (1.0 - noise_level(critic_step)) * (total[:rows] + direct[...])
        spread = (total[rows : rows + 16] + total[rows + 16 :])[:1, :1] / count + EPS
        gap = real[...].astype(jnp.float32) - fake[...].astype(jnp.float32)
        payload_ref[...] = (gap / spread + ADV_WEIGHT * adverse).astype(jnp.bfloat16)


def outer_kernel(
    count,
    fetches,
    arrived,
    target_in,
    student_rows,
    pair,
    student_mixed,
    student_inverse,
    critic_inverse,
    *refs,
):
    critic_mixed = refs[:count]
    sums_ref = refs[count]
    section = lax.axis_index("segment")
    place = lax.axis_index("seq")
    latent_width = student_rows.shape[1]

    def collect(target, inverse, latent, mixed):
        target = target.astype(jnp.bfloat16)
        weighted = inverse[:, :latent_width] * target.astype(jnp.float32)
        top, low = halves(weighted)
        for offset in range(count):
            piece = mixed[offset][...]
            sums_ref[place ^ offset] = (dot32_first(top, piece) + dot32_first(low, piece)).astype(
                jnp.bfloat16
            )
        near = dot32_first(top, latent) + dot32_first(low, latent)
        ones = jnp.ones((target.shape[0], sums_ref.shape[2] - latent_width), jnp.bfloat16)
        sums_ref[count] = jnp.concatenate([near, dot32_first(target, ones)], axis=1).astype(
            jnp.bfloat16
        )

    @pl.when(section == 0)
    def _():
        (times,) = fetches
        times.start()
        student_step, _ = steps_of(times)
        target = -noise_level(student_step) * arrived[...].astype(jnp.float32)
        mixed = [student_mixed.at[offset] for offset in range(count)]
        collect(target, student_inverse, student_rows[...], mixed)

    @pl.when(section == 1)
    def _():
        sums_ref[...] = jnp.zeros_like(sums_ref)

    @pl.when(section >= 2)
    def _():
        collect(target_in[...], critic_inverse, pair[:, :latent_width], critic_mixed)


def expand_kernel(
    count, groups, full_rows, fetches, own, from_first, from_second, from_third, embed_w, *refs
):
    heads_w = refs[:count]
    other_mods = refs[count : count + groups - 1]
    sums = refs[count + groups - 1 : count + 3 * groups - 1]
    grad_ref, total_ref, work, joined = refs[count + 3 * groups - 1 :]
    section = lax.axis_index("segment")
    place = lax.axis_index("seq")
    latent_width = embed_w.shape[1]
    model_width = embed_w.shape[2]
    picked = own[...].astype(jnp.float32)
    for source, value in ((0, from_first), (2, from_second), (1, from_third)):
        picked = jnp.where(section == source, value[...].astype(jnp.float32), picked)
    grad_ref[...] = picked.T

    @pl.when(section == 1)
    def _():
        total_ref[...] = jnp.zeros_like(total_ref)

    @pl.when(section != 1)
    def _():
        (late,) = fetches
        late.start()
        for group in range(groups):
            low = group * latent_width
            joined[:, low : low + latent_width] = sums[2 * group][...].astype(jnp.float32) + sums[
                2 * group + 1
            ][...].astype(jnp.float32)
        near_top = joined[count].astype(jnp.bfloat16)
        heads = [joined[place ^ offset].astype(jnp.bfloat16) for offset in range(count)]
        averages = None
        for first in range(0, model_width, TILE):
            span = slice(first, first + TILE)
            spread = None
            for head, rows_w in zip(heads, heads_w):
                product = dot32(head, rows_w[:, span])
                spread = product if spread is None else spread + product
            near = dot32(near_top[:, :latent_width], embed_w[0, :, span])
            mods = [late.ready(), *other_mods]
            gates = jnp.concatenate(
                [
                    jnp.broadcast_to(
                        slot_of(mod, 0, model_width, first, TILE), (latent_width, TILE)
                    )
                    for mod in mods
                ],
                axis=0,
            )
            value = near + gates * spread
            work[:, span] = value
            part = lane_sum(value)
            averages = part if averages is None else averages + part
        averages = jnp.sum(averages, axis=1, keepdims=True) / model_width
        counts = joined[count][:, latent_width : latent_width + 1]
        for first in range(0, model_width, TILE):
            span = slice(first, first + TILE)
            value = work[:, span] - averages
            total = None
            for group in range(groups):
                mine = slice(group * latent_width, (group + 1) * latent_width)
                product = value[mine] * (
                    1.0 + slot_of(mods[group], 2, model_width, first, TILE)
                ) + counts[mine] * slot_of(mods[group], 1, model_width, first, TILE)
                total = product if total is None else total + product
            total_ref[:, span] = total / full_rows


def step(
    clean, noise, timesteps, text_vec, w_embed, w_time, w_mod, w_qkv, w_out, qk_gain, w_final
):
    sections = lax.axis_size("segment")
    tok_rows = clean.shape[1]
    latent_width = clean.shape[2]
    model_width = w_embed.shape[2]
    mod_width = w_mod.shape[2]
    count = lax.axis_size("seq")
    full_rows = tok_rows * count
    head_width = w_qkv.shape[4]
    kind_w = jnp.transpose(w_qkv[0, :, 0], (1, 0, 2))
    final_w = jnp.transpose(w_final[0])
    heads_w = gather_doubling(w_out[0, 0], "seq", count)
    bf16, f32 = jnp.bfloat16, jnp.float32

    depth = packed_rows(mod_width)
    packed, noisy_student = run(
        condition_kernel,
        [
            array((tok_rows // 2 + 2 * depth, 2 * latent_width), bf16),
            array((tok_rows, latent_width), bf16),
        ],
        (),
        2 * model_width * mod_width,
        scratch=(
            pltpu.VMEM((model_width, mod_width), bf16),
            pltpu.VMEM((depth, 128), f32),
            pltpu.SemaphoreType.DMA((STREAMS,)),
        ),
        fetched=(timesteps, text_vec, w_time[0], jnp.transpose(clean[0]), noise[0]),
        streamed=(w_mod[0],),
    )
    packed_all = gather_near(packed, "seq", count)

    head_blocks = [array((tok_rows, head_width), bf16)] * count
    stored = [
        ((full_rows, 3 * head_width), f32),
        ((full_rows, 128), f32),
        ((full_rows, head_width), bf16),
        ((full_rows, head_width), bf16),
    ]
    short_shape = ((latent_width + 16, 3 * head_width), f32)
    *head_outs, short, late_mod = run(
        functools.partial(student_front_kernel, count, mod_width),
        head_blocks,
        (w_embed, kind_w, qk_gain, *packed_all),
        4 * latent_width * model_width * 3 * head_width,
        scratch=[
            pltpu.VMEM((1, 5 * model_width), f32),
            pltpu.VMEM(*short_shape),
            pltpu.VMEM((count, tok_rows, latent_width), bf16),
            pltpu.SemaphoreType.DMA((2,)),
        ]
        + [pltpu.VMEM(shape, kind) for shape, kind in stored],
        sent=[array(*short_shape), array((1, 3 * model_width), f32)],
    )
    student_mixed = scatter_near(head_outs, "seq", count)
    groups = lax.axis_size("dp")
    late_mods = gather_near(late_mod, "dp", groups)
    work = pltpu.VMEM((tok_rows, model_width), f32)
    inverse_shape = array((tok_rows, 128), f32)
    pair, saved, student_inverse = run(
        functools.partial(student_tail_kernel, count),
        [array((tok_rows, 2 * latent_width), bf16)],
        (noisy_student, w_embed, *student_mixed, *heads_w),
        2 * tok_rows * model_width * head_width * count,
        scratch=(
            work,
            pltpu.VMEM((tok_rows, 128), f32),
            pltpu.SemaphoreType.DMA((count + 1,)),
        ),
        fetched=(late_mod, final_w, noise[0], timesteps),
        sent=[array((count, tok_rows, head_width), bf16), inverse_shape],
    )
    moved = [lax.ppermute(pair, "segment", [(0, place)]) for place in range(1, sections)]
    pair, own_rows = run(
        functools.partial(pick_kernel, sections),
        [
            array((tok_rows, 2 * latent_width), bf16),
            array((tok_rows, latent_width), bf16),
        ],
        (pair, *moved),
        1000,
    )
    critic_rows = gather_near(own_rows, "seq", count)
    *head_outs, proj, inverse, keys, values = run(
        functools.partial(critic_front_kernel, count),
        head_blocks + [array(shape, kind) for shape, kind in stored],
        (w_embed, qk_gain, *critic_rows),
        4 * latent_width * model_width * full_rows,
        fetched=(short,),
    )
    critic_mixed = scatter_near(head_outs, "seq", count)
    small = array((tok_rows, latent_width), f32)
    thin = array((tok_rows, latent_width), bf16)
    *grad_heads, critic_inverse, term_rows, target, direct = run(
        functools.partial(critic_tail_kernel, count),
        head_blocks + [inverse_shape, thin, small, small],
        (pair, w_embed, *critic_mixed, *heads_w),
        4 * tok_rows * model_width * head_width * count,
        scratch=(pltpu.VMEM((tok_rows, latent_width), bf16), work, work),
        fetched=(late_mod, final_w, noise[0], timesteps),
    )
    grad_blocks = scatter_near(grad_heads, "seq", count)
    fake = lax.ppermute(term_rows, "segment", swaps(sections, 1))
    real = lax.ppermute(term_rows, "segment", swaps(sections, 2))
    (gram,) = run(
        gram_kernel,
        [array((2, latent_width, latent_width), bf16)],
        (w_embed,),
        6 * latent_width * latent_width * model_width,
    )
    parts = run(
        functools.partial(judge_back_kernel, count, model_width),
        [array((tok_rows + 32, latent_width), bf16)] * count,
        (short, gram, qk_gain, proj, inverse, keys, values, pair, real, *critic_rows, *grad_blocks),
        10 * full_rows * full_rows * head_width,
        scratch=(pltpu.VMEM((full_rows, head_width), f32),) * 3,
    )
    parts = scatter_near(parts, "seq", count)
    (payload,) = run(
        functools.partial(merge_kernel, count),
        [thin],
        (direct, real, fake, *parts),
        1000,
        fetched=(timesteps,),
    )
    ends = [(place, sections - 1 - place) for place in range(sections)]
    to_student = lax.ppermute(payload, "segment", ends)
    to_second = lax.ppermute(payload, "segment", swaps(sections, 1))
    to_third = lax.ppermute(payload, "segment", swaps(sections, 2))
    (sums,) = run(
        functools.partial(outer_kernel, count),
        [array((count + 1, latent_width, 128), bf16)],
        (
            to_student,
            target,
            noisy_student,
            pair,
            saved,
            student_inverse,
            critic_inverse,
            *critic_mixed,
        ),
        2 * tok_rows * latent_width * head_width * (count + 1),
        fetched=(timesteps,),
    )
    last = count // 2
    bit = 1
    while bit < last:
        moved = lax.ppermute(sums, "seq", swaps(count, bit))
        sums = (sums.astype(f32) + moved.astype(f32)).astype(bf16)
        bit *= 2
    sums_all = []
    for group in range(groups):
        for offset in (0, last):
            moves = [
                (place * groups + batch, (place ^ offset) * groups + (batch ^ group))
                for place in range(count)
                for batch in range(groups)
            ]
            sums_all.append(
                sums if offset == group == 0 else lax.ppermute(sums, ("seq", "dp"), moves)
            )
    grad_t, total_t = run(
        functools.partial(expand_kernel, count, groups, full_rows),
        [array((latent_width, tok_rows), f32), array((latent_width, model_width), f32)],
        (payload, to_student, to_second, to_third, w_embed, *heads_w, *late_mods[1:], *sums_all),
        4 * groups * latent_width * model_width * head_width * count,
        scratch=(
            pltpu.VMEM((groups * latent_width, model_width), f32),
            pltpu.VMEM((count + 1, groups * latent_width, 128), f32),
        ),
        fetched=(late_mod,),
    )
    return (jnp.transpose(grad_t)[None], jnp.transpose(total_t)[None])


def solution(mesh):
    placed = (
        P("dp", "seq", None),
        P("dp", "seq", None),
        P(),
        P("dp", None),
        P("segment", None, None),
        P("segment", None, None),
        P("segment", None, "seq"),
        P("segment", None, "seq", None, None),
        P("segment", "seq", None, None),
        P("segment", None, None),
        P("segment", None, None),
    )
    return jax.shard_map(
        step,
        mesh=mesh,
        in_specs=placed,
        out_specs=(P("dp", "seq", None), P("segment", None, None)),
        check_vma=False,
    )
```

```python
import functools
import math

import jax
import jax.numpy as jnp
from jax import lax
from jax.experimental import pallas as pl
from jax.experimental.pallas import tpu as pltpu
from jax.sharding import PartitionSpec as P


SHIFT = 7.0
EPS = 1e-06
ADV_WEIGHT = 3.0
TILE = 512
STREAMS = 6
SPARE = 8 << 20
VMEM = pl.BlockSpec(memory_space=pltpu.VMEM)
HBM = pl.BlockSpec(memory_space=pltpu.HBM)


def halves(values):
    top = values.astype(jnp.bfloat16)
    return (top, (values - top.astype(jnp.float32)).astype(jnp.bfloat16))


def swaps(count, offset):
    return [(place, place ^ offset) for place in range(count)]


def gather_near(value, axis, count):
    return [value] + [lax.ppermute(value, axis, swaps(count, offset)) for offset in range(1, count)]


def scatter_near(blocks, axis, count):
    return [blocks[0]] + [
        lax.ppermute(blocks[offset], axis, swaps(count, offset))
        for offset in range(1, count)
    ]


def spread_heads(own, count, groups):
    held = {0: [own]}
    bit = count // 2
    first = True
    while bit:
        for offset in sorted(held):
            if first and groups == 2:
                width = own.shape[1] // 2
                part = lax.dynamic_slice_in_dim(own, lax.axis_index("dp") * width, width, axis=1)
                near = lax.ppermute(part, "seq", swaps(count, bit))
                held[bit] = [near, lax.ppermute(near, "dp", swaps(groups, 1))]
            else:
                held[offset | bit] = [
                    lax.ppermute(piece, "seq", swaps(count, bit))
                    for piece in held[offset]
                ]
        first = False
        bit //= 2
    return [held[offset] for offset in range(count)]


def head_tile(pieces, first, size):
    if len(pieces) == 1:
        return pieces[0][:, first : first + size]
    width = pieces[0].shape[1]
    inside = slice(first % width, first % width + size)
    near = lax.axis_index("dp") == first // width
    return jnp.where(near, pieces[0][:, inside], pieces[1][:, inside])


def nested(refs, sizes):
    groups, first = [], 0
    for size in sizes:
        groups.append(refs[first : first + size])
        first += size
    return (groups, refs[first:])


def in_order(pieces, own_place):
    ordered = list(pieces)
    bit = 1
    while bit < len(ordered):
        flipped = (own_place & bit) != 0
        ordered = [
            jnp.where(flipped, ordered[place ^ bit], ordered[place])
            for place in range(len(ordered))
        ]
        bit *= 2
    return ordered


def dot32(left, right):
    return jnp.dot(left, right, preferred_element_type=jnp.float32)


def dot32_t(left, right):
    return lax.dot_general(
        left, right, (((1,), (1,)), ((), ())), preferred_element_type=jnp.float32
    )


def dot32_first(left, right):
    return lax.dot_general(
        left, right, (((0,), (0,)), ((), ())), preferred_element_type=jnp.float32
    )


def steps_of(times):
    times_ref = times.ready()
    place = lax.axis_index("dp")
    return (times_ref[place, 0], times_ref[place, 1])


def noise_level(step):
    fraction = jnp.full((1, 1), step, jnp.int32).astype(jnp.float32) / 1000.0
    return SHIFT * fraction / (1.0 + (SHIFT - 1.0) * fraction)


def slot_of(mod_ref, slot, width, first, size):
    return mod_ref[:, slot * width + first : slot * width + first + size]


def lane_sum(values):
    total = values[:, :128]
    for first in range(128, values.shape[1], 128):
        total = total + values[:, first : first + 128]
    return total


class Fetch:
    def __init__(self, source, target, arrival):
        self.copy = pltpu.make_async_copy(source, target, arrival)
        self.target = target
        self.waiting = True

    def start(self):
        self.copy.start()

    def ready(self):
        if self.waiting:
            self.copy.wait()
            self.waiting = False
        return self.target


def bytes_of(items):
    return sum(math.prod(item.shape) * jnp.dtype(item.dtype).itemsize for item in items)


def in_hbm(item):
    return pltpu.with_memory_space_constraint(item, pltpu.HBM)


def run(kernel, outputs, operands, flops, scratch=(), fetched=(), streamed=(), sent=()):
    inputs = len(operands)
    total = inputs + len(fetched) + len(streamed)
    results = len(outputs) + len(sent)

    def body(*refs):
        sources = refs[inputs:total]
        outs = refs[total : total + results]
        own = refs[total + results : total + results + len(scratch)]
        rest = refs[total + results + len(scratch) :]
        fetches = [
            Fetch(source, target, rest[-1].at[place])
            for place, (source, target) in enumerate(zip(sources, rest[:-1]))
        ]
        fetches += sources[len(fetched) :]
        kernel(fetches, *refs[:inputs], *outs, *own)

    places = [
        (pltpu.SMEM if item.dtype == jnp.int32 else pltpu.VMEM)(item.shape, item.dtype)
        for item in fetched
    ]
    held = bytes_of(
        [ref for ref in list(scratch) + places if ref.memory_space == pltpu.VMEM]
    )
    limit = min(60 << 20, SPARE + held + bytes_of(operands) + 2 * bytes_of(outputs))
    return pl.pallas_call(
        body,
        out_shape=list(outputs) + [pltpu.HBM(item.shape, item.dtype) for item in sent],
        in_specs=[VMEM] * inputs + [HBM] * (total - inputs),
        out_specs=[VMEM] * len(outputs) + [HBM] * len(sent),
        scratch_shapes=list(scratch)
        + places
        + [pltpu.SemaphoreType.DMA((max(1, len(fetched)),))],
        compiler_params=pltpu.CompilerParams(vmem_limit_bytes=limit),
        cost_estimate=pl.CostEstimate(
            flops=flops,
            bytes_accessed=bytes_of(list(operands) + list(fetched) + list(outputs)),
            transcendentals=0,
        ),
    )(*operands, *[in_hbm(item) for item in (*fetched, *streamed)])


def array(shape, dtype):
    return jax.ShapeDtypeStruct(shape, dtype)


def packed_rows(width):
    return -(-width // 2048) * 16


def condition_kernel(fetches, packed_out, noisy_out, held, mod_rows, arrivals):
    times, text, time_w, clean_t, noise, mod_w = fetches
    model_width = held.shape[0]
    rows = model_width // STREAMS
    for fetch in fetches[:-1]:
        fetch.start()
    copies = [
        pltpu.make_async_copy(
            mod_w.at[pl.ds(part * rows, rows)], held.at[pl.ds(part * rows, rows)], arrivals.at[part]
        )
        for part in range(STREAMS)
    ]
    for copy in copies:
        copy.start()
    student_step, critic_step = steps_of(times)
    step = jnp.where(lax.axis_index("segment") == 0, student_step, critic_step)
    text_ref = text.ready()
    half = text_ref.shape[1] // 2
    places = lax.broadcasted_iota(jnp.int32, (1, half), 1).astype(jnp.float32)
    frequency = jnp.exp(-math.log(10000.0) * places / half)
    angles = jnp.full((1, half), step, jnp.int32).astype(jnp.float32) * frequency
    features = jnp.concatenate([jnp.cos(angles), jnp.sin(angles)], axis=1) + text_ref[...]
    features = jnp.broadcast_to(features, (8, 2 * half)).astype(jnp.bfloat16)
    hidden = dot32(features, time_w.ready()[...])
    hidden = (hidden / (1.0 + jnp.exp(-hidden))).astype(jnp.bfloat16)
    sigma_student = noise_level(student_step)
    clean_ref, noise_ref = clean_t.ready(), noise.ready()
    noisy = (1.0 - sigma_student) * clean_ref[...].astype(jnp.float32).T + sigma_student * noise_ref[
        :, : clean_ref.shape[0]
    ].astype(jnp.float32)
    noisy = noisy.astype(jnp.bfloat16)
    noisy_out[...] = noisy
    top = noisy.shape[0] // 2
    packed_out[:top] = jnp.concatenate([noisy[:top], noisy[top:]], axis=1)
    mod_rows[...] = jnp.zeros_like(mod_rows)
    total = None
    for part in range(STREAMS):
        copies[part].wait()
        piece = dot32(
            hidden[:, part * rows : (part + 1) * rows], held[part * rows : (part + 1) * rows]
        )
        total = piece if total is None else total + piece
    width = total.shape[1]
    for row, first in enumerate(range(0, width, 128)):
        size = min(128, width - first)
        mod_rows[row : row + 1, :size] = total[:1, first : first + size]
    depth = mod_rows.shape[0]
    packed_out[top : top + depth], packed_out[top + depth :] = halves(mod_rows[...])


def rms_scale(values, gain_vec):
    inverse = lax.rsqrt(jnp.mean(values * values, axis=-1, keepdims=True) + EPS)
    unit_vec = values * inverse
    return (unit_vec * gain_vec, unit_vec, inverse)


def rms_back(gradient, unit_vec, inverse, gain_vec):
    scaled = gradient * gain_vec
    return inverse * (scaled - unit_vec * jnp.mean(scaled * unit_vec, axis=-1, keepdims=True))


def centred(embed_ref):
    values = embed_ref[0].astype(jnp.float32)
    return values - jnp.mean(values, axis=1, keepdims=True)


def front(rows, central, short, gains, head_outs, proj_ref, inverse_ref, key_ref, value_ref):
    latent_width = central.shape[0]
    model_width = central.shape[1]
    count = len(rows)
    head_width = gains.shape[2]
    scale = 1.0 / math.sqrt(head_width)
    size = rows[0].shape[0]
    short_top = None
    for place in range(count):
        block = rows[place][...]
        squares = None
        for first in range(0, model_width, TILE):
            piece = dot32(block, central[:, first : first + TILE])
            piece = lane_sum(piece * piece)
            squares = piece if squares is None else squares + piece
        inverse = lax.rsqrt(jnp.sum(squares, axis=1, keepdims=True) / model_width + EPS)
        if short_top is None:
            values = short()
            short_top, short_low = halves(values[:latent_width])
            short_shift = values[latent_width : latent_width + 1]
        projected = inverse * (dot32(block, short_top) + dot32(block, short_low)) + short_shift
        low = place * size
        proj_ref[low : low + size] = projected
        inverse_ref[low : low + size] = jnp.broadcast_to(inverse, (size, 128))
        keys, _, _ = rms_scale(projected[:, head_width : 2 * head_width], gains[0, 1:2])
        key_ref[low : low + size] = keys.astype(jnp.bfloat16)
        value_ref[low : low + size] = projected[:, 2 * head_width :].astype(jnp.bfloat16)
    for place in range(count):
        low = place * size
        queries, _, _ = rms_scale(proj_ref[low : low + size, :head_width], gains[0, :1])
        scores = dot32_t(queries.astype(jnp.bfloat16), key_ref[...]) * scale
        weights = jnp.exp(scores)
        soft_max = weights * (1.0 / jnp.sum(weights, axis=-1, keepdims=True))
        head_outs[place][...] = dot32(soft_max.astype(jnp.bfloat16), value_ref[...]).astype(
            jnp.bfloat16
        )


def student_front_kernel(count, width, fetches, embed_w, head_w, gains, *refs):
    packed = refs[:count]
    head_outs = refs[count : 2 * count]
    short_out, late_out, mod, short_ref, rows_ref, sends, *kept = refs[2 * count :]
    model_width = embed_w.shape[2]
    latent_width = embed_w.shape[1]
    size = rows_ref.shape[1]
    half = size // 2
    depth = packed_rows(width)
    parts = [
        piece[half : half + depth].astype(jnp.float32) + piece[half + depth :].astype(jnp.float32)
        for piece in packed
    ]
    for place, part in enumerate(in_order(parts, lax.axis_index("seq"))):
        for row, first in enumerate(range(0, width, 128)):
            lanes = min(128, width - first)
            low = place * width + first
            mod[:, low : low + lanes] = part[row : row + 1, :lanes]
    late = pltpu.make_async_copy(
        mod.at[:, pl.ds(2 * model_width, 3 * model_width)], late_out, sends.at[0]
    )
    late.start()
    for place in range(count):
        rows_ref[place, :half] = packed[place][:half, :latent_width]
        rows_ref[place, half:] = packed[place][:half, latent_width:]
    central = centred(embed_w)
    scale_in = slot_of(mod, 1, model_width, 0, model_width)
    shift_in = slot_of(mod, 0, model_width, 0, model_width)
    in_rows = jnp.concatenate(
        [central * (1.0 + scale_in), jnp.broadcast_to(shift_in, (16, model_width))], axis=0
    )
    in_top, in_low = halves(in_rows)
    in_both = jnp.concatenate([in_top, in_low], axis=0)
    both = jnp.concatenate([dot32(in_both, head_w[kind]) for kind in range(3)], axis=1)
    short = both[: in_rows.shape[0]] + both[in_rows.shape[0] :]
    short_ref[...] = short
    send = pltpu.make_async_copy(short_ref, short_out, sends.at[1])
    send.start()

    @pl.when(lax.axis_index("segment") == 0)
    def _():
        front(
            [rows_ref.at[place] for place in range(count)],
            central.astype(jnp.bfloat16),
            lambda: short,
            gains,
            head_outs,
            *kept,
        )

    late.wait()
    send.wait()


def critic_front_kernel(count, fetches, embed_w, gains, *refs):
    rows = refs[:count]
    head_outs = refs[count : 2 * count]
    kept = refs[2 * count :]
    (short,) = fetches

    @pl.when(lax.axis_index("segment") != 0)
    def _():
        short.start()
        front(
            rows,
            centred(embed_w).astype(jnp.bfloat16),
            lambda: short.ready()[...],
            gains,
            head_outs,
            *kept,
        )


def tail(late, latent, embed_w, final_t, mixed, heads_w, work):
    model_width = embed_w.shape[2]
    block = latent[...]
    sums = None
    for first in range(0, model_width, TILE):
        span = slice(first, first + TILE)
        attended = None
        for piece, rows_w in zip(mixed, heads_w):
            product = dot32(piece[...], head_tile(rows_w, first, TILE))
            attended = product if attended is None else attended + product
        mod = late.ready()
        residual = (
            dot32(block, embed_w[0, :, span]) + slot_of(mod, 0, model_width, first, TILE) * attended
        )
        work[:, span] = residual
        part = lane_sum(residual)
        sums = part if sums is None else sums + part
    row_mean = jnp.sum(sums, axis=1, keepdims=True) / model_width
    sums = None
    for first in range(0, model_width, TILE):
        span = slice(first, first + TILE)
        middle = work[:, span] - row_mean
        work[:, span] = middle
        part = lane_sum(middle * middle)
        sums = part if sums is None else sums + part
    inverse = lax.rsqrt(jnp.sum(sums, axis=1, keepdims=True) / model_width + EPS)
    result = None
    final_w = final_t.ready()
    for first in range(0, model_width, TILE):
        span = slice(first, first + TILE)
        normed = work[:, span] * inverse
        work[:, span] = normed
        final_in = (
            normed * (1.0 + slot_of(mod, 2, model_width, first, TILE))
            + slot_of(mod, 1, model_width, first, TILE)
        ).astype(jnp.bfloat16)
        product = dot32_t(final_in, final_w[:, span])
        result = product if result is None else result + product
    return (result, inverse)


def student_tail_kernel(count, sizes, fetches, latent, embed_w, *refs):
    mixed = refs[:count]
    heads_w, refs = nested(refs[count:], sizes)
    pair_ref, saved_out, inverse_out, work, inverse_ref, sends = refs
    late, final_t, noise, times = fetches
    latent_width = latent.shape[1]

    @pl.when(lax.axis_index("segment") == 0)
    def _():
        for fetch in fetches:
            fetch.start()
        copies = [
            pltpu.make_async_copy(mixed[place], saved_out.at[place], sends.at[place])
            for place in range(count)
        ]
        for copy in copies:
            copy.start()
        velocity, inverse = tail(late, latent, embed_w, final_t, mixed, heads_w, work)
        inverse_ref[...] = jnp.broadcast_to(inverse, inverse_ref.shape)
        copies.append(pltpu.make_async_copy(inverse_ref, inverse_out, sends.at[count]))
        copies[-1].start()
        student_step, critic_step = steps_of(times)
        sigma_student, sigma_critic = noise_level(student_step), noise_level(critic_step)
        sample = latent[...].astype(jnp.float32) - sigma_student * velocity
        second = noise.ready()[:, latent_width:].astype(jnp.float32)
        critic = (1.0 - sigma_critic) * sample + sigma_critic * second
        pair_ref[...] = jnp.concatenate([critic, sample], axis=1).astype(jnp.bfloat16)
        for copy in copies:
            copy.wait()


def pick_kernel(sections, fetches, own, *refs):
    moved = refs[: sections - 1]
    pair_ref, rows_ref = refs[sections - 1 :]
    section = lax.axis_index("segment")
    for place in range(sections):

        @pl.when(section == place)
        def _():
            chosen = own if place == 0 else moved[place - 1]
            pair_ref[...] = chosen[...]
            rows_ref[...] = chosen[:, : rows_ref.shape[1]]


def critic_tail_kernel(count, sizes, fetches, pair, embed_w, *refs):
    mixed = refs[:count]
    heads_w, refs = nested(refs[count:], sizes)
    grads = refs[:count]
    inverse_ref, term_ref, target_ref, direct_ref, latent, work, other = refs[count:]
    late, final_t, noise, times = fetches
    model_width = embed_w.shape[2]
    latent_width = latent.shape[1]
    section = lax.axis_index("segment")

    @pl.when(section != 0)
    def _():
        for fetch in fetches:
            fetch.start()
        both = pair[...].astype(jnp.float32)
        sample = both[:, latent_width:]
        latent[...] = pair[:, :latent_width]
        result, inverse = tail(late, latent, embed_w, final_t, mixed, heads_w, work)
        mod, final_w = late.ready(), final_t.ready()
        _, critic_step = steps_of(times)
        sigma_critic = noise_level(critic_step)
        inverse_ref[...] = jnp.broadcast_to(inverse, inverse_ref.shape)
        term_ref[...] = (sigma_critic * result).astype(jnp.bfloat16)
        second = noise.ready()[:, latent_width:].astype(jnp.float32)
        target_ref[...] = jnp.where(
            section == 2,
            2.0 * (result - (second - sample)),
            jnp.where(section == 3, 1.0 / (1.0 + jnp.exp(-result)), 0.0),
        )

        @pl.when(section == 1)
        def _():
            gaps = jnp.abs(sample - both[:, :latent_width] + sigma_critic * result)
            error = jnp.sum(jnp.sum(gaps, axis=1, keepdims=True), axis=0, keepdims=True)
            error = error / (gaps.shape[0] * latent_width)
            error_top, error_low = halves(jnp.broadcast_to(error, (16, grads[0].shape[1])))
            for place in range(count):
                grads[place][:16] = error_top
                grads[place][16:32] = error_low

        @pl.when(section == 3)
        def _():
            grad_logit = (-1.0 / (1.0 + jnp.exp(result))).astype(jnp.bfloat16)
            plain, along = None, None
            for first in range(0, model_width, TILE):
                span = slice(first, first + TILE)
                gradient = dot32(grad_logit, final_w[:, span]) * (
                    1.0 + slot_of(mod, 2, model_width, first, TILE)
                )
                other[:, span] = gradient
                part = lane_sum(gradient)
                plain = part if plain is None else plain + part
                part = lane_sum(gradient * work[:, span])
                along = part if along is None else along + part
            plain = jnp.sum(plain, axis=1, keepdims=True) / model_width
            along = jnp.sum(along, axis=1, keepdims=True) / model_width
            direct = None
            totals = [None] * count
            for first in range(0, model_width, TILE):
                span = slice(first, first + TILE)
                grad_residual = inverse * (other[:, span] - plain - work[:, span] * along)
                top, low = halves(grad_residual)
                product = dot32_t(top, embed_w[0, :, span]) + dot32_t(low, embed_w[0, :, span])
                direct = product if direct is None else direct + product
                grad_attended = (slot_of(mod, 0, model_width, first, TILE) * grad_residual).astype(
                    jnp.bfloat16
                )
                for place in range(count):
                    product = dot32_t(grad_attended, head_tile(heads_w[place], first, TILE))
                    held = totals[place]
                    totals[place] = product if held is None else held + product
            direct_ref[...] = direct
            for place in range(count):
                grads[place][...] = totals[place].astype(jnp.bfloat16)


def gram_kernel(fetches, embed_w, gram_ref):
    central_top, central_low = halves(centred(embed_w))
    gram = (
        dot32_t(central_top, central_top)
        + dot32_t(central_top, central_low)
        + dot32_t(central_low, central_top)
    )
    gram_ref[0], gram_ref[1] = halves(gram)


def judge_back_kernel(count, model_width, fetches, short_in, gram, gains, proj_ref, inverse_ref, key_ref, value_ref, term, *refs):
    rows = refs[:count]
    grads = refs[count : 2 * count]
    keep_ref, send_ref, real_ref, grad_key_ref, grad_value_ref, grad_query_ref = refs[2 * count :]
    section = lax.axis_index("segment")
    latent_width = rows[0].shape[1]
    head_width = gains.shape[2]
    scale = 1.0 / math.sqrt(head_width)
    size = rows[0].shape[0]

    @pl.when(section == 3)
    def _():
        for place in range(count):
            low = place * size
            span = slice(low, low + size)
            queries, _, _ = rms_scale(proj_ref[span, :head_width], gains[0, :1])
            query_b = queries.astype(jnp.bfloat16)
            weights = jnp.exp(dot32_t(query_b, key_ref[...]) * scale)
            soft_max = weights * (1.0 / jnp.sum(weights, axis=-1, keepdims=True))
            grad_out = grads[place][...]
            grad_soft = dot32_t(grad_out, value_ref[...])
            grad_value = dot32_first(soft_max.astype(jnp.bfloat16), grad_out)
            grad_scores = soft_max * (
                grad_soft - jnp.sum(soft_max * grad_soft, axis=-1, keepdims=True)
            )
            grad_scores_b = (grad_scores * scale).astype(jnp.bfloat16)
            grad_query_ref[span] = dot32(grad_scores_b, key_ref[...])
            grad_key = dot32_first(grad_scores_b, query_b)
            if place == 0:
                grad_value_ref[...] = grad_value
                grad_key_ref[...] = grad_key
            else:
                grad_value_ref[...] += grad_value
                grad_key_ref[...] += grad_key
        gram_top, gram_low = gram[0], gram[1]
        short_top, short_low = halves(short_in[:latent_width])
        for place in range(count):
            low = place * size
            span = slice(low, low + size)
            projected = proj_ref[span]
            _, q_unit, q_inverse = rms_scale(projected[:, :head_width], gains[0, :1])
            _, k_unit, k_inverse = rms_scale(
                projected[:, head_width : 2 * head_width], gains[0, 1:2]
            )
            grad_q = rms_back(grad_query_ref[span], q_unit, q_inverse, gains[0, :1])
            grad_k = rms_back(grad_key_ref[span], k_unit, k_inverse, gains[0, 1:2])
            grad_proj = jnp.concatenate([grad_q, grad_k, grad_value_ref[span]], axis=1).astype(
                jnp.bfloat16
            )
            through = dot32_t(grad_proj, short_top) + dot32_t(grad_proj, short_low)
            block = rows[place][...]
            along = jnp.sum(through * block.astype(jnp.float32), axis=1, keepdims=True) / model_width
            spanned = dot32(block, gram_top) + dot32(block, gram_low)
            inverse = inverse_ref[span, :1]
            target_ref = send_ref if place % 2 else keep_ref
            target_ref[place // 2] = (
                inverse * (through - spanned * (inverse * inverse * along))
            ).astype(jnp.bfloat16)

    @pl.when(section == 1)
    def _():
        error = None
        for grad in grads:
            part = grad[:16, :latent_width].astype(jnp.float32) + grad[
                16:32, :latent_width
            ].astype(jnp.float32)
            error = part if error is None else error + part
        real_ref[:size] = term[...]
        real_ref[size : size + 16], real_ref[size + 16 :] = halves(error / count + EPS)


def merge_kernel(fetches, direct, keep, moved, *outs):
    @pl.when(lax.axis_index("segment") == 3)
    def _():
        for place, out in enumerate(outs):
            total = keep[place].astype(jnp.float32) + moved[place].astype(jnp.float32)
            if place == 0:
                total = total + direct[...]
            out[...] = total.astype(jnp.bfloat16)


def outer_kernel(
    count,
    fetches,
    real,
    fake,
    target_in,
    student_rows,
    pair,
    student_mixed,
    student_inverse,
    critic_inverse,
    *refs,
):
    critic_mixed = refs[:count]
    arrived = refs[count : count + count // 2]
    sums_ref, sample_ref = refs[count + count // 2 :]
    section = lax.axis_index("segment")
    place = lax.axis_index("seq")
    latent_width = student_rows.shape[1]
    rows = student_rows.shape[0]

    def collect(target, inverse, latent, mixed):
        target = target.astype(jnp.bfloat16)
        weighted = inverse[:, :latent_width] * target.astype(jnp.float32)
        top, low = halves(weighted)
        for offset in range(count):
            piece = mixed[offset][...]
            sums_ref[place ^ offset] = (dot32_first(top, piece) + dot32_first(low, piece)).astype(
                jnp.bfloat16
            )
        near = dot32_first(top, latent) + dot32_first(low, latent)
        ones = jnp.ones((target.shape[0], sums_ref.shape[2] - latent_width), jnp.bfloat16)
        sums_ref[count] = jnp.concatenate([near, dot32_first(target, ones)], axis=1).astype(
            jnp.bfloat16
        )

    @pl.when(section == 0)
    def _():
        (times,) = fetches
        times.start()
        student_step, critic_step = steps_of(times)
        adverse = arrived[0][...].astype(jnp.float32)
        for part in arrived[1:]:
            adverse = adverse + part[...].astype(jnp.float32)
        adverse = (1.0 - noise_level(critic_step)) * adverse
        spread = (real[rows : rows + 1] .astype(jnp.float32) + real[rows + 16 : rows + 17].astype(jnp.float32))[
            :, :1
        ]
        gap = real[:rows].astype(jnp.float32) - fake[...].astype(jnp.float32)
        sample_grad = gap / spread + ADV_WEIGHT * adverse
        sample_ref[...] = sample_grad.astype(jnp.bfloat16)
        target = -noise_level(student_step) * sample_grad
        mixed = [student_mixed.at[offset] for offset in range(count)]
        collect(target, student_inverse, student_rows[...], mixed)

    @pl.when(section == 1)
    def _():
        sums_ref[...] = jnp.zeros_like(sums_ref)

    @pl.when(section >= 2)
    def _():
        collect(target_in[...], critic_inverse, pair[:, :latent_width], critic_mixed)


def expand_kernel(
    count, groups, sizes, full_rows, fetches, own, to_first, to_second, to_third, embed_w, *refs
):
    heads_w, refs = nested(refs, sizes)
    other_mods = refs[: groups - 1]
    sums = refs[groups - 1 : 3 * groups - 1]
    grad_ref, total_ref, work, joined = refs[3 * groups - 1 :]
    section = lax.axis_index("segment")
    place = lax.axis_index("seq")
    latent_width = embed_w.shape[1]
    model_width = embed_w.shape[2]
    picked = own[...].astype(jnp.float32)
    for source, value in ((1, to_first), (2, to_second), (3, to_third)):
        picked = jnp.where(section == source, value[...].astype(jnp.float32), picked)
    grad_ref[...] = picked.T

    @pl.when(section == 1)
    def _():
        total_ref[...] = jnp.zeros_like(total_ref)

    @pl.when(section != 1)
    def _():
        (late,) = fetches
        late.start()
        for group in range(groups):
            low = group * latent_width
            joined[:, low : low + latent_width] = sums[2 * group][...].astype(jnp.float32) + sums[
                2 * group + 1
            ][...].astype(jnp.float32)
        near_top = joined[count].astype(jnp.bfloat16)
        heads = [joined[place ^ offset].astype(jnp.bfloat16) for offset in range(count)]
        averages = None
        for first in range(0, model_width, TILE):
            span = slice(first, first + TILE)
            spread = None
            for head, rows_w in zip(heads, heads_w):
                product = dot32(head, head_tile(rows_w, first, TILE))
                spread = product if spread is None else spread + product
            near = dot32(near_top[:, :latent_width], embed_w[0, :, span])
            mods = [late.ready(), *other_mods]
            gates = jnp.concatenate(
                [
                    jnp.broadcast_to(
                        slot_of(mod, 0, model_width, first, TILE), (latent_width, TILE)
                    )
                    for mod in mods
                ],
                axis=0,
            )
            value = near + gates * spread
            work[:, span] = value
            part = lane_sum(value)
            averages = part if averages is None else averages + part
        averages = jnp.sum(averages, axis=1, keepdims=True) / model_width
        counts = joined[count][:, latent_width : latent_width + 1]
        for first in range(0, model_width, TILE):
            span = slice(first, first + TILE)
            value = work[:, span] - averages
            total = None
            for group in range(groups):
                mine = slice(group * latent_width, (group + 1) * latent_width)
                product = value[mine] * (
                    1.0 + slot_of(mods[group], 2, model_width, first, TILE)
                ) + counts[mine] * slot_of(mods[group], 1, model_width, first, TILE)
                total = product if total is None else total + product
            total_ref[:, span] = total / full_rows


def step(
    clean, noise, timesteps, text_vec, w_embed, w_time, w_mod, w_qkv, w_out, qk_gain, w_final
):
    sections = lax.axis_size("segment")
    tok_rows = clean.shape[1]
    latent_width = clean.shape[2]
    model_width = w_embed.shape[2]
    mod_width = w_mod.shape[2]
    count = lax.axis_size("seq")
    full_rows = tok_rows * count
    head_width = w_qkv.shape[4]
    kind_w = jnp.transpose(w_qkv[0, :, 0], (1, 0, 2))
    final_w = jnp.transpose(w_final[0])
    groups = lax.axis_size("dp")
    heads_w = spread_heads(w_out[0, 0], count, groups)
    sizes = [len(pieces) for pieces in heads_w]
    heads_w = sum(heads_w, [])
    bf16, f32 = jnp.bfloat16, jnp.float32

    depth = packed_rows(mod_width)
    packed, noisy_student = run(
        condition_kernel,
        [
            array((tok_rows // 2 + 2 * depth, 2 * latent_width), bf16),
            array((tok_rows, latent_width), bf16),
        ],
        (),
        2 * model_width * mod_width,
        scratch=(
            pltpu.VMEM((model_width, mod_width), bf16),
            pltpu.VMEM((depth, 128), f32),
            pltpu.SemaphoreType.DMA((STREAMS,)),
        ),
        fetched=(timesteps, text_vec, w_time[0], jnp.transpose(clean[0]), noise[0]),
        streamed=(w_mod[0],),
    )
    packed_all = gather_near(packed, "seq", count)

    head_blocks = [array((tok_rows, head_width), bf16)] * count
    stored = [
        ((full_rows, 3 * head_width), f32),
        ((full_rows, 128), f32),
        ((full_rows, head_width), bf16),
        ((full_rows, head_width), bf16),
    ]
    short_shape = ((latent_width + 16, 3 * head_width), f32)
    *head_outs, short, late_mod = run(
        functools.partial(student_front_kernel, count, mod_width),
        head_blocks,
        (w_embed, kind_w, qk_gain, *packed_all),
        4 * latent_width * model_width * 3 * head_width,
        scratch=[
            pltpu.VMEM((1, 5 * model_width), f32),
            pltpu.VMEM(*short_shape),
            pltpu.VMEM((count, tok_rows, latent_width), bf16),
            pltpu.SemaphoreType.DMA((2,)),
        ]
        + [pltpu.VMEM(shape, kind) for shape, kind in stored],
        sent=[array(*short_shape), array((1, 3 * model_width), f32)],
    )
    student_mixed = scatter_near(head_outs, "seq", count)
    late_mods = gather_near(late_mod, "dp", groups)
    work = pltpu.VMEM((tok_rows, model_width), f32)
    inverse_shape = array((tok_rows, 128), f32)
    pair, saved, student_inverse = run(
        functools.partial(student_tail_kernel, count, sizes),
        [array((tok_rows, 2 * latent_width), bf16)],
        (noisy_student, w_embed, *student_mixed, *heads_w),
        2 * tok_rows * model_width * head_width * count,
        scratch=(
            work,
            pltpu.VMEM((tok_rows, 128), f32),
            pltpu.SemaphoreType.DMA((count + 1,)),
        ),
        fetched=(late_mod, final_w, noise[0], timesteps),
        sent=[array((count, tok_rows, head_width), bf16), inverse_shape],
    )
    moved = [lax.ppermute(pair, "segment", [(0, place)]) for place in range(1, sections)]
    pair, own_rows = run(
        functools.partial(pick_kernel, sections),
        [
            array((tok_rows, 2 * latent_width), bf16),
            array((tok_rows, latent_width), bf16),
        ],
        (pair, *moved),
        1000,
    )
    critic_rows = gather_near(own_rows, "seq", count)
    *head_outs, proj, inverse, keys, values = run(
        functools.partial(critic_front_kernel, count),
        head_blocks + [array(shape, kind) for shape, kind in stored],
        (w_embed, qk_gain, *critic_rows),
        4 * latent_width * model_width * full_rows,
        fetched=(short,),
    )
    critic_mixed = scatter_near(head_outs, "seq", count)
    small = array((tok_rows, latent_width), f32)
    thin = array((tok_rows, latent_width), bf16)
    *grad_heads, critic_inverse, term_rows, target, direct = run(
        functools.partial(critic_tail_kernel, count, sizes),
        head_blocks + [inverse_shape, thin, small, small],
        (pair, w_embed, *critic_mixed, *heads_w),
        4 * tok_rows * model_width * head_width * count,
        scratch=(pltpu.VMEM((tok_rows, latent_width), bf16), work, work),
        fetched=(late_mod, final_w, noise[0], timesteps),
    )
    grad_blocks = scatter_near(grad_heads, "seq", count)
    fake = lax.ppermute(term_rows, "segment", swaps(sections, 2))
    half = count // 2
    rows_shape = array((half, tok_rows, latent_width), bf16)
    (gram,) = run(
        gram_kernel,
        [array((2, latent_width, latent_width), bf16)],
        (w_embed,),
        6 * latent_width * latent_width * model_width,
    )
    keep, away, real = run(
        functools.partial(judge_back_kernel, count, model_width),
        [rows_shape, rows_shape, array((tok_rows + 32, latent_width), bf16)],
        (short, gram, qk_gain, proj, inverse, keys, values, term_rows, *critic_rows, *grad_blocks),
        10 * full_rows * full_rows * head_width,
        scratch=(pltpu.VMEM((full_rows, head_width), f32),) * 3,
    )
    moved = lax.ppermute(away, "seq", swaps(count, 1))
    real = lax.ppermute(real, "segment", swaps(sections, 1))
    parts = run(merge_kernel, [thin] * half, (direct, keep, moved), 1000)
    to_student = [
        lax.ppermute(
            part,
            ("segment", "seq"),
            [
                (place * count + row, (place + 1) % sections * count + (row ^ (2 * index)))
                for place in range(sections)
                for row in range(count)
            ],
        )
        for index, part in enumerate(parts)
    ]
    sums, sample_grad = run(
        functools.partial(outer_kernel, count),
        [array((count + 1, latent_width, 128), bf16), thin],
        (
            real,
            fake,
            target,
            noisy_student,
            pair,
            saved,
            student_inverse,
            critic_inverse,
            *critic_mixed,
            *to_student,
        ),
        2 * tok_rows * latent_width * head_width * (count + 1),
        fetched=(timesteps,),
    )
    ends = [(place, sections - 1 - place) for place in range(sections)]
    to_third = lax.ppermute(sample_grad, "segment", ends)
    to_second = lax.ppermute(sample_grad, "segment", swaps(sections, 2))
    to_first = lax.ppermute(sample_grad, "segment", swaps(sections, 1))
    last = count // 2
    bit = 1
    while bit < last:
        moved = lax.ppermute(sums, "seq", swaps(count, bit))
        sums = (sums.astype(f32) + moved.astype(f32)).astype(bf16)
        bit *= 2
    sums_all = []
    for group in range(groups):
        for offset in (0, last):
            moves = [
                (place * groups + batch, (place ^ offset) * groups + (batch ^ group))
                for place in range(count)
                for batch in range(groups)
            ]
            sums_all.append(
                sums if offset == group == 0 else lax.ppermute(sums, ("seq", "dp"), moves)
            )
    grad_t, total_t = run(
        functools.partial(expand_kernel, count, groups, sizes, full_rows),
        [array((latent_width, tok_rows), f32), array((latent_width, model_width), f32)],
        (sample_grad, to_first, to_second, to_third, w_embed, *heads_w, *late_mods[1:], *sums_all),
        4 * groups * latent_width * model_width * head_width * count,
        scratch=(
            pltpu.VMEM((groups * latent_width, model_width), f32),
            pltpu.VMEM((count + 1, groups * latent_width, 128), f32),
        ),
        fetched=(late_mod,),
    )
    return (jnp.transpose(grad_t)[None], jnp.transpose(total_t)[None])


def solution(mesh):
    placed = (
        P("dp", "seq", None),
        P("dp", "seq", None),
        P(),
        P("dp", None),
        P("segment", None, None),
        P("segment", None, None),
        P("segment", None, "seq"),
        P("segment", None, "seq", None, None),
        P("segment", "seq", None, None),
        P("segment", None, None),
        P("segment", None, None),
    )
    return jax.shard_map(
        step,
        mesh=mesh,
        in_specs=placed,
        out_specs=(P("dp", "seq", None), P("segment", None, None)),
        check_vma=False,
    )
```

```python
import functools
import math

import jax
import jax.numpy as jnp
from jax import lax
from jax.experimental import pallas as pl
from jax.experimental.pallas import tpu as pltpu
from jax.sharding import PartitionSpec as P


SHIFT = 7.0
EPS = 1e-06
ADV_WEIGHT = 3.0
TILE = 512
STREAMS = 12
SPARE = 8 << 20
VMEM = pl.BlockSpec(memory_space=pltpu.VMEM)
HBM = pl.BlockSpec(memory_space=pltpu.HBM)


def halves(values):
    top = values.astype(jnp.bfloat16)
    return (top, (values - top.astype(jnp.float32)).astype(jnp.bfloat16))


def swaps(count, offset):
    return [(place, place ^ offset) for place in range(count)]


def gather_near(value, axis, count):
    return [value] + [lax.ppermute(value, axis, swaps(count, offset)) for offset in range(1, count)]


def scatter_near(blocks, axis, count):
    return [blocks[0]] + [
        lax.ppermute(blocks[offset], axis, swaps(count, offset))
        for offset in range(1, count)
    ]


def spread_heads(own, count, groups, stage):
    held = {0: [own]}
    bit = count // 2
    first = True
    while bit:
        for offset in sorted(held):
            if first and groups == 2:
                width = own.shape[1] // 3
                shift = lax.axis_index("dp") * width
                part = lax.dynamic_slice_in_dim(own, shift, 2 * width, axis=1)
                near = lax.ppermute(part, "seq", swaps(count, bit))
                held[bit] = [near, lax.ppermute(stage(near), "dp", swaps(groups, 1))]
            else:
                held[offset | bit] = [
                    lax.ppermute(piece, "seq", swaps(count, bit))
                    for piece in held[offset]
                ]
        first = False
        bit //= 2
    return [held[offset] for offset in range(count)]


def head_tile(pieces, first, size):
    if len(pieces) == 1:
        return pieces[0][:, first : first + size]
    near, far = pieces
    width = far.shape[1]
    low = slice(first % width, first % width + size)
    high = slice(width + first % width, width + first % width + size)
    choices = (
        (near[:, low], far[:, low]),
        (near[:, high], near[:, low]),
        (far[:, low], near[:, high]),
    )[first // width]
    return jnp.where(lax.axis_index("dp") == 0, *choices)


def nested(refs, sizes):
    groups, first = [], 0
    for size in sizes:
        groups.append(refs[first : first + size])
        first += size
    return (groups, refs[first:])


def in_order(pieces, own_place):
    ordered = list(pieces)
    bit = 1
    while bit < len(ordered):
        flipped = (own_place & bit) != 0
        ordered = [
            jnp.where(flipped, ordered[place ^ bit], ordered[place])
            for place in range(len(ordered))
        ]
        bit *= 2
    return ordered


def dot32(left, right):
    return jnp.dot(left, right, preferred_element_type=jnp.float32)


def dot32_t(left, right):
    return lax.dot_general(
        left, right, (((1,), (1,)), ((), ())), preferred_element_type=jnp.float32
    )


def dot32_first(left, right):
    return lax.dot_general(
        left, right, (((0,), (0,)), ((), ())), preferred_element_type=jnp.float32
    )


def steps_of(times):
    times_ref = times.ready()
    place = lax.axis_index("dp")
    return (times_ref[place, 0], times_ref[place, 1])


def noise_level(step):
    fraction = jnp.full((1, 1), step, jnp.int32).astype(jnp.float32) / 1000.0
    return SHIFT * fraction / (1.0 + (SHIFT - 1.0) * fraction)


def slot_of(mod_ref, slot, width, first, size):
    return mod_ref[:, slot * width + first : slot * width + first + size]


def lane_sum(values):
    total = values[:, :128]
    for first in range(128, values.shape[1], 128):
        total = total + values[:, first : first + 128]
    return total


class Fetch:
    def __init__(self, source, target, arrival):
        self.copy = pltpu.make_async_copy(source, target, arrival)
        self.target = target
        self.waiting = True

    def start(self):
        self.copy.start()

    def ready(self):
        if self.waiting:
            self.copy.wait()
            self.waiting = False
        return self.target


def bytes_of(items):
    return sum(math.prod(item.shape) * jnp.dtype(item.dtype).itemsize for item in items)


def in_hbm(item):
    return pltpu.with_memory_space_constraint(item, pltpu.HBM)


def run(kernel, outputs, operands, flops, scratch=(), fetched=(), streamed=(), sent=()):
    inputs = len(operands)
    total = inputs + len(fetched) + len(streamed)
    results = len(outputs) + len(sent)

    def body(*refs):
        sources = refs[inputs:total]
        outs = refs[total : total + results]
        own = refs[total + results : total + results + len(scratch)]
        rest = refs[total + results + len(scratch) :]
        fetches = [
            Fetch(source, target, rest[-1].at[place])
            for place, (source, target) in enumerate(zip(sources, rest[:-1]))
        ]
        fetches += sources[len(fetched) :]
        kernel(fetches, *refs[:inputs], *outs, *own)

    places = [
        (pltpu.SMEM if item.dtype == jnp.int32 else pltpu.VMEM)(item.shape, item.dtype)
        for item in fetched
    ]
    held = bytes_of(
        [ref for ref in list(scratch) + places if ref.memory_space == pltpu.VMEM]
    )
    limit = min(60 << 20, SPARE + held + bytes_of(operands) + 2 * bytes_of(outputs))
    return pl.pallas_call(
        body,
        out_shape=list(outputs) + [pltpu.HBM(item.shape, item.dtype) for item in sent],
        in_specs=[VMEM] * inputs + [HBM] * (total - inputs),
        out_specs=[VMEM] * len(outputs) + [HBM] * len(sent),
        scratch_shapes=list(scratch)
        + places
        + [pltpu.SemaphoreType.DMA((max(1, len(fetched)),))],
        compiler_params=pltpu.CompilerParams(vmem_limit_bytes=limit),
        cost_estimate=pl.CostEstimate(
            flops=flops,
            bytes_accessed=bytes_of(list(operands) + list(fetched) + list(outputs)),
            transcendentals=0,
        ),
    )(*operands, *[in_hbm(item) for item in (*fetched, *streamed)])


def array(shape, dtype):
    return jax.ShapeDtypeStruct(shape, dtype)


def packed_rows(width):
    return -(-width // 2048) * 16


def condition_kernel(fetches, packed_out, noisy_out, held, mod_rows, arrivals):
    times, text, time_w, clean_t, noise, mod_w = fetches
    model_width = held.shape[0]
    rows = model_width // STREAMS
    for fetch in fetches[:-1]:
        fetch.start()
    copies = [
        pltpu.make_async_copy(
            mod_w.at[pl.ds(part * rows, rows)], held.at[pl.ds(part * rows, rows)], arrivals.at[part]
        )
        for part in range(STREAMS)
    ]
    for copy in copies:
        copy.start()
    student_step, critic_step = steps_of(times)
    step = jnp.where(lax.axis_index("segment") == 0, student_step, critic_step)
    text_ref = text.ready()
    half = text_ref.shape[1] // 2
    places = lax.broadcasted_iota(jnp.int32, (1, half), 1).astype(jnp.float32)
    frequency = jnp.exp(-math.log(10000.0) * places / half)
    angles = jnp.full((1, half), step, jnp.int32).astype(jnp.float32) * frequency
    features = jnp.concatenate([jnp.cos(angles), jnp.sin(angles)], axis=1) + text_ref[...]
    features = jnp.broadcast_to(features, (8, 2 * half)).astype(jnp.bfloat16)
    hidden = dot32(features, time_w.ready()[...])
    hidden = (hidden / (1.0 + jnp.exp(-hidden))).astype(jnp.bfloat16)
    sigma_student = noise_level(student_step)
    clean_ref, noise_ref = clean_t.ready(), noise.ready()
    noisy = (1.0 - sigma_student) * clean_ref[...].astype(jnp.float32).T + sigma_student * noise_ref[
        :, : clean_ref.shape[0]
    ].astype(jnp.float32)
    noisy = noisy.astype(jnp.bfloat16)
    noisy_out[...] = noisy
    top = noisy.shape[0] // 2
    packed_out[:top] = jnp.concatenate([noisy[:top], noisy[top:]], axis=1)
    mod_rows[...] = jnp.zeros_like(mod_rows)
    total = None
    for part in range(STREAMS):
        copies[part].wait()
        piece = dot32(
            hidden[:, part * rows : (part + 1) * rows], held[part * rows : (part + 1) * rows]
        )
        total = piece if total is None else total + piece
    width = total.shape[1]
    for row, first in enumerate(range(0, width, 128)):
        size = min(128, width - first)
        mod_rows[row : row + 1, :size] = total[:1, first : first + size]
    depth = mod_rows.shape[0]
    packed_out[top : top + depth], packed_out[top + depth :] = halves(mod_rows[...])


def rms_scale(values, gain_vec):
    inverse = lax.rsqrt(jnp.mean(values * values, axis=-1, keepdims=True) + EPS)
    unit_vec = values * inverse
    return (unit_vec * gain_vec, unit_vec, inverse)


def rms_back(gradient, unit_vec, inverse, gain_vec):
    scaled = gradient * gain_vec
    return inverse * (scaled - unit_vec * jnp.mean(scaled * unit_vec, axis=-1, keepdims=True))


def centred(embed_ref):
    values = embed_ref[0].astype(jnp.float32)
    return values - jnp.mean(values, axis=1, keepdims=True)


def front(rows, central, short, gains, head_outs, proj_ref, inverse_ref, key_ref, value_ref):
    latent_width = central.shape[0]
    model_width = central.shape[1]
    count = len(rows)
    head_width = gains.shape[2]
    scale = 1.0 / math.sqrt(head_width)
    size = rows[0].shape[0]
    short_top = None
    for place in range(count):
        block = rows[place][...]
        squares = None
        for first in range(0, model_width, TILE):
            piece = dot32(block, central[:, first : first + TILE])
            piece = lane_sum(piece * piece)
            squares = piece if squares is None else squares + piece
        inverse = lax.rsqrt(jnp.sum(squares, axis=1, keepdims=True) / model_width + EPS)
        if short_top is None:
            values = short()
            short_top, short_low = halves(values[:latent_width])
            short_shift = values[latent_width : latent_width + 1]
        projected = inverse * (dot32(block, short_top) + dot32(block, short_low)) + short_shift
        low = place * size
        proj_ref[low : low + size] = projected
        inverse_ref[low : low + size] = jnp.broadcast_to(inverse, (size, 128))
        keys, _, _ = rms_scale(projected[:, head_width : 2 * head_width], gains[0, 1:2])
        key_ref[low : low + size] = keys.astype(jnp.bfloat16)
        value_ref[low : low + size] = projected[:, 2 * head_width :].astype(jnp.bfloat16)
    for place in range(count):
        low = place * size
        queries, _, _ = rms_scale(proj_ref[low : low + size, :head_width], gains[0, :1])
        scores = dot32_t(queries.astype(jnp.bfloat16), key_ref[...]) * scale
        weights = jnp.exp(scores)
        soft_max = weights * (1.0 / jnp.sum(weights, axis=-1, keepdims=True))
        head_outs[place][...] = dot32(soft_max.astype(jnp.bfloat16), value_ref[...]).astype(
            jnp.bfloat16
        )


def stage_kernel(fetches, near, kind_out, part_out, arrival):
    copy = pltpu.make_async_copy(fetches[0], kind_out, arrival.at[0])
    copy.start()
    width = part_out.shape[1]
    for place in range(2):

        @pl.when(lax.axis_index("dp") == place)
        def _():
            part_out[...] = near[:, place * width : (place + 1) * width]

    copy.wait()


def student_front_kernel(count, width, fetches, embed_w, head_w, gains, *refs):
    packed = refs[:count]
    head_outs = refs[count : 2 * count]
    short_out, late_out, mod, rows_ref, sends, *kept = refs[2 * count :]
    model_width = embed_w.shape[2]
    latent_width = embed_w.shape[1]
    size = rows_ref.shape[1]
    half = size // 2
    depth = packed_rows(width)
    parts = [
        piece[half : half + depth].astype(jnp.float32) + piece[half + depth :].astype(jnp.float32)
        for piece in packed
    ]
    for place, part in enumerate(in_order(parts, lax.axis_index("seq"))):
        for row, first in enumerate(range(0, width, 128)):
            lanes = min(128, width - first)
            low = place * width + first
            mod[:, low : low + lanes] = part[row : row + 1, :lanes]
    late = pltpu.make_async_copy(
        mod.at[:, pl.ds(2 * model_width, 3 * model_width)], late_out, sends.at[0]
    )
    late.start()
    for place in range(count):
        rows_ref[place, :half] = packed[place][:half, :latent_width]
        rows_ref[place, half:] = packed[place][:half, latent_width:]
    central = centred(embed_w)
    scale_in = slot_of(mod, 1, model_width, 0, model_width)
    shift_in = slot_of(mod, 0, model_width, 0, model_width)
    in_rows = jnp.concatenate(
        [central * (1.0 + scale_in), jnp.broadcast_to(shift_in, (16, model_width))], axis=0
    )
    in_top, in_low = halves(in_rows)
    in_both = jnp.concatenate([in_top, in_low], axis=0)
    both = jnp.concatenate([dot32(in_both, head_w[kind]) for kind in range(3)], axis=1)
    short = both[: in_rows.shape[0]] + both[in_rows.shape[0] :]
    short_out[...] = short

    @pl.when(lax.axis_index("segment") == 0)
    def _():
        front(
            [rows_ref.at[place] for place in range(count)],
            central.astype(jnp.bfloat16),
            lambda: short,
            gains,
            head_outs,
            *kept,
        )

    late.wait()


def critic_front_kernel(count, fetches, short, embed_w, gains, *refs):
    rows = refs[:count]
    head_outs = refs[count : 2 * count]
    kept = refs[2 * count :]

    @pl.when(lax.axis_index("segment") != 0)
    def _():
        front(
            rows,
            centred(embed_w).astype(jnp.bfloat16),
            lambda: short[...],
            gains,
            head_outs,
            *kept,
        )


def tail(late, latent, embed_w, final_t, mixed, heads_w, work):
    model_width = embed_w.shape[2]
    block = latent[...]
    sums = None
    for first in range(0, model_width, TILE):
        span = slice(first, first + TILE)
        attended = None
        for piece, rows_w in zip(mixed, heads_w):
            product = dot32(piece[...], head_tile(rows_w, first, TILE))
            attended = product if attended is None else attended + product
        mod = late.ready()
        residual = (
            dot32(block, embed_w[0, :, span]) + slot_of(mod, 0, model_width, first, TILE) * attended
        )
        work[:, span] = residual
        part = lane_sum(residual)
        sums = part if sums is None else sums + part
    row_mean = jnp.sum(sums, axis=1, keepdims=True) / model_width
    sums = None
    for first in range(0, model_width, TILE):
        span = slice(first, first + TILE)
        middle = work[:, span] - row_mean
        work[:, span] = middle
        part = lane_sum(middle * middle)
        sums = part if sums is None else sums + part
    inverse = lax.rsqrt(jnp.sum(sums, axis=1, keepdims=True) / model_width + EPS)
    result = None
    final_w = final_t.ready()
    for first in range(0, model_width, TILE):
        span = slice(first, first + TILE)
        normed = work[:, span] * inverse
        work[:, span] = normed
        final_in = (
            normed * (1.0 + slot_of(mod, 2, model_width, first, TILE))
            + slot_of(mod, 1, model_width, first, TILE)
        ).astype(jnp.bfloat16)
        product = dot32_t(final_in, final_w[:, span])
        result = product if result is None else result + product
    return (result, inverse)


def student_tail_kernel(count, sizes, fetches, latent, embed_w, *refs):
    mixed = refs[:count]
    heads_w, refs = nested(refs[count:], sizes)
    pair_ref, saved_out, inverse_out, work, inverse_ref, sends = refs
    late, final_t, noise, times = fetches
    latent_width = latent.shape[1]

    @pl.when(lax.axis_index("segment") == 0)
    def _():
        for fetch in fetches:
            fetch.start()
        copies = [
            pltpu.make_async_copy(mixed[place], saved_out.at[place], sends.at[place])
            for place in range(count)
        ]
        for copy in copies:
            copy.start()
        velocity, inverse = tail(late, latent, embed_w, final_t, mixed, heads_w, work)
        inverse_ref[...] = jnp.broadcast_to(inverse, inverse_ref.shape)
        copies.append(pltpu.make_async_copy(inverse_ref, inverse_out, sends.at[count]))
        copies[-1].start()
        student_step, critic_step = steps_of(times)
        sigma_student, sigma_critic = noise_level(student_step), noise_level(critic_step)
        sample = latent[...].astype(jnp.float32) - sigma_student * velocity
        second = noise.ready()[:, latent_width:].astype(jnp.float32)
        critic = (1.0 - sigma_critic) * sample + sigma_critic * second
        pair_ref[...] = jnp.concatenate([critic, sample], axis=1).astype(jnp.bfloat16)
        for copy in copies:
            copy.wait()


def pick_kernel(sections, fetches, own, *refs):
    moved = refs[: sections - 1]
    pair_ref, rows_ref = refs[sections - 1 :]
    section = lax.axis_index("segment")
    for place in range(sections):

        @pl.when(section == place)
        def _():
            chosen = own if place == 0 else moved[place - 1]
            pair_ref[...] = chosen[...]
            rows_ref[...] = chosen[:, : rows_ref.shape[1]]


def critic_tail_kernel(count, sizes, fetches, pair, embed_w, *refs):
    mixed = refs[:count]
    heads_w, refs = nested(refs[count:], sizes)
    grads = refs[:count]
    inverse_ref, term_ref, target_ref, direct_ref, latent, work, other = refs[count:]
    late, final_t, noise, times = fetches
    model_width = embed_w.shape[2]
    latent_width = latent.shape[1]
    section = lax.axis_index("segment")

    @pl.when(section != 0)
    def _():
        for fetch in fetches:
            fetch.start()
        both = pair[...].astype(jnp.float32)
        sample = both[:, latent_width:]
        latent[...] = pair[:, :latent_width]
        result, inverse = tail(late, latent, embed_w, final_t, mixed, heads_w, work)
        mod, final_w = late.ready(), final_t.ready()
        _, critic_step = steps_of(times)
        sigma_critic = noise_level(critic_step)
        inverse_ref[...] = jnp.broadcast_to(inverse, inverse_ref.shape)
        term_ref[...] = (sigma_critic * result).astype(jnp.bfloat16)
        second = noise.ready()[:, latent_width:].astype(jnp.float32)
        target_ref[...] = jnp.where(
            section == 2,
            2.0 * (result - (second - sample)),
            jnp.where(section == 3, 1.0 / (1.0 + jnp.exp(-result)), 0.0),
        )

        @pl.when(section == 1)
        def _():
            gaps = jnp.abs(sample - both[:, :latent_width] + sigma_critic * result)
            error = jnp.sum(jnp.sum(gaps, axis=1, keepdims=True), axis=0, keepdims=True)
            error = error / (gaps.shape[0] * latent_width)
            error_top, error_low = halves(jnp.broadcast_to(error, (16, grads[0].shape[1])))
            for place in range(count):
                grads[place][:16] = error_top
                grads[place][16:32] = error_low

        @pl.when(section == 3)
        def _():
            grad_logit = (-1.0 / (1.0 + jnp.exp(result))).astype(jnp.bfloat16)
            plain, along = None, None
            for first in range(0, model_width, TILE):
                span = slice(first, first + TILE)
                gradient = dot32(grad_logit, final_w[:, span]) * (
                    1.0 + slot_of(mod, 2, model_width, first, TILE)
                )
                other[:, span] = gradient
                part = lane_sum(gradient)
                plain = part if plain is None else plain + part
                part = lane_sum(gradient * work[:, span])
                along = part if along is None else along + part
            plain = jnp.sum(plain, axis=1, keepdims=True) / model_width
            along = jnp.sum(along, axis=1, keepdims=True) / model_width
            direct = None
            totals = [None] * count
            for first in range(0, model_width, TILE):
                span = slice(first, first + TILE)
                grad_residual = inverse * (other[:, span] - plain - work[:, span] * along)
                top, low = halves(grad_residual)
                product = dot32_t(top, embed_w[0, :, span]) + dot32_t(low, embed_w[0, :, span])
                direct = product if direct is None else direct + product
                grad_attended = (slot_of(mod, 0, model_width, first, TILE) * grad_residual).astype(
                    jnp.bfloat16
                )
                for place in range(count):
                    product = dot32_t(grad_attended, head_tile(heads_w[place], first, TILE))
                    held = totals[place]
                    totals[place] = product if held is None else held + product
            direct_ref[...] = direct
            for place in range(count):
                grads[place][...] = totals[place].astype(jnp.bfloat16)


def gram_kernel(fetches, embed_w, gram_ref):
    central_top, central_low = halves(centred(embed_w))
    gram = (
        dot32_t(central_top, central_top)
        + dot32_t(central_top, central_low)
        + dot32_t(central_low, central_top)
    )
    gram_ref[0], gram_ref[1] = halves(gram)


def judge_back_kernel(count, model_width, fetches, short_in, gram, gains, proj_ref, inverse_ref, key_ref, value_ref, term, *refs):
    rows = refs[:count]
    grads = refs[count : 2 * count]
    keep_ref, send_ref, real_ref, grad_key_ref, grad_value_ref, grad_query_ref = refs[2 * count :]
    section = lax.axis_index("segment")
    latent_width = rows[0].shape[1]
    head_width = gains.shape[2]
    scale = 1.0 / math.sqrt(head_width)
    size = rows[0].shape[0]

    @pl.when(section == 3)
    def _():
        for place in range(count):
            low = place * size
            span = slice(low, low + size)
            queries, _, _ = rms_scale(proj_ref[span, :head_width], gains[0, :1])
            query_b = queries.astype(jnp.bfloat16)
            weights = jnp.exp(dot32_t(query_b, key_ref[...]) * scale)
            soft_max = weights * (1.0 / jnp.sum(weights, axis=-1, keepdims=True))
            grad_out = grads[place][...]
            grad_soft = dot32_t(grad_out, value_ref[...])
            grad_value = dot32_first(soft_max.astype(jnp.bfloat16), grad_out)
            grad_scores = soft_max * (
                grad_soft - jnp.sum(soft_max * grad_soft, axis=-1, keepdims=True)
            )
            grad_scores_b = (grad_scores * scale).astype(jnp.bfloat16)
            grad_query_ref[span] = dot32(grad_scores_b, key_ref[...])
            grad_key = dot32_first(grad_scores_b, query_b)
            if place == 0:
                grad_value_ref[...] = grad_value
                grad_key_ref[...] = grad_key
            else:
                grad_value_ref[...] += grad_value
                grad_key_ref[...] += grad_key
        gram_top, gram_low = gram[0], gram[1]
        short_top, short_low = halves(short_in[:latent_width])
        for place in range(count):
            low = place * size
            span = slice(low, low + size)
            projected = proj_ref[span]
            _, q_unit, q_inverse = rms_scale(projected[:, :head_width], gains[0, :1])
            _, k_unit, k_inverse = rms_scale(
                projected[:, head_width : 2 * head_width], gains[0, 1:2]
            )
            grad_q = rms_back(grad_query_ref[span], q_unit, q_inverse, gains[0, :1])
            grad_k = rms_back(grad_key_ref[span], k_unit, k_inverse, gains[0, 1:2])
            grad_proj = jnp.concatenate([grad_q, grad_k, grad_value_ref[span]], axis=1).astype(
                jnp.bfloat16
            )
            through = dot32_t(grad_proj, short_top) + dot32_t(grad_proj, short_low)
            block = rows[place][...]
            along = jnp.sum(through * block.astype(jnp.float32), axis=1, keepdims=True) / model_width
            spanned = dot32(block, gram_top) + dot32(block, gram_low)
            inverse = inverse_ref[span, :1]
            target_ref = send_ref if place % 2 else keep_ref
            target_ref[place // 2] = (
                inverse * (through - spanned * (inverse * inverse * along))
            ).astype(jnp.bfloat16)

    @pl.when(section == 1)
    def _():
        error = None
        for grad in grads:
            part = grad[:16, :latent_width].astype(jnp.float32) + grad[
                16:32, :latent_width
            ].astype(jnp.float32)
            error = part if error is None else error + part
        real_ref[:size] = term[...]
        real_ref[size : size + 16], real_ref[size + 16 :] = halves(error / count + EPS)


def merge_kernel(fetches, direct, keep, moved, *outs):
    @pl.when(lax.axis_index("segment") == 3)
    def _():
        for place, out in enumerate(outs):
            total = keep[place].astype(jnp.float32) + moved[place].astype(jnp.float32)
            if place == 0:
                total = total + direct[...]
            out[...] = total.astype(jnp.bfloat16)


def outer_kernel(
    count,
    fetches,
    real,
    fake,
    target_in,
    student_rows,
    pair,
    student_mixed,
    student_inverse,
    critic_inverse,
    *refs,
):
    critic_mixed = refs[:count]
    arrived = refs[count : count + count // 2]
    sums_ref, sample_ref = refs[count + count // 2 :]
    section = lax.axis_index("segment")
    place = lax.axis_index("seq")
    latent_width = student_rows.shape[1]
    rows = student_rows.shape[0]

    def collect(target, inverse, latent, mixed):
        target = target.astype(jnp.bfloat16)
        weighted = inverse[:, :latent_width] * target.astype(jnp.float32)
        top, low = halves(weighted)
        for offset in range(count):
            piece = mixed[offset][...]
            sums_ref[place ^ offset] = (dot32_first(top, piece) + dot32_first(low, piece)).astype(
                jnp.bfloat16
            )
        near = dot32_first(top, latent) + dot32_first(low, latent)
        ones = jnp.ones((target.shape[0], sums_ref.shape[2] - latent_width), jnp.bfloat16)
        sums_ref[count] = jnp.concatenate([near, dot32_first(target, ones)], axis=1).astype(
            jnp.bfloat16
        )

    @pl.when(section == 0)
    def _():
        (times,) = fetches
        times.start()
        student_step, critic_step = steps_of(times)
        adverse = arrived[0][...].astype(jnp.float32)
        for part in arrived[1:]:
            adverse = adverse + part[...].astype(jnp.float32)
        adverse = (1.0 - noise_level(critic_step)) * adverse
        spread = (real[rows : rows + 1] .astype(jnp.float32) + real[rows + 16 : rows + 17].astype(jnp.float32))[
            :, :1
        ]
        gap = real[:rows].astype(jnp.float32) - fake[...].astype(jnp.float32)
        sample_grad = gap / spread + ADV_WEIGHT * adverse
        sample_ref[...] = sample_grad.astype(jnp.bfloat16)
        target = -noise_level(student_step) * sample_grad
        mixed = [student_mixed.at[offset] for offset in range(count)]
        collect(target, student_inverse, student_rows[...], mixed)

    @pl.when(section == 1)
    def _():
        sums_ref[...] = jnp.zeros_like(sums_ref)

    @pl.when(section >= 2)
    def _():
        collect(target_in[...], critic_inverse, pair[:, :latent_width], critic_mixed)


def emit_kernel(fetches, own, to_first, to_second, to_third, grad_ref):
    section = lax.axis_index("segment")
    for place, value in enumerate((own, to_first, to_second, to_third)):

        @pl.when(section == place)
        def _():
            grad_ref[...] = value[...].astype(jnp.float32).T


def expand_kernel(count, groups, sizes, full_rows, fetches, embed_w, *refs):
    heads_w, refs = nested(refs, sizes)
    other_mods = refs[: groups - 1]
    sums = refs[groups - 1 : 3 * groups - 1]
    total_ref, work, joined = refs[3 * groups - 1 :]
    section = lax.axis_index("segment")
    place = lax.axis_index("seq")
    latent_width = embed_w.shape[1]
    model_width = embed_w.shape[2]

    @pl.when(section == 1)
    def _():
        total_ref[...] = jnp.zeros_like(total_ref)

    @pl.when(section != 1)
    def _():
        (late,) = fetches
        late.start()
        for group in range(groups):
            low = group * latent_width
            joined[:, low : low + latent_width] = sums[2 * group][...].astype(jnp.float32) + sums[
                2 * group + 1
            ][...].astype(jnp.float32)
        near_top = joined[count].astype(jnp.bfloat16)
        heads = [joined[place ^ offset].astype(jnp.bfloat16) for offset in range(count)]
        averages = None
        for first in range(0, model_width, TILE):
            span = slice(first, first + TILE)
            spread = None
            for head, rows_w in zip(heads, heads_w):
                product = dot32(head, head_tile(rows_w, first, TILE))
                spread = product if spread is None else spread + product
            near = dot32(near_top[:, :latent_width], embed_w[0, :, span])
            mods = [late.ready(), *other_mods]
            gates = jnp.concatenate(
                [
                    jnp.broadcast_to(
                        slot_of(mod, 0, model_width, first, TILE), (latent_width, TILE)
                    )
                    for mod in mods
                ],
                axis=0,
            )
            value = near + gates * spread
            work[:, span] = value
            part = lane_sum(value)
            averages = part if averages is None else averages + part
        averages = jnp.sum(averages, axis=1, keepdims=True) / model_width
        counts = joined[count][:, latent_width : latent_width + 1]
        for first in range(0, model_width, TILE):
            span = slice(first, first + TILE)
            value = work[:, span] - averages
            total = None
            for group in range(groups):
                mine = slice(group * latent_width, (group + 1) * latent_width)
                product = value[mine] * (
                    1.0 + slot_of(mods[group], 2, model_width, first, TILE)
                ) + counts[mine] * slot_of(mods[group], 1, model_width, first, TILE)
                total = product if total is None else total + product
            total_ref[:, span] = total / full_rows


def step(
    clean, noise, timesteps, text_vec, w_embed, w_time, w_mod, w_qkv, w_out, qk_gain, w_final
):
    sections = lax.axis_size("segment")
    tok_rows = clean.shape[1]
    latent_width = clean.shape[2]
    model_width = w_embed.shape[2]
    mod_width = w_mod.shape[2]
    count = lax.axis_size("seq")
    full_rows = tok_rows * count
    head_width = w_qkv.shape[4]
    bf16, f32 = jnp.bfloat16, jnp.float32
    kind_w = jnp.transpose(w_qkv[0, :, 0], (1, 0, 2))
    final_w = jnp.transpose(w_final[0])
    groups = lax.axis_size("dp")
    staged = []

    def stage(near):
        rows, width = near.shape
        kinds, part = run(
            stage_kernel,
            [pltpu.VMEM(kind_w.shape, bf16), array((rows, width // 2), bf16)],
            (near,),
            1000,
            scratch=(pltpu.SemaphoreType.DMA((1,)),),
            streamed=(kind_w,),
        )
        staged.append(kinds)
        return part

    heads_w = spread_heads(w_out[0, 0], count, groups, stage)
    if staged:
        kind_w = pltpu.with_memory_space_constraint(staged[0], pltpu.VMEM)
    sizes = [len(pieces) for pieces in heads_w]
    heads_w = sum(heads_w, [])

    depth = packed_rows(mod_width)
    packed, noisy_student = run(
        condition_kernel,
        [
            array((tok_rows // 2 + 2 * depth, 2 * latent_width), bf16),
            array((tok_rows, latent_width), bf16),
        ],
        (),
        2 * model_width * mod_width,
        scratch=(
            pltpu.VMEM((model_width, mod_width), bf16),
            pltpu.VMEM((depth, 128), f32),
            pltpu.SemaphoreType.DMA((STREAMS,)),
        ),
        fetched=(timesteps, text_vec, w_time[0], jnp.transpose(clean[0]), noise[0]),
        streamed=(w_mod[0],),
    )
    packed_all = gather_near(packed, "seq", count)

    head_blocks = [array((tok_rows, head_width), bf16)] * count
    stored = [
        ((full_rows, 3 * head_width), f32),
        ((full_rows, 128), f32),
        ((full_rows, head_width), bf16),
        ((full_rows, head_width), bf16),
    ]
    short_shape = ((latent_width + 16, 3 * head_width), f32)
    *head_outs, short, late_mod = run(
        functools.partial(student_front_kernel, count, mod_width),
        head_blocks + [pltpu.VMEM(*short_shape)],
        (w_embed, kind_w, qk_gain, *packed_all),
        4 * latent_width * model_width * 3 * head_width,
        scratch=[
            pltpu.VMEM((1, 5 * model_width), f32),
            pltpu.VMEM((count, tok_rows, latent_width), bf16),
            pltpu.SemaphoreType.DMA((1,)),
        ]
        + [pltpu.VMEM(shape, kind) for shape, kind in stored],
        sent=[array((1, 3 * model_width), f32)],
    )
    student_mixed = scatter_near(head_outs, "seq", count)
    late_mods = gather_near(late_mod, "dp", groups)
    work = pltpu.VMEM((tok_rows, model_width), f32)
    inverse_shape = array((tok_rows, 128), f32)
    pair, saved, student_inverse = run(
        functools.partial(student_tail_kernel, count, sizes),
        [array((tok_rows, 2 * latent_width), bf16)],
        (noisy_student, w_embed, *student_mixed, *heads_w),
        2 * tok_rows * model_width * head_width * count,
        scratch=(
            work,
            pltpu.VMEM((tok_rows, 128), f32),
            pltpu.SemaphoreType.DMA((count + 1,)),
        ),
        fetched=(late_mod, final_w, noise[0], timesteps),
        sent=[array((count, tok_rows, head_width), bf16), inverse_shape],
    )
    moved = [lax.ppermute(pair, "segment", [(0, place)]) for place in range(1, sections)]
    pair, own_rows = run(
        functools.partial(pick_kernel, sections),
        [
            array((tok_rows, 2 * latent_width), bf16),
            array((tok_rows, latent_width), bf16),
        ],
        (pair, *moved),
        1000,
    )
    critic_rows = gather_near(own_rows, "seq", count)
    *head_outs, proj, inverse, keys, values = run(
        functools.partial(critic_front_kernel, count),
        head_blocks + [array(shape, kind) for shape, kind in stored],
        (
            pltpu.with_memory_space_constraint(short, pltpu.VMEM),
            w_embed,
            qk_gain,
            *critic_rows,
        ),
        4 * latent_width * model_width * full_rows,
    )
    critic_mixed = scatter_near(head_outs, "seq", count)
    small = array((tok_rows, latent_width), f32)
    thin = array((tok_rows, latent_width), bf16)
    *grad_heads, critic_inverse, term_rows, target, direct = run(
        functools.partial(critic_tail_kernel, count, sizes),
        head_blocks + [inverse_shape, thin, small, small],
        (pair, w_embed, *critic_mixed, *heads_w),
        4 * tok_rows * model_width * head_width * count,
        scratch=(pltpu.VMEM((tok_rows, latent_width), bf16), work, work),
        fetched=(late_mod, final_w, noise[0], timesteps),
    )
    grad_blocks = scatter_near(grad_heads, "seq", count)
    fake = lax.ppermute(term_rows, "segment", swaps(sections, 2))
    half = count // 2
    rows_shape = array((half, tok_rows, latent_width), bf16)
    (gram,) = run(
        gram_kernel,
        [array((2, latent_width, latent_width), bf16)],
        (w_embed,),
        6 * latent_width * latent_width * model_width,
    )
    keep, away, real = run(
        functools.partial(judge_back_kernel, count, model_width),
        [rows_shape, rows_shape, array((tok_rows + 32, latent_width), bf16)],
        (short, gram, qk_gain, proj, inverse, keys, values, term_rows, *critic_rows, *grad_blocks),
        10 * full_rows * full_rows * head_width,
        scratch=(pltpu.VMEM((full_rows, head_width), f32),) * 3,
    )
    moved = lax.ppermute(away, "seq", swaps(count, 1))
    real = lax.ppermute(real, "segment", swaps(sections, 1))
    parts = run(merge_kernel, [thin] * half, (direct, keep, moved), 1000)
    to_student = [
        lax.ppermute(
            part,
            ("segment", "seq"),
            [
                (place * count + row, (place + 1) % sections * count + (row ^ (2 * index)))
                for place in range(sections)
                for row in range(count)
            ],
        )
        for index, part in enumerate(parts)
    ]
    sums, sample_grad = run(
        functools.partial(outer_kernel, count),
        [array((count + 1, latent_width, 128), bf16), thin],
        (
            real,
            fake,
            target,
            noisy_student,
            pair,
            saved,
            student_inverse,
            critic_inverse,
            *critic_mixed,
            *to_student,
        ),
        2 * tok_rows * latent_width * head_width * (count + 1),
        fetched=(timesteps,),
    )
    ends = [(place, sections - 1 - place) for place in range(sections)]
    to_third = lax.ppermute(sample_grad, "segment", ends)
    to_second = lax.ppermute(sample_grad, "segment", swaps(sections, 2))
    to_first = lax.ppermute(sample_grad, "segment", swaps(sections, 1))
    last = count // 2
    bit = 1
    while bit < last:
        moved = lax.ppermute(sums, "seq", swaps(count, bit))
        sums = (sums.astype(f32) + moved.astype(f32)).astype(bf16)
        bit *= 2
    sums_all = []
    for group in range(groups):
        for offset in (0, last):
            moves = [
                (place * groups + batch, (place ^ offset) * groups + (batch ^ group))
                for place in range(count)
                for batch in range(groups)
            ]
            sums_all.append(
                sums if offset == group == 0 else lax.ppermute(sums, ("seq", "dp"), moves)
            )
    (total_t,) = run(
        functools.partial(expand_kernel, count, groups, sizes, full_rows),
        [array((latent_width, model_width), f32)],
        (
            w_embed,
            *heads_w,
            *late_mods[1:],
            *sums_all,
        ),
        4 * groups * latent_width * model_width * head_width * count,
        scratch=(
            pltpu.VMEM((groups * latent_width, model_width), f32),
            pltpu.VMEM((count + 1, groups * latent_width, 128), f32),
        ),
        fetched=(late_mod,),
    )
    (grad_t,) = run(
        emit_kernel,
        [array((latent_width, tok_rows), f32)],
        (sample_grad, to_first, to_second, to_third),
        1000,
    )
    return (jnp.transpose(grad_t)[None], jnp.transpose(total_t)[None])


def solution(mesh):
    placed = (
        P("dp", "seq", None),
        P("dp", "seq", None),
        P(),
        P("dp", None),
        P("segment", None, None),
        P("segment", None, None),
        P("segment", None, "seq"),
        P("segment", None, "seq", None, None),
        P("segment", "seq", None, None),
        P("segment", None, None),
        P("segment", None, None),
    )
    return jax.shard_map(
        step,
        mesh=mesh,
        in_specs=placed,
        out_specs=(P("dp", "seq", None), P("segment", None, None)),
        check_vma=False,
    )
```

```python
import functools
import math

import jax
import jax.numpy as jnp
from jax import lax
from jax.experimental import pallas as pl
from jax.experimental.pallas import tpu as pltpu
from jax.sharding import PartitionSpec as P


SHIFT = 7.0
EPS = 1e-06
ADV_WEIGHT = 3.0
TILE = 512
STREAMS = 6
SPARE = 8 << 20
VMEM = pl.BlockSpec(memory_space=pltpu.VMEM)
HBM = pl.BlockSpec(memory_space=pltpu.HBM)


def halves(values):
    top = values.astype(jnp.bfloat16)
    return (top, (values - top.astype(jnp.float32)).astype(jnp.bfloat16))


def swaps(count, offset):
    return [(place, place ^ offset) for place in range(count)]


def gather_near(value, axis, count):
    return [value] + [lax.ppermute(value, axis, swaps(count, offset)) for offset in range(1, count)]


def scatter_near(blocks, axis, count):
    return [blocks[0]] + [
        lax.ppermute(blocks[offset], axis, swaps(count, offset))
        for offset in range(1, count)
    ]


def spread_heads(own, count, groups, stage):
    held = {0: [own]}
    bit = count // 2
    first = True
    while bit:
        for offset in sorted(held):
            if first and groups == 2:
                width = own.shape[1] // 3
                shift = lax.axis_index("dp") * width
                part = lax.dynamic_slice_in_dim(own, shift, 2 * width, axis=1)
                near = lax.ppermute(part, "seq", swaps(count, bit))
                held[bit] = [near, lax.ppermute(stage(near), "dp", swaps(groups, 1))]
            else:
                held[offset | bit] = [
                    lax.ppermute(piece, "seq", swaps(count, bit))
                    for piece in held[offset]
                ]
        first = False
        bit //= 2
    return [held[offset] for offset in range(count)]


def head_tile(pieces, first, size):
    if len(pieces) == 1:
        return pieces[0][:, first : first + size]
    near, far = pieces
    width = far.shape[1]
    low = slice(first % width, first % width + size)
    high = slice(width + first % width, width + first % width + size)
    choices = (
        (near[:, low], far[:, low]),
        (near[:, high], near[:, low]),
        (far[:, low], near[:, high]),
    )[first // width]
    return jnp.where(lax.axis_index("dp") == 0, *choices)


def nested(refs, sizes):
    groups, first = [], 0
    for size in sizes:
        groups.append(refs[first : first + size])
        first += size
    return (groups, refs[first:])


def in_order(pieces, own_place):
    ordered = list(pieces)
    bit = 1
    while bit < len(ordered):
        flipped = (own_place & bit) != 0
        ordered = [
            jnp.where(flipped, ordered[place ^ bit], ordered[place])
            for place in range(len(ordered))
        ]
        bit *= 2
    return ordered


def dot32(left, right):
    return jnp.dot(left, right, preferred_element_type=jnp.float32)


def dot32_t(left, right):
    return lax.dot_general(
        left, right, (((1,), (1,)), ((), ())), preferred_element_type=jnp.float32
    )


def dot32_first(left, right):
    return lax.dot_general(
        left, right, (((0,), (0,)), ((), ())), preferred_element_type=jnp.float32
    )


def steps_of(times):
    times_ref = times.ready()
    place = lax.axis_index("dp")
    return (times_ref[place, 0], times_ref[place, 1])


def noise_level(step):
    fraction = jnp.full((1, 1), step, jnp.int32).astype(jnp.float32) / 1000.0
    return SHIFT * fraction / (1.0 + (SHIFT - 1.0) * fraction)


def slot_of(mod_ref, slot, width, first, size):
    return mod_ref[:, slot * width + first : slot * width + first + size]


def lane_sum(values):
    total = values[:, :128]
    for first in range(128, values.shape[1], 128):
        total = total + values[:, first : first + 128]
    return total


class Fetch:
    def __init__(self, source, target, arrival):
        self.copy = pltpu.make_async_copy(source, target, arrival)
        self.target = target
        self.waiting = True

    def start(self):
        self.copy.start()

    def ready(self):
        if self.waiting:
            self.copy.wait()
            self.waiting = False
        return self.target


def bytes_of(items):
    return sum(math.prod(item.shape) * jnp.dtype(item.dtype).itemsize for item in items)


def in_hbm(item):
    return pltpu.with_memory_space_constraint(item, pltpu.HBM)


def run(kernel, outputs, operands, flops, scratch=(), fetched=(), streamed=(), sent=()):
    inputs = len(operands)
    total = inputs + len(fetched) + len(streamed)
    results = len(outputs) + len(sent)

    def body(*refs):
        sources = refs[inputs:total]
        outs = refs[total : total + results]
        own = refs[total + results : total + results + len(scratch)]
        rest = refs[total + results + len(scratch) :]
        fetches = [
            Fetch(source, target, rest[-1].at[place])
            for place, (source, target) in enumerate(zip(sources, rest[:-1]))
        ]
        fetches += sources[len(fetched) :]
        kernel(fetches, *refs[:inputs], *outs, *own)

    places = [
        (pltpu.SMEM if item.dtype == jnp.int32 else pltpu.VMEM)(item.shape, item.dtype)
        for item in fetched
    ]
    held = bytes_of(
        [ref for ref in list(scratch) + places if ref.memory_space == pltpu.VMEM]
    )
    limit = min(60 << 20, SPARE + held + bytes_of(operands) + 2 * bytes_of(outputs))
    return pl.pallas_call(
        body,
        out_shape=list(outputs) + [pltpu.HBM(item.shape, item.dtype) for item in sent],
        in_specs=[VMEM] * inputs + [HBM] * (total - inputs),
        out_specs=[VMEM] * len(outputs) + [HBM] * len(sent),
        scratch_shapes=list(scratch)
        + places
        + [pltpu.SemaphoreType.DMA((max(1, len(fetched)),))],
        compiler_params=pltpu.CompilerParams(vmem_limit_bytes=limit),
        cost_estimate=pl.CostEstimate(
            flops=flops,
            bytes_accessed=bytes_of(list(operands) + list(fetched) + list(outputs)),
            transcendentals=0,
        ),
    )(*operands, *[in_hbm(item) for item in (*fetched, *streamed)])


def array(shape, dtype):
    return jax.ShapeDtypeStruct(shape, dtype)


def packed_rows(width):
    return -(-width // 2048) * 16


def condition_kernel(fetches, packed_out, noisy_out, kind_out, held, mod_rows, arrivals):
    times, text, time_w, clean_t, noise, mod_w, kind_w = fetches
    model_width = held.shape[0]
    rows = model_width // STREAMS
    for fetch in fetches[:-2]:
        fetch.start()
    copies = [
        pltpu.make_async_copy(
            mod_w.at[pl.ds(part * rows, rows)], held.at[pl.ds(part * rows, rows)], arrivals.at[part]
        )
        for part in range(STREAMS)
    ]
    copies.append(pltpu.make_async_copy(kind_w, kind_out, arrivals.at[STREAMS]))
    for copy in copies:
        copy.start()
    student_step, critic_step = steps_of(times)
    step = jnp.where(lax.axis_index("segment") == 0, student_step, critic_step)
    text_ref = text.ready()
    half = text_ref.shape[1] // 2
    places = lax.broadcasted_iota(jnp.int32, (1, half), 1).astype(jnp.float32)
    frequency = jnp.exp(-math.log(10000.0) * places / half)
    angles = jnp.full((1, half), step, jnp.int32).astype(jnp.float32) * frequency
    features = jnp.concatenate([jnp.cos(angles), jnp.sin(angles)], axis=1) + text_ref[...]
    features = jnp.broadcast_to(features, (8, 2 * half)).astype(jnp.bfloat16)
    hidden = dot32(features, time_w.ready()[...])
    hidden = (hidden / (1.0 + jnp.exp(-hidden))).astype(jnp.bfloat16)
    mod_rows[...] = jnp.zeros_like(mod_rows)
    total = None
    for part in range(STREAMS):
        copies[part].wait()
        piece = dot32(
            hidden[:, part * rows : (part + 1) * rows], held[part * rows : (part + 1) * rows]
        )
        total = piece if total is None else total + piece
    sigma_student = noise_level(student_step)
    clean_ref, noise_ref = clean_t.ready(), noise.ready()
    noisy = (1.0 - sigma_student) * clean_ref[...].astype(jnp.float32).T + sigma_student * noise_ref[
        :, : clean_ref.shape[0]
    ].astype(jnp.float32)
    noisy = noisy.astype(jnp.bfloat16)
    noisy_out[...] = noisy
    top = noisy.shape[0] // 2
    packed_out[:top] = jnp.concatenate([noisy[:top], noisy[top:]], axis=1)
    width = total.shape[1]
    for row, first in enumerate(range(0, width, 128)):
        size = min(128, width - first)
        mod_rows[row : row + 1, :size] = total[:1, first : first + size]
    depth = mod_rows.shape[0]
    packed_out[top : top + depth], packed_out[top + depth :] = halves(mod_rows[...])
    copies[STREAMS].wait()


def rms_scale(values, gain_vec):
    inverse = lax.rsqrt(jnp.mean(values * values, axis=-1, keepdims=True) + EPS)
    unit_vec = values * inverse
    return (unit_vec * gain_vec, unit_vec, inverse)


def rms_back(gradient, unit_vec, inverse, gain_vec):
    scaled = gradient * gain_vec
    return inverse * (scaled - unit_vec * jnp.mean(scaled * unit_vec, axis=-1, keepdims=True))


def centred(embed_ref):
    values = embed_ref[0].astype(jnp.float32)
    return values - jnp.mean(values, axis=1, keepdims=True)


def front(rows, central, short, gains, head_outs, proj_ref, inverse_ref, key_ref, value_ref):
    latent_width = central.shape[0]
    model_width = central.shape[1]
    count = len(rows)
    head_width = gains.shape[2]
    scale = 1.0 / math.sqrt(head_width)
    size = rows[0].shape[0]
    short_top = None
    for place in range(count):
        block = rows[place][...]
        squares = None
        for first in range(0, model_width, TILE):
            piece = dot32(block, central[:, first : first + TILE])
            piece = lane_sum(piece * piece)
            squares = piece if squares is None else squares + piece
        inverse = lax.rsqrt(jnp.sum(squares, axis=1, keepdims=True) / model_width + EPS)
        if short_top is None:
            values = short()
            short_top, short_low = halves(values[:latent_width])
            short_shift = values[latent_width : latent_width + 1]
        projected = inverse * (dot32(block, short_top) + dot32(block, short_low)) + short_shift
        low = place * size
        proj_ref[low : low + size] = projected
        inverse_ref[low : low + size] = jnp.broadcast_to(inverse, (size, 128))
        keys, _, _ = rms_scale(projected[:, head_width : 2 * head_width], gains[0, 1:2])
        key_ref[low : low + size] = keys.astype(jnp.bfloat16)
        value_ref[low : low + size] = projected[:, 2 * head_width :].astype(jnp.bfloat16)
    for place in range(count):
        low = place * size
        queries, _, _ = rms_scale(proj_ref[low : low + size, :head_width], gains[0, :1])
        scores = dot32_t(queries.astype(jnp.bfloat16), key_ref[...]) * scale
        weights = jnp.exp(scores)
        soft_max = weights * (1.0 / jnp.sum(weights, axis=-1, keepdims=True))
        head_outs[place][...] = dot32(soft_max.astype(jnp.bfloat16), value_ref[...]).astype(
            jnp.bfloat16
        )


def stage_kernel(fetches, near, part_out):
    width = part_out.shape[1]
    for place in range(2):

        @pl.when(lax.axis_index("dp") == place)
        def _():
            part_out[...] = near[:, place * width : (place + 1) * width]


def student_front_kernel(count, width, fetches, embed_w, head_w, gains, *refs):
    packed = refs[:count]
    head_outs = refs[count : 2 * count]
    short_out, late_out, mod, rows_ref, sends, *kept = refs[2 * count :]
    model_width = embed_w.shape[2]
    latent_width = embed_w.shape[1]
    size = rows_ref.shape[1]
    half = size // 2
    depth = packed_rows(width)
    parts = [
        piece[half : half + depth].astype(jnp.float32) + piece[half + depth :].astype(jnp.float32)
        for piece in packed
    ]
    for place, part in enumerate(in_order(parts, lax.axis_index("seq"))):
        for row, first in enumerate(range(0, width, 128)):
            lanes = min(128, width - first)
            low = place * width + first
            mod[:, low : low + lanes] = part[row : row + 1, :lanes]
    late = pltpu.make_async_copy(
        mod.at[:, pl.ds(2 * model_width, 3 * model_width)], late_out, sends.at[0]
    )
    late.start()
    for place in range(count):
        rows_ref[place, :half] = packed[place][:half, :latent_width]
        rows_ref[place, half:] = packed[place][:half, latent_width:]
    central = centred(embed_w)
    scale_in = slot_of(mod, 1, model_width, 0, model_width)
    shift_in = slot_of(mod, 0, model_width, 0, model_width)
    in_rows = jnp.concatenate(
        [central * (1.0 + scale_in), jnp.broadcast_to(shift_in, (16, model_width))], axis=0
    )
    in_top, in_low = halves(in_rows)
    in_both = jnp.concatenate([in_top, in_low], axis=0)
    both = jnp.concatenate([dot32(in_both, head_w[kind]) for kind in range(3)], axis=1)
    short = both[: in_rows.shape[0]] + both[in_rows.shape[0] :]
    short_out[...] = short

    @pl.when(lax.axis_index("segment") == 0)
    def _():
        front(
            [rows_ref.at[place] for place in range(count)],
            central.astype(jnp.bfloat16),
            lambda: short,
            gains,
            head_outs,
            *kept,
        )

    late.wait()


def critic_front_kernel(count, fetches, short, embed_w, gains, *refs):
    rows = refs[:count]
    head_outs = refs[count : 2 * count]
    kept = refs[2 * count :]

    @pl.when(lax.axis_index("segment") != 0)
    def _():
        front(
            rows,
            centred(embed_w).astype(jnp.bfloat16),
            lambda: short[...],
            gains,
            head_outs,
            *kept,
        )


def tail(late, latent, embed_w, final_t, mixed, heads_w, work):
    model_width = embed_w.shape[2]
    block = latent[...]
    sums = None
    for first in range(0, model_width, TILE):
        span = slice(first, first + TILE)
        attended = None
        for piece, rows_w in zip(mixed, heads_w):
            product = dot32(piece[...], head_tile(rows_w, first, TILE))
            attended = product if attended is None else attended + product
        mod = late.ready()
        residual = (
            dot32(block, embed_w[0, :, span]) + slot_of(mod, 0, model_width, first, TILE) * attended
        )
        work[:, span] = residual
        part = lane_sum(residual)
        sums = part if sums is None else sums + part
    row_mean = jnp.sum(sums, axis=1, keepdims=True) / model_width
    sums = None
    for first in range(0, model_width, TILE):
        span = slice(first, first + TILE)
        middle = work[:, span] - row_mean
        work[:, span] = middle
        part = lane_sum(middle * middle)
        sums = part if sums is None else sums + part
    inverse = lax.rsqrt(jnp.sum(sums, axis=1, keepdims=True) / model_width + EPS)
    result = None
    final_w = final_t.ready()
    for first in range(0, model_width, TILE):
        span = slice(first, first + TILE)
        normed = work[:, span] * inverse
        work[:, span] = normed
        final_in = (
            normed * (1.0 + slot_of(mod, 2, model_width, first, TILE))
            + slot_of(mod, 1, model_width, first, TILE)
        ).astype(jnp.bfloat16)
        product = dot32_t(final_in, final_w[:, span])
        result = product if result is None else result + product
    return (result, inverse)


def student_tail_kernel(count, sizes, fetches, latent, embed_w, *refs):
    mixed = refs[:count]
    heads_w, refs = nested(refs[count:], sizes)
    pair_ref, saved_out, inverse_out, work, inverse_ref, sends = refs
    late, final_t, noise, times = fetches
    latent_width = latent.shape[1]

    @pl.when(lax.axis_index("segment") == 0)
    def _():
        for fetch in fetches:
            fetch.start()
        copies = [
            pltpu.make_async_copy(mixed[place], saved_out.at[place], sends.at[place])
            for place in range(count)
        ]
        for copy in copies:
            copy.start()
        velocity, inverse = tail(late, latent, embed_w, final_t, mixed, heads_w, work)
        inverse_ref[...] = jnp.broadcast_to(inverse, inverse_ref.shape)
        copies.append(pltpu.make_async_copy(inverse_ref, inverse_out, sends.at[count]))
        copies[-1].start()
        student_step, critic_step = steps_of(times)
        sigma_student, sigma_critic = noise_level(student_step), noise_level(critic_step)
        sample = latent[...].astype(jnp.float32) - sigma_student * velocity
        second = noise.ready()[:, latent_width:].astype(jnp.float32)
        critic = (1.0 - sigma_critic) * sample + sigma_critic * second
        pair_ref[...] = jnp.concatenate([critic, sample], axis=1).astype(jnp.bfloat16)
        for copy in copies:
            copy.wait()


def pick_kernel(sections, fetches, own, *refs):
    moved = refs[: sections - 1]
    pair_ref, rows_ref = refs[sections - 1 :]
    section = lax.axis_index("segment")
    for place in range(sections):

        @pl.when(section == place)
        def _():
            chosen = own if place == 0 else moved[place - 1]
            pair_ref[...] = chosen[...]
            rows_ref[...] = chosen[:, : rows_ref.shape[1]]


def critic_tail_kernel(count, sizes, fetches, pair, embed_w, *refs):
    mixed = refs[:count]
    heads_w, refs = nested(refs[count:], sizes)
    grads = refs[:count]
    inverse_ref, term_ref, target_ref, direct_ref, latent, work, other = refs[count:]
    late, final_t, noise, times = fetches
    model_width = embed_w.shape[2]
    latent_width = latent.shape[1]
    section = lax.axis_index("segment")

    @pl.when(section != 0)
    def _():
        for fetch in fetches:
            fetch.start()
        both = pair[...].astype(jnp.float32)
        sample = both[:, latent_width:]
        latent[...] = pair[:, :latent_width]
        result, inverse = tail(late, latent, embed_w, final_t, mixed, heads_w, work)
        mod, final_w = late.ready(), final_t.ready()
        _, critic_step = steps_of(times)
        sigma_critic = noise_level(critic_step)
        inverse_ref[...] = jnp.broadcast_to(inverse, inverse_ref.shape)
        term_ref[...] = (sigma_critic * result).astype(jnp.bfloat16)
        second = noise.ready()[:, latent_width:].astype(jnp.float32)
        target_ref[...] = jnp.where(
            section == 2,
            2.0 * (result - (second - sample)),
            jnp.where(section == 3, 1.0 / (1.0 + jnp.exp(-result)), 0.0),
        )

        @pl.when(section == 1)
        def _():
            gaps = jnp.abs(sample - both[:, :latent_width] + sigma_critic * result)
            error = jnp.sum(jnp.sum(gaps, axis=1, keepdims=True), axis=0, keepdims=True)
            error = error / (gaps.shape[0] * latent_width)
            error_top, error_low = halves(jnp.broadcast_to(error, (16, grads[0].shape[1])))
            for place in range(count):
                grads[place][:16] = error_top
                grads[place][16:32] = error_low

        @pl.when(section == 3)
        def _():
            grad_logit = (-1.0 / (1.0 + jnp.exp(result))).astype(jnp.bfloat16)
            plain, along = None, None
            for first in range(0, model_width, TILE):
                span = slice(first, first + TILE)
                gradient = dot32(grad_logit, final_w[:, span]) * (
                    1.0 + slot_of(mod, 2, model_width, first, TILE)
                )
                other[:, span] = gradient
                part = lane_sum(gradient)
                plain = part if plain is None else plain + part
                part = lane_sum(gradient * work[:, span])
                along = part if along is None else along + part
            plain = jnp.sum(plain, axis=1, keepdims=True) / model_width
            along = jnp.sum(along, axis=1, keepdims=True) / model_width
            direct = None
            totals = [None] * count
            for first in range(0, model_width, TILE):
                span = slice(first, first + TILE)
                grad_residual = inverse * (other[:, span] - plain - work[:, span] * along)
                top, low = halves(grad_residual)
                product = dot32_t(top, embed_w[0, :, span]) + dot32_t(low, embed_w[0, :, span])
                direct = product if direct is None else direct + product
                grad_attended = (slot_of(mod, 0, model_width, first, TILE) * grad_residual).astype(
                    jnp.bfloat16
                )
                for place in range(count):
                    product = dot32_t(grad_attended, head_tile(heads_w[place], first, TILE))
                    held = totals[place]
                    totals[place] = product if held is None else held + product
            direct_ref[...] = direct
            for place in range(count):
                grads[place][...] = totals[place].astype(jnp.bfloat16)


def gram_kernel(fetches, embed_w, gram_ref):
    central_top, central_low = halves(centred(embed_w))
    gram = (
        dot32_t(central_top, central_top)
        + dot32_t(central_top, central_low)
        + dot32_t(central_low, central_top)
    )
    gram_ref[0], gram_ref[1] = halves(gram)


def judge_back_kernel(count, model_width, fetches, short_in, gram, gains, proj_ref, inverse_ref, key_ref, value_ref, term, *refs):
    rows = refs[:count]
    grads = refs[count : 2 * count]
    keep_ref, send_ref, real_ref, grad_key_ref, grad_value_ref, grad_query_ref = refs[2 * count :]
    section = lax.axis_index("segment")
    latent_width = rows[0].shape[1]
    head_width = gains.shape[2]
    scale = 1.0 / math.sqrt(head_width)
    size = rows[0].shape[0]

    @pl.when(section == 3)
    def _():
        for place in range(count):
            low = place * size
            span = slice(low, low + size)
            queries, _, _ = rms_scale(proj_ref[span, :head_width], gains[0, :1])
            query_b = queries.astype(jnp.bfloat16)
            weights = jnp.exp(dot32_t(query_b, key_ref[...]) * scale)
            soft_max = weights * (1.0 / jnp.sum(weights, axis=-1, keepdims=True))
            grad_out = grads[place][...]
            grad_soft = dot32_t(grad_out, value_ref[...])
            grad_value = dot32_first(soft_max.astype(jnp.bfloat16), grad_out)
            grad_scores = soft_max * (
                grad_soft - jnp.sum(soft_max * grad_soft, axis=-1, keepdims=True)
            )
            grad_scores_b = (grad_scores * scale).astype(jnp.bfloat16)
            grad_query_ref[span] = dot32(grad_scores_b, key_ref[...])
            grad_key = dot32_first(grad_scores_b, query_b)
            if place == 0:
                grad_value_ref[...] = grad_value
                grad_key_ref[...] = grad_key
            else:
                grad_value_ref[...] += grad_value
                grad_key_ref[...] += grad_key
        gram_top, gram_low = gram[0], gram[1]
        short_top, short_low = halves(short_in[:latent_width])
        for place in range(count):
            low = place * size
            span = slice(low, low + size)
            projected = proj_ref[span]
            _, q_unit, q_inverse = rms_scale(projected[:, :head_width], gains[0, :1])
            _, k_unit, k_inverse = rms_scale(
                projected[:, head_width : 2 * head_width], gains[0, 1:2]
            )
            grad_q = rms_back(grad_query_ref[span], q_unit, q_inverse, gains[0, :1])
            grad_k = rms_back(grad_key_ref[span], k_unit, k_inverse, gains[0, 1:2])
            grad_proj = jnp.concatenate([grad_q, grad_k, grad_value_ref[span]], axis=1).astype(
                jnp.bfloat16
            )
            through = dot32_t(grad_proj, short_top) + dot32_t(grad_proj, short_low)
            block = rows[place][...]
            along = jnp.sum(through * block.astype(jnp.float32), axis=1, keepdims=True) / model_width
            spanned = dot32(block, gram_top) + dot32(block, gram_low)
            inverse = inverse_ref[span, :1]
            target_ref = send_ref if place % 2 else keep_ref
            target_ref[place // 2] = (
                inverse * (through - spanned * (inverse * inverse * along))
            ).astype(jnp.bfloat16)

    @pl.when(section == 1)
    def _():
        error = None
        for grad in grads:
            part = grad[:16, :latent_width].astype(jnp.float32) + grad[
                16:32, :latent_width
            ].astype(jnp.float32)
            error = part if error is None else error + part
        real_ref[:size] = term[...]
        real_ref[size : size + 16], real_ref[size + 16 :] = halves(error / count + EPS)


def merge_kernel(fetches, direct, keep, moved, *outs):
    @pl.when(lax.axis_index("segment") == 3)
    def _():
        for place, out in enumerate(outs):
            total = keep[place].astype(jnp.float32) + moved[place].astype(jnp.float32)
            if place == 0:
                total = total + direct[...]
            out[...] = total.astype(jnp.bfloat16)


def outer_kernel(
    count,
    fetches,
    real,
    fake,
    target_in,
    student_rows,
    pair,
    student_mixed,
    student_inverse,
    critic_inverse,
    *refs,
):
    critic_mixed = refs[:count]
    arrived = refs[count : count + count // 2]
    sums_ref, sample_ref = refs[count + count // 2 :]
    section = lax.axis_index("segment")
    place = lax.axis_index("seq")
    latent_width = student_rows.shape[1]
    rows = student_rows.shape[0]

    def collect(target, inverse, latent, mixed):
        target = target.astype(jnp.bfloat16)
        weighted = inverse[:, :latent_width] * target.astype(jnp.float32)
        top, low = halves(weighted)
        for offset in range(count):
            piece = mixed[offset][...]
            sums_ref[place ^ offset] = (dot32_first(top, piece) + dot32_first(low, piece)).astype(
                jnp.bfloat16
            )
        near = dot32_first(top, latent) + dot32_first(low, latent)
        ones = jnp.ones((target.shape[0], sums_ref.shape[2] - latent_width), jnp.bfloat16)
        sums_ref[count] = jnp.concatenate([near, dot32_first(target, ones)], axis=1).astype(
            jnp.bfloat16
        )

    @pl.when(section == 0)
    def _():
        (times,) = fetches
        times.start()
        student_step, critic_step = steps_of(times)
        adverse = arrived[0][...].astype(jnp.float32)
        for part in arrived[1:]:
            adverse = adverse + part[...].astype(jnp.float32)
        adverse = (1.0 - noise_level(critic_step)) * adverse
        spread = (real[rows : rows + 1] .astype(jnp.float32) + real[rows + 16 : rows + 17].astype(jnp.float32))[
            :, :1
        ]
        gap = real[:rows].astype(jnp.float32) - fake[...].astype(jnp.float32)
        sample_grad = gap / spread + ADV_WEIGHT * adverse
        sample_ref[...] = sample_grad.astype(jnp.bfloat16)
        target = -noise_level(student_step) * sample_grad
        mixed = [student_mixed.at[offset] for offset in range(count)]
        collect(target, student_inverse, student_rows[...], mixed)

    @pl.when(section == 1)
    def _():
        sums_ref[...] = jnp.zeros_like(sums_ref)

    @pl.when(section >= 2)
    def _():
        collect(target_in[...], critic_inverse, pair[:, :latent_width], critic_mixed)


def emit_kernel(fetches, own, to_first, to_second, to_third, grad_ref):
    section = lax.axis_index("segment")
    for place, value in enumerate((own, to_first, to_second, to_third)):

        @pl.when(section == place)
        def _():
            grad_ref[...] = value[...].astype(jnp.float32).T


def expand_kernel(count, groups, sizes, full_rows, fetches, embed_w, *refs):
    heads_w, refs = nested(refs, sizes)
    other_mods = refs[: groups - 1]
    sums = refs[groups - 1 : 3 * groups - 1]
    total_ref, work, joined = refs[3 * groups - 1 :]
    section = lax.axis_index("segment")
    place = lax.axis_index("seq")
    latent_width = embed_w.shape[1]
    model_width = embed_w.shape[2]

    @pl.when(section == 1)
    def _():
        total_ref[...] = jnp.zeros_like(total_ref)

    @pl.when(section != 1)
    def _():
        (late,) = fetches
        late.start()
        for group in range(groups):
            low = group * latent_width
            joined[:, low : low + latent_width] = sums[2 * group][...].astype(jnp.float32) + sums[
                2 * group + 1
            ][...].astype(jnp.float32)
        near_top = joined[count].astype(jnp.bfloat16)
        heads = [joined[place ^ offset].astype(jnp.bfloat16) for offset in range(count)]
        averages = None
        for first in range(0, model_width, TILE):
            span = slice(first, first + TILE)
            spread = None
            for head, rows_w in zip(heads, heads_w):
                product = dot32(head, head_tile(rows_w, first, TILE))
                spread = product if spread is None else spread + product
            near = dot32(near_top[:, :latent_width], embed_w[0, :, span])
            mods = [late.ready(), *other_mods]
            gates = jnp.concatenate(
                [
                    jnp.broadcast_to(
                        slot_of(mod, 0, model_width, first, TILE), (latent_width, TILE)
                    )
                    for mod in mods
                ],
                axis=0,
            )
            value = near + gates * spread
            work[:, span] = value
            part = lane_sum(value)
            averages = part if averages is None else averages + part
        averages = jnp.sum(averages, axis=1, keepdims=True) / model_width
        counts = joined[count][:, latent_width : latent_width + 1]
        for first in range(0, model_width, TILE):
            span = slice(first, first + TILE)
            value = work[:, span] - averages
            total = None
            for group in range(groups):
                mine = slice(group * latent_width, (group + 1) * latent_width)
                product = value[mine] * (
                    1.0 + slot_of(mods[group], 2, model_width, first, TILE)
                ) + counts[mine] * slot_of(mods[group], 1, model_width, first, TILE)
                total = product if total is None else total + product
            total_ref[:, span] = total / full_rows


def step(
    clean, noise, timesteps, text_vec, w_embed, w_time, w_mod, w_qkv, w_out, qk_gain, w_final
):
    sections = lax.axis_size("segment")
    tok_rows = clean.shape[1]
    latent_width = clean.shape[2]
    model_width = w_embed.shape[2]
    mod_width = w_mod.shape[2]
    count = lax.axis_size("seq")
    full_rows = tok_rows * count
    head_width = w_qkv.shape[4]
    bf16, f32 = jnp.bfloat16, jnp.float32
    kind_w = jnp.transpose(w_qkv[0, :, 0], (1, 0, 2))
    final_w = jnp.transpose(w_final[0])
    groups = lax.axis_size("dp")

    def stage(near):
        rows, width = near.shape
        (part,) = run(stage_kernel, [array((rows, width // 2), bf16)], (near,), 1000)
        return part

    heads_w = spread_heads(w_out[0, 0], count, groups, stage)
    sizes = [len(pieces) for pieces in heads_w]
    heads_w = sum(heads_w, [])

    depth = packed_rows(mod_width)
    packed, noisy_student, kind_w = run(
        condition_kernel,
        [
            array((tok_rows // 2 + 2 * depth, 2 * latent_width), bf16),
            array((tok_rows, latent_width), bf16),
            pltpu.VMEM(kind_w.shape, bf16),
        ],
        (),
        2 * model_width * mod_width,
        scratch=(
            pltpu.VMEM((model_width, mod_width), bf16),
            pltpu.VMEM((depth, 128), f32),
            pltpu.SemaphoreType.DMA((STREAMS + 1,)),
        ),
        fetched=(timesteps, text_vec, w_time[0], jnp.transpose(clean[0]), noise[0]),
        streamed=(w_mod[0], kind_w),
    )
    kind_w = pltpu.with_memory_space_constraint(kind_w, pltpu.VMEM)
    packed_all = gather_near(packed, "seq", count)

    head_blocks = [array((tok_rows, head_width), bf16)] * count
    stored = [
        ((full_rows, 3 * head_width), f32),
        ((full_rows, 128), f32),
        ((full_rows, head_width), bf16),
        ((full_rows, head_width), bf16),
    ]
    short_shape = ((latent_width + 16, 3 * head_width), f32)
    *head_outs, short, late_mod = run(
        functools.partial(student_front_kernel, count, mod_width),
        head_blocks + [pltpu.VMEM(*short_shape)],
        (w_embed, kind_w, qk_gain, *packed_all),
        4 * latent_width * model_width * 3 * head_width,
        scratch=[
            pltpu.VMEM((1, 5 * model_width), f32),
            pltpu.VMEM((count, tok_rows, latent_width), bf16),
            pltpu.SemaphoreType.DMA((1,)),
        ]
        + [pltpu.VMEM(shape, kind) for shape, kind in stored],
        sent=[array((1, 3 * model_width), f32)],
    )
    student_mixed = scatter_near(head_outs, "seq", count)
    late_mods = gather_near(late_mod, "dp", groups)
    work = pltpu.VMEM((tok_rows, model_width), f32)
    inverse_shape = array((tok_rows, 128), f32)
    pair, saved, student_inverse = run(
        functools.partial(student_tail_kernel, count, sizes),
        [array((tok_rows, 2 * latent_width), bf16)],
        (noisy_student, w_embed, *student_mixed, *heads_w),
        2 * tok_rows * model_width * head_width * count,
        scratch=(
            work,
            pltpu.VMEM((tok_rows, 128), f32),
            pltpu.SemaphoreType.DMA((count + 1,)),
        ),
        fetched=(late_mod, final_w, noise[0], timesteps),
        sent=[array((count, tok_rows, head_width), bf16), inverse_shape],
    )
    moved = [lax.ppermute(pair, "segment", [(0, place)]) for place in range(1, sections)]
    pair, own_rows = run(
        functools.partial(pick_kernel, sections),
        [
            array((tok_rows, 2 * latent_width), bf16),
            array((tok_rows, latent_width), bf16),
        ],
        (pair, *moved),
        1000,
    )
    critic_rows = gather_near(own_rows, "seq", count)
    *head_outs, proj, inverse, keys, values = run(
        functools.partial(critic_front_kernel, count),
        head_blocks + [array(shape, kind) for shape, kind in stored],
        (
            pltpu.with_memory_space_constraint(short, pltpu.VMEM),
            w_embed,
            qk_gain,
            *critic_rows,
        ),
        4 * latent_width * model_width * full_rows,
    )
    critic_mixed = scatter_near(head_outs, "seq", count)
    small = array((tok_rows, latent_width), f32)
    thin = array((tok_rows, latent_width), bf16)
    *grad_heads, critic_inverse, term_rows, target, direct = run(
        functools.partial(critic_tail_kernel, count, sizes),
        head_blocks + [inverse_shape, thin, small, small],
        (pair, w_embed, *critic_mixed, *heads_w),
        4 * tok_rows * model_width * head_width * count,
        scratch=(pltpu.VMEM((tok_rows, latent_width), bf16), work, work),
        fetched=(late_mod, final_w, noise[0], timesteps),
    )
    grad_blocks = scatter_near(grad_heads, "seq", count)
    fake = lax.ppermute(term_rows, "segment", swaps(sections, 2))
    half = count // 2
    rows_shape = array((half, tok_rows, latent_width), bf16)
    (gram,) = run(
        gram_kernel,
        [array((2, latent_width, latent_width), bf16)],
        (w_embed,),
        6 * latent_width * latent_width * model_width,
    )
    keep, away, real = run(
        functools.partial(judge_back_kernel, count, model_width),
        [rows_shape, rows_shape, array((tok_rows + 32, latent_width), bf16)],
        (short, gram, qk_gain, proj, inverse, keys, values, term_rows, *critic_rows, *grad_blocks),
        10 * full_rows * full_rows * head_width,
        scratch=(pltpu.VMEM((full_rows, head_width), f32),) * 3,
    )
    moved = lax.ppermute(away, "seq", swaps(count, 1))
    real = lax.ppermute(real, "segment", swaps(sections, 1))
    parts = run(merge_kernel, [thin] * half, (direct, keep, moved), 1000)
    to_student = [
        lax.ppermute(
            part,
            ("segment", "seq"),
            [
                (place * count + row, (place + 1) % sections * count + (row ^ (2 * index)))
                for place in range(sections)
                for row in range(count)
            ],
        )
        for index, part in enumerate(parts)
    ]
    sums, sample_grad = run(
        functools.partial(outer_kernel, count),
        [array((count + 1, latent_width, 128), bf16), thin],
        (
            real,
            fake,
            target,
            noisy_student,
            pair,
            saved,
            student_inverse,
            critic_inverse,
            *critic_mixed,
            *to_student,
        ),
        2 * tok_rows * latent_width * head_width * (count + 1),
        fetched=(timesteps,),
    )
    ends = [(place, sections - 1 - place) for place in range(sections)]
    to_third = lax.ppermute(sample_grad, "segment", ends)
    to_second = lax.ppermute(sample_grad, "segment", swaps(sections, 2))
    to_first = lax.ppermute(sample_grad, "segment", swaps(sections, 1))
    last = count // 2
    bit = 1
    while bit < last:
        moved = lax.ppermute(sums, "seq", swaps(count, bit))
        sums = (sums.astype(f32) + moved.astype(f32)).astype(bf16)
        bit *= 2
    sums_all = []
    for group in range(groups):
        for offset in (0, last):
            moves = [
                (place * groups + batch, (place ^ offset) * groups + (batch ^ group))
                for place in range(count)
                for batch in range(groups)
            ]
            sums_all.append(
                sums if offset == group == 0 else lax.ppermute(sums, ("seq", "dp"), moves)
            )
    (total_t,) = run(
        functools.partial(expand_kernel, count, groups, sizes, full_rows),
        [array((latent_width, model_width), f32)],
        (
            w_embed,
            *heads_w,
            *late_mods[1:],
            *sums_all,
        ),
        4 * groups * latent_width * model_width * head_width * count,
        scratch=(
            pltpu.VMEM((groups * latent_width, model_width), f32),
            pltpu.VMEM((count + 1, groups * latent_width, 128), f32),
        ),
        fetched=(late_mod,),
    )
    (grad_t,) = run(
        emit_kernel,
        [array((latent_width, tok_rows), f32)],
        (sample_grad, to_first, to_second, to_third),
        1000,
    )
    return (jnp.transpose(grad_t)[None], jnp.transpose(total_t)[None])


def solution(mesh):
    placed = (
        P("dp", "seq", None),
        P("dp", "seq", None),
        P(),
        P("dp", None),
        P("segment", None, None),
        P("segment", None, None),
        P("segment", None, "seq"),
        P("segment", None, "seq", None, None),
        P("segment", "seq", None, None),
        P("segment", None, None),
        P("segment", None, None),
    )
    return jax.shard_map(
        step,
        mesh=mesh,
        in_specs=placed,
        out_specs=(P("dp", "seq", None), P("segment", None, None)),
        check_vma=False,
    )
```

```python
import functools
import math

import jax
import jax.numpy as jnp
from jax import lax
from jax.experimental import pallas as pl
from jax.experimental.pallas import tpu as pltpu
from jax.sharding import PartitionSpec as P


SHIFT = 7.0
EPS = 1e-06
ADV_WEIGHT = 3.0
TILE = 512
STREAMS = 6
SPARE = 8 << 20
VMEM = pl.BlockSpec(memory_space=pltpu.VMEM)
HBM = pl.BlockSpec(memory_space=pltpu.HBM)


def halves(values):
    top = values.astype(jnp.bfloat16)
    return (top, (values - top.astype(jnp.float32)).astype(jnp.bfloat16))


def swaps(count, offset):
    return [(place, place ^ offset) for place in range(count)]


def gather_near(value, axis, count):
    return [value] + [lax.ppermute(value, axis, swaps(count, offset)) for offset in range(1, count)]


def scatter_near(blocks, axis, count):
    return [blocks[0]] + [
        lax.ppermute(blocks[offset], axis, swaps(count, offset))
        for offset in range(1, count)
    ]


def spread_heads(own, count, groups, stage):
    held = {0: [own]}
    bit = count // 2
    first = True
    while bit:
        for offset in sorted(held):
            if first and groups == 2:
                width = own.shape[1] // 3
                shift = lax.axis_index("dp") * width
                part = lax.dynamic_slice_in_dim(own, shift, 2 * width, axis=1)
                near = lax.ppermute(part, "seq", swaps(count, bit))
                held[bit] = [near, lax.ppermute(stage(near), "dp", swaps(groups, 1))]
            else:
                held[offset | bit] = [
                    lax.ppermute(piece, "seq", swaps(count, bit))
                    for piece in held[offset]
                ]
        first = False
        bit //= 2
    return [held[offset] for offset in range(count)]


def head_tile(pieces, first, size):
    if len(pieces) == 1:
        return pieces[0][:, first : first + size]
    near, far = pieces
    width = far.shape[1]
    low = slice(first % width, first % width + size)
    high = slice(width + first % width, width + first % width + size)
    choices = (
        (near[:, low], far[:, low]),
        (near[:, high], near[:, low]),
        (far[:, low], near[:, high]),
    )[first // width]
    return jnp.where(lax.axis_index("dp") == 0, *choices)


def stacked_tile(heads_w, first):
    return jnp.concatenate([head_tile(pieces, first, TILE) for pieces in heads_w], axis=0)


def nested(refs, sizes):
    groups, first = [], 0
    for size in sizes:
        groups.append(refs[first : first + size])
        first += size
    return (groups, refs[first:])


def in_order(pieces, own_place):
    ordered = list(pieces)
    bit = 1
    while bit < len(ordered):
        flipped = (own_place & bit) != 0
        ordered = [
            jnp.where(flipped, ordered[place ^ bit], ordered[place])
            for place in range(len(ordered))
        ]
        bit *= 2
    return ordered


def dot32(left, right):
    return jnp.dot(left, right, preferred_element_type=jnp.float32)


def dot32_t(left, right):
    return lax.dot_general(
        left, right, (((1,), (1,)), ((), ())), preferred_element_type=jnp.float32
    )


def dot32_first(left, right):
    return lax.dot_general(
        left, right, (((0,), (0,)), ((), ())), preferred_element_type=jnp.float32
    )


def steps_of(times):
    times_ref = times.ready()
    place = lax.axis_index("dp")
    return (times_ref[place, 0], times_ref[place, 1])


def noise_level(step):
    fraction = jnp.full((1, 1), step, jnp.int32).astype(jnp.float32) / 1000.0
    return SHIFT * fraction / (1.0 + (SHIFT - 1.0) * fraction)


def slot_of(mod_ref, slot, width, first, size):
    return mod_ref[:, slot * width + first : slot * width + first + size]


def lane_sum(values):
    total = values[:, :128]
    for first in range(128, values.shape[1], 128):
        total = total + values[:, first : first + 128]
    return total


class Fetch:
    def __init__(self, source, target, arrival):
        self.copy = pltpu.make_async_copy(source, target, arrival)
        self.target = target
        self.waiting = True

    def start(self):
        self.copy.start()

    def ready(self):
        if self.waiting:
            self.copy.wait()
            self.waiting = False
        return self.target


def bytes_of(items):
    return sum(math.prod(item.shape) * jnp.dtype(item.dtype).itemsize for item in items)


def in_hbm(item):
    return pltpu.with_memory_space_constraint(item, pltpu.HBM)


def run(kernel, outputs, operands, flops, scratch=(), fetched=(), streamed=(), sent=()):
    inputs = len(operands)
    total = inputs + len(fetched) + len(streamed)
    results = len(outputs) + len(sent)

    def body(*refs):
        sources = refs[inputs:total]
        outs = refs[total : total + results]
        own = refs[total + results : total + results + len(scratch)]
        rest = refs[total + results + len(scratch) :]
        fetches = [
            Fetch(source, target, rest[-1].at[place])
            for place, (source, target) in enumerate(zip(sources, rest[:-1]))
        ]
        fetches += sources[len(fetched) :]
        kernel(fetches, *refs[:inputs], *outs, *own)

    places = [
        (pltpu.SMEM if item.dtype == jnp.int32 else pltpu.VMEM)(item.shape, item.dtype)
        for item in fetched
    ]
    held = bytes_of(
        [ref for ref in list(scratch) + places if ref.memory_space == pltpu.VMEM]
    )
    limit = min(60 << 20, SPARE + held + bytes_of(operands) + 2 * bytes_of(outputs))
    return pl.pallas_call(
        body,
        out_shape=list(outputs) + [pltpu.HBM(item.shape, item.dtype) for item in sent],
        in_specs=[VMEM] * inputs + [HBM] * (total - inputs),
        out_specs=[VMEM] * len(outputs) + [HBM] * len(sent),
        scratch_shapes=list(scratch)
        + places
        + [pltpu.SemaphoreType.DMA((max(1, len(fetched)),))],
        compiler_params=pltpu.CompilerParams(vmem_limit_bytes=limit),
        cost_estimate=pl.CostEstimate(
            flops=flops,
            bytes_accessed=bytes_of(list(operands) + list(fetched) + list(outputs)),
            transcendentals=0,
        ),
    )(*operands, *[in_hbm(item) for item in (*fetched, *streamed)])


def array(shape, dtype):
    return jax.ShapeDtypeStruct(shape, dtype)


def packed_rows(width):
    return -(-width // 2048) * 16


def condition_kernel(fetches, packed_out, noisy_out, kind_out, gram_out, held, mod_rows, arrivals):
    times, text, time_w, clean_t, noise, embed_w, mod_w, kind_w = fetches
    model_width = held.shape[0]
    rows = model_width // STREAMS
    for fetch in fetches[:-2]:
        fetch.start()
    copies = [
        pltpu.make_async_copy(
            mod_w.at[pl.ds(part * rows, rows)], held.at[pl.ds(part * rows, rows)], arrivals.at[part]
        )
        for part in range(STREAMS)
    ]
    copies.append(pltpu.make_async_copy(kind_w, kind_out, arrivals.at[STREAMS]))
    for copy in copies:
        copy.start()
    student_step, critic_step = steps_of(times)
    step = jnp.where(lax.axis_index("segment") == 0, student_step, critic_step)
    text_ref = text.ready()
    half = text_ref.shape[1] // 2
    places = lax.broadcasted_iota(jnp.int32, (1, half), 1).astype(jnp.float32)
    frequency = jnp.exp(-math.log(10000.0) * places / half)
    angles = jnp.full((1, half), step, jnp.int32).astype(jnp.float32) * frequency
    features = jnp.concatenate([jnp.cos(angles), jnp.sin(angles)], axis=1) + text_ref[...]
    features = jnp.broadcast_to(features, (8, 2 * half)).astype(jnp.bfloat16)
    hidden = dot32(features, time_w.ready()[...])
    hidden = (hidden / (1.0 + jnp.exp(-hidden))).astype(jnp.bfloat16)
    mod_rows[...] = jnp.zeros_like(mod_rows)
    total = None
    for part in range(STREAMS):
        copies[part].wait()
        piece = dot32(
            hidden[:, part * rows : (part + 1) * rows], held[part * rows : (part + 1) * rows]
        )
        total = piece if total is None else total + piece
        if part == STREAMS // 2:
            sigma_student = noise_level(student_step)
            clean_ref, noise_ref = clean_t.ready(), noise.ready()
            noisy = (1.0 - sigma_student) * clean_ref[...].astype(jnp.float32).T + sigma_student * noise_ref[
                :, : clean_ref.shape[0]
            ].astype(jnp.float32)
            noisy = noisy.astype(jnp.bfloat16)
            noisy_out[...] = noisy
            top = noisy.shape[0] // 2
            packed_out[:top] = jnp.concatenate([noisy[:top], noisy[top:]], axis=1)
            central_top, central_low = halves(centred(embed_w.ready()))
            gram = (
                dot32_t(central_top, central_top)
                + dot32_t(central_top, central_low)
                + dot32_t(central_low, central_top)
            )
            gram_out[0], gram_out[1] = halves(gram)
    width = total.shape[1]
    for row, first in enumerate(range(0, width, 128)):
        size = min(128, width - first)
        mod_rows[row : row + 1, :size] = total[:1, first : first + size]
    depth = mod_rows.shape[0]
    top = noisy_out.shape[0] // 2
    packed_out[top : top + depth], packed_out[top + depth :] = halves(mod_rows[...])
    copies[STREAMS].wait()


def rms_scale(values, gain_vec):
    inverse = lax.rsqrt(jnp.mean(values * values, axis=-1, keepdims=True) + EPS)
    unit_vec = values * inverse
    return (unit_vec * gain_vec, unit_vec, inverse)


def rms_back(gradient, unit_vec, inverse, gain_vec):
    scaled = gradient * gain_vec
    return inverse * (scaled - unit_vec * jnp.mean(scaled * unit_vec, axis=-1, keepdims=True))


def centred(embed_ref):
    values = embed_ref[0].astype(jnp.float32)
    return values - jnp.mean(values, axis=1, keepdims=True)


def front(rows, gram, model_width, short, gains, head_outs, proj_ref, inverse_ref, key_ref, value_ref):
    latent_width = gram.shape[1]
    count = len(rows)
    head_width = gains.shape[2]
    scale = 1.0 / math.sqrt(head_width)
    size = rows[0].shape[0]
    short_top = None
    for place in range(count):
        block = rows[place][...]
        spanned = dot32(block, gram[0]) + dot32(block, gram[1])
        squares = jnp.sum(spanned * block.astype(jnp.float32), axis=1, keepdims=True)
        inverse = lax.rsqrt(jnp.maximum(squares, 0.0) / model_width + EPS)
        if short_top is None:
            values = short()
            short_top, short_low = halves(values[:latent_width])
            short_shift = values[latent_width : latent_width + 1]
        projected = inverse * (dot32(block, short_top) + dot32(block, short_low)) + short_shift
        low = place * size
        proj_ref[low : low + size] = projected
        inverse_ref[low : low + size] = jnp.broadcast_to(inverse, (size, 128))
        keys, _, _ = rms_scale(projected[:, head_width : 2 * head_width], gains[0, 1:2])
        key_ref[low : low + size] = keys.astype(jnp.bfloat16)
        value_ref[low : low + size] = projected[:, 2 * head_width :].astype(jnp.bfloat16)
    for place in range(count):
        low = place * size
        queries, _, _ = rms_scale(proj_ref[low : low + size, :head_width], gains[0, :1])
        scores = dot32_t(queries.astype(jnp.bfloat16), key_ref[...]) * scale
        weights = jnp.exp(scores)
        soft_max = weights * (1.0 / jnp.sum(weights, axis=-1, keepdims=True))
        head_outs[place][...] = dot32(soft_max.astype(jnp.bfloat16), value_ref[...]).astype(
            jnp.bfloat16
        )


def stage_kernel(fetches, near, part_out):
    width = part_out.shape[1]
    for place in range(2):

        @pl.when(lax.axis_index("dp") == place)
        def _():
            part_out[...] = near[:, place * width : (place + 1) * width]


def student_front_kernel(count, width, fetches, embed_w, head_w, gram, gains, *refs):
    packed = refs[:count]
    head_outs = refs[count : 2 * count]
    short_out, late_out, mod, rows_ref, sends, *kept = refs[2 * count :]
    model_width = embed_w.shape[2]
    latent_width = embed_w.shape[1]
    size = rows_ref.shape[1]
    half = size // 2
    depth = packed_rows(width)
    parts = [
        piece[half : half + depth].astype(jnp.float32) + piece[half + depth :].astype(jnp.float32)
        for piece in packed
    ]
    for place, part in enumerate(in_order(parts, lax.axis_index("seq"))):
        for row, first in enumerate(range(0, width, 128)):
            lanes = min(128, width - first)
            low = place * width + first
            mod[:, low : low + lanes] = part[row : row + 1, :lanes]
    late = pltpu.make_async_copy(
        mod.at[:, pl.ds(2 * model_width, 3 * model_width)], late_out, sends.at[0]
    )
    late.start()
    for place in range(count):
        rows_ref[place, :half] = packed[place][:half, :latent_width]
        rows_ref[place, half:] = packed[place][:half, latent_width:]
    central = centred(embed_w)
    scale_in = slot_of(mod, 1, model_width, 0, model_width)
    shift_in = slot_of(mod, 0, model_width, 0, model_width)
    in_rows = jnp.concatenate(
        [central * (1.0 + scale_in), jnp.broadcast_to(shift_in, (16, model_width))], axis=0
    )
    in_top, in_low = halves(in_rows)
    in_both = jnp.concatenate([in_top, in_low], axis=0)
    both = jnp.concatenate([dot32(in_both, head_w[kind]) for kind in range(3)], axis=1)
    short = both[: in_rows.shape[0]] + both[in_rows.shape[0] :]
    short_out[...] = short

    @pl.when(lax.axis_index("segment") == 0)
    def _():
        front(
            [rows_ref.at[place] for place in range(count)],
            gram,
            model_width,
            lambda: short,
            gains,
            head_outs,
            *kept,
        )

    late.wait()


def critic_front_kernel(count, model_width, fetches, short, gram, gains, *refs):
    rows = refs[:count]
    head_outs = refs[count : 2 * count]
    kept = refs[2 * count :]

    @pl.when(lax.axis_index("segment") != 0)
    def _():
        front(
            rows,
            gram,
            model_width,
            lambda: short[...],
            gains,
            head_outs,
            *kept,
        )


def tail(late, latent, embed_w, final_t, mixed, heads_w, work):
    model_width = embed_w.shape[2]
    block = latent[...]
    joined_heads = jnp.concatenate([piece[...] for piece in mixed], axis=1)
    sums = None
    for first in range(0, model_width, TILE):
        span = slice(first, first + TILE)
        attended = dot32(joined_heads, stacked_tile(heads_w, first))
        mod = late.ready()
        residual = (
            dot32(block, embed_w[0, :, span]) + slot_of(mod, 0, model_width, first, TILE) * attended
        )
        work[:, span] = residual
        part = lane_sum(residual)
        sums = part if sums is None else sums + part
    row_mean = jnp.sum(sums, axis=1, keepdims=True) / model_width
    sums = None
    for first in range(0, model_width, TILE):
        span = slice(first, first + TILE)
        middle = work[:, span] - row_mean
        work[:, span] = middle
        part = lane_sum(middle * middle)
        sums = part if sums is None else sums + part
    inverse = lax.rsqrt(jnp.sum(sums, axis=1, keepdims=True) / model_width + EPS)
    result = None
    final_w = final_t.ready()
    for first in range(0, model_width, TILE):
        span = slice(first, first + TILE)
        normed = work[:, span] * inverse
        work[:, span] = normed
        final_in = (
            normed * (1.0 + slot_of(mod, 2, model_width, first, TILE))
            + slot_of(mod, 1, model_width, first, TILE)
        ).astype(jnp.bfloat16)
        product = dot32_t(final_in, final_w[:, span])
        result = product if result is None else result + product
    return (result, inverse)


def student_tail_kernel(count, sizes, fetches, latent, embed_w, *refs):
    mixed = refs[:count]
    heads_w, refs = nested(refs[count:], sizes)
    pair_ref, saved_out, inverse_out, work, inverse_ref, sends = refs
    late, final_t, noise, times = fetches
    latent_width = latent.shape[1]

    @pl.when(lax.axis_index("segment") == 0)
    def _():
        for fetch in fetches:
            fetch.start()
        copies = [
            pltpu.make_async_copy(mixed[place], saved_out.at[place], sends.at[place])
            for place in range(count)
        ]
        for copy in copies:
            copy.start()
        velocity, inverse = tail(late, latent, embed_w, final_t, mixed, heads_w, work)
        inverse_ref[...] = jnp.broadcast_to(inverse, inverse_ref.shape)
        copies.append(pltpu.make_async_copy(inverse_ref, inverse_out, sends.at[count]))
        copies[-1].start()
        student_step, critic_step = steps_of(times)
        sigma_student, sigma_critic = noise_level(student_step), noise_level(critic_step)
        sample = latent[...].astype(jnp.float32) - sigma_student * velocity
        second = noise.ready()[:, latent_width:].astype(jnp.float32)
        critic = (1.0 - sigma_critic) * sample + sigma_critic * second
        pair_ref[...] = jnp.concatenate([critic, sample], axis=1).astype(jnp.bfloat16)
        for copy in copies:
            copy.wait()


def pick_kernel(sections, fetches, own, *refs):
    moved = refs[: sections - 1]
    pair_ref, rows_ref = refs[sections - 1 :]
    section = lax.axis_index("segment")
    for place in range(sections):

        @pl.when(section == place)
        def _():
            chosen = own if place == 0 else moved[place - 1]
            pair_ref[...] = chosen[...]
            rows_ref[...] = chosen[:, : rows_ref.shape[1]]


def critic_tail_kernel(count, sizes, fetches, pair, embed_w, *refs):
    mixed = refs[:count]
    heads_w, refs = nested(refs[count:], sizes)
    grads = refs[:count]
    inverse_ref, term_ref, target_ref, direct_ref, latent, work, other = refs[count:]
    late, final_t, noise, times = fetches
    model_width = embed_w.shape[2]
    latent_width = latent.shape[1]
    section = lax.axis_index("segment")

    @pl.when(section != 0)
    def _():
        for fetch in fetches:
            fetch.start()
        both = pair[...].astype(jnp.float32)
        sample = both[:, latent_width:]
        latent[...] = pair[:, :latent_width]
        result, inverse = tail(late, latent, embed_w, final_t, mixed, heads_w, work)
        mod, final_w = late.ready(), final_t.ready()
        _, critic_step = steps_of(times)
        sigma_critic = noise_level(critic_step)
        inverse_ref[...] = jnp.broadcast_to(inverse, inverse_ref.shape)
        term_ref[...] = (sigma_critic * result).astype(jnp.bfloat16)
        second = noise.ready()[:, latent_width:].astype(jnp.float32)
        target_ref[...] = jnp.where(
            section == 2,
            2.0 * (result - (second - sample)),
            jnp.where(section == 3, 1.0 / (1.0 + jnp.exp(-result)), 0.0),
        )

        @pl.when(section == 1)
        def _():
            gaps = jnp.abs(sample - both[:, :latent_width] + sigma_critic * result)
            error = jnp.sum(jnp.sum(gaps, axis=1, keepdims=True), axis=0, keepdims=True)
            error = error / (gaps.shape[0] * latent_width)
            error_top, error_low = halves(jnp.broadcast_to(error, (16, grads[0].shape[1])))
            for place in range(count):
                grads[place][:16] = error_top
                grads[place][16:32] = error_low

        @pl.when(section == 3)
        def _():
            grad_logit = (-1.0 / (1.0 + jnp.exp(result))).astype(jnp.bfloat16)
            plain, along = None, None
            for first in range(0, model_width, TILE):
                span = slice(first, first + TILE)
                gradient = dot32(grad_logit, final_w[:, span]) * (
                    1.0 + slot_of(mod, 2, model_width, first, TILE)
                )
                other[:, span] = gradient
                part = lane_sum(gradient)
                plain = part if plain is None else plain + part
                part = lane_sum(gradient * work[:, span])
                along = part if along is None else along + part
            plain = jnp.sum(plain, axis=1, keepdims=True) / model_width
            along = jnp.sum(along, axis=1, keepdims=True) / model_width
            direct = None
            totals = None
            for first in range(0, model_width, TILE):
                span = slice(first, first + TILE)
                grad_residual = inverse * (other[:, span] - plain - work[:, span] * along)
                top, low = halves(grad_residual)
                product = dot32_t(top, embed_w[0, :, span]) + dot32_t(low, embed_w[0, :, span])
                direct = product if direct is None else direct + product
                grad_attended = (slot_of(mod, 0, model_width, first, TILE) * grad_residual).astype(
                    jnp.bfloat16
                )
                product = dot32_t(grad_attended, stacked_tile(heads_w, first))
                totals = product if totals is None else totals + product
            direct_ref[...] = direct
            width = totals.shape[1] // count
            for place in range(count):
                grads[place][...] = totals[:, place * width : (place + 1) * width].astype(
                    jnp.bfloat16
                )


def judge_back_kernel(count, model_width, fetches, short_in, gram, gains, proj_ref, inverse_ref, key_ref, value_ref, term, *refs):
    rows = refs[:count]
    grads = refs[count : 2 * count]
    keep_ref, send_ref, real_ref, grad_key_ref, grad_value_ref, grad_query_ref = refs[2 * count :]
    section = lax.axis_index("segment")
    latent_width = rows[0].shape[1]
    head_width = gains.shape[2]
    scale = 1.0 / math.sqrt(head_width)
    size = rows[0].shape[0]

    @pl.when(section == 3)
    def _():
        for place in range(count):
            low = place * size
            span = slice(low, low + size)
            queries, _, _ = rms_scale(proj_ref[span, :head_width], gains[0, :1])
            query_b = queries.astype(jnp.bfloat16)
            weights = jnp.exp(dot32_t(query_b, key_ref[...]) * scale)
            soft_max = weights * (1.0 / jnp.sum(weights, axis=-1, keepdims=True))
            grad_out = grads[place][...]
            grad_soft = dot32_t(grad_out, value_ref[...])
            grad_value = dot32_first(soft_max.astype(jnp.bfloat16), grad_out)
            grad_scores = soft_max * (
                grad_soft - jnp.sum(soft_max * grad_soft, axis=-1, keepdims=True)
            )
            grad_scores_b = (grad_scores * scale).astype(jnp.bfloat16)
            grad_query_ref[span] = dot32(grad_scores_b, key_ref[...])
            grad_key = dot32_first(grad_scores_b, query_b)
            if place == 0:
                grad_value_ref[...] = grad_value
                grad_key_ref[...] = grad_key
            else:
                grad_value_ref[...] += grad_value
                grad_key_ref[...] += grad_key
        gram_top, gram_low = gram[0], gram[1]
        short_top, short_low = halves(short_in[:latent_width])
        for place in range(count):
            low = place * size
            span = slice(low, low + size)
            projected = proj_ref[span]
            _, q_unit, q_inverse = rms_scale(projected[:, :head_width], gains[0, :1])
            _, k_unit, k_inverse = rms_scale(
                projected[:, head_width : 2 * head_width], gains[0, 1:2]
            )
            grad_q = rms_back(grad_query_ref[span], q_unit, q_inverse, gains[0, :1])
            grad_k = rms_back(grad_key_ref[span], k_unit, k_inverse, gains[0, 1:2])
            grad_proj = jnp.concatenate([grad_q, grad_k, grad_value_ref[span]], axis=1).astype(
                jnp.bfloat16
            )
            through = dot32_t(grad_proj, short_top) + dot32_t(grad_proj, short_low)
            block = rows[place][...]
            along = jnp.sum(through * block.astype(jnp.float32), axis=1, keepdims=True) / model_width
            spanned = dot32(block, gram_top) + dot32(block, gram_low)
            inverse = inverse_ref[span, :1]
            target_ref = send_ref if place % 2 else keep_ref
            target_ref[place // 2] = (
                inverse * (through - spanned * (inverse * inverse * along))
            ).astype(jnp.bfloat16)

    @pl.when(section == 1)
    def _():
        error = None
        for grad in grads:
            part = grad[:16, :latent_width].astype(jnp.float32) + grad[
                16:32, :latent_width
            ].astype(jnp.float32)
            error = part if error is None else error + part
        real_ref[:size] = term[...]
        real_ref[size : size + 16], real_ref[size + 16 :] = halves(error / count + EPS)


def merge_kernel(fetches, direct, keep, moved, *outs):
    @pl.when(lax.axis_index("segment") == 3)
    def _():
        for place, out in enumerate(outs):
            total = keep[place].astype(jnp.float32) + moved[place].astype(jnp.float32)
            if place == 0:
                total = total + direct[...]
            out[...] = total.astype(jnp.bfloat16)


def outer_kernel(
    count,
    fetches,
    real,
    fake,
    target_in,
    student_rows,
    pair,
    student_mixed,
    student_inverse,
    critic_inverse,
    *refs,
):
    critic_mixed = refs[:count]
    arrived = refs[count : count + count // 2]
    sums_ref, sample_ref = refs[count + count // 2 :]
    section = lax.axis_index("segment")
    place = lax.axis_index("seq")
    latent_width = student_rows.shape[1]
    rows = student_rows.shape[0]

    def collect(target, inverse, latent, mixed):
        target = target.astype(jnp.bfloat16)
        weighted = inverse[:, :latent_width] * target.astype(jnp.float32)
        top, low = halves(weighted)
        for offset in range(count):
            piece = mixed[offset][...]
            sums_ref[place ^ offset] = (dot32_first(top, piece) + dot32_first(low, piece)).astype(
                jnp.bfloat16
            )
        near = dot32_first(top, latent) + dot32_first(low, latent)
        ones = jnp.ones((target.shape[0], sums_ref.shape[2] - latent_width), jnp.bfloat16)
        sums_ref[count] = jnp.concatenate([near, dot32_first(target, ones)], axis=1).astype(
            jnp.bfloat16
        )

    @pl.when(section == 0)
    def _():
        (times,) = fetches
        times.start()
        student_step, critic_step = steps_of(times)
        adverse = arrived[0][...].astype(jnp.float32)
        for part in arrived[1:]:
            adverse = adverse + part[...].astype(jnp.float32)
        adverse = (1.0 - noise_level(critic_step)) * adverse
        spread = (real[rows : rows + 1] .astype(jnp.float32) + real[rows + 16 : rows + 17].astype(jnp.float32))[
            :, :1
        ]
        gap = real[:rows].astype(jnp.float32) - fake[...].astype(jnp.float32)
        sample_grad = gap / spread + ADV_WEIGHT * adverse
        sample_ref[...] = sample_grad.astype(jnp.bfloat16)
        target = -noise_level(student_step) * sample_grad
        mixed = [student_mixed.at[offset] for offset in range(count)]
        collect(target, student_inverse, student_rows[...], mixed)

    @pl.when(section == 1)
    def _():
        sums_ref[...] = jnp.zeros_like(sums_ref)

    @pl.when(section >= 2)
    def _():
        collect(target_in[...], critic_inverse, pair[:, :latent_width], critic_mixed)


def emit_kernel(fetches, own, to_first, to_second, to_third, grad_ref):
    section = lax.axis_index("segment")
    for place, value in enumerate((own, to_first, to_second, to_third)):

        @pl.when(section == place)
        def _():
            grad_ref[...] = value[...].astype(jnp.float32).T


def expand_kernel(count, groups, sizes, full_rows, fetches, embed_w, *refs):
    heads_w, refs = nested(refs, sizes)
    other_mods = refs[: groups - 1]
    sums = refs[groups - 1 : 3 * groups - 1]
    total_ref, work, joined = refs[3 * groups - 1 :]
    section = lax.axis_index("segment")
    place = lax.axis_index("seq")
    latent_width = embed_w.shape[1]
    model_width = embed_w.shape[2]

    @pl.when(section == 1)
    def _():
        total_ref[...] = jnp.zeros_like(total_ref)

    @pl.when(section != 1)
    def _():
        (late,) = fetches
        late.start()
        for group in range(groups):
            low = group * latent_width
            joined[:, low : low + latent_width] = sums[2 * group][...].astype(jnp.float32) + sums[
                2 * group + 1
            ][...].astype(jnp.float32)
        near_top = joined[count].astype(jnp.bfloat16)
        heads = jnp.concatenate(
            [joined[place ^ offset].astype(jnp.bfloat16) for offset in range(count)], axis=1
        )
        averages = None
        for first in range(0, model_width, TILE):
            span = slice(first, first + TILE)
            spread = dot32(heads, stacked_tile(heads_w, first))
            near = dot32(near_top[:, :latent_width], embed_w[0, :, span])
            mods = [late.ready(), *other_mods]
            gates = jnp.concatenate(
                [
                    jnp.broadcast_to(
                        slot_of(mod, 0, model_width, first, TILE), (latent_width, TILE)
                    )
                    for mod in mods
                ],
                axis=0,
            )
            value = near + gates * spread
            work[:, span] = value
            part = lane_sum(value)
            averages = part if averages is None else averages + part
        averages = jnp.sum(averages, axis=1, keepdims=True) / model_width
        counts = joined[count][:, latent_width : latent_width + 1]
        for first in range(0, model_width, TILE):
            span = slice(first, first + TILE)
            value = work[:, span] - averages
            total = None
            for group in range(groups):
                mine = slice(group * latent_width, (group + 1) * latent_width)
                product = value[mine] * (
                    1.0 + slot_of(mods[group], 2, model_width, first, TILE)
                ) + counts[mine] * slot_of(mods[group], 1, model_width, first, TILE)
                total = product if total is None else total + product
            total_ref[:, span] = total / full_rows


def step(
    clean, noise, timesteps, text_vec, w_embed, w_time, w_mod, w_qkv, w_out, qk_gain, w_final
):
    sections = lax.axis_size("segment")
    tok_rows = clean.shape[1]
    latent_width = clean.shape[2]
    model_width = w_embed.shape[2]
    mod_width = w_mod.shape[2]
    count = lax.axis_size("seq")
    full_rows = tok_rows * count
    head_width = w_qkv.shape[4]
    bf16, f32 = jnp.bfloat16, jnp.float32
    kind_w = jnp.transpose(w_qkv[0, :, 0], (1, 0, 2))
    final_w = jnp.transpose(w_final[0])
    groups = lax.axis_size("dp")

    def stage(near):
        rows, width = near.shape
        (part,) = run(stage_kernel, [array((rows, width // 2), bf16)], (near,), 1000)
        return part

    heads_w = spread_heads(w_out[0, 0], count, groups, stage)
    sizes = [len(pieces) for pieces in heads_w]
    heads_w = sum(heads_w, [])

    depth = packed_rows(mod_width)
    packed, noisy_student, kind_w, gram = run(
        condition_kernel,
        [
            array((tok_rows // 2 + 2 * depth, 2 * latent_width), bf16),
            array((tok_rows, latent_width), bf16),
            pltpu.VMEM(kind_w.shape, bf16),
            array((2, latent_width, latent_width), bf16),
        ],
        (),
        2 * model_width * mod_width,
        scratch=(
            pltpu.VMEM((model_width, mod_width), bf16),
            pltpu.VMEM((depth, 128), f32),
            pltpu.SemaphoreType.DMA((STREAMS + 1,)),
        ),
        fetched=(timesteps, text_vec, w_time[0], jnp.transpose(clean[0]), noise[0], w_embed),
        streamed=(w_mod[0], kind_w),
    )
    kind_w = pltpu.with_memory_space_constraint(kind_w, pltpu.VMEM)
    packed_all = gather_near(packed, "seq", count)

    head_blocks = [array((tok_rows, head_width), bf16)] * count
    stored = [
        ((full_rows, 3 * head_width), f32),
        ((full_rows, 128), f32),
        ((full_rows, head_width), bf16),
        ((full_rows, head_width), bf16),
    ]
    short_shape = ((latent_width + 16, 3 * head_width), f32)
    *head_outs, short, late_mod = run(
        functools.partial(student_front_kernel, count, mod_width),
        head_blocks + [pltpu.VMEM(*short_shape)],
        (w_embed, kind_w, gram, qk_gain, *packed_all),
        4 * latent_width * model_width * 3 * head_width,
        scratch=[
            pltpu.VMEM((1, 5 * model_width), f32),
            pltpu.VMEM((count, tok_rows, latent_width), bf16),
            pltpu.SemaphoreType.DMA((1,)),
        ]
        + [pltpu.VMEM(shape, kind) for shape, kind in stored],
        sent=[array((1, 3 * model_width), f32)],
    )
    student_mixed = scatter_near(head_outs, "seq", count)
    late_mods = gather_near(late_mod, "dp", groups)
    work = pltpu.VMEM((tok_rows, model_width), f32)
    inverse_shape = array((tok_rows, 128), f32)
    pair, saved, student_inverse = run(
        functools.partial(student_tail_kernel, count, sizes),
        [array((tok_rows, 2 * latent_width), bf16)],
        (noisy_student, w_embed, *student_mixed, *heads_w),
        2 * tok_rows * model_width * head_width * count,
        scratch=(
            work,
            pltpu.VMEM((tok_rows, 128), f32),
            pltpu.SemaphoreType.DMA((count + 1,)),
        ),
        fetched=(late_mod, final_w, noise[0], timesteps),
        sent=[array((count, tok_rows, head_width), bf16), inverse_shape],
    )
    moved = [lax.ppermute(pair, "segment", [(0, place)]) for place in range(1, sections)]
    pair, own_rows = run(
        functools.partial(pick_kernel, sections),
        [
            array((tok_rows, 2 * latent_width), bf16),
            array((tok_rows, latent_width), bf16),
        ],
        (pair, *moved),
        1000,
    )
    critic_rows = gather_near(own_rows, "seq", count)
    *head_outs, proj, inverse, keys, values = run(
        functools.partial(critic_front_kernel, count, model_width),
        head_blocks + [array(shape, kind) for shape, kind in stored],
        (
            pltpu.with_memory_space_constraint(short, pltpu.VMEM),
            gram,
            qk_gain,
            *critic_rows,
        ),
        4 * latent_width * model_width * full_rows,
    )
    critic_mixed = scatter_near(head_outs, "seq", count)
    small = array((tok_rows, latent_width), f32)
    thin = array((tok_rows, latent_width), bf16)
    *grad_heads, critic_inverse, term_rows, target, direct = run(
        functools.partial(critic_tail_kernel, count, sizes),
        head_blocks + [inverse_shape, thin, small, small],
        (pair, w_embed, *critic_mixed, *heads_w),
        4 * tok_rows * model_width * head_width * count,
        scratch=(pltpu.VMEM((tok_rows, latent_width), bf16), work, work),
        fetched=(late_mod, final_w, noise[0], timesteps),
    )
    grad_blocks = scatter_near(grad_heads, "seq", count)
    fake = lax.ppermute(term_rows, "segment", swaps(sections, 2))
    half = count // 2
    rows_shape = array((half, tok_rows, latent_width), bf16)
    keep, away, real = run(
        functools.partial(judge_back_kernel, count, model_width),
        [rows_shape, rows_shape, array((tok_rows + 32, latent_width), bf16)],
        (short, gram, qk_gain, proj, inverse, keys, values, term_rows, *critic_rows, *grad_blocks),
        10 * full_rows * full_rows * head_width,
        scratch=(pltpu.VMEM((full_rows, head_width), f32),) * 3,
    )
    moved = lax.ppermute(away, "seq", swaps(count, 1))
    real = lax.ppermute(real, "segment", swaps(sections, 1))
    parts = run(merge_kernel, [thin] * half, (direct, keep, moved), 1000)
    to_student = [
        lax.ppermute(
            part,
            ("segment", "seq"),
            [
                (place * count + row, (place + 1) % sections * count + (row ^ (2 * index)))
                for place in range(sections)
                for row in range(count)
            ],
        )
        for index, part in enumerate(parts)
    ]
    sums, sample_grad = run(
        functools.partial(outer_kernel, count),
        [array((count + 1, latent_width, 128), bf16), thin],
        (
            real,
            fake,
            target,
            noisy_student,
            pair,
            saved,
            student_inverse,
            critic_inverse,
            *critic_mixed,
            *to_student,
        ),
        2 * tok_rows * latent_width * head_width * (count + 1),
        fetched=(timesteps,),
    )
    ends = [(place, sections - 1 - place) for place in range(sections)]
    to_third = lax.ppermute(sample_grad, "segment", ends)
    to_second = lax.ppermute(sample_grad, "segment", swaps(sections, 2))
    to_first = lax.ppermute(sample_grad, "segment", swaps(sections, 1))
    last = count // 2
    bit = 1
    while bit < last:
        moved = lax.ppermute(sums, "seq", swaps(count, bit))
        sums = (sums.astype(f32) + moved.astype(f32)).astype(bf16)
        bit *= 2
    sums_all = []
    for group in range(groups):
        for offset in (0, last):
            moves = [
                (place * groups + batch, (place ^ offset) * groups + (batch ^ group))
                for place in range(count)
                for batch in range(groups)
            ]
            sums_all.append(
                sums if offset == group == 0 else lax.ppermute(sums, ("seq", "dp"), moves)
            )
    (total_t,) = run(
        functools.partial(expand_kernel, count, groups, sizes, full_rows),
        [array((latent_width, model_width), f32)],
        (
            w_embed,
            *heads_w,
            *late_mods[1:],
            *sums_all,
        ),
        4 * groups * latent_width * model_width * head_width * count,
        scratch=(
            pltpu.VMEM((groups * latent_width, model_width), f32),
            pltpu.VMEM((count + 1, groups * latent_width, 128), f32),
        ),
        fetched=(late_mod,),
    )
    (grad_t,) = run(
        emit_kernel,
        [array((latent_width, tok_rows), f32)],
        (sample_grad, to_first, to_second, to_third),
        1000,
    )
    return (jnp.transpose(grad_t)[None], jnp.transpose(total_t)[None])


def solution(mesh):
    placed = (
        P("dp", "seq", None),
        P("dp", "seq", None),
        P(),
        P("dp", None),
        P("segment", None, None),
        P("segment", None, None),
        P("segment", None, "seq"),
        P("segment", None, "seq", None, None),
        P("segment", "seq", None, None),
        P("segment", None, None),
        P("segment", None, None),
    )
    return jax.shard_map(
        step,
        mesh=mesh,
        in_specs=placed,
        out_specs=(P("dp", "seq", None), P("segment", None, None)),
        check_vma=False,
    )
```

```python
import functools
import math

import jax
import jax.numpy as jnp
from jax import lax
from jax.experimental import pallas as pl
from jax.experimental.pallas import tpu as pltpu
from jax.sharding import PartitionSpec as P


SHIFT = 7.0
EPS = 1e-06
ADV_WEIGHT = 3.0
TILE = 512
STREAMS = 6
SPARE = 8 << 20
VMEM = pl.BlockSpec(memory_space=pltpu.VMEM)
HBM = pl.BlockSpec(memory_space=pltpu.HBM)


def halves(values):
    top = values.astype(jnp.bfloat16)
    return (top, (values - top.astype(jnp.float32)).astype(jnp.bfloat16))


def swaps(count, offset):
    return [(place, place ^ offset) for place in range(count)]


def gather_near(value, axis, count):
    return [value] + [lax.ppermute(value, axis, swaps(count, offset)) for offset in range(1, count)]


def scatter_near(blocks, axis, count):
    return [blocks[0]] + [
        lax.ppermute(blocks[offset], axis, swaps(count, offset))
        for offset in range(1, count)
    ]


def spread_heads(own, count, groups, stage):
    held = {0: [own]}
    bit = count // 2
    first = True
    while bit:
        for offset in sorted(held):
            if first and groups == 2:
                width = own.shape[1] // 3
                shift = lax.axis_index("dp") * width
                part = lax.dynamic_slice_in_dim(own, shift, 2 * width, axis=1)
                near = lax.ppermute(part, "seq", swaps(count, bit))
                held[bit] = [near, lax.ppermute(stage(near), "dp", swaps(groups, 1))]
            else:
                held[offset | bit] = [
                    lax.ppermute(piece, "seq", swaps(count, bit))
                    for piece in held[offset]
                ]
        first = False
        bit //= 2
    return [held[offset] for offset in range(count)]


def head_tile(pieces, first, size):
    if len(pieces) == 1:
        return pieces[0][:, first : first + size]
    near, far = pieces
    width = far.shape[1]
    low = slice(first % width, first % width + size)
    high = slice(width + first % width, width + first % width + size)
    choices = (
        (near[:, low], far[:, low]),
        (near[:, high], near[:, low]),
        (far[:, low], near[:, high]),
    )[first // width]
    return jnp.where(lax.axis_index("dp") == 0, *choices)


def stacked_tile(heads_w, first):
    return jnp.concatenate([head_tile(pieces, first, TILE) for pieces in heads_w], axis=0)


def nested(refs, sizes):
    groups, first = [], 0
    for size in sizes:
        groups.append(refs[first : first + size])
        first += size
    return (groups, refs[first:])


def in_order(pieces, own_place):
    ordered = list(pieces)
    bit = 1
    while bit < len(ordered):
        flipped = (own_place & bit) != 0
        ordered = [
            jnp.where(flipped, ordered[place ^ bit], ordered[place])
            for place in range(len(ordered))
        ]
        bit *= 2
    return ordered


def dot32(left, right):
    return jnp.dot(left, right, preferred_element_type=jnp.float32)


def dot32_t(left, right):
    return lax.dot_general(
        left, right, (((1,), (1,)), ((), ())), preferred_element_type=jnp.float32
    )


def dot32_first(left, right):
    return lax.dot_general(
        left, right, (((0,), (0,)), ((), ())), preferred_element_type=jnp.float32
    )


def steps_of(times):
    times_ref = times.ready()
    place = lax.axis_index("dp")
    return (times_ref[place, 0], times_ref[place, 1])


def noise_level(step):
    fraction = jnp.full((1, 1), step, jnp.int32).astype(jnp.float32) / 1000.0
    return SHIFT * fraction / (1.0 + (SHIFT - 1.0) * fraction)


def slot_of(mod_ref, slot, width, first, size):
    return mod_ref[:, slot * width + first : slot * width + first + size]


def lane_sum(values):
    total = values[:, :128]
    for first in range(128, values.shape[1], 128):
        total = total + values[:, first : first + 128]
    return total


class Fetch:
    def __init__(self, source, target, arrival):
        self.copy = pltpu.make_async_copy(source, target, arrival)
        self.target = target
        self.waiting = True

    def start(self):
        self.copy.start()

    def ready(self):
        if self.waiting:
            self.copy.wait()
            self.waiting = False
        return self.target


def bytes_of(items):
    return sum(math.prod(item.shape) * jnp.dtype(item.dtype).itemsize for item in items)


def in_hbm(item):
    return pltpu.with_memory_space_constraint(item, pltpu.HBM)


def run(kernel, outputs, operands, flops, scratch=(), fetched=(), streamed=(), sent=()):
    inputs = len(operands)
    total = inputs + len(fetched) + len(streamed)
    results = len(outputs) + len(sent)

    def body(*refs):
        sources = refs[inputs:total]
        outs = refs[total : total + results]
        own = refs[total + results : total + results + len(scratch)]
        rest = refs[total + results + len(scratch) :]
        fetches = [
            Fetch(source, target, rest[-1].at[place])
            for place, (source, target) in enumerate(zip(sources, rest[:-1]))
        ]
        fetches += sources[len(fetched) :]
        kernel(fetches, *refs[:inputs], *outs, *own)

    places = [
        (pltpu.SMEM if item.dtype == jnp.int32 else pltpu.VMEM)(item.shape, item.dtype)
        for item in fetched
    ]
    held = bytes_of(
        [ref for ref in list(scratch) + places if ref.memory_space == pltpu.VMEM]
    )
    limit = min(60 << 20, SPARE + held + bytes_of(operands) + 2 * bytes_of(outputs))
    return pl.pallas_call(
        body,
        out_shape=list(outputs) + [pltpu.HBM(item.shape, item.dtype) for item in sent],
        in_specs=[VMEM] * inputs + [HBM] * (total - inputs),
        out_specs=[VMEM] * len(outputs) + [HBM] * len(sent),
        scratch_shapes=list(scratch)
        + places
        + [pltpu.SemaphoreType.DMA((max(1, len(fetched)),))],
        compiler_params=pltpu.CompilerParams(vmem_limit_bytes=limit),
        cost_estimate=pl.CostEstimate(
            flops=flops,
            bytes_accessed=bytes_of(list(operands) + list(fetched) + list(outputs)),
            transcendentals=0,
        ),
    )(*operands, *[in_hbm(item) for item in (*fetched, *streamed)])


def array(shape, dtype):
    return jax.ShapeDtypeStruct(shape, dtype)


def packed_rows(width):
    return -(-width // 2048) * 16


def condition_kernel(fetches, packed_out, noisy_out, kind_out, gram_out, held, mod_rows, arrivals):
    times, text, time_w, clean_t, noise, embed_w, mod_w, kind_w = fetches
    model_width = held.shape[0]
    rows = model_width // STREAMS
    for fetch in fetches[:-2]:
        fetch.start()
    copies = [
        pltpu.make_async_copy(
            mod_w.at[pl.ds(part * rows, rows)], held.at[pl.ds(part * rows, rows)], arrivals.at[part]
        )
        for part in range(STREAMS)
    ]
    copies.append(pltpu.make_async_copy(kind_w, kind_out, arrivals.at[STREAMS]))
    for copy in copies:
        copy.start()
    student_step, critic_step = steps_of(times)
    step = jnp.where(lax.axis_index("segment") == 0, student_step, critic_step)
    text_ref = text.ready()
    half = text_ref.shape[1] // 2
    places = lax.broadcasted_iota(jnp.int32, (1, half), 1).astype(jnp.float32)
    frequency = jnp.exp(-math.log(10000.0) * places / half)
    angles = jnp.full((1, half), step, jnp.int32).astype(jnp.float32) * frequency
    features = jnp.concatenate([jnp.cos(angles), jnp.sin(angles)], axis=1) + text_ref[...]
    features = jnp.broadcast_to(features, (8, 2 * half)).astype(jnp.bfloat16)
    hidden = dot32(features, time_w.ready()[...])
    hidden = (hidden / (1.0 + jnp.exp(-hidden))).astype(jnp.bfloat16)
    mod_rows[...] = jnp.zeros_like(mod_rows)
    total = None
    for part in range(STREAMS):
        copies[part].wait()
        piece = dot32(
            hidden[:, part * rows : (part + 1) * rows], held[part * rows : (part + 1) * rows]
        )
        total = piece if total is None else total + piece
        if part == STREAMS // 2:
            sigma_student = noise_level(student_step)
            clean_ref, noise_ref = clean_t.ready(), noise.ready()
            noisy = (1.0 - sigma_student) * clean_ref[...].astype(jnp.float32).T + sigma_student * noise_ref[
                :, : clean_ref.shape[0]
            ].astype(jnp.float32)
            noisy = noisy.astype(jnp.bfloat16)
            noisy_out[...] = noisy
            top = noisy.shape[0] // 2
            packed_out[:top] = jnp.concatenate([noisy[:top], noisy[top:]], axis=1)
            central_top, central_low = halves(centred(embed_w.ready()))
            gram = (
                dot32_t(central_top, central_top)
                + dot32_t(central_top, central_low)
                + dot32_t(central_low, central_top)
            )
            gram_out[0], gram_out[1] = halves(gram)
    width = total.shape[1]
    for row, first in enumerate(range(0, width, 128)):
        size = min(128, width - first)
        mod_rows[row : row + 1, :size] = total[:1, first : first + size]
    depth = mod_rows.shape[0]
    top = noisy_out.shape[0] // 2
    packed_out[top : top + depth], packed_out[top + depth :] = halves(mod_rows[...])
    copies[STREAMS].wait()


def rms_scale(values, gain_vec):
    inverse = lax.rsqrt(jnp.mean(values * values, axis=-1, keepdims=True) + EPS)
    unit_vec = values * inverse
    return (unit_vec * gain_vec, unit_vec, inverse)


def rms_back(gradient, unit_vec, inverse, gain_vec):
    scaled = gradient * gain_vec
    return inverse * (scaled - unit_vec * jnp.mean(scaled * unit_vec, axis=-1, keepdims=True))


def centred(embed_ref):
    values = embed_ref[0].astype(jnp.float32)
    return values - jnp.mean(values, axis=1, keepdims=True)


def front(rows, gram, model_width, short, gains, head_outs, proj_ref, inverse_ref, key_ref, value_ref):
    latent_width = gram.shape[1]
    count = len(rows)
    head_width = gains.shape[2]
    scale = 1.0 / math.sqrt(head_width)
    size = rows[0].shape[0]
    short_top = None
    for place in range(count):
        block = rows[place][...]
        spanned = dot32(block, gram[0]) + dot32(block, gram[1])
        squares = jnp.sum(spanned * block.astype(jnp.float32), axis=1, keepdims=True)
        inverse = lax.rsqrt(jnp.maximum(squares, 0.0) / model_width + EPS)
        if short_top is None:
            values = short()
            short_top, short_low = halves(values[:latent_width])
            short_shift = values[latent_width : latent_width + 1]
        projected = inverse * (dot32(block, short_top) + dot32(block, short_low)) + short_shift
        low = place * size
        proj_ref[low : low + size] = projected
        inverse_ref[low : low + size] = jnp.broadcast_to(inverse, (size, 128))
        keys, _, _ = rms_scale(projected[:, head_width : 2 * head_width], gains[0, 1:2])
        key_ref[low : low + size] = keys.astype(jnp.bfloat16)
        value_ref[low : low + size] = projected[:, 2 * head_width :].astype(jnp.bfloat16)
    for place in range(count):
        low = place * size
        queries, _, _ = rms_scale(proj_ref[low : low + size, :head_width], gains[0, :1])
        scores = dot32_t(queries.astype(jnp.bfloat16), key_ref[...]) * scale
        weights = jnp.exp(scores)
        soft_max = weights * (1.0 / jnp.sum(weights, axis=-1, keepdims=True))
        head_outs[place][...] = dot32(soft_max.astype(jnp.bfloat16), value_ref[...]).astype(
            jnp.bfloat16
        )


def stage_kernel(fetches, near, part_out):
    width = part_out.shape[1]
    for place in range(2):

        @pl.when(lax.axis_index("dp") == place)
        def _():
            part_out[...] = near[:, place * width : (place + 1) * width]


def student_front_kernel(count, width, fetches, embed_w, head_w, gram, gains, *refs):
    packed = refs[:count]
    head_outs = refs[count : 2 * count]
    short_out, late_out, mod, rows_ref, sends, *kept = refs[2 * count :]
    model_width = embed_w.shape[2]
    latent_width = embed_w.shape[1]
    size = rows_ref.shape[1]
    half = size // 2
    depth = packed_rows(width)
    parts = [
        piece[half : half + depth].astype(jnp.float32) + piece[half + depth :].astype(jnp.float32)
        for piece in packed
    ]
    for place, part in enumerate(in_order(parts, lax.axis_index("seq"))):
        for row, first in enumerate(range(0, width, 128)):
            lanes = min(128, width - first)
            low = place * width + first
            mod[:, low : low + lanes] = part[row : row + 1, :lanes]
    late = pltpu.make_async_copy(
        mod.at[:, pl.ds(2 * model_width, 3 * model_width)], late_out, sends.at[0]
    )
    late.start()
    for place in range(count):
        rows_ref[place, :half] = packed[place][:half, :latent_width]
        rows_ref[place, half:] = packed[place][:half, latent_width:]
    central = centred(embed_w)
    scale_in = slot_of(mod, 1, model_width, 0, model_width)
    shift_in = slot_of(mod, 0, model_width, 0, model_width)
    in_rows = jnp.concatenate(
        [central * (1.0 + scale_in), jnp.broadcast_to(shift_in, (16, model_width))], axis=0
    )
    in_top, in_low = halves(in_rows)
    in_both = jnp.concatenate([in_top, in_low], axis=0)
    both = jnp.concatenate([dot32(in_both, head_w[kind]) for kind in range(3)], axis=1)
    short = both[: in_rows.shape[0]] + both[in_rows.shape[0] :]
    short_out[...] = short

    @pl.when(lax.axis_index("segment") == 0)
    def _():
        front(
            [rows_ref.at[place] for place in range(count)],
            gram,
            model_width,
            lambda: short,
            gains,
            head_outs,
            *kept,
        )

    late.wait()


def critic_front_kernel(count, model_width, fetches, short, gram, gains, *refs):
    rows = refs[:count]
    head_outs = refs[count : 2 * count]
    kept = refs[2 * count :]

    @pl.when(lax.axis_index("segment") != 0)
    def _():
        front(
            rows,
            gram,
            model_width,
            lambda: short[...],
            gains,
            head_outs,
            *kept,
        )


def tail(late, latent, embed_w, final_t, mixed, heads_w, work):
    model_width = embed_w.shape[2]
    block = latent[...]
    joined_heads = jnp.concatenate([piece[...] for piece in mixed], axis=1)
    sums = None
    for first in range(0, model_width, TILE):
        span = slice(first, first + TILE)
        attended = dot32(joined_heads, stacked_tile(heads_w, first))
        mod = late.ready()
        residual = (
            dot32(block, embed_w[0, :, span]) + slot_of(mod, 0, model_width, first, TILE) * attended
        )
        work[:, span] = residual
        part = lane_sum(residual)
        sums = part if sums is None else sums + part
    row_mean = jnp.sum(sums, axis=1, keepdims=True) / model_width
    sums = None
    for first in range(0, model_width, TILE):
        span = slice(first, first + TILE)
        middle = work[:, span] - row_mean
        work[:, span] = middle
        part = lane_sum(middle * middle)
        sums = part if sums is None else sums + part
    inverse = lax.rsqrt(jnp.sum(sums, axis=1, keepdims=True) / model_width + EPS)
    result = None
    final_w = final_t.ready()
    for first in range(0, model_width, TILE):
        span = slice(first, first + TILE)
        normed = work[:, span] * inverse
        work[:, span] = normed
        final_in = (
            normed * (1.0 + slot_of(mod, 2, model_width, first, TILE))
            + slot_of(mod, 1, model_width, first, TILE)
        ).astype(jnp.bfloat16)
        product = dot32_t(final_in, final_w[:, span])
        result = product if result is None else result + product
    return (result, inverse)


def student_tail_kernel(count, sizes, fetches, latent, embed_w, *refs):
    mixed = refs[:count]
    heads_w, refs = nested(refs[count:], sizes)
    pair_ref, saved_out, inverse_out, work, inverse_ref, sends = refs
    late, final_t, noise, times = fetches
    latent_width = latent.shape[1]

    @pl.when(lax.axis_index("segment") == 0)
    def _():
        for fetch in fetches:
            fetch.start()
        copies = [
            pltpu.make_async_copy(mixed[place], saved_out.at[place], sends.at[place])
            for place in range(count)
        ]
        for copy in copies:
            copy.start()
        velocity, inverse = tail(late, latent, embed_w, final_t, mixed, heads_w, work)
        inverse_ref[...] = jnp.broadcast_to(inverse, inverse_ref.shape)
        copies.append(pltpu.make_async_copy(inverse_ref, inverse_out, sends.at[count]))
        copies[-1].start()
        student_step, critic_step = steps_of(times)
        sigma_student, sigma_critic = noise_level(student_step), noise_level(critic_step)
        sample = latent[...].astype(jnp.float32) - sigma_student * velocity
        second = noise.ready()[:, latent_width:].astype(jnp.float32)
        critic = (1.0 - sigma_critic) * sample + sigma_critic * second
        pair_ref[...] = jnp.concatenate([critic, sample], axis=1).astype(jnp.bfloat16)
        for copy in copies:
            copy.wait()


def pick_kernel(sections, fetches, own, *refs):
    moved = refs[: sections - 1]
    pair_ref, rows_ref = refs[sections - 1 :]
    section = lax.axis_index("segment")
    for place in range(sections):

        @pl.when(section == place)
        def _():
            chosen = own if place == 0 else moved[place - 1]
            pair_ref[...] = chosen[...]
            rows_ref[...] = chosen[:, : rows_ref.shape[1]]


def critic_tail_kernel(count, sizes, fetches, pair, embed_w, *refs):
    mixed = refs[:count]
    heads_w, refs = nested(refs[count:], sizes)
    grads = refs[:count]
    inverse_ref, term_ref, target_ref, direct_ref, latent, work, other = refs[count:]
    late, final_t, noise, times = fetches
    model_width = embed_w.shape[2]
    latent_width = latent.shape[1]
    section = lax.axis_index("segment")

    @pl.when(section != 0)
    def _():
        for fetch in fetches:
            fetch.start()
        both = pair[...].astype(jnp.float32)
        sample = both[:, latent_width:]
        latent[...] = pair[:, :latent_width]
        result, inverse = tail(late, latent, embed_w, final_t, mixed, heads_w, work)
        mod, final_w = late.ready(), final_t.ready()
        _, critic_step = steps_of(times)
        sigma_critic = noise_level(critic_step)
        inverse_ref[...] = jnp.broadcast_to(inverse, inverse_ref.shape)
        term_ref[...] = (sigma_critic * result).astype(jnp.bfloat16)
        second = noise.ready()[:, latent_width:].astype(jnp.float32)
        target_ref[...] = jnp.where(
            section == 2,
            2.0 * (result - (second - sample)),
            jnp.where(section == 3, 1.0 / (1.0 + jnp.exp(-result)), 0.0),
        )

        @pl.when(section == 1)
        def _():
            gaps = jnp.abs(sample - both[:, :latent_width] + sigma_critic * result)
            error = jnp.sum(jnp.sum(gaps, axis=1, keepdims=True), axis=0, keepdims=True)
            error = error / (gaps.shape[0] * latent_width)
            error_top, error_low = halves(jnp.broadcast_to(error, (16, grads[0].shape[1])))
            for place in range(count):
                grads[place][:16] = error_top
                grads[place][16:32] = error_low

        @pl.when(section == 3)
        def _():
            grad_logit = (-1.0 / (1.0 + jnp.exp(result))).astype(jnp.bfloat16)
            plain, along = None, None
            for first in range(0, model_width, TILE):
                span = slice(first, first + TILE)
                gradient = dot32(grad_logit, final_w[:, span]) * (
                    1.0 + slot_of(mod, 2, model_width, first, TILE)
                )
                other[:, span] = gradient
                part = lane_sum(gradient)
                plain = part if plain is None else plain + part
                part = lane_sum(gradient * work[:, span])
                along = part if along is None else along + part
            plain = jnp.sum(plain, axis=1, keepdims=True) / model_width
            along = jnp.sum(along, axis=1, keepdims=True) / model_width
            direct = None
            totals = None
            for first in range(0, model_width, TILE):
                span = slice(first, first + TILE)
                grad_residual = inverse * (other[:, span] - plain - work[:, span] * along)
                top, low = halves(grad_residual)
                product = dot32_t(top, embed_w[0, :, span]) + dot32_t(low, embed_w[0, :, span])
                direct = product if direct is None else direct + product
                grad_attended = (slot_of(mod, 0, model_width, first, TILE) * grad_residual).astype(
                    jnp.bfloat16
                )
                product = dot32_t(stacked_tile(heads_w, first), grad_attended)
                totals = product if totals is None else totals + product
            direct_ref[...] = direct
            width = totals.shape[0] // count
            for place in range(count):
                grads[place][...] = totals[place * width : (place + 1) * width].T.astype(
                    jnp.bfloat16
                )


def judge_back_kernel(count, model_width, fetches, short_in, gram, gains, proj_ref, inverse_ref, key_ref, value_ref, term, *refs):
    rows = refs[:count]
    grads = refs[count : 2 * count]
    keep_ref, send_ref, real_ref, grad_key_ref, grad_value_ref, grad_query_ref = refs[2 * count :]
    section = lax.axis_index("segment")
    latent_width = rows[0].shape[1]
    head_width = gains.shape[2]
    scale = 1.0 / math.sqrt(head_width)
    size = rows[0].shape[0]

    @pl.when(section == 3)
    def _():
        for place in range(count):
            low = place * size
            span = slice(low, low + size)
            queries, _, _ = rms_scale(proj_ref[span, :head_width], gains[0, :1])
            query_b = queries.astype(jnp.bfloat16)
            weights = jnp.exp(dot32_t(query_b, key_ref[...]) * scale)
            soft_max = weights * (1.0 / jnp.sum(weights, axis=-1, keepdims=True))
            grad_out = grads[place][...]
            grad_soft = dot32_t(grad_out, value_ref[...])
            grad_value = dot32_first(soft_max.astype(jnp.bfloat16), grad_out)
            grad_scores = soft_max * (
                grad_soft - jnp.sum(soft_max * grad_soft, axis=-1, keepdims=True)
            )
            grad_scores_b = (grad_scores * scale).astype(jnp.bfloat16)
            grad_query_ref[span] = dot32(grad_scores_b, key_ref[...])
            grad_key = dot32_first(grad_scores_b, query_b)
            if place == 0:
                grad_value_ref[...] = grad_value
                grad_key_ref[...] = grad_key
            else:
                grad_value_ref[...] += grad_value
                grad_key_ref[...] += grad_key
        gram_top, gram_low = gram[0], gram[1]
        short_top, short_low = halves(short_in[:latent_width])
        for place in range(count):
            low = place * size
            span = slice(low, low + size)
            projected = proj_ref[span]
            _, q_unit, q_inverse = rms_scale(projected[:, :head_width], gains[0, :1])
            _, k_unit, k_inverse = rms_scale(
                projected[:, head_width : 2 * head_width], gains[0, 1:2]
            )
            grad_q = rms_back(grad_query_ref[span], q_unit, q_inverse, gains[0, :1])
            grad_k = rms_back(grad_key_ref[span], k_unit, k_inverse, gains[0, 1:2])
            grad_proj = jnp.concatenate([grad_q, grad_k, grad_value_ref[span]], axis=1).astype(
                jnp.bfloat16
            )
            through = dot32_t(grad_proj, short_top) + dot32_t(grad_proj, short_low)
            block = rows[place][...]
            along = jnp.sum(through * block.astype(jnp.float32), axis=1, keepdims=True) / model_width
            spanned = dot32(block, gram_top) + dot32(block, gram_low)
            inverse = inverse_ref[span, :1]
            target_ref = send_ref if place % 2 else keep_ref
            target_ref[place // 2] = (
                inverse * (through - spanned * (inverse * inverse * along))
            ).astype(jnp.bfloat16)

    @pl.when(section == 1)
    def _():
        error = None
        for grad in grads:
            part = grad[:16, :latent_width].astype(jnp.float32) + grad[
                16:32, :latent_width
            ].astype(jnp.float32)
            error = part if error is None else error + part
        real_ref[:size] = term[...]
        real_ref[size : size + 16], real_ref[size + 16 :] = halves(error / count + EPS)


def merge_kernel(fetches, direct, keep, moved, *outs):
    @pl.when(lax.axis_index("segment") == 3)
    def _():
        for place, out in enumerate(outs):
            total = keep[place].astype(jnp.float32) + moved[place].astype(jnp.float32)
            if place == 0:
                total = total + direct[...]
            out[...] = total.astype(jnp.bfloat16)


def outer_kernel(
    count,
    fetches,
    real,
    fake,
    target_in,
    student_rows,
    pair,
    student_mixed,
    student_inverse,
    critic_inverse,
    *refs,
):
    critic_mixed = refs[:count]
    arrived = refs[count : count + count // 2]
    sums_ref, sample_ref = refs[count + count // 2 :]
    section = lax.axis_index("segment")
    place = lax.axis_index("seq")
    latent_width = student_rows.shape[1]
    rows = student_rows.shape[0]

    def collect(target, inverse, latent, mixed):
        target = target.astype(jnp.bfloat16)
        weighted = inverse[:, :latent_width] * target.astype(jnp.float32)
        top, low = halves(weighted)
        for offset in range(count):
            piece = mixed[offset][...]
            sums_ref[place ^ offset] = (dot32_first(top, piece) + dot32_first(low, piece)).astype(
                jnp.bfloat16
            )
        near = dot32_first(top, latent) + dot32_first(low, latent)
        ones = jnp.ones((target.shape[0], sums_ref.shape[2] - latent_width), jnp.bfloat16)
        sums_ref[count] = jnp.concatenate([near, dot32_first(target, ones)], axis=1).astype(
            jnp.bfloat16
        )

    @pl.when(section == 0)
    def _():
        (times,) = fetches
        times.start()
        student_step, critic_step = steps_of(times)
        adverse = arrived[0][...].astype(jnp.float32)
        for part in arrived[1:]:
            adverse = adverse + part[...].astype(jnp.float32)
        adverse = (1.0 - noise_level(critic_step)) * adverse
        spread = (real[rows : rows + 1] .astype(jnp.float32) + real[rows + 16 : rows + 17].astype(jnp.float32))[
            :, :1
        ]
        gap = real[:rows].astype(jnp.float32) - fake[...].astype(jnp.float32)
        sample_grad = gap / spread + ADV_WEIGHT * adverse
        sample_ref[...] = sample_grad.astype(jnp.bfloat16)
        target = -noise_level(student_step) * sample_grad
        mixed = [student_mixed.at[offset] for offset in range(count)]
        collect(target, student_inverse, student_rows[...], mixed)

    @pl.when(section == 1)
    def _():
        sums_ref[...] = jnp.zeros_like(sums_ref)

    @pl.when(section >= 2)
    def _():
        collect(target_in[...], critic_inverse, pair[:, :latent_width], critic_mixed)


def emit_kernel(fetches, own, to_first, to_second, to_third, grad_ref):
    section = lax.axis_index("segment")
    for place, value in enumerate((own, to_first, to_second, to_third)):

        @pl.when(section == place)
        def _():
            grad_ref[...] = value[...].astype(jnp.float32).T


def expand_kernel(count, groups, sizes, full_rows, fetches, embed_w, *refs):
    heads_w, refs = nested(refs, sizes)
    other_mods = refs[: groups - 1]
    sums = refs[groups - 1 : 3 * groups - 1]
    total_out, work, joined, total_ref, sends = refs[3 * groups - 1 :]
    section = lax.axis_index("segment")
    place = lax.axis_index("seq")
    latent_width = embed_w.shape[1]
    model_width = embed_w.shape[2]

    @pl.when(section == 1)
    def _():
        total_ref[...] = jnp.zeros_like(total_ref)
        copy = pltpu.make_async_copy(total_ref, total_out, sends.at[0])
        copy.start()
        copy.wait()

    @pl.when(section != 1)
    def _():
        (late,) = fetches
        late.start()
        for group in range(groups):
            low = group * latent_width
            joined[:, low : low + latent_width] = sums[2 * group][...].astype(jnp.float32) + sums[
                2 * group + 1
            ][...].astype(jnp.float32)
        near_top = joined[count].astype(jnp.bfloat16)
        heads = jnp.concatenate(
            [joined[place ^ offset].astype(jnp.bfloat16) for offset in range(count)], axis=1
        )
        averages = None
        for first in range(0, model_width, TILE):
            span = slice(first, first + TILE)
            spread = dot32(heads, stacked_tile(heads_w, first))
            near = dot32(near_top[:, :latent_width], embed_w[0, :, span])
            mods = [late.ready(), *other_mods]
            gates = jnp.concatenate(
                [
                    jnp.broadcast_to(
                        slot_of(mod, 0, model_width, first, TILE), (latent_width, TILE)
                    )
                    for mod in mods
                ],
                axis=0,
            )
            value = near + gates * spread
            work[:, span] = value
            part = lane_sum(value)
            averages = part if averages is None else averages + part
        averages = jnp.sum(averages, axis=1, keepdims=True) / model_width
        counts = joined[count][:, latent_width : latent_width + 1]
        copies = []
        for number, first in enumerate(range(0, model_width, TILE)):
            span = slice(first, first + TILE)
            value = work[:, span] - averages
            total = None
            for group in range(groups):
                mine = slice(group * latent_width, (group + 1) * latent_width)
                product = value[mine] * (
                    1.0 + slot_of(mods[group], 2, model_width, first, TILE)
                ) + counts[mine] * slot_of(mods[group], 1, model_width, first, TILE)
                total = product if total is None else total + product
            total_ref[:, span] = total / full_rows
            area = (slice(None), pl.ds(first, TILE))
            copies.append(
                pltpu.make_async_copy(total_ref.at[area], total_out.at[area], sends.at[number])
            )
            copies[-1].start()
        for copy in copies:
            copy.wait()


def step(
    clean, noise, timesteps, text_vec, w_embed, w_time, w_mod, w_qkv, w_out, qk_gain, w_final
):
    sections = lax.axis_size("segment")
    tok_rows = clean.shape[1]
    latent_width = clean.shape[2]
    model_width = w_embed.shape[2]
    mod_width = w_mod.shape[2]
    count = lax.axis_size("seq")
    full_rows = tok_rows * count
    head_width = w_qkv.shape[4]
    bf16, f32 = jnp.bfloat16, jnp.float32
    kind_w = jnp.transpose(w_qkv[0, :, 0], (1, 0, 2))
    final_w = jnp.transpose(w_final[0])
    groups = lax.axis_size("dp")

    def stage(near):
        rows, width = near.shape
        (part,) = run(stage_kernel, [array((rows, width // 2), bf16)], (near,), 1000)
        return part

    heads_w = spread_heads(w_out[0, 0], count, groups, stage)
    sizes = [len(pieces) for pieces in heads_w]
    heads_w = sum(heads_w, [])

    depth = packed_rows(mod_width)
    packed, noisy_student, kind_w, gram = run(
        condition_kernel,
        [
            array((tok_rows // 2 + 2 * depth, 2 * latent_width), bf16),
            array((tok_rows, latent_width), bf16),
            pltpu.VMEM(kind_w.shape, bf16),
            array((2, latent_width, latent_width), bf16),
        ],
        (),
        2 * model_width * mod_width,
        scratch=(
            pltpu.VMEM((model_width, mod_width), bf16),
            pltpu.VMEM((depth, 128), f32),
            pltpu.SemaphoreType.DMA((STREAMS + 1,)),
        ),
        fetched=(timesteps, text_vec, w_time[0], jnp.transpose(clean[0]), noise[0], w_embed),
        streamed=(w_mod[0], kind_w),
    )
    kind_w = pltpu.with_memory_space_constraint(kind_w, pltpu.VMEM)
    packed_all = gather_near(packed, "seq", count)

    head_blocks = [array((tok_rows, head_width), bf16)] * count
    stored = [
        ((full_rows, 3 * head_width), f32),
        ((full_rows, 128), f32),
        ((full_rows, head_width), bf16),
        ((full_rows, head_width), bf16),
    ]
    short_shape = ((latent_width + 16, 3 * head_width), f32)
    *head_outs, short, late_mod = run(
        functools.partial(student_front_kernel, count, mod_width),
        head_blocks + [pltpu.VMEM(*short_shape)],
        (w_embed, kind_w, gram, qk_gain, *packed_all),
        4 * latent_width * model_width * 3 * head_width,
        scratch=[
            pltpu.VMEM((1, 5 * model_width), f32),
            pltpu.VMEM((count, tok_rows, latent_width), bf16),
            pltpu.SemaphoreType.DMA((1,)),
        ]
        + [pltpu.VMEM(shape, kind) for shape, kind in stored],
        sent=[array((1, 3 * model_width), f32)],
    )
    student_mixed = scatter_near(head_outs, "seq", count)
    late_mods = gather_near(late_mod, "dp", groups)
    work = pltpu.VMEM((tok_rows, model_width), f32)
    inverse_shape = array((tok_rows, 128), f32)
    pair, saved, student_inverse = run(
        functools.partial(student_tail_kernel, count, sizes),
        [array((tok_rows, 2 * latent_width), bf16)],
        (noisy_student, w_embed, *student_mixed, *heads_w),
        2 * tok_rows * model_width * head_width * count,
        scratch=(
            work,
            pltpu.VMEM((tok_rows, 128), f32),
            pltpu.SemaphoreType.DMA((count + 1,)),
        ),
        fetched=(late_mod, final_w, noise[0], timesteps),
        sent=[array((count, tok_rows, head_width), bf16), inverse_shape],
    )
    moved = [lax.ppermute(pair, "segment", [(0, place)]) for place in range(1, sections)]
    pair, own_rows = run(
        functools.partial(pick_kernel, sections),
        [
            array((tok_rows, 2 * latent_width), bf16),
            array((tok_rows, latent_width), bf16),
        ],
        (pair, *moved),
        1000,
    )
    critic_rows = gather_near(own_rows, "seq", count)
    *head_outs, proj, inverse, keys, values = run(
        functools.partial(critic_front_kernel, count, model_width),
        head_blocks + [array(shape, kind) for shape, kind in stored],
        (
            pltpu.with_memory_space_constraint(short, pltpu.VMEM),
            gram,
            qk_gain,
            *critic_rows,
        ),
        4 * latent_width * model_width * full_rows,
    )
    critic_mixed = scatter_near(head_outs, "seq", count)
    small = array((tok_rows, latent_width), f32)
    thin = array((tok_rows, latent_width), bf16)
    *grad_heads, critic_inverse, term_rows, target, direct = run(
        functools.partial(critic_tail_kernel, count, sizes),
        head_blocks + [inverse_shape, thin, small, small],
        (pair, w_embed, *critic_mixed, *heads_w),
        4 * tok_rows * model_width * head_width * count,
        scratch=(pltpu.VMEM((tok_rows, latent_width), bf16), work, work),
        fetched=(late_mod, final_w, noise[0], timesteps),
    )
    grad_blocks = scatter_near(grad_heads, "seq", count)
    fake = lax.ppermute(term_rows, "segment", swaps(sections, 2))
    half = count // 2
    rows_shape = array((half, tok_rows, latent_width), bf16)
    keep, away, real = run(
        functools.partial(judge_back_kernel, count, model_width),
        [rows_shape, rows_shape, array((tok_rows + 32, latent_width), bf16)],
        (short, gram, qk_gain, proj, inverse, keys, values, term_rows, *critic_rows, *grad_blocks),
        10 * full_rows * full_rows * head_width,
        scratch=(pltpu.VMEM((full_rows, head_width), f32),) * 3,
    )
    moved = lax.ppermute(away, "seq", swaps(count, 1))
    real = lax.ppermute(real, "segment", swaps(sections, 1))
    parts = run(merge_kernel, [thin] * half, (direct, keep, moved), 1000)
    to_student = [
        lax.ppermute(
            part,
            ("segment", "seq"),
            [
                (place * count + row, (place + 1) % sections * count + (row ^ (2 * index)))
                for place in range(sections)
                for row in range(count)
            ],
        )
        for index, part in enumerate(parts)
    ]
    sums, sample_grad = run(
        functools.partial(outer_kernel, count),
        [array((count + 1, latent_width, 128), bf16), thin],
        (
            real,
            fake,
            target,
            noisy_student,
            pair,
            saved,
            student_inverse,
            critic_inverse,
            *critic_mixed,
            *to_student,
        ),
        2 * tok_rows * latent_width * head_width * (count + 1),
        fetched=(timesteps,),
    )
    ends = [(place, sections - 1 - place) for place in range(sections)]
    to_third = lax.ppermute(sample_grad, "segment", ends)
    to_second = lax.ppermute(sample_grad, "segment", swaps(sections, 2))
    to_first = lax.ppermute(sample_grad, "segment", swaps(sections, 1))
    last = count // 2
    bit = 1
    while bit < last:
        moved = lax.ppermute(sums, "seq", swaps(count, bit))
        sums = (sums.astype(f32) + moved.astype(f32)).astype(bf16)
        bit *= 2
    sums_all = []
    for group in range(groups):
        for offset in (0, last):
            moves = [
                (place * groups + batch, (place ^ offset) * groups + (batch ^ group))
                for place in range(count)
                for batch in range(groups)
            ]
            sums_all.append(
                sums if offset == group == 0 else lax.ppermute(sums, ("seq", "dp"), moves)
            )
    (total_t,) = run(
        functools.partial(expand_kernel, count, groups, sizes, full_rows),
        [],
        (
            w_embed,
            *heads_w,
            *late_mods[1:],
            *sums_all,
        ),
        4 * groups * latent_width * model_width * head_width * count,
        scratch=(
            pltpu.VMEM((groups * latent_width, model_width), f32),
            pltpu.VMEM((count + 1, groups * latent_width, 128), f32),
            pltpu.VMEM((latent_width, model_width), f32),
            pltpu.SemaphoreType.DMA((model_width // TILE,)),
        ),
        fetched=(late_mod,),
        sent=[array((latent_width, model_width), f32)],
    )
    (grad_t,) = run(
        emit_kernel,
        [array((latent_width, tok_rows), f32)],
        (sample_grad, to_first, to_second, to_third),
        1000,
    )
    return (jnp.transpose(grad_t)[None], jnp.transpose(total_t)[None])


def solution(mesh):
    placed = (
        P("dp", "seq", None),
        P("dp", "seq", None),
        P(),
        P("dp", None),
        P("segment", None, None),
        P("segment", None, None),
        P("segment", None, "seq"),
        P("segment", None, "seq", None, None),
        P("segment", "seq", None, None),
        P("segment", None, None),
        P("segment", None, None),
    )
    return jax.shard_map(
        step,
        mesh=mesh,
        in_specs=placed,
        out_specs=(P("dp", "seq", None), P("segment", None, None)),
        check_vma=False,
    )
```

```python
import functools
import math

import jax
import jax.numpy as jnp
from jax import lax
from jax.experimental import pallas as pl
from jax.experimental.pallas import tpu as pltpu
from jax.sharding import PartitionSpec as P


SHIFT = 7.0
EPS = 1e-06
ADV_WEIGHT = 3.0
TILE = 512
STREAMS = 6
SPARE = 8 << 20
VMEM = pl.BlockSpec(memory_space=pltpu.VMEM)
HBM = pl.BlockSpec(memory_space=pltpu.HBM)


def halves(values):
    top = values.astype(jnp.bfloat16)
    return (top, (values - top.astype(jnp.float32)).astype(jnp.bfloat16))


def swaps(count, offset):
    return [(place, place ^ offset) for place in range(count)]


def gather_near(value, axis, count):
    return [value] + [lax.ppermute(value, axis, swaps(count, offset)) for offset in range(1, count)]


def scatter_near(blocks, axis, count):
    return [blocks[0]] + [
        lax.ppermute(blocks[offset], axis, swaps(count, offset))
        for offset in range(1, count)
    ]


def window_kernel(fetches, part_out, arrival):
    width = part_out.shape[1] // 2
    first = pl.multiple_of(lax.axis_index("dp") * width, width)
    copy = pltpu.make_async_copy(
        fetches[0].at[:, pl.ds(first, 2 * width)], part_out, arrival.at[0]
    )
    copy.start()
    copy.wait()


def spread_heads(own, count, groups, stage):
    held = {0: [own]}
    bit = count // 2
    first = True
    while bit:
        for offset in sorted(held):
            if first and groups == 2:
                width = own.shape[1] // 3
                (part,) = run(
                    window_kernel,
                    [array((own.shape[0], 2 * width), own.dtype)],
                    (),
                    1000,
                    scratch=(pltpu.SemaphoreType.DMA((1,)),),
                    streamed=(own,),
                )
                near = lax.ppermute(part, "seq", swaps(count, bit))
                held[bit] = [near, lax.ppermute(stage(near), "dp", swaps(groups, 1))]
            else:
                held[offset | bit] = [
                    lax.ppermute(piece, "seq", swaps(count, bit))
                    for piece in held[offset]
                ]
        first = False
        bit //= 2
    return [held[offset] for offset in range(count)]


def head_tile(pieces, first, size):
    if len(pieces) == 1:
        return pieces[0][:, first : first + size]
    near, far = pieces
    width = far.shape[1]
    low = slice(first % width, first % width + size)
    high = slice(width + first % width, width + first % width + size)
    choices = (
        (near[:, low], far[:, low]),
        (near[:, high], near[:, low]),
        (far[:, low], near[:, high]),
    )[first // width]
    return jnp.where(lax.axis_index("dp") == 0, *choices)


def stacked_tile(heads_w, first):
    return jnp.concatenate([head_tile(pieces, first, TILE) for pieces in heads_w], axis=0)


def nested(refs, sizes):
    groups, first = [], 0
    for size in sizes:
        groups.append(refs[first : first + size])
        first += size
    return (groups, refs[first:])


def in_order(pieces, own_place):
    ordered = list(pieces)
    bit = 1
    while bit < len(ordered):
        flipped = (own_place & bit) != 0
        ordered = [
            jnp.where(flipped, ordered[place ^ bit], ordered[place])
            for place in range(len(ordered))
        ]
        bit *= 2
    return ordered


def dot32(left, right):
    return jnp.dot(left, right, preferred_element_type=jnp.float32)


def dot32_t(left, right):
    return lax.dot_general(
        left, right, (((1,), (1,)), ((), ())), preferred_element_type=jnp.float32
    )


def dot32_first(left, right):
    return lax.dot_general(
        left, right, (((0,), (0,)), ((), ())), preferred_element_type=jnp.float32
    )


def steps_of(times):
    times_ref = times.ready()
    place = lax.axis_index("dp")
    return (times_ref[place, 0], times_ref[place, 1])


def noise_level(step):
    fraction = jnp.full((1, 1), step, jnp.int32).astype(jnp.float32) / 1000.0
    return SHIFT * fraction / (1.0 + (SHIFT - 1.0) * fraction)


def slot_of(mod_ref, slot, width, first, size):
    return mod_ref[:, slot * width + first : slot * width + first + size]


def lane_sum(values):
    total = values[:, :128]
    for first in range(128, values.shape[1], 128):
        total = total + values[:, first : first + 128]
    return total


class Fetch:
    def __init__(self, source, target, arrival):
        self.copy = pltpu.make_async_copy(source, target, arrival)
        self.target = target
        self.waiting = True

    def start(self):
        self.copy.start()

    def ready(self):
        if self.waiting:
            self.copy.wait()
            self.waiting = False
        return self.target


def bytes_of(items):
    return sum(math.prod(item.shape) * jnp.dtype(item.dtype).itemsize for item in items)


def in_hbm(item):
    return pltpu.with_memory_space_constraint(item, pltpu.HBM)


def run(kernel, outputs, operands, flops, scratch=(), fetched=(), streamed=(), sent=()):
    inputs = len(operands)
    total = inputs + len(fetched) + len(streamed)
    results = len(outputs) + len(sent)

    def body(*refs):
        sources = refs[inputs:total]
        outs = refs[total : total + results]
        own = refs[total + results : total + results + len(scratch)]
        rest = refs[total + results + len(scratch) :]
        fetches = [
            Fetch(source, target, rest[-1].at[place])
            for place, (source, target) in enumerate(zip(sources, rest[:-1]))
        ]
        fetches += sources[len(fetched) :]
        kernel(fetches, *refs[:inputs], *outs, *own)

    places = [
        (pltpu.SMEM if item.dtype == jnp.int32 else pltpu.VMEM)(item.shape, item.dtype)
        for item in fetched
    ]
    held = bytes_of(
        [ref for ref in list(scratch) + places if ref.memory_space == pltpu.VMEM]
    )
    limit = min(60 << 20, SPARE + held + bytes_of(operands) + 2 * bytes_of(outputs))
    return pl.pallas_call(
        body,
        out_shape=list(outputs) + [pltpu.HBM(item.shape, item.dtype) for item in sent],
        in_specs=[VMEM] * inputs + [HBM] * (total - inputs),
        out_specs=[VMEM] * len(outputs) + [HBM] * len(sent),
        scratch_shapes=list(scratch)
        + places
        + [pltpu.SemaphoreType.DMA((max(1, len(fetched)),))],
        compiler_params=pltpu.CompilerParams(vmem_limit_bytes=limit),
        cost_estimate=pl.CostEstimate(
            flops=flops,
            bytes_accessed=bytes_of(list(operands) + list(fetched) + list(outputs)),
            transcendentals=0,
        ),
    )(*operands, *[in_hbm(item) for item in (*fetched, *streamed)])


def array(shape, dtype):
    return jax.ShapeDtypeStruct(shape, dtype)


def packed_rows(width):
    return -(-width // 2048) * 16


def condition_kernel(fetches, packed_out, noisy_out, kind_out, gram_out, held, mod_rows, arrivals):
    times, text, time_w, clean_t, noise, embed_w, mod_w, kind_w = fetches
    model_width = held.shape[0]
    rows = model_width // STREAMS
    for fetch in fetches[:-2]:
        fetch.start()
    copies = [
        pltpu.make_async_copy(
            mod_w.at[pl.ds(part * rows, rows)], held.at[pl.ds(part * rows, rows)], arrivals.at[part]
        )
        for part in range(STREAMS)
    ]
    copies.append(pltpu.make_async_copy(kind_w, kind_out, arrivals.at[STREAMS]))
    for copy in copies:
        copy.start()
    student_step, critic_step = steps_of(times)
    step = jnp.where(lax.axis_index("segment") == 0, student_step, critic_step)
    text_ref = text.ready()
    half = text_ref.shape[1] // 2
    places = lax.broadcasted_iota(jnp.int32, (1, half), 1).astype(jnp.float32)
    frequency = jnp.exp(-math.log(10000.0) * places / half)
    angles = jnp.full((1, half), step, jnp.int32).astype(jnp.float32) * frequency
    features = jnp.concatenate([jnp.cos(angles), jnp.sin(angles)], axis=1) + text_ref[...]
    features = jnp.broadcast_to(features, (8, 2 * half)).astype(jnp.bfloat16)
    hidden = dot32(features, time_w.ready()[...])
    hidden = (hidden / (1.0 + jnp.exp(-hidden))).astype(jnp.bfloat16)
    mod_rows[...] = jnp.zeros_like(mod_rows)
    total = None
    for part in range(STREAMS):
        copies[part].wait()
        piece = dot32(
            hidden[:, part * rows : (part + 1) * rows], held[part * rows : (part + 1) * rows]
        )
        total = piece if total is None else total + piece
        if part == STREAMS // 2:
            sigma_student = noise_level(student_step)
            clean_ref, noise_ref = clean_t.ready(), noise.ready()
            noisy = (1.0 - sigma_student) * clean_ref[...].astype(jnp.float32).T + sigma_student * noise_ref[
                :, : clean_ref.shape[0]
            ].astype(jnp.float32)
            noisy = noisy.astype(jnp.bfloat16)
            noisy_out[...] = noisy
            top = noisy.shape[0] // 2
            packed_out[:top] = jnp.concatenate([noisy[:top], noisy[top:]], axis=1)
            central_top, central_low = halves(centred(embed_w.ready()))
            gram = (
                dot32_t(central_top, central_top)
                + dot32_t(central_top, central_low)
                + dot32_t(central_low, central_top)
            )
            gram_out[0], gram_out[1] = halves(gram)
    width = total.shape[1]
    for row, first in enumerate(range(0, width, 128)):
        size = min(128, width - first)
        mod_rows[row : row + 1, :size] = total[:1, first : first + size]
    depth = mod_rows.shape[0]
    top = noisy_out.shape[0] // 2
    packed_out[top : top + depth], packed_out[top + depth :] = halves(mod_rows[...])
    copies[STREAMS].wait()


def rms_scale(values, gain_vec):
    inverse = lax.rsqrt(jnp.mean(values * values, axis=-1, keepdims=True) + EPS)
    unit_vec = values * inverse
    return (unit_vec * gain_vec, unit_vec, inverse)


def rms_back(gradient, unit_vec, inverse, gain_vec):
    scaled = gradient * gain_vec
    return inverse * (scaled - unit_vec * jnp.mean(scaled * unit_vec, axis=-1, keepdims=True))


def centred(embed_ref):
    values = embed_ref[0].astype(jnp.float32)
    return values - jnp.mean(values, axis=1, keepdims=True)


def front(rows, gram, model_width, short, gains, head_outs, proj_ref, inverse_ref, key_ref, value_ref):
    latent_width = gram.shape[1]
    count = len(rows)
    head_width = gains.shape[2]
    scale = 1.0 / math.sqrt(head_width)
    size = rows[0].shape[0]
    short_top = None
    for place in range(count):
        block = rows[place][...]
        spanned = dot32(block, gram[0]) + dot32(block, gram[1])
        squares = jnp.sum(spanned * block.astype(jnp.float32), axis=1, keepdims=True)
        inverse = lax.rsqrt(jnp.maximum(squares, 0.0) / model_width + EPS)
        if short_top is None:
            values = short()
            short_top, short_low = halves(values[:latent_width])
            short_shift = values[latent_width : latent_width + 1]
        projected = inverse * (dot32(block, short_top) + dot32(block, short_low)) + short_shift
        low = place * size
        proj_ref[low : low + size] = projected
        inverse_ref[low : low + size] = jnp.broadcast_to(inverse, (size, 128))
        keys, _, _ = rms_scale(projected[:, head_width : 2 * head_width], gains[0, 1:2])
        key_ref[low : low + size] = keys.astype(jnp.bfloat16)
        value_ref[low : low + size] = projected[:, 2 * head_width :].astype(jnp.bfloat16)
    for place in range(count):
        low = place * size
        queries, _, _ = rms_scale(proj_ref[low : low + size, :head_width], gains[0, :1])
        scores = dot32_t(queries.astype(jnp.bfloat16), key_ref[...]) * scale
        weights = jnp.exp(scores)
        soft_max = weights * (1.0 / jnp.sum(weights, axis=-1, keepdims=True))
        head_outs[place][...] = dot32(soft_max.astype(jnp.bfloat16), value_ref[...]).astype(
            jnp.bfloat16
        )


def stage_kernel(fetches, near, part_out):
    width = part_out.shape[1]
    for place in range(2):

        @pl.when(lax.axis_index("dp") == place)
        def _():
            part_out[...] = near[:, place * width : (place + 1) * width]


def student_front_kernel(count, width, fetches, embed_w, head_w, gram, gains, *refs):
    packed = refs[:count]
    head_outs = refs[count : 2 * count]
    short_out, late_out, mod, rows_ref, sends, *kept = refs[2 * count :]
    model_width = embed_w.shape[2]
    latent_width = embed_w.shape[1]
    size = rows_ref.shape[1]
    half = size // 2
    depth = packed_rows(width)
    parts = [
        piece[half : half + depth].astype(jnp.float32) + piece[half + depth :].astype(jnp.float32)
        for piece in packed
    ]
    for place, part in enumerate(in_order(parts, lax.axis_index("seq"))):
        for row, first in enumerate(range(0, width, 128)):
            lanes = min(128, width - first)
            low = place * width + first
            mod[:, low : low + lanes] = part[row : row + 1, :lanes]
    late = pltpu.make_async_copy(
        mod.at[:, pl.ds(2 * model_width, 3 * model_width)], late_out, sends.at[0]
    )
    late.start()
    for place in range(count):
        rows_ref[place, :half] = packed[place][:half, :latent_width]
        rows_ref[place, half:] = packed[place][:half, latent_width:]
    central = centred(embed_w)
    scale_in = slot_of(mod, 1, model_width, 0, model_width)
    shift_in = slot_of(mod, 0, model_width, 0, model_width)
    in_rows = jnp.concatenate(
        [central * (1.0 + scale_in), jnp.broadcast_to(shift_in, (16, model_width))], axis=0
    )
    in_top, in_low = halves(in_rows)
    in_both = jnp.concatenate([in_top, in_low], axis=0)
    both = jnp.concatenate([dot32(in_both, head_w[kind]) for kind in range(3)], axis=1)
    short = both[: in_rows.shape[0]] + both[in_rows.shape[0] :]
    short_out[...] = short

    @pl.when(lax.axis_index("segment") == 0)
    def _():
        front(
            [rows_ref.at[place] for place in range(count)],
            gram,
            model_width,
            lambda: short,
            gains,
            head_outs,
            *kept,
        )

    late.wait()


def critic_front_kernel(count, model_width, fetches, short, gram, gains, *refs):
    rows = refs[:count]
    head_outs = refs[count : 2 * count]
    kept = refs[2 * count :]

    @pl.when(lax.axis_index("segment") != 0)
    def _():
        front(
            rows,
            gram,
            model_width,
            lambda: short[...],
            gains,
            head_outs,
            *kept,
        )


def tail(late, latent, embed_w, final_t, mixed, heads_w, work):
    model_width = embed_w.shape[2]
    block = latent[...]
    joined_heads = jnp.concatenate([piece[...] for piece in mixed], axis=1)
    sums = None
    for first in range(0, model_width, TILE):
        span = slice(first, first + TILE)
        attended = dot32(joined_heads, stacked_tile(heads_w, first))
        mod = late.ready()
        residual = (
            dot32(block, embed_w[0, :, span]) + slot_of(mod, 0, model_width, first, TILE) * attended
        )
        work[:, span] = residual
        part = lane_sum(residual)
        sums = part if sums is None else sums + part
    row_mean = jnp.sum(sums, axis=1, keepdims=True) / model_width
    sums = None
    for first in range(0, model_width, TILE):
        span = slice(first, first + TILE)
        middle = work[:, span] - row_mean
        work[:, span] = middle
        part = lane_sum(middle * middle)
        sums = part if sums is None else sums + part
    inverse = lax.rsqrt(jnp.sum(sums, axis=1, keepdims=True) / model_width + EPS)
    result = None
    final_w = final_t.ready()
    for first in range(0, model_width, TILE):
        span = slice(first, first + TILE)
        normed = work[:, span] * inverse
        work[:, span] = normed
        final_in = (
            normed * (1.0 + slot_of(mod, 2, model_width, first, TILE))
            + slot_of(mod, 1, model_width, first, TILE)
        ).astype(jnp.bfloat16)
        product = dot32_t(final_in, final_w[:, span])
        result = product if result is None else result + product
    return (result, inverse)


def student_tail_kernel(count, sizes, fetches, latent, embed_w, *refs):
    mixed = refs[:count]
    heads_w, refs = nested(refs[count:], sizes)
    pair_ref, saved_out, inverse_out, work, inverse_ref, sends = refs
    late, final_t, noise, times = fetches
    latent_width = latent.shape[1]

    @pl.when(lax.axis_index("segment") == 0)
    def _():
        for fetch in fetches:
            fetch.start()
        copies = [
            pltpu.make_async_copy(mixed[place], saved_out.at[place], sends.at[place])
            for place in range(count)
        ]
        for copy in copies:
            copy.start()
        velocity, inverse = tail(late, latent, embed_w, final_t, mixed, heads_w, work)
        student_step, critic_step = steps_of(times)
        sigma_student, sigma_critic = noise_level(student_step), noise_level(critic_step)
        rows, lanes = inverse_ref.shape
        rest = (lanes - latent_width) // 2
        inverse_ref[...] = jnp.concatenate(
            [
                jnp.broadcast_to(inverse, (rows, latent_width)),
                jnp.broadcast_to(sigma_student, (rows, rest)),
                jnp.broadcast_to(sigma_critic, (rows, rest)),
            ],
            axis=1,
        )
        copies.append(pltpu.make_async_copy(inverse_ref, inverse_out, sends.at[count]))
        copies[-1].start()
        sample = latent[...].astype(jnp.float32) - sigma_student * velocity
        second = noise.ready()[:, latent_width:].astype(jnp.float32)
        critic = (1.0 - sigma_critic) * sample + sigma_critic * second
        pair_ref[...] = jnp.concatenate([critic, sample], axis=1).astype(jnp.bfloat16)
        for copy in copies:
            copy.wait()


def pick_kernel(sections, fetches, own, *refs):
    moved = refs[: sections - 1]
    pair_ref, rows_ref = refs[sections - 1 :]
    section = lax.axis_index("segment")
    for place in range(sections):

        @pl.when(section == place)
        def _():
            chosen = own if place == 0 else moved[place - 1]
            pair_ref[...] = chosen[...]
            rows_ref[...] = chosen[:, : rows_ref.shape[1]]


def critic_tail_kernel(count, sizes, fetches, pair, embed_w, *refs):
    mixed = refs[:count]
    heads_w, refs = nested(refs[count:], sizes)
    grads = refs[:count]
    inverse_ref, term_ref, target_ref, direct_ref, latent, work, other = refs[count:]
    late, final_t, noise, times = fetches
    model_width = embed_w.shape[2]
    latent_width = latent.shape[1]
    section = lax.axis_index("segment")

    @pl.when(section != 0)
    def _():
        for fetch in fetches:
            fetch.start()
        both = pair[...].astype(jnp.float32)
        sample = both[:, latent_width:]
        latent[...] = pair[:, :latent_width]
        result, inverse = tail(late, latent, embed_w, final_t, mixed, heads_w, work)
        mod, final_w = late.ready(), final_t.ready()
        _, critic_step = steps_of(times)
        sigma_critic = noise_level(critic_step)
        inverse_ref[...] = jnp.broadcast_to(inverse, inverse_ref.shape)
        term_ref[...] = (sigma_critic * result).astype(jnp.bfloat16)
        second = noise.ready()[:, latent_width:].astype(jnp.float32)
        target_ref[...] = jnp.where(
            section == 2,
            2.0 * (result - (second - sample)),
            jnp.where(section == 3, 1.0 / (1.0 + jnp.exp(-result)), 0.0),
        )

        @pl.when(section == 1)
        def _():
            gaps = jnp.abs(sample - both[:, :latent_width] + sigma_critic * result)
            error = jnp.sum(jnp.sum(gaps, axis=1, keepdims=True), axis=0, keepdims=True)
            error = error / (gaps.shape[0] * latent_width)
            error_top, error_low = halves(jnp.broadcast_to(error, (16, grads[0].shape[1])))
            for place in range(count):
                grads[place][:16] = error_top
                grads[place][16:32] = error_low

        @pl.when(section == 3)
        def _():
            grad_logit = (-1.0 / (1.0 + jnp.exp(result))).astype(jnp.bfloat16)
            plain, along = None, None
            for first in range(0, model_width, TILE):
                span = slice(first, first + TILE)
                gradient = dot32(grad_logit, final_w[:, span]) * (
                    1.0 + slot_of(mod, 2, model_width, first, TILE)
                )
                other[:, span] = gradient
                part = lane_sum(gradient)
                plain = part if plain is None else plain + part
                part = lane_sum(gradient * work[:, span])
                along = part if along is None else along + part
            plain = jnp.sum(plain, axis=1, keepdims=True) / model_width
            along = jnp.sum(along, axis=1, keepdims=True) / model_width
            direct = None
            totals = [None] * count
            for first in range(0, model_width, TILE):
                span = slice(first, first + TILE)
                grad_residual = inverse * (other[:, span] - plain - work[:, span] * along)
                top, low = halves(grad_residual)
                product = dot32_t(top, embed_w[0, :, span]) + dot32_t(low, embed_w[0, :, span])
                direct = product if direct is None else direct + product
                grad_attended = (slot_of(mod, 0, model_width, first, TILE) * grad_residual).astype(
                    jnp.bfloat16
                )
                for place in range(count):
                    product = dot32_t(grad_attended, head_tile(heads_w[place], first, TILE))
                    held = totals[place]
                    totals[place] = product if held is None else held + product
            direct_ref[...] = direct
            for place in range(count):
                grads[place][...] = totals[place].astype(jnp.bfloat16)


def judge_back_kernel(count, model_width, fetches, short_in, gram, gains, proj_ref, inverse_ref, key_ref, value_ref, term, *refs):
    rows = refs[:count]
    grads = refs[count : 2 * count]
    keep_ref, send_ref, real_ref, grad_key_ref, grad_value_ref, grad_query_ref = refs[2 * count :]
    section = lax.axis_index("segment")
    latent_width = rows[0].shape[1]
    head_width = gains.shape[2]
    scale = 1.0 / math.sqrt(head_width)
    size = rows[0].shape[0]

    @pl.when(section == 3)
    def _():
        for place in range(count):
            low = place * size
            span = slice(low, low + size)
            queries, _, _ = rms_scale(proj_ref[span, :head_width], gains[0, :1])
            query_b = queries.astype(jnp.bfloat16)
            weights = jnp.exp(dot32_t(query_b, key_ref[...]) * scale)
            soft_max = weights * (1.0 / jnp.sum(weights, axis=-1, keepdims=True))
            grad_out = grads[place][...]
            grad_soft = dot32_t(grad_out, value_ref[...])
            grad_value = dot32_first(soft_max.astype(jnp.bfloat16), grad_out)
            grad_scores = soft_max * (
                grad_soft - jnp.sum(soft_max * grad_soft, axis=-1, keepdims=True)
            )
            grad_scores_b = (grad_scores * scale).astype(jnp.bfloat16)
            grad_query_ref[span] = dot32(grad_scores_b, key_ref[...])
            grad_key = dot32_first(grad_scores_b, query_b)
            if place == 0:
                grad_value_ref[...] = grad_value
                grad_key_ref[...] = grad_key
            else:
                grad_value_ref[...] += grad_value
                grad_key_ref[...] += grad_key
        gram_top, gram_low = gram[0], gram[1]
        short_top, short_low = halves(short_in[:latent_width])
        for place in range(count):
            low = place * size
            span = slice(low, low + size)
            projected = proj_ref[span]
            _, q_unit, q_inverse = rms_scale(projected[:, :head_width], gains[0, :1])
            _, k_unit, k_inverse = rms_scale(
                projected[:, head_width : 2 * head_width], gains[0, 1:2]
            )
            grad_q = rms_back(grad_query_ref[span], q_unit, q_inverse, gains[0, :1])
            grad_k = rms_back(grad_key_ref[span], k_unit, k_inverse, gains[0, 1:2])
            grad_proj = jnp.concatenate([grad_q, grad_k, grad_value_ref[span]], axis=1).astype(
                jnp.bfloat16
            )
            through = dot32_t(grad_proj, short_top) + dot32_t(grad_proj, short_low)
            block = rows[place][...]
            along = jnp.sum(through * block.astype(jnp.float32), axis=1, keepdims=True) / model_width
            spanned = dot32(block, gram_top) + dot32(block, gram_low)
            inverse = inverse_ref[span, :1]
            target_ref = send_ref if place % 2 else keep_ref
            target_ref[place // 2] = (
                inverse * (through - spanned * (inverse * inverse * along))
            ).astype(jnp.bfloat16)

    @pl.when(section == 1)
    def _():
        error = None
        for grad in grads:
            part = grad[:16, :latent_width].astype(jnp.float32) + grad[
                16:32, :latent_width
            ].astype(jnp.float32)
            error = part if error is None else error + part
        real_ref[:size] = term[...]
        real_ref[size : size + 16], real_ref[size + 16 :] = halves(error / count + EPS)


def merge_kernel(fetches, direct, keep, moved, *outs):
    @pl.when(lax.axis_index("segment") == 3)
    def _():
        for place, out in enumerate(outs):
            total = keep[place].astype(jnp.float32) + moved[place].astype(jnp.float32)
            if place == 0:
                total = total + direct[...]
            out[...] = total.astype(jnp.bfloat16)


def outer_kernel(
    count,
    fetches,
    real,
    fake,
    target_in,
    student_rows,
    pair,
    student_mixed,
    student_inverse,
    critic_inverse,
    *refs,
):
    critic_mixed = refs[:count]
    arrived = refs[count : count + count // 2]
    sums_ref, sample_ref = refs[count + count // 2 :]
    section = lax.axis_index("segment")
    place = lax.axis_index("seq")
    latent_width = student_rows.shape[1]
    rows = student_rows.shape[0]

    def collect(target, inverse, latent, mixed):
        target = target.astype(jnp.bfloat16)
        weighted = inverse[:, :latent_width] * target.astype(jnp.float32)
        top, low = halves(weighted)
        for offset in range(count):
            piece = mixed[offset][...]
            sums_ref[place ^ offset] = (dot32_first(top, piece) + dot32_first(low, piece)).astype(
                jnp.bfloat16
            )
        near = dot32_first(top, latent) + dot32_first(low, latent)
        ones = jnp.ones((target.shape[0], sums_ref.shape[2] - latent_width), jnp.bfloat16)
        sums_ref[count] = jnp.concatenate([near, dot32_first(target, ones)], axis=1).astype(
            jnp.bfloat16
        )

    @pl.when(section == 0)
    def _():
        lanes = student_inverse.shape[1]
        middle = (lanes + latent_width) // 2
        sigma_student = student_inverse[:1, latent_width : latent_width + 1]
        sigma_critic = student_inverse[:1, middle : middle + 1]
        adverse = arrived[0][...].astype(jnp.float32)
        for part in arrived[1:]:
            adverse = adverse + part[...].astype(jnp.float32)
        adverse = (1.0 - sigma_critic) * adverse
        spread = (real[rows : rows + 1] .astype(jnp.float32) + real[rows + 16 : rows + 17].astype(jnp.float32))[
            :, :1
        ]
        gap = real[:rows].astype(jnp.float32) - fake[...].astype(jnp.float32)
        sample_grad = gap / spread + ADV_WEIGHT * adverse
        sample_ref[...] = sample_grad.astype(jnp.bfloat16)
        target = -sigma_student * sample_grad
        mixed = [student_mixed.at[offset] for offset in range(count)]
        collect(target, student_inverse, student_rows[...], mixed)

    @pl.when(section == 1)
    def _():
        sums_ref[...] = jnp.zeros_like(sums_ref)

    @pl.when(section >= 2)
    def _():
        collect(target_in[...], critic_inverse, pair[:, :latent_width], critic_mixed)


def emit_kernel(fetches, own, to_first, to_second, to_third, grad_ref):
    section = lax.axis_index("segment")
    for place, value in enumerate((own, to_first, to_second, to_third)):

        @pl.when(section == place)
        def _():
            grad_ref[...] = value[...].astype(jnp.float32).T


def expand_kernel(count, groups, sizes, full_rows, fetches, embed_w, *refs):
    heads_w, refs = nested(refs, sizes)
    other_mods = refs[: groups - 1]
    sums = refs[groups - 1 : 3 * groups - 1]
    total_out, work, joined, total_ref, sends = refs[3 * groups - 1 :]
    section = lax.axis_index("segment")
    place = lax.axis_index("seq")
    latent_width = embed_w.shape[1]
    model_width = embed_w.shape[2]

    @pl.when(section == 1)
    def _():
        total_ref[...] = jnp.zeros_like(total_ref)
        copy = pltpu.make_async_copy(total_ref, total_out, sends.at[0])
        copy.start()
        copy.wait()

    @pl.when(section != 1)
    def _():
        (late,) = fetches
        late.start()
        for group in range(groups):
            low = group * latent_width
            joined[:, low : low + latent_width] = sums[2 * group][...].astype(jnp.float32) + sums[
                2 * group + 1
            ][...].astype(jnp.float32)
        near_top = joined[count].astype(jnp.bfloat16)
        heads = jnp.concatenate(
            [joined[place ^ offset].astype(jnp.bfloat16) for offset in range(count)], axis=1
        )
        averages = None
        for first in range(0, model_width, TILE):
            span = slice(first, first + TILE)
            spread = dot32(heads, stacked_tile(heads_w, first))
            near = dot32(near_top[:, :latent_width], embed_w[0, :, span])
            mods = [late.ready(), *other_mods]
            gates = jnp.concatenate(
                [
                    jnp.broadcast_to(
                        slot_of(mod, 0, model_width, first, TILE), (latent_width, TILE)
                    )
                    for mod in mods
                ],
                axis=0,
            )
            value = near + gates * spread
            work[:, span] = value
            part = lane_sum(value)
            averages = part if averages is None else averages + part
        averages = jnp.sum(averages, axis=1, keepdims=True) / model_width
        counts = joined[count][:, latent_width : latent_width + 1]
        copies = []
        for number, first in enumerate(range(0, model_width, TILE)):
            span = slice(first, first + TILE)
            value = work[:, span] - averages
            total = None
            for group in range(groups):
                mine = slice(group * latent_width, (group + 1) * latent_width)
                product = value[mine] * (
                    1.0 + slot_of(mods[group], 2, model_width, first, TILE)
                ) + counts[mine] * slot_of(mods[group], 1, model_width, first, TILE)
                total = product if total is None else total + product
            total_ref[:, span] = total / full_rows
            area = (slice(None), pl.ds(first, TILE))
            copies.append(
                pltpu.make_async_copy(total_ref.at[area], total_out.at[area], sends.at[number])
            )
            copies[-1].start()
        for copy in copies:
            copy.wait()


def step(
    clean, noise, timesteps, text_vec, w_embed, w_time, w_mod, w_qkv, w_out, qk_gain, w_final
):
    sections = lax.axis_size("segment")
    tok_rows = clean.shape[1]
    latent_width = clean.shape[2]
    model_width = w_embed.shape[2]
    mod_width = w_mod.shape[2]
    count = lax.axis_size("seq")
    full_rows = tok_rows * count
    head_width = w_qkv.shape[4]
    bf16, f32 = jnp.bfloat16, jnp.float32
    kind_w = jnp.transpose(w_qkv[0, :, 0], (1, 0, 2))
    final_w = jnp.transpose(w_final[0])
    groups = lax.axis_size("dp")

    def stage(near):
        rows, width = near.shape
        (part,) = run(stage_kernel, [array((rows, width // 2), bf16)], (near,), 1000)
        return part

    heads_w = spread_heads(w_out[0, 0], count, groups, stage)
    sizes = [len(pieces) for pieces in heads_w]
    heads_w = sum(heads_w, [])

    depth = packed_rows(mod_width)
    packed, noisy_student, kind_w, gram = run(
        condition_kernel,
        [
            array((tok_rows // 2 + 2 * depth, 2 * latent_width), bf16),
            array((tok_rows, latent_width), bf16),
            pltpu.VMEM(kind_w.shape, bf16),
            array((2, latent_width, latent_width), bf16),
        ],
        (),
        2 * model_width * mod_width,
        scratch=(
            pltpu.VMEM((model_width, mod_width), bf16),
            pltpu.VMEM((depth, 128), f32),
            pltpu.SemaphoreType.DMA((STREAMS + 1,)),
        ),
        fetched=(timesteps, text_vec, w_time[0], jnp.transpose(clean[0]), noise[0], w_embed),
        streamed=(w_mod[0], kind_w),
    )
    kind_w = pltpu.with_memory_space_constraint(kind_w, pltpu.VMEM)
    packed_all = gather_near(packed, "seq", count)

    head_blocks = [array((tok_rows, head_width), bf16)] * count
    stored = [
        ((full_rows, 3 * head_width), f32),
        ((full_rows, 128), f32),
        ((full_rows, head_width), bf16),
        ((full_rows, head_width), bf16),
    ]
    short_shape = ((latent_width + 16, 3 * head_width), f32)
    *head_outs, short, late_mod = run(
        functools.partial(student_front_kernel, count, mod_width),
        head_blocks + [pltpu.VMEM(*short_shape)],
        (w_embed, kind_w, gram, qk_gain, *packed_all),
        4 * latent_width * model_width * 3 * head_width,
        scratch=[
            pltpu.VMEM((1, 5 * model_width), f32),
            pltpu.VMEM((count, tok_rows, latent_width), bf16),
            pltpu.SemaphoreType.DMA((1,)),
        ]
        + [pltpu.VMEM(shape, kind) for shape, kind in stored],
        sent=[array((1, 3 * model_width), f32)],
    )
    student_mixed = scatter_near(head_outs, "seq", count)
    late_mods = gather_near(late_mod, "dp", groups)
    work = pltpu.VMEM((tok_rows, model_width), f32)
    inverse_shape = array((tok_rows, 128), f32)
    pair, saved, student_inverse = run(
        functools.partial(student_tail_kernel, count, sizes),
        [array((tok_rows, 2 * latent_width), bf16)],
        (noisy_student, w_embed, *student_mixed, *heads_w),
        2 * tok_rows * model_width * head_width * count,
        scratch=(
            work,
            pltpu.VMEM((tok_rows, 128), f32),
            pltpu.SemaphoreType.DMA((count + 1,)),
        ),
        fetched=(late_mod, final_w, noise[0], timesteps),
        sent=[array((count, tok_rows, head_width), bf16), inverse_shape],
    )
    moved = [lax.ppermute(pair, "segment", [(0, place)]) for place in range(1, sections)]
    pair, own_rows = run(
        functools.partial(pick_kernel, sections),
        [
            array((tok_rows, 2 * latent_width), bf16),
            array((tok_rows, latent_width), bf16),
        ],
        (pair, *moved),
        1000,
    )
    critic_rows = gather_near(own_rows, "seq", count)
    *head_outs, proj, inverse, keys, values = run(
        functools.partial(critic_front_kernel, count, model_width),
        head_blocks + [array(shape, kind) for shape, kind in stored],
        (
            pltpu.with_memory_space_constraint(short, pltpu.VMEM),
            gram,
            qk_gain,
            *critic_rows,
        ),
        4 * latent_width * model_width * full_rows,
    )
    critic_mixed = scatter_near(head_outs, "seq", count)
    small = array((tok_rows, latent_width), f32)
    thin = array((tok_rows, latent_width), bf16)
    *grad_heads, critic_inverse, term_rows, target, direct = run(
        functools.partial(critic_tail_kernel, count, sizes),
        head_blocks + [inverse_shape, thin, small, small],
        (pair, w_embed, *critic_mixed, *heads_w),
        4 * tok_rows * model_width * head_width * count,
        scratch=(pltpu.VMEM((tok_rows, latent_width), bf16), work, work),
        fetched=(late_mod, final_w, noise[0], timesteps),
    )
    grad_blocks = scatter_near(grad_heads, "seq", count)
    fake = lax.ppermute(term_rows, "segment", swaps(sections, 2))
    half = count // 2
    rows_shape = array((half, tok_rows, latent_width), bf16)
    keep, away, real = run(
        functools.partial(judge_back_kernel, count, model_width),
        [rows_shape, rows_shape, array((tok_rows + 32, latent_width), bf16)],
        (short, gram, qk_gain, proj, inverse, keys, values, term_rows, *critic_rows, *grad_blocks),
        10 * full_rows * full_rows * head_width,
        scratch=(pltpu.VMEM((full_rows, head_width), f32),) * 3,
    )
    moved = lax.ppermute(away, "seq", swaps(count, 1))
    real = lax.ppermute(real, "segment", swaps(sections, 1))
    parts = run(merge_kernel, [thin] * half, (direct, keep, moved), 1000)
    to_student = [
        lax.ppermute(
            part,
            ("segment", "seq"),
            [
                (place * count + row, (place + 1) % sections * count + (row ^ (2 * index)))
                for place in range(sections)
                for row in range(count)
            ],
        )
        for index, part in enumerate(parts)
    ]
    sums, sample_grad = run(
        functools.partial(outer_kernel, count),
        [array((count + 1, latent_width, 128), bf16), thin],
        (
            real,
            fake,
            target,
            noisy_student,
            pair,
            saved,
            student_inverse,
            critic_inverse,
            *critic_mixed,
            *to_student,
        ),
        2 * tok_rows * latent_width * head_width * (count + 1),
    )
    ends = [(place, sections - 1 - place) for place in range(sections)]
    to_third = lax.ppermute(sample_grad, "segment", ends)
    to_second = lax.ppermute(sample_grad, "segment", swaps(sections, 2))
    to_first = lax.ppermute(sample_grad, "segment", swaps(sections, 1))
    last = count // 2
    bit = 1
    while bit < last:
        moved = lax.ppermute(sums, "seq", swaps(count, bit))
        sums = (sums.astype(f32) + moved.astype(f32)).astype(bf16)
        bit *= 2
    sums_all = []
    for group in range(groups):
        for offset in (0, last):
            moves = [
                (place * groups + batch, (place ^ offset) * groups + (batch ^ group))
                for place in range(count)
                for batch in range(groups)
            ]
            sums_all.append(
                sums if offset == group == 0 else lax.ppermute(sums, ("seq", "dp"), moves)
            )
    (total_t,) = run(
        functools.partial(expand_kernel, count, groups, sizes, full_rows),
        [],
        (
            w_embed,
            *heads_w,
            *late_mods[1:],
            *sums_all,
        ),
        4 * groups * latent_width * model_width * head_width * count,
        scratch=(
            pltpu.VMEM((groups * latent_width, model_width), f32),
            pltpu.VMEM((count + 1, groups * latent_width, 128), f32),
            pltpu.VMEM((latent_width, model_width), f32),
            pltpu.SemaphoreType.DMA((model_width // TILE,)),
        ),
        fetched=(late_mod,),
        sent=[array((latent_width, model_width), f32)],
    )
    (grad_t,) = run(
        emit_kernel,
        [array((latent_width, tok_rows), f32)],
        (sample_grad, to_first, to_second, to_third),
        1000,
    )
    return (jnp.transpose(grad_t)[None], jnp.transpose(total_t)[None])


def solution(mesh):
    placed = (
        P("dp", "seq", None),
        P("dp", "seq", None),
        P(),
        P("dp", None),
        P("segment", None, None),
        P("segment", None, None),
        P("segment", None, "seq"),
        P("segment", None, "seq", None, None),
        P("segment", "seq", None, None),
        P("segment", None, None),
        P("segment", None, None),
    )
    return jax.shard_map(
        step,
        mesh=mesh,
        in_specs=placed,
        out_specs=(P("dp", "seq", None), P("segment", None, None)),
        check_vma=False,
    )
```

```python
import functools
import math

import jax
import jax.numpy as jnp
from jax import lax
from jax.experimental import pallas as pl
from jax.experimental.pallas import tpu as pltpu
from jax.sharding import PartitionSpec as P


SHIFT = 7.0
EPS = 1e-06
ADV_WEIGHT = 3.0
TILE = 512
STREAMS = 6
SPARE = 8 << 20
VMEM = pl.BlockSpec(memory_space=pltpu.VMEM)
HBM = pl.BlockSpec(memory_space=pltpu.HBM)


def halves(values):
    top = values.astype(jnp.bfloat16)
    return (top, (values - top.astype(jnp.float32)).astype(jnp.bfloat16))


def swaps(count, offset):
    return [(place, place ^ offset) for place in range(count)]


def gather_near(value, axis, count):
    return [value] + [lax.ppermute(value, axis, swaps(count, offset)) for offset in range(1, count)]


def scatter_near(blocks, axis, count):
    return [blocks[0]] + [
        lax.ppermute(blocks[offset], axis, swaps(count, offset))
        for offset in range(1, count)
    ]


def window_kernel(fetches, part_out, arrival):
    width = part_out.shape[1] // 2
    first = pl.multiple_of(lax.axis_index("dp") * width, width)
    copy = pltpu.make_async_copy(
        fetches[0].at[:, pl.ds(first, 2 * width)], part_out, arrival.at[0]
    )
    copy.start()
    copy.wait()


def spread_heads(own, count, groups, stage):
    held = {0: [own]}
    bit = count // 2
    first = True
    while bit:
        for offset in sorted(held):
            if first and groups == 2:
                width = own.shape[1] // 3
                (part,) = run(
                    window_kernel,
                    [array((own.shape[0], 2 * width), own.dtype)],
                    (),
                    1000,
                    scratch=(pltpu.SemaphoreType.DMA((1,)),),
                    streamed=(own,),
                )
                near = lax.ppermute(part, "seq", swaps(count, bit))
                held[bit] = [near, lax.ppermute(stage(near), "dp", swaps(groups, 1))]
            else:
                held[offset | bit] = [
                    lax.ppermute(piece, "seq", swaps(count, bit))
                    for piece in held[offset]
                ]
        first = False
        bit //= 2
    return [held[offset] for offset in range(count)]


def head_tile(pieces, first, size):
    if len(pieces) == 1:
        return pieces[0][:, first : first + size]
    near, far = pieces
    width = far.shape[1]
    low = slice(first % width, first % width + size)
    high = slice(width + first % width, width + first % width + size)
    choices = (
        (near[:, low], far[:, low]),
        (near[:, high], near[:, low]),
        (far[:, low], near[:, high]),
    )[first // width]
    return jnp.where(lax.axis_index("dp") == 0, *choices)


def stacked_tile(heads_w, first):
    return jnp.concatenate([head_tile(pieces, first, TILE) for pieces in heads_w], axis=0)


def nested(refs, sizes):
    groups, first = [], 0
    for size in sizes:
        groups.append(refs[first : first + size])
        first += size
    return (groups, refs[first:])


def in_order(pieces, own_place):
    ordered = list(pieces)
    bit = 1
    while bit < len(ordered):
        flipped = (own_place & bit) != 0
        ordered = [
            jnp.where(flipped, ordered[place ^ bit], ordered[place])
            for place in range(len(ordered))
        ]
        bit *= 2
    return ordered


def dot32(left, right):
    return jnp.dot(left, right, preferred_element_type=jnp.float32)


def dot32_t(left, right):
    return lax.dot_general(
        left, right, (((1,), (1,)), ((), ())), preferred_element_type=jnp.float32
    )


def dot32_first(left, right):
    return lax.dot_general(
        left, right, (((0,), (0,)), ((), ())), preferred_element_type=jnp.float32
    )


def steps_of(times):
    times_ref = times.ready()
    place = lax.axis_index("dp")
    return (times_ref[place, 0], times_ref[place, 1])


def noise_level(step):
    fraction = jnp.full((1, 1), step, jnp.int32).astype(jnp.float32) / 1000.0
    return SHIFT * fraction / (1.0 + (SHIFT - 1.0) * fraction)


def slot_of(mod_ref, slot, width, first, size):
    return mod_ref[:, slot * width + first : slot * width + first + size]


def lane_sum(values):
    total = values[:, :128]
    for first in range(128, values.shape[1], 128):
        total = total + values[:, first : first + 128]
    return total


class Fetch:
    def __init__(self, source, target, arrival):
        self.copy = pltpu.make_async_copy(source, target, arrival)
        self.target = target
        self.waiting = True

    def start(self):
        self.copy.start()

    def ready(self):
        if self.waiting:
            self.copy.wait()
            self.waiting = False
        return self.target


def bytes_of(items):
    return sum(math.prod(item.shape) * jnp.dtype(item.dtype).itemsize for item in items)


def in_hbm(item):
    return pltpu.with_memory_space_constraint(item, pltpu.HBM)


def run(kernel, outputs, operands, flops, scratch=(), fetched=(), streamed=(), sent=()):
    inputs = len(operands)
    total = inputs + len(fetched) + len(streamed)
    results = len(outputs) + len(sent)

    def body(*refs):
        sources = refs[inputs:total]
        outs = refs[total : total + results]
        own = refs[total + results : total + results + len(scratch)]
        rest = refs[total + results + len(scratch) :]
        fetches = [
            Fetch(source, target, rest[-1].at[place])
            for place, (source, target) in enumerate(zip(sources, rest[:-1]))
        ]
        fetches += sources[len(fetched) :]
        kernel(fetches, *refs[:inputs], *outs, *own)

    places = [
        (pltpu.SMEM if item.dtype == jnp.int32 else pltpu.VMEM)(item.shape, item.dtype)
        for item in fetched
    ]
    held = bytes_of(
        [ref for ref in list(scratch) + places if ref.memory_space == pltpu.VMEM]
    )
    limit = min(60 << 20, SPARE + held + bytes_of(operands) + 2 * bytes_of(outputs))
    return pl.pallas_call(
        body,
        out_shape=list(outputs) + [pltpu.HBM(item.shape, item.dtype) for item in sent],
        in_specs=[VMEM] * inputs + [HBM] * (total - inputs),
        out_specs=[VMEM] * len(outputs) + [HBM] * len(sent),
        scratch_shapes=list(scratch)
        + places
        + [pltpu.SemaphoreType.DMA((max(1, len(fetched)),))],
        compiler_params=pltpu.CompilerParams(vmem_limit_bytes=limit),
        cost_estimate=pl.CostEstimate(
            flops=flops,
            bytes_accessed=bytes_of(list(operands) + list(fetched) + list(outputs)),
            transcendentals=0,
        ),
    )(*operands, *[in_hbm(item) for item in (*fetched, *streamed)])


def array(shape, dtype):
    return jax.ShapeDtypeStruct(shape, dtype)


def packed_rows(width):
    return -(-width // 2048) * 16


def condition_kernel(fetches, packed_out, noisy_out, kind_out, gram_out, held, mod_rows, arrivals):
    times, text, time_w, clean_t, noise, embed_w, mod_w, kind_w = fetches
    model_width = held.shape[0]
    rows = model_width // STREAMS
    for fetch in fetches[:-2]:
        fetch.start()
    copies = [
        pltpu.make_async_copy(
            mod_w.at[pl.ds(part * rows, rows)], held.at[pl.ds(part * rows, rows)], arrivals.at[part]
        )
        for part in range(STREAMS)
    ]
    copies.append(pltpu.make_async_copy(kind_w, kind_out, arrivals.at[STREAMS]))
    for copy in copies:
        copy.start()
    student_step, critic_step = steps_of(times)
    step = jnp.where(lax.axis_index("segment") == 0, student_step, critic_step)
    text_ref = text.ready()
    half = text_ref.shape[1] // 2
    places = lax.broadcasted_iota(jnp.int32, (1, half), 1).astype(jnp.float32)
    frequency = jnp.exp(-math.log(10000.0) * places / half)
    angles = jnp.full((1, half), step, jnp.int32).astype(jnp.float32) * frequency
    features = jnp.concatenate([jnp.cos(angles), jnp.sin(angles)], axis=1) + text_ref[...]
    features = jnp.broadcast_to(features, (8, 2 * half)).astype(jnp.bfloat16)
    hidden = dot32(features, time_w.ready()[...])
    hidden = (hidden / (1.0 + jnp.exp(-hidden))).astype(jnp.bfloat16)
    mod_rows[...] = jnp.zeros_like(mod_rows)
    total = None
    for part in range(STREAMS):
        copies[part].wait()
        piece = dot32(
            hidden[:, part * rows : (part + 1) * rows], held[part * rows : (part + 1) * rows]
        )
        total = piece if total is None else total + piece
        if part == STREAMS // 2:
            sigma_student = noise_level(student_step)
            clean_ref, noise_ref = clean_t.ready(), noise.ready()
            noisy = (1.0 - sigma_student) * clean_ref[...].astype(jnp.float32).T + sigma_student * noise_ref[
                :, : clean_ref.shape[0]
            ].astype(jnp.float32)
            noisy = noisy.astype(jnp.bfloat16)
            noisy_out[...] = noisy
            top = noisy.shape[0] // 2
            packed_out[:top] = jnp.concatenate([noisy[:top], noisy[top:]], axis=1)
            central_top, central_low = halves(centred(embed_w.ready()))
            gram = (
                dot32_t(central_top, central_top)
                + dot32_t(central_top, central_low)
                + dot32_t(central_low, central_top)
            )
            gram_out[0], gram_out[1] = halves(gram)
    width = total.shape[1]
    for row, first in enumerate(range(0, width, 128)):
        size = min(128, width - first)
        mod_rows[row : row + 1, :size] = total[:1, first : first + size]
    depth = mod_rows.shape[0]
    top = noisy_out.shape[0] // 2
    packed_out[top : top + depth], packed_out[top + depth :] = halves(mod_rows[...])
    copies[STREAMS].wait()


def rms_scale(values, gain_vec):
    inverse = lax.rsqrt(jnp.mean(values * values, axis=-1, keepdims=True) + EPS)
    unit_vec = values * inverse
    return (unit_vec * gain_vec, unit_vec, inverse)


def rms_back(gradient, unit_vec, inverse, gain_vec):
    scaled = gradient * gain_vec
    return inverse * (scaled - unit_vec * jnp.mean(scaled * unit_vec, axis=-1, keepdims=True))


def centred(embed_ref):
    values = embed_ref[0].astype(jnp.float32)
    return values - jnp.mean(values, axis=1, keepdims=True)


def front(rows, gram, model_width, short, gains, head_outs, proj_ref, inverse_ref, key_ref, value_ref):
    latent_width = gram.shape[1]
    count = len(rows)
    head_width = gains.shape[2]
    scale = 1.0 / math.sqrt(head_width)
    size = rows[0].shape[0]
    short_top = None
    for place in range(count):
        block = rows[place][...]
        spanned = dot32(block, gram[0]) + dot32(block, gram[1])
        squares = jnp.sum(spanned * block.astype(jnp.float32), axis=1, keepdims=True)
        inverse = lax.rsqrt(jnp.maximum(squares, 0.0) / model_width + EPS)
        if short_top is None:
            values = short()
            short_top, short_low = halves(values[:latent_width])
            short_shift = values[latent_width : latent_width + 1]
        projected = inverse * (dot32(block, short_top) + dot32(block, short_low)) + short_shift
        low = place * size
        proj_ref[low : low + size] = projected
        inverse_ref[low : low + size] = jnp.broadcast_to(inverse, (size, 128))
        keys, _, _ = rms_scale(projected[:, head_width : 2 * head_width], gains[0, 1:2])
        key_ref[low : low + size] = keys.astype(jnp.bfloat16)
        value_ref[low : low + size] = projected[:, 2 * head_width :].astype(jnp.bfloat16)
    for place in range(count):
        low = place * size
        queries, _, _ = rms_scale(proj_ref[low : low + size, :head_width], gains[0, :1])
        scores = dot32_t(queries.astype(jnp.bfloat16), key_ref[...]) * scale
        weights = jnp.exp(scores)
        soft_max = weights * (1.0 / jnp.sum(weights, axis=-1, keepdims=True))
        head_outs[place][...] = dot32(soft_max.astype(jnp.bfloat16), value_ref[...]).astype(
            jnp.bfloat16
        )


def stage_kernel(fetches, near, part_out):
    width = part_out.shape[1]
    for place in range(2):

        @pl.when(lax.axis_index("dp") == place)
        def _():
            part_out[...] = near[:, place * width : (place + 1) * width]


def student_front_kernel(count, width, fetches, embed_w, head_w, gram, gains, *refs):
    packed = refs[:count]
    head_outs = refs[count : 2 * count]
    short_out, late_out, mod, rows_ref, sends, *kept = refs[2 * count :]
    model_width = embed_w.shape[2]
    latent_width = embed_w.shape[1]
    size = rows_ref.shape[1]
    half = size // 2
    depth = packed_rows(width)
    parts = [
        piece[half : half + depth].astype(jnp.float32) + piece[half + depth :].astype(jnp.float32)
        for piece in packed
    ]
    for place, part in enumerate(in_order(parts, lax.axis_index("seq"))):
        for row, first in enumerate(range(0, width, 128)):
            lanes = min(128, width - first)
            low = place * width + first
            mod[:, low : low + lanes] = part[row : row + 1, :lanes]
    late = pltpu.make_async_copy(
        mod.at[:, pl.ds(2 * model_width, 3 * model_width)], late_out, sends.at[0]
    )
    late.start()
    for place in range(count):
        rows_ref[place, :half] = packed[place][:half, :latent_width]
        rows_ref[place, half:] = packed[place][:half, latent_width:]
    central = centred(embed_w)
    scale_in = slot_of(mod, 1, model_width, 0, model_width)
    shift_in = slot_of(mod, 0, model_width, 0, model_width)
    in_rows = jnp.concatenate(
        [central * (1.0 + scale_in), jnp.broadcast_to(shift_in, (16, model_width))], axis=0
    )
    in_top, in_low = halves(in_rows)
    in_both = jnp.concatenate([in_top, in_low], axis=0)
    both = jnp.concatenate([dot32(in_both, head_w[kind]) for kind in range(3)], axis=1)
    short = both[: in_rows.shape[0]] + both[in_rows.shape[0] :]
    short_out[...] = short

    @pl.when(lax.axis_index("segment") == 0)
    def _():
        front(
            [rows_ref.at[place] for place in range(count)],
            gram,
            model_width,
            lambda: short,
            gains,
            head_outs,
            *kept,
        )

    late.wait()


def critic_front_kernel(count, model_width, fetches, short, gram, gains, *refs):
    rows = refs[:count]
    head_outs = refs[count : 2 * count]
    kept = refs[2 * count :]

    @pl.when(lax.axis_index("segment") != 0)
    def _():
        front(
            rows,
            gram,
            model_width,
            lambda: short[...],
            gains,
            head_outs,
            *kept,
        )


def tail(late, latent, embed_w, final_t, mixed, heads_w, work, stacked, keep):
    model_width = embed_w.shape[2]
    block = latent[...]
    if stacked:
        joined_heads = jnp.concatenate([piece[...] for piece in mixed], axis=1)
    sums = None
    for first in range(0, model_width, TILE):
        span = slice(first, first + TILE)
        if stacked:
            attended = dot32(joined_heads, stacked_tile(heads_w, first))
        else:
            attended = None
            for piece, pieces in zip(mixed, heads_w):
                product = dot32(piece[...], head_tile(pieces, first, TILE))
                attended = product if attended is None else attended + product
        mod = late.ready()
        residual = (
            dot32(block, embed_w[0, :, span]) + slot_of(mod, 0, model_width, first, TILE) * attended
        )
        work[:, span] = residual
        part = lane_sum(residual)
        sums = part if sums is None else sums + part
    row_mean = jnp.sum(sums, axis=1, keepdims=True) / model_width
    sums = None
    for first in range(0, model_width, TILE):
        span = slice(first, first + TILE)
        middle = work[:, span] - row_mean
        work[:, span] = middle
        part = lane_sum(middle * middle)
        sums = part if sums is None else sums + part
    inverse = lax.rsqrt(jnp.sum(sums, axis=1, keepdims=True) / model_width + EPS)
    keep(inverse)
    result = None
    final_w = final_t.ready()
    for first in range(0, model_width, TILE):
        span = slice(first, first + TILE)
        normed = work[:, span] * inverse
        work[:, span] = normed
        final_in = (
            normed * (1.0 + slot_of(mod, 2, model_width, first, TILE))
            + slot_of(mod, 1, model_width, first, TILE)
        ).astype(jnp.bfloat16)
        product = dot32_t(final_in, final_w[:, span])
        result = product if result is None else result + product
    return (result, inverse)


def student_tail_kernel(count, sizes, fetches, latent, embed_w, *refs):
    mixed = refs[:count]
    heads_w, refs = nested(refs[count:], sizes)
    pair_ref, saved_out, inverse_out, work, inverse_ref, sends = refs
    late, final_t, noise, times = fetches
    latent_width = latent.shape[1]

    @pl.when(lax.axis_index("segment") == 0)
    def _():
        for fetch in fetches:
            fetch.start()
        copies = [
            pltpu.make_async_copy(mixed[place], saved_out.at[place], sends.at[place])
            for place in range(count)
        ]
        for copy in copies:
            copy.start()
        levels = []

        def keep(inverse):
            levels.extend(noise_level(step) for step in steps_of(times))
            sigma_student, sigma_critic = levels
            rows, lanes = inverse_ref.shape
            rest = (lanes - latent_width) // 2
            inverse_ref[...] = jnp.concatenate(
                [
                    jnp.broadcast_to(inverse, (rows, latent_width)),
                    jnp.broadcast_to(sigma_student, (rows, rest)),
                    jnp.broadcast_to(sigma_critic, (rows, rest)),
                ],
                axis=1,
            )
            copies.append(pltpu.make_async_copy(inverse_ref, inverse_out, sends.at[count]))
            copies[-1].start()

        velocity, _ = tail(
            late, latent, embed_w, final_t, mixed, heads_w, work, stacked=True, keep=keep
        )
        sigma_student, sigma_critic = levels
        sample = latent[...].astype(jnp.float32) - sigma_student * velocity
        second = noise.ready()[:, latent_width:].astype(jnp.float32)
        critic = (1.0 - sigma_critic) * sample + sigma_critic * second
        pair_ref[...] = jnp.concatenate([critic, sample], axis=1).astype(jnp.bfloat16)
        for copy in copies:
            copy.wait()


def pick_kernel(sections, fetches, own, *refs):
    moved = refs[: sections - 1]
    pair_ref, rows_ref = refs[sections - 1 :]
    section = lax.axis_index("segment")
    for place in range(sections):

        @pl.when(section == place)
        def _():
            chosen = own if place == 0 else moved[place - 1]
            pair_ref[...] = chosen[...]
            rows_ref[...] = chosen[:, : rows_ref.shape[1]]


def critic_tail_kernel(count, sizes, fetches, pair, embed_w, *refs):
    mixed = refs[:count]
    heads_w, refs = nested(refs[count:], sizes)
    grads = refs[:count]
    inverse_ref, term_ref, target_ref, direct_ref, latent, work, other = refs[count:]
    late, final_t, noise, times = fetches
    model_width = embed_w.shape[2]
    latent_width = latent.shape[1]
    section = lax.axis_index("segment")

    @pl.when(section != 0)
    def _():
        for fetch in fetches:
            fetch.start()
        both = pair[...].astype(jnp.float32)
        sample = both[:, latent_width:]
        latent[...] = pair[:, :latent_width]
        result, inverse = tail(
            late,
            latent,
            embed_w,
            final_t,
            mixed,
            heads_w,
            work,
            stacked=False,
            keep=lambda inverse: None,
        )
        mod, final_w = late.ready(), final_t.ready()
        _, critic_step = steps_of(times)
        sigma_critic = noise_level(critic_step)
        inverse_ref[...] = jnp.broadcast_to(inverse, inverse_ref.shape)
        term_ref[...] = (sigma_critic * result).astype(jnp.bfloat16)
        second = noise.ready()[:, latent_width:].astype(jnp.float32)
        target_ref[...] = jnp.where(
            section == 2,
            2.0 * (result - (second - sample)),
            jnp.where(section == 3, 1.0 / (1.0 + jnp.exp(-result)), 0.0),
        )

        @pl.when(section == 1)
        def _():
            gaps = jnp.abs(sample - both[:, :latent_width] + sigma_critic * result)
            error = jnp.sum(jnp.sum(gaps, axis=1, keepdims=True), axis=0, keepdims=True)
            error = error / (gaps.shape[0] * latent_width)
            error_top, error_low = halves(jnp.broadcast_to(error, (16, grads[0].shape[1])))
            for place in range(count):
                grads[place][:16] = error_top
                grads[place][16:32] = error_low

        @pl.when(section == 3)
        def _():
            grad_logit = (-1.0 / (1.0 + jnp.exp(result))).astype(jnp.bfloat16)
            plain, along = None, None
            for first in range(0, model_width, TILE):
                span = slice(first, first + TILE)
                gradient = dot32(grad_logit, final_w[:, span]) * (
                    1.0 + slot_of(mod, 2, model_width, first, TILE)
                )
                other[:, span] = gradient
                part = lane_sum(gradient)
                plain = part if plain is None else plain + part
                part = lane_sum(gradient * work[:, span])
                along = part if along is None else along + part
            plain = jnp.sum(plain, axis=1, keepdims=True) / model_width
            along = jnp.sum(along, axis=1, keepdims=True) / model_width
            direct = None
            totals = [None] * count
            for first in range(0, model_width, TILE):
                span = slice(first, first + TILE)
                grad_residual = inverse * (other[:, span] - plain - work[:, span] * along)
                top, low = halves(grad_residual)
                product = dot32_t(top, embed_w[0, :, span]) + dot32_t(low, embed_w[0, :, span])
                direct = product if direct is None else direct + product
                grad_attended = (slot_of(mod, 0, model_width, first, TILE) * grad_residual).astype(
                    jnp.bfloat16
                )
                for place in range(count):
                    product = dot32_t(grad_attended, head_tile(heads_w[place], first, TILE))
                    held = totals[place]
                    totals[place] = product if held is None else held + product
            direct_ref[...] = direct
            for place in range(count):
                grads[place][...] = totals[place].astype(jnp.bfloat16)


def judge_back_kernel(count, model_width, fetches, short_in, gram, gains, proj_ref, inverse_ref, key_ref, value_ref, term, *refs):
    rows = refs[:count]
    grads = refs[count : 2 * count]
    keep_ref, send_ref, real_ref, grad_key_ref, grad_value_ref, grad_query_ref = refs[2 * count :]
    section = lax.axis_index("segment")
    latent_width = rows[0].shape[1]
    head_width = gains.shape[2]
    scale = 1.0 / math.sqrt(head_width)
    size = rows[0].shape[0]

    @pl.when(section == 3)
    def _():
        for place in range(count):
            low = place * size
            span = slice(low, low + size)
            queries, _, _ = rms_scale(proj_ref[span, :head_width], gains[0, :1])
            query_b = queries.astype(jnp.bfloat16)
            weights = jnp.exp(dot32_t(query_b, key_ref[...]) * scale)
            soft_max = weights * (1.0 / jnp.sum(weights, axis=-1, keepdims=True))
            grad_out = grads[place][...]
            grad_soft = dot32_t(grad_out, value_ref[...])
            grad_value = dot32_first(soft_max.astype(jnp.bfloat16), grad_out)
            grad_scores = soft_max * (
                grad_soft - jnp.sum(soft_max * grad_soft, axis=-1, keepdims=True)
            )
            grad_scores_b = (grad_scores * scale).astype(jnp.bfloat16)
            grad_query_ref[span] = dot32(grad_scores_b, key_ref[...])
            grad_key = dot32_first(grad_scores_b, query_b)
            if place == 0:
                grad_value_ref[...] = grad_value
                grad_key_ref[...] = grad_key
            else:
                grad_value_ref[...] += grad_value
                grad_key_ref[...] += grad_key
        gram_top, gram_low = gram[0], gram[1]
        short_top, short_low = halves(short_in[:latent_width])
        for place in range(count):
            low = place * size
            span = slice(low, low + size)
            projected = proj_ref[span]
            _, q_unit, q_inverse = rms_scale(projected[:, :head_width], gains[0, :1])
            _, k_unit, k_inverse = rms_scale(
                projected[:, head_width : 2 * head_width], gains[0, 1:2]
            )
            grad_q = rms_back(grad_query_ref[span], q_unit, q_inverse, gains[0, :1])
            grad_k = rms_back(grad_key_ref[span], k_unit, k_inverse, gains[0, 1:2])
            grad_proj = jnp.concatenate([grad_q, grad_k, grad_value_ref[span]], axis=1).astype(
                jnp.bfloat16
            )
            through = dot32_t(grad_proj, short_top) + dot32_t(grad_proj, short_low)
            block = rows[place][...]
            along = jnp.sum(through * block.astype(jnp.float32), axis=1, keepdims=True) / model_width
            spanned = dot32(block, gram_top) + dot32(block, gram_low)
            inverse = inverse_ref[span, :1]
            target_ref = send_ref if place % 2 else keep_ref
            target_ref[place // 2] = (
                inverse * (through - spanned * (inverse * inverse * along))
            ).astype(jnp.bfloat16)

    @pl.when(section == 1)
    def _():
        error = None
        for grad in grads:
            part = grad[:16, :latent_width].astype(jnp.float32) + grad[
                16:32, :latent_width
            ].astype(jnp.float32)
            error = part if error is None else error + part
        real_ref[:size] = term[...]
        real_ref[size : size + 16], real_ref[size + 16 :] = halves(error / count + EPS)


def merge_kernel(fetches, direct, keep, moved, *outs):
    @pl.when(lax.axis_index("segment") == 3)
    def _():
        for place, out in enumerate(outs):
            total = keep[place].astype(jnp.float32) + moved[place].astype(jnp.float32)
            if place == 0:
                total = total + direct[...]
            out[...] = total.astype(jnp.bfloat16)


def outer_kernel(
    count,
    fetches,
    real,
    fake,
    target_in,
    student_rows,
    pair,
    student_mixed,
    student_inverse,
    critic_inverse,
    *refs,
):
    critic_mixed = refs[:count]
    arrived = refs[count : count + count // 2]
    sums_ref, sample_ref = refs[count + count // 2 :]
    section = lax.axis_index("segment")
    place = lax.axis_index("seq")
    latent_width = student_rows.shape[1]
    rows = student_rows.shape[0]

    def collect(target, inverse, latent, mixed):
        target = target.astype(jnp.bfloat16)
        weighted = inverse[:, :latent_width] * target.astype(jnp.float32)
        top, low = halves(weighted)
        for offset in range(count):
            piece = mixed[offset][...]
            sums_ref[place ^ offset] = (dot32_first(top, piece) + dot32_first(low, piece)).astype(
                jnp.bfloat16
            )
        near = dot32_first(top, latent) + dot32_first(low, latent)
        ones = jnp.ones((target.shape[0], sums_ref.shape[2] - latent_width), jnp.bfloat16)
        sums_ref[count] = jnp.concatenate([near, dot32_first(target, ones)], axis=1).astype(
            jnp.bfloat16
        )

    @pl.when(section == 0)
    def _():
        lanes = student_inverse.shape[1]
        middle = (lanes + latent_width) // 2
        sigma_student = student_inverse[:1, latent_width : latent_width + 1]
        sigma_critic = student_inverse[:1, middle : middle + 1]
        adverse = arrived[0][...].astype(jnp.float32)
        for part in arrived[1:]:
            adverse = adverse + part[...].astype(jnp.float32)
        adverse = (1.0 - sigma_critic) * adverse
        spread = (real[rows : rows + 1] .astype(jnp.float32) + real[rows + 16 : rows + 17].astype(jnp.float32))[
            :, :1
        ]
        gap = real[:rows].astype(jnp.float32) - fake[...].astype(jnp.float32)
        sample_grad = gap / spread + ADV_WEIGHT * adverse
        sample_ref[...] = sample_grad.astype(jnp.bfloat16)
        target = -sigma_student * sample_grad
        mixed = [student_mixed.at[offset] for offset in range(count)]
        collect(target, student_inverse, student_rows[...], mixed)

    @pl.when(section == 1)
    def _():
        sums_ref[...] = jnp.zeros_like(sums_ref)

    @pl.when(section >= 2)
    def _():
        collect(target_in[...], critic_inverse, pair[:, :latent_width], critic_mixed)


def emit_kernel(fetches, own, to_first, to_second, to_third, grad_ref):
    section = lax.axis_index("segment")
    for place, value in enumerate((own, to_first, to_second, to_third)):

        @pl.when(section == place)
        def _():
            grad_ref[...] = value[...].astype(jnp.float32).T


def expand_kernel(count, groups, sizes, full_rows, fetches, embed_w, *refs):
    heads_w, refs = nested(refs, sizes)
    other_mods = refs[: groups - 1]
    sums = refs[groups - 1 : 3 * groups - 1]
    total_out, work, joined, total_ref, sends = refs[3 * groups - 1 :]
    section = lax.axis_index("segment")
    place = lax.axis_index("seq")
    latent_width = embed_w.shape[1]
    model_width = embed_w.shape[2]

    @pl.when(section == 1)
    def _():
        total_ref[...] = jnp.zeros_like(total_ref)
        copy = pltpu.make_async_copy(total_ref, total_out, sends.at[0])
        copy.start()
        copy.wait()

    @pl.when(section != 1)
    def _():
        (late,) = fetches
        late.start()
        for group in range(groups):
            low = group * latent_width
            joined[:, low : low + latent_width] = sums[2 * group][...].astype(jnp.float32) + sums[
                2 * group + 1
            ][...].astype(jnp.float32)
        near_top = joined[count].astype(jnp.bfloat16)
        heads = jnp.concatenate(
            [joined[place ^ offset].astype(jnp.bfloat16) for offset in range(count)], axis=1
        )
        averages = None
        for first in range(0, model_width, TILE):
            span = slice(first, first + TILE)
            spread = dot32(heads, stacked_tile(heads_w, first))
            near = dot32(near_top[:, :latent_width], embed_w[0, :, span])
            mods = [late.ready(), *other_mods]
            gates = jnp.concatenate(
                [
                    jnp.broadcast_to(
                        slot_of(mod, 0, model_width, first, TILE), (latent_width, TILE)
                    )
                    for mod in mods
                ],
                axis=0,
            )
            value = near + gates * spread
            work[:, span] = value
            part = lane_sum(value)
            averages = part if averages is None else averages + part
        averages = jnp.sum(averages, axis=1, keepdims=True) / model_width
        counts = joined[count][:, latent_width : latent_width + 1]
        copies = []
        for number, first in enumerate(range(0, model_width, TILE)):
            span = slice(first, first + TILE)
            value = work[:, span] - averages
            total = None
            for group in range(groups):
                mine = slice(group * latent_width, (group + 1) * latent_width)
                product = value[mine] * (
                    1.0 + slot_of(mods[group], 2, model_width, first, TILE)
                ) + counts[mine] * slot_of(mods[group], 1, model_width, first, TILE)
                total = product if total is None else total + product
            total_ref[:, span] = total / full_rows
            area = (slice(None), pl.ds(first, TILE))
            copies.append(
                pltpu.make_async_copy(total_ref.at[area], total_out.at[area], sends.at[number])
            )
            copies[-1].start()
        for copy in copies:
            copy.wait()


def step(
    clean, noise, timesteps, text_vec, w_embed, w_time, w_mod, w_qkv, w_out, qk_gain, w_final
):
    sections = lax.axis_size("segment")
    tok_rows = clean.shape[1]
    latent_width = clean.shape[2]
    model_width = w_embed.shape[2]
    mod_width = w_mod.shape[2]
    count = lax.axis_size("seq")
    full_rows = tok_rows * count
    head_width = w_qkv.shape[4]
    bf16, f32 = jnp.bfloat16, jnp.float32
    kind_w = jnp.transpose(w_qkv[0, :, 0], (1, 0, 2))
    final_w = jnp.transpose(w_final[0])
    groups = lax.axis_size("dp")

    def stage(near):
        rows, width = near.shape
        (part,) = run(stage_kernel, [array((rows, width // 2), bf16)], (near,), 1000)
        return part

    heads_w = spread_heads(w_out[0, 0], count, groups, stage)
    sizes = [len(pieces) for pieces in heads_w]
    heads_w = sum(heads_w, [])

    depth = packed_rows(mod_width)
    packed, noisy_student, kind_w, gram = run(
        condition_kernel,
        [
            array((tok_rows // 2 + 2 * depth, 2 * latent_width), bf16),
            array((tok_rows, latent_width), bf16),
            pltpu.VMEM(kind_w.shape, bf16),
            array((2, latent_width, latent_width), bf16),
        ],
        (),
        2 * model_width * mod_width,
        scratch=(
            pltpu.VMEM((model_width, mod_width), bf16),
            pltpu.VMEM((depth, 128), f32),
            pltpu.SemaphoreType.DMA((STREAMS + 1,)),
        ),
        fetched=(timesteps, text_vec, w_time[0], jnp.transpose(clean[0]), noise[0], w_embed),
        streamed=(w_mod[0], kind_w),
    )
    kind_w = pltpu.with_memory_space_constraint(kind_w, pltpu.VMEM)
    packed_all = gather_near(packed, "seq", count)

    head_blocks = [array((tok_rows, head_width), bf16)] * count
    stored = [
        ((full_rows, 3 * head_width), f32),
        ((full_rows, 128), f32),
        ((full_rows, head_width), bf16),
        ((full_rows, head_width), bf16),
    ]
    short_shape = ((latent_width + 16, 3 * head_width), f32)
    *head_outs, short, late_mod = run(
        functools.partial(student_front_kernel, count, mod_width),
        head_blocks + [pltpu.VMEM(*short_shape)],
        (w_embed, kind_w, gram, qk_gain, *packed_all),
        4 * latent_width * model_width * 3 * head_width,
        scratch=[
            pltpu.VMEM((1, 5 * model_width), f32),
            pltpu.VMEM((count, tok_rows, latent_width), bf16),
            pltpu.SemaphoreType.DMA((1,)),
        ]
        + [pltpu.VMEM(shape, kind) for shape, kind in stored],
        sent=[array((1, 3 * model_width), f32)],
    )
    student_mixed = scatter_near(head_outs, "seq", count)
    late_mods = gather_near(late_mod, "dp", groups)
    work = pltpu.VMEM((tok_rows, model_width), f32)
    inverse_shape = array((tok_rows, 128), f32)
    pair, saved, student_inverse = run(
        functools.partial(student_tail_kernel, count, sizes),
        [array((tok_rows, 2 * latent_width), bf16)],
        (noisy_student, w_embed, *student_mixed, *heads_w),
        2 * tok_rows * model_width * head_width * count,
        scratch=(
            work,
            pltpu.VMEM((tok_rows, 128), f32),
            pltpu.SemaphoreType.DMA((count + 1,)),
        ),
        fetched=(late_mod, final_w, noise[0], timesteps),
        sent=[array((count, tok_rows, head_width), bf16), inverse_shape],
    )
    moved = [lax.ppermute(pair, "segment", [(0, place)]) for place in range(1, sections)]
    pair, own_rows = run(
        functools.partial(pick_kernel, sections),
        [
            array((tok_rows, 2 * latent_width), bf16),
            array((tok_rows, latent_width), bf16),
        ],
        (pair, *moved),
        1000,
    )
    critic_rows = gather_near(own_rows, "seq", count)
    *head_outs, proj, inverse, keys, values = run(
        functools.partial(critic_front_kernel, count, model_width),
        head_blocks + [array(shape, kind) for shape, kind in stored],
        (
            pltpu.with_memory_space_constraint(short, pltpu.VMEM),
            gram,
            qk_gain,
            *critic_rows,
        ),
        4 * latent_width * model_width * full_rows,
    )
    critic_mixed = scatter_near(head_outs, "seq", count)
    small = array((tok_rows, latent_width), f32)
    thin = array((tok_rows, latent_width), bf16)
    *grad_heads, critic_inverse, term_rows, target, direct = run(
        functools.partial(critic_tail_kernel, count, sizes),
        head_blocks + [inverse_shape, thin, small, small],
        (pair, w_embed, *critic_mixed, *heads_w),
        4 * tok_rows * model_width * head_width * count,
        scratch=(pltpu.VMEM((tok_rows, latent_width), bf16), work, work),
        fetched=(late_mod, final_w, noise[0], timesteps),
    )
    grad_blocks = scatter_near(grad_heads, "seq", count)
    fake = lax.ppermute(term_rows, "segment", swaps(sections, 2))
    half = count // 2
    rows_shape = array((half, tok_rows, latent_width), bf16)
    keep, away, real = run(
        functools.partial(judge_back_kernel, count, model_width),
        [rows_shape, rows_shape, array((tok_rows + 32, latent_width), bf16)],
        (short, gram, qk_gain, proj, inverse, keys, values, term_rows, *critic_rows, *grad_blocks),
        10 * full_rows * full_rows * head_width,
        scratch=(pltpu.VMEM((full_rows, head_width), f32),) * 3,
    )
    moved = lax.ppermute(away, "seq", swaps(count, 1))
    real = lax.ppermute(real, "segment", swaps(sections, 1))
    parts = run(merge_kernel, [thin] * half, (direct, keep, moved), 1000)
    to_student = [
        lax.ppermute(
            part,
            ("segment", "seq"),
            [
                (place * count + row, (place + 1) % sections * count + (row ^ (2 * index)))
                for place in range(sections)
                for row in range(count)
            ],
        )
        for index, part in enumerate(parts)
    ]
    sums, sample_grad = run(
        functools.partial(outer_kernel, count),
        [array((count + 1, latent_width, 128), bf16), thin],
        (
            real,
            fake,
            target,
            noisy_student,
            pair,
            saved,
            student_inverse,
            critic_inverse,
            *critic_mixed,
            *to_student,
        ),
        2 * tok_rows * latent_width * head_width * (count + 1),
    )
    ends = [(place, sections - 1 - place) for place in range(sections)]
    to_third = lax.ppermute(sample_grad, "segment", ends)
    to_second = lax.ppermute(sample_grad, "segment", swaps(sections, 2))
    to_first = lax.ppermute(sample_grad, "segment", swaps(sections, 1))
    last = count // 2
    bit = 1
    while bit < last:
        moved = lax.ppermute(sums, "seq", swaps(count, bit))
        sums = (sums.astype(f32) + moved.astype(f32)).astype(bf16)
        bit *= 2
    sums_all = []
    for group in range(groups):
        for offset in (0, last):
            moves = [
                (place * groups + batch, (place ^ offset) * groups + (batch ^ group))
                for place in range(count)
                for batch in range(groups)
            ]
            sums_all.append(
                sums if offset == group == 0 else lax.ppermute(sums, ("seq", "dp"), moves)
            )
    (total_t,) = run(
        functools.partial(expand_kernel, count, groups, sizes, full_rows),
        [],
        (
            w_embed,
            *heads_w,
            *late_mods[1:],
            *sums_all,
        ),
        4 * groups * latent_width * model_width * head_width * count,
        scratch=(
            pltpu.VMEM((groups * latent_width, model_width), f32),
            pltpu.VMEM((count + 1, groups * latent_width, 128), f32),
            pltpu.VMEM((latent_width, model_width), f32),
            pltpu.SemaphoreType.DMA((model_width // TILE,)),
        ),
        fetched=(late_mod,),
        sent=[array((latent_width, model_width), f32)],
    )
    (grad_t,) = run(
        emit_kernel,
        [array((latent_width, tok_rows), f32)],
        (sample_grad, to_first, to_second, to_third),
        1000,
    )
    return (jnp.transpose(grad_t)[None], jnp.transpose(total_t)[None])


def solution(mesh):
    placed = (
        P("dp", "seq", None),
        P("dp", "seq", None),
        P(),
        P("dp", None),
        P("segment", None, None),
        P("segment", None, None),
        P("segment", None, "seq"),
        P("segment", None, "seq", None, None),
        P("segment", "seq", None, None),
        P("segment", None, None),
        P("segment", None, None),
    )
    return jax.shard_map(
        step,
        mesh=mesh,
        in_specs=placed,
        out_specs=(P("dp", "seq", None), P("segment", None, None)),
        check_vma=False,
    )
```

```python
import functools
import math

import jax
import jax.numpy as jnp
from jax import lax
from jax.experimental import pallas as pl
from jax.experimental.pallas import tpu as pltpu
from jax.sharding import PartitionSpec as P


SHIFT = 7.0
EPS = 1e-06
ADV_WEIGHT = 3.0
TILE = 512
STREAMS = 4
SPARE = 8 << 20
VMEM = pl.BlockSpec(memory_space=pltpu.VMEM)
HBM = pl.BlockSpec(memory_space=pltpu.HBM)


def halves(values):
    top = values.astype(jnp.bfloat16)
    return (top, (values - top.astype(jnp.float32)).astype(jnp.bfloat16))


def swaps(count, offset):
    return [(place, place ^ offset) for place in range(count)]


def gather_near(value, axis, count):
    return [value] + [lax.ppermute(value, axis, swaps(count, offset)) for offset in range(1, count)]


def scatter_near(blocks, axis, count):
    return [blocks[0]] + [
        lax.ppermute(blocks[offset], axis, swaps(count, offset))
        for offset in range(1, count)
    ]


def window_kernel(fetches, part_out, arrival):
    width = part_out.shape[1] // 2
    first = pl.multiple_of(lax.axis_index("dp") * width, width)
    copy = pltpu.make_async_copy(
        fetches[0].at[:, pl.ds(first, 2 * width)], part_out, arrival.at[0]
    )
    copy.start()
    copy.wait()


def spread_heads(own, count, groups, stage):
    held = {0: [own]}
    bit = count // 2
    first = True
    while bit:
        for offset in sorted(held):
            if first and groups == 2:
                width = own.shape[1] // 3
                (part,) = run(
                    window_kernel,
                    [array((own.shape[0], 2 * width), own.dtype)],
                    (),
                    1000,
                    scratch=(pltpu.SemaphoreType.DMA((1,)),),
                    streamed=(own,),
                )
                near = lax.ppermute(part, "seq", swaps(count, bit))
                held[bit] = [near, lax.ppermute(stage(near), "dp", swaps(groups, 1))]
            else:
                held[offset | bit] = [
                    lax.ppermute(piece, "seq", swaps(count, bit))
                    for piece in held[offset]
                ]
        first = False
        bit //= 2
    return [held[offset] for offset in range(count)]


def head_tile(pieces, first, size):
    if len(pieces) == 1:
        return pieces[0][:, first : first + size]
    near, far = pieces
    width = far.shape[1]
    low = slice(first % width, first % width + size)
    high = slice(width + first % width, width + first % width + size)
    choices = (
        (near[:, low], far[:, low]),
        (near[:, high], near[:, low]),
        (far[:, low], near[:, high]),
    )[first // width]
    return jnp.where(lax.axis_index("dp") == 0, *choices)


def stacked_tile(heads_w, first):
    return jnp.concatenate([head_tile(pieces, first, TILE) for pieces in heads_w], axis=0)


def nested(refs, sizes):
    groups, first = [], 0
    for size in sizes:
        groups.append(refs[first : first + size])
        first += size
    return (groups, refs[first:])


def in_order(pieces, own_place):
    ordered = list(pieces)
    bit = 1
    while bit < len(ordered):
        flipped = (own_place & bit) != 0
        ordered = [
            jnp.where(flipped, ordered[place ^ bit], ordered[place])
            for place in range(len(ordered))
        ]
        bit *= 2
    return ordered


def dot32(left, right):
    return jnp.dot(left, right, preferred_element_type=jnp.float32)


def dot32_t(left, right):
    return lax.dot_general(
        left, right, (((1,), (1,)), ((), ())), preferred_element_type=jnp.float32
    )


def dot32_first(left, right):
    return lax.dot_general(
        left, right, (((0,), (0,)), ((), ())), preferred_element_type=jnp.float32
    )


def steps_of(times):
    times_ref = times.ready()
    place = lax.axis_index("dp")
    return (times_ref[place, 0], times_ref[place, 1])


def noise_level(step):
    fraction = jnp.full((1, 1), step, jnp.int32).astype(jnp.float32) / 1000.0
    return SHIFT * fraction / (1.0 + (SHIFT - 1.0) * fraction)


def slot_of(mod_ref, slot, width, first, size):
    return mod_ref[:, slot * width + first : slot * width + first + size]


def lane_sum(values):
    total = values[:, :128]
    for first in range(128, values.shape[1], 128):
        total = total + values[:, first : first + 128]
    return total


class Fetch:
    def __init__(self, source, target, arrival):
        self.copy = pltpu.make_async_copy(source, target, arrival)
        self.target = target
        self.waiting = True

    def start(self):
        self.copy.start()

    def ready(self):
        if self.waiting:
            self.copy.wait()
            self.waiting = False
        return self.target


def bytes_of(items):
    return sum(math.prod(item.shape) * jnp.dtype(item.dtype).itemsize for item in items)


def in_hbm(item):
    return pltpu.with_memory_space_constraint(item, pltpu.HBM)


def run(kernel, outputs, operands, flops, scratch=(), fetched=(), streamed=(), sent=()):
    inputs = len(operands)
    total = inputs + len(fetched) + len(streamed)
    results = len(outputs) + len(sent)

    def body(*refs):
        sources = refs[inputs:total]
        outs = refs[total : total + results]
        own = refs[total + results : total + results + len(scratch)]
        rest = refs[total + results + len(scratch) :]
        fetches = [
            Fetch(source, target, rest[-1].at[place])
            for place, (source, target) in enumerate(zip(sources, rest[:-1]))
        ]
        fetches += sources[len(fetched) :]
        kernel(fetches, *refs[:inputs], *outs, *own)

    places = [
        (pltpu.SMEM if item.dtype == jnp.int32 else pltpu.VMEM)(item.shape, item.dtype)
        for item in fetched
    ]
    held = bytes_of(
        [ref for ref in list(scratch) + places if ref.memory_space == pltpu.VMEM]
    )
    limit = min(60 << 20, SPARE + held + bytes_of(operands) + 2 * bytes_of(outputs))
    return pl.pallas_call(
        body,
        out_shape=list(outputs) + [pltpu.HBM(item.shape, item.dtype) for item in sent],
        in_specs=[VMEM] * inputs + [HBM] * (total - inputs),
        out_specs=[VMEM] * len(outputs) + [HBM] * len(sent),
        scratch_shapes=list(scratch)
        + places
        + [pltpu.SemaphoreType.DMA((max(1, len(fetched)),))],
        compiler_params=pltpu.CompilerParams(vmem_limit_bytes=limit),
        cost_estimate=pl.CostEstimate(
            flops=flops,
            bytes_accessed=bytes_of(list(operands) + list(fetched) + list(outputs)),
            transcendentals=0,
        ),
    )(*operands, *[in_hbm(item) for item in (*fetched, *streamed)])


def array(shape, dtype):
    return jax.ShapeDtypeStruct(shape, dtype)


def packed_rows(width):
    return -(-width // 2048) * 16


def condition_kernel(fetches, packed_out, noisy_out, kind_out, gram_out, held, mod_rows, arrivals):
    times, text, time_w, clean_t, noise, embed_w, mod_w, kind_w = fetches
    model_width = held.shape[0]
    rows = model_width // STREAMS
    for fetch in fetches[:-2]:
        fetch.start()
    copies = [
        pltpu.make_async_copy(
            mod_w.at[pl.ds(part * rows, rows)], held.at[pl.ds(part * rows, rows)], arrivals.at[part]
        )
        for part in range(STREAMS)
    ]
    copies.append(pltpu.make_async_copy(kind_w, kind_out, arrivals.at[STREAMS]))
    for copy in copies:
        copy.start()
    student_step, critic_step = steps_of(times)
    step = jnp.where(lax.axis_index("segment") == 0, student_step, critic_step)
    text_ref = text.ready()
    half = text_ref.shape[1] // 2
    places = lax.broadcasted_iota(jnp.int32, (1, half), 1).astype(jnp.float32)
    frequency = jnp.exp(-math.log(10000.0) * places / half)
    angles = jnp.full((1, half), step, jnp.int32).astype(jnp.float32) * frequency
    features = jnp.concatenate([jnp.cos(angles), jnp.sin(angles)], axis=1) + text_ref[...]
    features = jnp.broadcast_to(features, (8, 2 * half)).astype(jnp.bfloat16)
    hidden = dot32(features, time_w.ready()[...])
    hidden = (hidden / (1.0 + jnp.exp(-hidden))).astype(jnp.bfloat16)
    mod_rows[...] = jnp.zeros_like(mod_rows)
    total = None
    for part in range(STREAMS):
        copies[part].wait()
        piece = dot32(
            hidden[:, part * rows : (part + 1) * rows], held[part * rows : (part + 1) * rows]
        )
        total = piece if total is None else total + piece
        if part == STREAMS // 2:
            sigma_student = noise_level(student_step)
            clean_ref, noise_ref = clean_t.ready(), noise.ready()
            noisy = (1.0 - sigma_student) * clean_ref[...].astype(jnp.float32).T + sigma_student * noise_ref[
                :, : clean_ref.shape[0]
            ].astype(jnp.float32)
            noisy = noisy.astype(jnp.bfloat16)
            noisy_out[...] = noisy
            top = noisy.shape[0] // 2
            packed_out[:top] = jnp.concatenate([noisy[:top], noisy[top:]], axis=1)
            central_top, central_low = halves(centred(embed_w.ready()))
            gram = (
                dot32_t(central_top, central_top)
                + dot32_t(central_top, central_low)
                + dot32_t(central_low, central_top)
            )
            gram_out[0], gram_out[1] = halves(gram)
    width = total.shape[1]
    for row, first in enumerate(range(0, width, 128)):
        size = min(128, width - first)
        mod_rows[row : row + 1, :size] = total[:1, first : first + size]
    depth = mod_rows.shape[0]
    top = noisy_out.shape[0] // 2
    packed_out[top : top + depth], packed_out[top + depth :] = halves(mod_rows[...])
    copies[STREAMS].wait()


def rms_scale(values, gain_vec):
    inverse = lax.rsqrt(jnp.mean(values * values, axis=-1, keepdims=True) + EPS)
    unit_vec = values * inverse
    return (unit_vec * gain_vec, unit_vec, inverse)


def rms_back(gradient, unit_vec, inverse, gain_vec):
    scaled = gradient * gain_vec
    return inverse * (scaled - unit_vec * jnp.mean(scaled * unit_vec, axis=-1, keepdims=True))


def centred(embed_ref):
    values = embed_ref[0].astype(jnp.float32)
    return values - jnp.mean(values, axis=1, keepdims=True)


def front(rows, gram, model_width, short, gains, head_outs, proj_ref, inverse_ref, key_ref, value_ref):
    latent_width = gram.shape[1]
    count = len(rows)
    head_width = gains.shape[2]
    scale = 1.0 / math.sqrt(head_width)
    size = rows[0].shape[0]
    short_top = None
    for place in range(count):
        block = rows[place][...]
        spanned = dot32(block, gram[0]) + dot32(block, gram[1])
        squares = jnp.sum(spanned * block.astype(jnp.float32), axis=1, keepdims=True)
        inverse = lax.rsqrt(jnp.maximum(squares, 0.0) / model_width + EPS)
        if short_top is None:
            values = short()
            short_top, short_low = halves(values[:latent_width])
            short_shift = values[latent_width : latent_width + 1]
        projected = inverse * (dot32(block, short_top) + dot32(block, short_low)) + short_shift
        low = place * size
        proj_ref[low : low + size] = projected
        inverse_ref[low : low + size] = jnp.broadcast_to(inverse, (size, 128))
        keys, _, _ = rms_scale(projected[:, head_width : 2 * head_width], gains[0, 1:2])
        key_ref[low : low + size] = keys.astype(jnp.bfloat16)
        value_ref[low : low + size] = projected[:, 2 * head_width :].astype(jnp.bfloat16)
    for place in range(count):
        low = place * size
        queries, _, _ = rms_scale(proj_ref[low : low + size, :head_width], gains[0, :1])
        scores = dot32_t(queries.astype(jnp.bfloat16), key_ref[...]) * scale
        weights = jnp.exp(scores)
        soft_max = weights * (1.0 / jnp.sum(weights, axis=-1, keepdims=True))
        head_outs[place][...] = dot32(soft_max.astype(jnp.bfloat16), value_ref[...]).astype(
            jnp.bfloat16
        )


def stage_kernel(fetches, near, part_out):
    width = part_out.shape[1]
    for place in range(2):

        @pl.when(lax.axis_index("dp") == place)
        def _():
            part_out[...] = near[:, place * width : (place + 1) * width]


def student_front_kernel(count, width, fetches, embed_w, head_w, gram, gains, *refs):
    packed = refs[:count]
    head_outs = refs[count : 2 * count]
    short_out, late_out, mod, rows_ref, sends, *kept = refs[2 * count :]
    model_width = embed_w.shape[2]
    latent_width = embed_w.shape[1]
    size = rows_ref.shape[1]
    half = size // 2
    depth = packed_rows(width)
    parts = [
        piece[half : half + depth].astype(jnp.float32) + piece[half + depth :].astype(jnp.float32)
        for piece in packed
    ]
    for place, part in enumerate(in_order(parts, lax.axis_index("seq"))):
        for row, first in enumerate(range(0, width, 128)):
            lanes = min(128, width - first)
            low = place * width + first
            mod[:, low : low + lanes] = part[row : row + 1, :lanes]
    late = pltpu.make_async_copy(
        mod.at[:, pl.ds(2 * model_width, 3 * model_width)], late_out, sends.at[0]
    )
    late.start()
    for place in range(count):
        rows_ref[place, :half] = packed[place][:half, :latent_width]
        rows_ref[place, half:] = packed[place][:half, latent_width:]
    central = centred(embed_w)
    scale_in = slot_of(mod, 1, model_width, 0, model_width)
    shift_in = slot_of(mod, 0, model_width, 0, model_width)
    in_rows = jnp.concatenate(
        [central * (1.0 + scale_in), jnp.broadcast_to(shift_in, (16, model_width))], axis=0
    )
    in_top, in_low = halves(in_rows)
    in_both = jnp.concatenate([in_top, in_low], axis=0)
    both = jnp.concatenate([dot32(in_both, head_w[kind]) for kind in range(3)], axis=1)
    short = both[: in_rows.shape[0]] + both[in_rows.shape[0] :]
    short_out[...] = short

    @pl.when(lax.axis_index("segment") == 0)
    def _():
        front(
            [rows_ref.at[place] for place in range(count)],
            gram,
            model_width,
            lambda: short,
            gains,
            head_outs,
            *kept,
        )

    late.wait()


def critic_front_kernel(count, model_width, fetches, short, embed_w, gram, gains, *refs):
    rows = refs[:count]
    head_outs = refs[count : 2 * count]
    kept = refs[2 * count :]

    @pl.when(lax.axis_index("segment") != 0)
    def _():
        front(
            rows,
            gram,
            model_width,
            lambda: short[...],
            gains,
            head_outs,
            *kept,
        )


def tail(late, latent, embed_w, final_t, mixed, heads_w, work, stacked, keep):
    model_width = embed_w.shape[2]
    block = latent[...]
    if stacked:
        joined_heads = jnp.concatenate([piece[...] for piece in mixed], axis=1)
    sums = None
    for first in range(0, model_width, TILE):
        span = slice(first, first + TILE)
        if stacked:
            attended = dot32(joined_heads, stacked_tile(heads_w, first))
        else:
            attended = None
            for piece, pieces in zip(mixed, heads_w):
                product = dot32(piece[...], head_tile(pieces, first, TILE))
                attended = product if attended is None else attended + product
        mod = late.ready()
        residual = (
            dot32(block, embed_w[0, :, span]) + slot_of(mod, 0, model_width, first, TILE) * attended
        )
        work[:, span] = residual
        part = lane_sum(residual)
        sums = part if sums is None else sums + part
    row_mean = jnp.sum(sums, axis=1, keepdims=True) / model_width
    sums = None
    for first in range(0, model_width, TILE):
        span = slice(first, first + TILE)
        middle = work[:, span] - row_mean
        work[:, span] = middle
        part = lane_sum(middle * middle)
        sums = part if sums is None else sums + part
    inverse = lax.rsqrt(jnp.sum(sums, axis=1, keepdims=True) / model_width + EPS)
    keep(inverse)
    result = None
    final_w = final_t.ready()
    for first in range(0, model_width, TILE):
        span = slice(first, first + TILE)
        normed = work[:, span] * inverse
        work[:, span] = normed
        final_in = (
            normed * (1.0 + slot_of(mod, 2, model_width, first, TILE))
            + slot_of(mod, 1, model_width, first, TILE)
        ).astype(jnp.bfloat16)
        product = dot32_t(final_in, final_w[:, span])
        result = product if result is None else result + product
    return (result, inverse)


def student_tail_kernel(count, sizes, fetches, latent, embed_w, *refs):
    mixed = refs[:count]
    heads_w, refs = nested(refs[count:], sizes)
    pair_ref, saved_out, inverse_out, work, inverse_ref, sends = refs
    late, final_t, noise, times = fetches
    latent_width = latent.shape[1]

    @pl.when(lax.axis_index("segment") == 0)
    def _():
        for fetch in fetches:
            fetch.start()
        copies = [
            pltpu.make_async_copy(mixed[place], saved_out.at[place], sends.at[place])
            for place in range(count)
        ]
        for copy in copies:
            copy.start()
        levels = []

        def keep(inverse):
            levels.extend(noise_level(step) for step in steps_of(times))
            sigma_student, sigma_critic = levels
            rows, lanes = inverse_ref.shape
            rest = (lanes - latent_width) // 2
            inverse_ref[...] = jnp.concatenate(
                [
                    jnp.broadcast_to(inverse, (rows, latent_width)),
                    jnp.broadcast_to(sigma_student, (rows, rest)),
                    jnp.broadcast_to(sigma_critic, (rows, rest)),
                ],
                axis=1,
            )
            copies.append(pltpu.make_async_copy(inverse_ref, inverse_out, sends.at[count]))
            copies[-1].start()

        velocity, _ = tail(
            late, latent, embed_w, final_t, mixed, heads_w, work, stacked=True, keep=keep
        )
        sigma_student, sigma_critic = levels
        sample = latent[...].astype(jnp.float32) - sigma_student * velocity
        second = noise.ready()[:, latent_width:].astype(jnp.float32)
        critic = (1.0 - sigma_critic) * sample + sigma_critic * second
        pair_ref[...] = jnp.concatenate([critic, sample], axis=1).astype(jnp.bfloat16)
        for copy in copies:
            copy.wait()


def pick_kernel(sections, fetches, own, *refs):
    moved = refs[: sections - 1]
    pair_ref, rows_ref = refs[sections - 1 :]
    section = lax.axis_index("segment")
    for place in range(sections):

        @pl.when(section == place)
        def _():
            chosen = own if place == 0 else moved[place - 1]
            pair_ref[...] = chosen[...]
            rows_ref[...] = chosen[:, : rows_ref.shape[1]]


def critic_tail_kernel(count, sizes, fetches, pair, embed_w, *refs):
    mixed = refs[:count]
    heads_w, refs = nested(refs[count:], sizes)
    grads = refs[:count]
    inverse_ref, term_ref, target_ref, direct_ref, latent, work, other = refs[count:]
    late, final_t, noise, times = fetches
    model_width = embed_w.shape[2]
    latent_width = latent.shape[1]
    section = lax.axis_index("segment")

    @pl.when(section != 0)
    def _():
        for fetch in fetches:
            fetch.start()
        both = pair[...].astype(jnp.float32)
        sample = both[:, latent_width:]
        latent[...] = pair[:, :latent_width]
        result, inverse = tail(
            late,
            latent,
            embed_w,
            final_t,
            mixed,
            heads_w,
            work,
            stacked=False,
            keep=lambda inverse: None,
        )
        mod, final_w = late.ready(), final_t.ready()
        _, critic_step = steps_of(times)
        sigma_critic = noise_level(critic_step)
        inverse_ref[...] = jnp.broadcast_to(inverse, inverse_ref.shape)
        term_ref[...] = (sigma_critic * result).astype(jnp.bfloat16)
        second = noise.ready()[:, latent_width:].astype(jnp.float32)
        target_ref[...] = jnp.where(
            section == 2,
            2.0 * (result - (second - sample)),
            jnp.where(section == 3, 1.0 / (1.0 + jnp.exp(-result)), 0.0),
        )

        @pl.when(section == 1)
        def _():
            gaps = jnp.abs(sample - both[:, :latent_width] + sigma_critic * result)
            error = jnp.sum(jnp.sum(gaps, axis=1, keepdims=True), axis=0, keepdims=True)
            error = error / (gaps.shape[0] * latent_width)
            error_top, error_low = halves(jnp.broadcast_to(error, (16, grads[0].shape[1])))
            for place in range(count):
                grads[place][:16] = error_top
                grads[place][16:32] = error_low

        @pl.when(section == 3)
        def _():
            grad_logit = (-1.0 / (1.0 + jnp.exp(result))).astype(jnp.bfloat16)
            plain, along = None, None
            for first in range(0, model_width, TILE):
                span = slice(first, first + TILE)
                gradient = dot32(grad_logit, final_w[:, span]) * (
                    1.0 + slot_of(mod, 2, model_width, first, TILE)
                )
                other[:, span] = gradient
                part = lane_sum(gradient)
                plain = part if plain is None else plain + part
                part = lane_sum(gradient * work[:, span])
                along = part if along is None else along + part
            plain = jnp.sum(plain, axis=1, keepdims=True) / model_width
            along = jnp.sum(along, axis=1, keepdims=True) / model_width
            direct = None
            totals = [None] * count
            for first in range(0, model_width, TILE):
                span = slice(first, first + TILE)
                grad_residual = inverse * (other[:, span] - plain - work[:, span] * along)
                top, low = halves(grad_residual)
                product = dot32_t(top, embed_w[0, :, span]) + dot32_t(low, embed_w[0, :, span])
                direct = product if direct is None else direct + product
                grad_attended = (slot_of(mod, 0, model_width, first, TILE) * grad_residual).astype(
                    jnp.bfloat16
                )
                for place in range(count):
                    product = dot32_t(grad_attended, head_tile(heads_w[place], first, TILE))
                    held = totals[place]
                    totals[place] = product if held is None else held + product
            direct_ref[...] = direct
            for place in range(count):
                grads[place][...] = totals[place].astype(jnp.bfloat16)


def judge_back_kernel(count, model_width, fetches, short_in, gram, gains, proj_ref, inverse_ref, key_ref, value_ref, term, *refs):
    rows = refs[:count]
    grads = refs[count : 2 * count]
    keep_ref, send_ref, real_ref, grad_key_ref, grad_value_ref, grad_query_ref = refs[2 * count :]
    section = lax.axis_index("segment")
    latent_width = rows[0].shape[1]
    head_width = gains.shape[2]
    scale = 1.0 / math.sqrt(head_width)
    size = rows[0].shape[0]

    @pl.when(section == 3)
    def _():
        for place in range(count):
            low = place * size
            span = slice(low, low + size)
            queries, _, _ = rms_scale(proj_ref[span, :head_width], gains[0, :1])
            query_b = queries.astype(jnp.bfloat16)
            weights = jnp.exp(dot32_t(query_b, key_ref[...]) * scale)
            soft_max = weights * (1.0 / jnp.sum(weights, axis=-1, keepdims=True))
            grad_out = grads[place][...]
            grad_soft = dot32_t(grad_out, value_ref[...])
            grad_value = dot32_first(soft_max.astype(jnp.bfloat16), grad_out)
            grad_scores = soft_max * (
                grad_soft - jnp.sum(soft_max * grad_soft, axis=-1, keepdims=True)
            )
            grad_scores_b = (grad_scores * scale).astype(jnp.bfloat16)
            grad_query_ref[span] = dot32(grad_scores_b, key_ref[...])
            grad_key = dot32_first(grad_scores_b, query_b)
            if place == 0:
                grad_value_ref[...] = grad_value
                grad_key_ref[...] = grad_key
            else:
                grad_value_ref[...] += grad_value
                grad_key_ref[...] += grad_key
        gram_top, gram_low = gram[0], gram[1]
        short_top, short_low = halves(short_in[:latent_width])
        for place in range(count):
            low = place * size
            span = slice(low, low + size)
            projected = proj_ref[span]
            _, q_unit, q_inverse = rms_scale(projected[:, :head_width], gains[0, :1])
            _, k_unit, k_inverse = rms_scale(
                projected[:, head_width : 2 * head_width], gains[0, 1:2]
            )
            grad_q = rms_back(grad_query_ref[span], q_unit, q_inverse, gains[0, :1])
            grad_k = rms_back(grad_key_ref[span], k_unit, k_inverse, gains[0, 1:2])
            grad_proj = jnp.concatenate([grad_q, grad_k, grad_value_ref[span]], axis=1).astype(
                jnp.bfloat16
            )
            through = dot32_t(grad_proj, short_top) + dot32_t(grad_proj, short_low)
            block = rows[place][...]
            along = jnp.sum(through * block.astype(jnp.float32), axis=1, keepdims=True) / model_width
            spanned = dot32(block, gram_top) + dot32(block, gram_low)
            inverse = inverse_ref[span, :1]
            target_ref = send_ref if place % 2 else keep_ref
            target_ref[place // 2] = (
                inverse * (through - spanned * (inverse * inverse * along))
            ).astype(jnp.bfloat16)

    @pl.when(section == 1)
    def _():
        error = None
        for grad in grads:
            part = grad[:16, :latent_width].astype(jnp.float32) + grad[
                16:32, :latent_width
            ].astype(jnp.float32)
            error = part if error is None else error + part
        real_ref[:size] = term[...]
        real_ref[size : size + 16], real_ref[size + 16 :] = halves(error / count + EPS)


def merge_kernel(fetches, direct, keep, moved, *outs):
    @pl.when(lax.axis_index("segment") == 3)
    def _():
        for place, out in enumerate(outs):
            total = keep[place].astype(jnp.float32) + moved[place].astype(jnp.float32)
            if place == 0:
                total = total + direct[...]
            out[...] = total.astype(jnp.bfloat16)


def outer_kernel(
    count,
    fetches,
    real,
    fake,
    target_in,
    student_rows,
    pair,
    student_mixed,
    student_inverse,
    critic_inverse,
    *refs,
):
    critic_mixed = refs[:count]
    arrived = refs[count : count + count // 2]
    sums_ref, sample_ref = refs[count + count // 2 :]
    section = lax.axis_index("segment")
    place = lax.axis_index("seq")
    latent_width = student_rows.shape[1]
    rows = student_rows.shape[0]

    def collect(target, inverse, latent, mixed):
        target = target.astype(jnp.bfloat16)
        weighted = inverse[:, :latent_width] * target.astype(jnp.float32)
        top, low = halves(weighted)
        for offset in range(count):
            piece = mixed[offset][...]
            sums_ref[place ^ offset] = (dot32_first(top, piece) + dot32_first(low, piece)).astype(
                jnp.bfloat16
            )
        near = dot32_first(top, latent) + dot32_first(low, latent)
        ones = jnp.ones((target.shape[0], sums_ref.shape[2] - latent_width), jnp.bfloat16)
        sums_ref[count] = jnp.concatenate([near, dot32_first(target, ones)], axis=1).astype(
            jnp.bfloat16
        )

    @pl.when(section == 0)
    def _():
        lanes = student_inverse.shape[1]
        middle = (lanes + latent_width) // 2
        sigma_student = student_inverse[:1, latent_width : latent_width + 1]
        sigma_critic = student_inverse[:1, middle : middle + 1]
        adverse = arrived[0][...].astype(jnp.float32)
        for part in arrived[1:]:
            adverse = adverse + part[...].astype(jnp.float32)
        adverse = (1.0 - sigma_critic) * adverse
        spread = (real[rows : rows + 1] .astype(jnp.float32) + real[rows + 16 : rows + 17].astype(jnp.float32))[
            :, :1
        ]
        gap = real[:rows].astype(jnp.float32) - fake[...].astype(jnp.float32)
        sample_grad = gap / spread + ADV_WEIGHT * adverse
        sample_ref[...] = sample_grad.astype(jnp.bfloat16)
        target = -sigma_student * sample_grad
        mixed = [student_mixed.at[offset] for offset in range(count)]
        collect(target, student_inverse, student_rows[...], mixed)

    @pl.when(section == 1)
    def _():
        sums_ref[...] = jnp.zeros_like(sums_ref)

    @pl.when(section >= 2)
    def _():
        collect(target_in[...], critic_inverse, pair[:, :latent_width], critic_mixed)


def emit_kernel(fetches, own, to_first, to_second, to_third, grad_ref):
    section = lax.axis_index("segment")
    for place, value in enumerate((own, to_first, to_second, to_third)):

        @pl.when(section == place)
        def _():
            grad_ref[...] = value[...].astype(jnp.float32).T


def expand_kernel(count, groups, sizes, full_rows, fetches, embed_w, *refs):
    heads_w, refs = nested(refs, sizes)
    other_mods = refs[: groups - 1]
    sums = refs[groups - 1 : 3 * groups - 1]
    total_out, work, joined, total_ref, sends = refs[3 * groups - 1 :]
    section = lax.axis_index("segment")
    place = lax.axis_index("seq")
    latent_width = embed_w.shape[1]
    model_width = embed_w.shape[2]

    @pl.when(section == 1)
    def _():
        total_ref[...] = jnp.zeros_like(total_ref)
        copy = pltpu.make_async_copy(total_ref, total_out, sends.at[0])
        copy.start()
        copy.wait()

    @pl.when(section != 1)
    def _():
        (late,) = fetches
        late.start()
        for group in range(groups):
            low = group * latent_width
            joined[:, low : low + latent_width] = sums[2 * group][...].astype(jnp.float32) + sums[
                2 * group + 1
            ][...].astype(jnp.float32)
        near_top = joined[count].astype(jnp.bfloat16)
        heads = jnp.concatenate(
            [joined[place ^ offset].astype(jnp.bfloat16) for offset in range(count)], axis=1
        )
        averages = None
        for first in range(0, model_width, TILE):
            span = slice(first, first + TILE)
            spread = dot32(heads, stacked_tile(heads_w, first))
            near = dot32(near_top[:, :latent_width], embed_w[0, :, span])
            mods = [late.ready(), *other_mods]
            gates = jnp.concatenate(
                [
                    jnp.broadcast_to(
                        slot_of(mod, 0, model_width, first, TILE), (latent_width, TILE)
                    )
                    for mod in mods
                ],
                axis=0,
            )
            value = near + gates * spread
            work[:, span] = value
            part = lane_sum(value)
            averages = part if averages is None else averages + part
        averages = jnp.sum(averages, axis=1, keepdims=True) / model_width
        counts = joined[count][:, latent_width : latent_width + 1]
        copies = []
        for number, first in enumerate(range(0, model_width, TILE)):
            span = slice(first, first + TILE)
            value = work[:, span] - averages
            total = None
            for group in range(groups):
                mine = slice(group * latent_width, (group + 1) * latent_width)
                product = value[mine] * (
                    1.0 + slot_of(mods[group], 2, model_width, first, TILE)
                ) + counts[mine] * slot_of(mods[group], 1, model_width, first, TILE)
                total = product if total is None else total + product
            total_ref[:, span] = total / full_rows
            area = (slice(None), pl.ds(first, TILE))
            copies.append(
                pltpu.make_async_copy(total_ref.at[area], total_out.at[area], sends.at[number])
            )
            copies[-1].start()
        for copy in copies:
            copy.wait()


def step(
    clean, noise, timesteps, text_vec, w_embed, w_time, w_mod, w_qkv, w_out, qk_gain, w_final
):
    sections = lax.axis_size("segment")
    tok_rows = clean.shape[1]
    latent_width = clean.shape[2]
    model_width = w_embed.shape[2]
    mod_width = w_mod.shape[2]
    count = lax.axis_size("seq")
    full_rows = tok_rows * count
    head_width = w_qkv.shape[4]
    bf16, f32 = jnp.bfloat16, jnp.float32
    kind_w = jnp.transpose(w_qkv[0, :, 0], (1, 0, 2))
    final_w = jnp.transpose(w_final[0])
    groups = lax.axis_size("dp")

    def stage(near):
        rows, width = near.shape
        (part,) = run(stage_kernel, [array((rows, width // 2), bf16)], (near,), 1000)
        return part

    heads_w = spread_heads(w_out[0, 0], count, groups, stage)
    sizes = [len(pieces) for pieces in heads_w]
    heads_w = sum(heads_w, [])

    depth = packed_rows(mod_width)
    packed, noisy_student, kind_w, gram = run(
        condition_kernel,
        [
            array((tok_rows // 2 + 2 * depth, 2 * latent_width), bf16),
            array((tok_rows, latent_width), bf16),
            pltpu.VMEM(kind_w.shape, bf16),
            array((2, latent_width, latent_width), bf16),
        ],
        (),
        2 * model_width * mod_width,
        scratch=(
            pltpu.VMEM((model_width, mod_width), bf16),
            pltpu.VMEM((depth, 128), f32),
            pltpu.SemaphoreType.DMA((STREAMS + 1,)),
        ),
        fetched=(timesteps, text_vec, w_time[0], jnp.transpose(clean[0]), noise[0], w_embed),
        streamed=(w_mod[0], kind_w),
    )
    kind_w = pltpu.with_memory_space_constraint(kind_w, pltpu.VMEM)
    packed_all = gather_near(packed, "seq", count)

    head_blocks = [array((tok_rows, head_width), bf16)] * count
    stored = [
        ((full_rows, 3 * head_width), f32),
        ((full_rows, 128), f32),
        ((full_rows, head_width), bf16),
        ((full_rows, head_width), bf16),
    ]
    short_shape = ((latent_width + 16, 3 * head_width), f32)
    *head_outs, short, late_mod = run(
        functools.partial(student_front_kernel, count, mod_width),
        head_blocks + [pltpu.VMEM(*short_shape)],
        (w_embed, kind_w, gram, qk_gain, *packed_all),
        4 * latent_width * model_width * 3 * head_width,
        scratch=[
            pltpu.VMEM((1, 5 * model_width), f32),
            pltpu.VMEM((count, tok_rows, latent_width), bf16),
            pltpu.SemaphoreType.DMA((1,)),
        ]
        + [pltpu.VMEM(shape, kind) for shape, kind in stored],
        sent=[array((1, 3 * model_width), f32)],
    )
    student_mixed = scatter_near(head_outs, "seq", count)
    late_mods = gather_near(late_mod, "dp", groups)
    work = pltpu.VMEM((tok_rows, model_width), f32)
    inverse_shape = array((tok_rows, 128), f32)
    pair, saved, student_inverse = run(
        functools.partial(student_tail_kernel, count, sizes),
        [array((tok_rows, 2 * latent_width), bf16)],
        (noisy_student, w_embed, *student_mixed, *heads_w),
        2 * tok_rows * model_width * head_width * count,
        scratch=(
            work,
            pltpu.VMEM((tok_rows, 128), f32),
            pltpu.SemaphoreType.DMA((count + 1,)),
        ),
        fetched=(late_mod, final_w, noise[0], timesteps),
        sent=[array((count, tok_rows, head_width), bf16), inverse_shape],
    )
    moved = [lax.ppermute(pair, "segment", [(0, place)]) for place in range(1, sections)]
    pair, own_rows = run(
        functools.partial(pick_kernel, sections),
        [
            array((tok_rows, 2 * latent_width), bf16),
            array((tok_rows, latent_width), bf16),
        ],
        (pair, *moved),
        1000,
    )
    critic_rows = gather_near(own_rows, "seq", count)
    *head_outs, proj, inverse, keys, values = run(
        functools.partial(critic_front_kernel, count, model_width),
        head_blocks + [array(shape, kind) for shape, kind in stored],
        (
            pltpu.with_memory_space_constraint(short, pltpu.VMEM),
            w_embed,
            gram,
            qk_gain,
            *critic_rows,
        ),
        4 * latent_width * model_width * full_rows,
    )
    critic_mixed = scatter_near(head_outs, "seq", count)
    small = array((tok_rows, latent_width), f32)
    thin = array((tok_rows, latent_width), bf16)
    *grad_heads, critic_inverse, term_rows, target, direct = run(
        functools.partial(critic_tail_kernel, count, sizes),
        head_blocks + [inverse_shape, thin, small, small],
        (pair, w_embed, *critic_mixed, *heads_w),
        4 * tok_rows * model_width * head_width * count,
        scratch=(pltpu.VMEM((tok_rows, latent_width), bf16), work, work),
        fetched=(late_mod, final_w, noise[0], timesteps),
    )
    grad_blocks = scatter_near(grad_heads, "seq", count)
    fake = lax.ppermute(term_rows, "segment", swaps(sections, 2))
    half = count // 2
    rows_shape = array((half, tok_rows, latent_width), bf16)
    keep, away, real = run(
        functools.partial(judge_back_kernel, count, model_width),
        [rows_shape, rows_shape, array((tok_rows + 32, latent_width), bf16)],
        (short, gram, qk_gain, proj, inverse, keys, values, term_rows, *critic_rows, *grad_blocks),
        10 * full_rows * full_rows * head_width,
        scratch=(pltpu.VMEM((full_rows, head_width), f32),) * 3,
    )
    moved = lax.ppermute(away, "seq", swaps(count, 1))
    real = lax.ppermute(real, "segment", swaps(sections, 1))
    parts = run(merge_kernel, [thin] * half, (direct, keep, moved), 1000)
    to_student = [
        lax.ppermute(
            part,
            ("segment", "seq"),
            [
                (place * count + row, (place + 1) % sections * count + (row ^ (2 * index)))
                for place in range(sections)
                for row in range(count)
            ],
        )
        for index, part in enumerate(parts)
    ]
    sums, sample_grad = run(
        functools.partial(outer_kernel, count),
        [array((count + 1, latent_width, 128), bf16), thin],
        (
            real,
            fake,
            target,
            noisy_student,
            pair,
            saved,
            student_inverse,
            critic_inverse,
            *critic_mixed,
            *to_student,
        ),
        2 * tok_rows * latent_width * head_width * (count + 1),
    )
    ends = [(place, sections - 1 - place) for place in range(sections)]
    to_third = lax.ppermute(sample_grad, "segment", ends)
    to_second = lax.ppermute(sample_grad, "segment", swaps(sections, 2))
    to_first = lax.ppermute(sample_grad, "segment", swaps(sections, 1))
    last = count // 2
    bit = 1
    while bit < last:
        moved = lax.ppermute(sums, "seq", swaps(count, bit))
        sums = (sums.astype(f32) + moved.astype(f32)).astype(bf16)
        bit *= 2
    sums_all = []
    for group in range(groups):
        for offset in (0, last):
            moves = [
                (place * groups + batch, (place ^ offset) * groups + (batch ^ group))
                for place in range(count)
                for batch in range(groups)
            ]
            sums_all.append(
                sums if offset == group == 0 else lax.ppermute(sums, ("seq", "dp"), moves)
            )
    (total_t,) = run(
        functools.partial(expand_kernel, count, groups, sizes, full_rows),
        [],
        (
            w_embed,
            *heads_w,
            *late_mods[1:],
            *sums_all,
        ),
        4 * groups * latent_width * model_width * head_width * count,
        scratch=(
            pltpu.VMEM((groups * latent_width, model_width), f32),
            pltpu.VMEM((count + 1, groups * latent_width, 128), f32),
            pltpu.VMEM((latent_width, model_width), f32),
            pltpu.SemaphoreType.DMA((model_width // TILE,)),
        ),
        fetched=(late_mod,),
        sent=[array((latent_width, model_width), f32)],
    )
    (grad_t,) = run(
        emit_kernel,
        [array((latent_width, tok_rows), f32)],
        (sample_grad, to_first, to_second, to_third),
        1000,
    )
    return (jnp.transpose(grad_t)[None], jnp.transpose(total_t)[None])


def solution(mesh):
    placed = (
        P("dp", "seq", None),
        P("dp", "seq", None),
        P(),
        P("dp", None),
        P("segment", None, None),
        P("segment", None, None),
        P("segment", None, "seq"),
        P("segment", None, "seq", None, None),
        P("segment", "seq", None, None),
        P("segment", None, None),
        P("segment", None, None),
    )
    return jax.shard_map(
        step,
        mesh=mesh,
        in_specs=placed,
        out_specs=(P("dp", "seq", None), P("segment", None, None)),
        check_vma=False,
    )
```
